32 devices in a mesh: fsdp: 4 (over z), ctx: 4 (over y, x), tp: 2 (over core).
Axes of the slice: x: 2, y: 2, z: 4, core: 2. Of those that a mesh axis runs over, the one named last changes fastest.
Arguments:
- hidden_in: bfloat16 [16, 1024, 768], P('fsdp', 'ctx'), may hold values from -6 to 6
- valid_mask: int32 [16, 1024], P('fsdp', 'ctx'), may hold values from 0 to 1, as said below
- teacher: bfloat16 [16, 1024, 768], P('fsdp', 'ctx'), may hold values from -6 to 6
- qkv_weight: bfloat16 [768, 3, 768], P('fsdp', None, 'tp'), may hold values from -0.21875 to 0.21875
- qv_bias: float32 [2, 768], P(None, 'tp'), may hold values from -0.6 to 0.6
- out_weight: bfloat16 [768, 768], P('fsdp', 'tp'), may hold values from -1.75 to 1.75
- out_bias: float32 [768], replicated, may hold values from -1.2 to 1.2
- norm1_gain: float32 [768], replicated, may hold values from 0.5 to 1.5
- norm1_shift: float32 [768], replicated, may hold values from -1.2 to 1.2
- up_weight: bfloat16 [768, 3072], P('fsdp', 'tp'), may hold values from -0.21875 to 0.21875
- up_bias: float32 [3072], P('tp'), may hold values from -3 to 3
- down_weight: bfloat16 [768, 3072], P('fsdp', 'tp'), may hold values from -0.109375 to 0.109375
- down_bias: float32 [768], replicated, may hold values from -1.2 to 1.2
- norm2_gain: float32 [768], replicated, may hold values from 0.5 to 1.5
- norm2_shift: float32 [768], replicated, may hold values from -1.2 to 1.2
Outputs:
- layer_out: bfloat16 [16, 1024, 768], P('fsdp', 'ctx')
- input_grad: float32 [16, 1024, 768], P('fsdp', 'ctx')
- loss: float32 [], replicated
- qkv_weight_grad: float32 [768, 3, 768], P('fsdp', None, 'tp')
- qv_bias_grad: float32 [2, 768], P(None, 'tp')
- out_weight_grad: float32 [768, 768], P('fsdp', 'tp')
- out_bias_grad: float32 [768], replicated
- norm1_gain_grad: float32 [768], replicated
- norm1_shift_grad: float32 [768], replicated
- up_weight_grad: float32 [768, 3072], P('fsdp', 'tp')
- up_bias_grad: float32 [3072], P('tp')
- down_weight_grad: float32 [768, 3072], P('fsdp', 'tp')
- down_bias_grad: float32 [768], replicated
- norm2_gain_grad: float32 [768], replicated
- norm2_shift_grad: float32 [768], replicated
The draws below stay inside these ranges and needn't reach their ends.
Inputs may be any that keep to these rules, and one draw needn't show every extreme that they name: `valid_mask`: in each sequence the valid tokens form a prefix that holds a quarter of its 1024 positions or more; the first sequence is valid throughout and the second holds exactly a quarter of them.
All inputs are finite; a program needn't handle non-finite values.
Results may differ from the reference program's by a relative error of at most 0.018.
Values may be sent and summed in bfloat16 or wider, within the bound.
No kernel may reach another device: no remote copies, remote signals or barrier semaphores. Data moves between devices by JAX's collectives and lax.ppermute only.
A program may use at most 320 MiB of HBM per device.

```python
import jax
import jax.numpy as jnp
from jax import lax

D = 768
HEADS = 12
HEAD_DIM = 64
FF = 3072
BLOCK = 256
LEN = 1024
SEQ_TOTAL = 16
TOKENS = 16384


def draw_valid_mask(key, part):
    lengths = jax.random.randint(key, (SEQ_TOTAL,), LEN // 4, LEN + 1)
    seq_index = jnp.arange(SEQ_TOTAL, dtype=jnp.int32)
    lengths = jnp.where(seq_index == 0, LEN, jnp.where(seq_index == 1, LEN // 4, lengths))
    positions = jnp.arange(LEN, dtype=jnp.int32)
    return (positions[None, :] < lengths[:, None]).astype(jnp.int32)


def steps_of(own_key, extent, cuts, least, high):
    def one(dim, shards_of):
        draws = jax.random.uniform(jax.random.fold_in(jax.random.fold_in(own_key, 6), dim), (shards_of,), jnp.float32, least / len(cuts), high / len(cuts))
        return jnp.repeat(jnp.exp(draws), extent[dim] // shards_of).reshape((-1,) + (1,) * (len(extent) - dim - 1))

    gain = one(*cuts[0])
    for cut in cuts[1:]:
        gain = gain * one(*cut)
    return gain


def noise(key, extent, deviation, bound, split=(), kind=jnp.bfloat16):
    gain = steps_of(key, extent, split, -0.22, 0.18) if split else 1.0
    entries = jax.random.normal(key, extent, jnp.float32) * deviation * gain
    return jnp.minimum(jnp.maximum(entries, -bound), bound).astype(kind)


def setup_inputs(seed: int = 0) -> dict:
    keys = jax.random.split(jax.random.key(seed), 16)
    return {
        "hidden_in": noise(keys[0], (SEQ_TOTAL, LEN, D), 1.0, 6.0, ((0, 4), (1, 4))),
        "valid_mask": draw_valid_mask(jax.random.fold_in(keys[15], 71), 0),
        "teacher": noise(keys[2], (SEQ_TOTAL, LEN, D), 1.0, 6.0, ((0, 4), (1, 4))),
        "qkv_weight": noise(keys[3], (D, 3, D), D ** -0.5, 0.21875, ((0, 4), (2, 2))),
        "qv_bias": noise(keys[4], (2, D), 0.1, 0.6, ((1, 2),), jnp.float32),
        "out_weight": noise(keys[5], (D, D), (D // 64) ** -0.5, 1.75, ((0, 4), (1, 2))),
        "out_bias": noise(keys[6], (D,), 0.2, 1.2, (), jnp.float32),
        "norm1_gain": jnp.clip(1.0 + 0.1 * jax.random.normal(keys[7], (D,), jnp.float32), 0.5, 1.5),
        "norm1_shift": noise(keys[8], (D,), 0.2, 1.2, (), jnp.float32),
        "up_weight": noise(keys[9], (D, FF), D ** -0.5, 0.21875, ((0, 4), (1, 2))),
        "up_bias": noise(keys[10], (FF,), 0.5, 3.0, ((0, 2),), jnp.float32),
        "down_weight": noise(keys[11], (D, FF), FF ** -0.5, 0.109375, ((0, 4), (1, 2))),
        "down_bias": noise(keys[12], (D,), 0.2, 1.2, (), jnp.float32),
        "norm2_gain": jnp.clip(1.0 + 0.1 * jax.random.normal(keys[13], (D,), jnp.float32), 0.5, 1.5),
        "norm2_shift": noise(keys[14], (D,), 0.2, 1.2, (), jnp.float32),
    }


@jax.custom_vjp
def low(v):
    return lax.optimization_barrier(v.astype(jnp.bfloat16)).astype(jnp.float32)

@jax.custom_vjp
def low_back(v):
    return v

def low_keep(v):
    return (low(v), None)

def low_pass(kept, grad):
    return (grad,)

def back_keep(v):
    return (v, None)

def back_low(kept, grad):
    return (low(grad),)
low.defvjp(low_keep, low_pass)
low_back.defvjp(back_keep, back_low)
NORM_EPS = 1e-05
MASKED = -1e+30

def layer_norm(values_in, gain_vec, shift_vec):
    row_mean = lax.optimization_barrier(jnp.mean(values_in, axis=-1, keepdims=True))
    centered = values_in - row_mean
    row_var = lax.optimization_barrier(jnp.mean(centered * centered, axis=-1, keepdims=True))
    return centered * lax.rsqrt(row_var + NORM_EPS) * gain_vec + shift_vec

def sequence_forward(seq_in, seq_keep, weights):
    qkv_weight, qv_bias, out_weight, out_bias, norm1_gain, norm1_shift, up_weight, up_bias, down_weight, down_bias, norm2_gain, norm2_shift = weights
    highest = lax.Precision.HIGHEST
    full_bias = jnp.stack([qv_bias[0], jnp.zeros_like(qv_bias[0]), qv_bias[1]])
    projected = jnp.einsum('td,dje->tje', seq_in, qkv_weight, precision=highest) + full_bias
    projected = low(low_back(projected))
    queries = projected[:, 0].reshape(LEN, HEADS, HEAD_DIM)
    keys_in = projected[:, 1].reshape(LEN, HEADS, HEAD_DIM)
    values_in = projected[:, 2].reshape(LEN, HEADS, HEAD_DIM)
    key_blocks = jnp.arange(LEN, dtype=jnp.int32) // BLOCK
    live_keys = seq_keep > 0.5
    scaling = HEAD_DIM ** (-0.5)

    def attend(block_index):
        query_rows = lax.dynamic_slice_in_dim(queries, (block_index * BLOCK).astype(jnp.int32), BLOCK, 0)
        raw_scores = jnp.einsum('qhd,khd->hqk', query_rows, keys_in, precision=highest) * scaling
        allowed = jnp.logical_and(live_keys, key_blocks <= block_index)
        raw_scores = low_back(jnp.where(allowed[None, None, :], raw_scores, MASKED))
        row_top = lax.optimization_barrier(jnp.max(raw_scores, axis=-1, keepdims=True))
        shifted = jnp.exp(raw_scores - row_top)
        softmax_probs = shifted / lax.optimization_barrier(jnp.sum(shifted, axis=-1, keepdims=True))
        return jnp.einsum('hqk,khd->qhd', low(softmax_probs), values_in, precision=highest)
    attended = lax.map(jax.checkpoint(attend), jnp.arange(LEN // BLOCK, dtype=jnp.int32))
    attended = low(low_back(attended.reshape(LEN, D)))
    attn_branch = low_back(jnp.dot(attended, out_weight.T, precision=highest))
    normed1 = layer_norm(seq_in + attn_branch + out_bias, norm1_gain, norm1_shift)
    pre_act = low_back(jnp.dot(low(normed1), up_weight, precision=highest) + up_bias)
    active = low(jax.nn.gelu(pre_act, approximate=False))
    ffn_branch = low_back(jnp.dot(active, down_weight.T, precision=highest))
    return layer_norm(normed1 + ffn_branch + down_bias, norm2_gain, norm2_shift)

def reference(hidden_in, valid_mask, teacher, qkv_weight, qv_bias, out_weight, out_bias, norm1_gain, norm1_shift, up_weight, up_bias, down_weight, down_bias, norm2_gain, norm2_shift):
    weights = tuple((item.astype(jnp.float32) for item in (qkv_weight, qv_bias, out_weight, out_bias, norm1_gain, norm1_shift, up_weight, up_bias, down_weight, down_bias, norm2_gain, norm2_shift)))
    keep_float = valid_mask.astype(jnp.float32)

    def forward(inputs, params):

        def one_seq(carried, seq_item):
            seq_in, seq_keep = seq_item
            return (carried, sequence_forward(seq_in, seq_keep, params))
        _, outputs = lax.scan(one_seq, jnp.zeros((), jnp.float32), (inputs, keep_float))
        return outputs
    output, pullback = jax.vjp(forward, hidden_in.astype(jnp.float32), weights)
    residue = (output - teacher.astype(jnp.float32)) * keep_float[..., None]
    counted = jnp.sum(keep_float)
    loss = jnp.sum(residue * residue) / (counted * D)
    ratio = TOKENS / counted
    grad_input, grads = pullback(residue)
    return (output.astype(jnp.bfloat16), grad_input * ratio, loss, grads[0] * ratio, grads[1] * ratio, grads[2] * ratio, grads[3] * ratio, grads[4] * ratio, grads[5] * ratio, grads[6] * ratio, grads[7] * ratio, grads[8] * ratio, grads[9] * ratio, grads[10] * ratio, grads[11] * ratio)
```

```python
import jax
import jax.numpy as jnp
from jax import lax
from jax.experimental import pallas as pl
from jax.experimental.pallas import tpu as pltpu
from jax.sharding import PartitionSpec as P

HEAD_DIM = 64
NORM_EPS = 1e-05
MASKED = -1e30
LANES = 128


def layer_norm(values_in, gain_vec, shift_vec):
    row_mean = jnp.mean(values_in, axis=-1, keepdims=True)
    centered = values_in - row_mean
    row_var = jnp.mean(centered * centered, axis=-1, keepdims=True)
    return centered * lax.rsqrt(row_var + NORM_EPS) * gain_vec + shift_vec


def gelu_exact(pre_act):
    return jax.nn.gelu(pre_act, approximate=False)


def split_heads(packed):
    return packed.reshape(packed.shape[0], packed.shape[1], packed.shape[2] // HEAD_DIM, HEAD_DIM)


def scores_of(query_heads, key_heads, allowed, scaling):
    raw_scores = (
        jnp.einsum("sqhd,skhd->shqk", query_heads, key_heads, preferred_element_type=jnp.float32)
        * scaling
    )
    return jnp.where(allowed, raw_scores, MASKED)


def rows_by_rows(left, right):
    return lax.dot_general(left, right, (((1,), (1,)), ((), ())), preferred_element_type=jnp.float32)


def plain_dot(left, right):
    return jnp.dot(left, right, preferred_element_type=jnp.float32)


def lanes_of(head, lane):
    own = (lane < HEAD_DIM) if head == 0 else (lane >= HEAD_DIM)
    spare = HEAD_DIM if head == 0 else 0
    return own, lane == spare


def head_operands(query_ref, key_ref, slot, start, block, valid_count, head):
    lane = lax.broadcasted_iota(jnp.int32, (block, LANES), 1)
    own, spare = lanes_of(head, lane)
    position = start + lax.broadcasted_iota(jnp.int32, (block, LANES), 0)
    bias = jnp.where(position < valid_count, 0.0, MASKED)
    rows = pl.ds(slot * block, block)
    query = query_ref[rows, :].astype(jnp.float32) * (HEAD_DIM ** -0.5)
    key = key_ref[rows, :].astype(jnp.float32)
    query_side = jnp.where(spare, 1.0, query).astype(jnp.bfloat16)
    key_side = jnp.where(own, key, jnp.where(spare, bias, 0.0)).astype(jnp.bfloat16)
    return query_side, key_side


def attend_kernel(facts, query_ref, key_ref, value_ref, out_ref, log_ref, *, block):
    place, valid_count = facts[0], facts[1]
    blocks = query_ref.shape[0] // block
    slots = [lax.bitwise_xor(place, jnp.int32(i)) for i in range(blocks)]
    value_t = [
        value_ref[pl.ds(slots[j] * block, block), :].astype(jnp.float32).T.astype(jnp.bfloat16)
        for j in range(blocks)
    ]
    outs = [[] for _ in range(blocks)]
    for head in range(2):
        sides = [
            head_operands(query_ref, key_ref, slots[j], j * block, block, valid_count, head)
            for j in range(blocks)
        ]
        span = slice(head * HEAD_DIM, (head + 1) * HEAD_DIM)
        for i in range(blocks):
            scores = [rows_by_rows(sides[j][1], sides[i][0]) for j in range(i + 1)]
            top = scores[0].max(axis=0, keepdims=True)
            for j in range(1, i + 1):
                top = jnp.maximum(top, scores[j].max(axis=0, keepdims=True))
            total = jnp.zeros_like(top)
            mixed = jnp.zeros((HEAD_DIM, block), jnp.float32)
            for j in range(i + 1):
                weight = jnp.exp(scores[j] - top)
                total = total + weight.sum(axis=0, keepdims=True)
                mixed = mixed + plain_dot(value_t[j][span, :], weight.astype(jnp.bfloat16))
            outs[i].append(mixed / total)
            log_ref[0, head : head + 1, i * block : (i + 1) * block] = top + jnp.log(total)
    for i in range(blocks):
        both = jnp.concatenate(outs[i], axis=0)
        out_ref[pl.ds(slots[i] * block, block), :] = both.T.astype(out_ref.dtype)


def attend_back_kernel(
    facts, query_ref, key_ref, value_ref, grad_ref, log_ref, out_ref, grad_key, grad_value, *, block
):
    place, valid_count = facts[0], facts[1]
    blocks = query_ref.shape[0] // block
    slots = [lax.bitwise_xor(place, jnp.int32(i)) for i in range(blocks)]
    scaling = HEAD_DIM ** -0.5
    lane = lax.broadcasted_iota(jnp.int32, (block, LANES), 1)
    key_t, grads, queries, values = [], [], [], []
    for j in range(blocks):
        rows = pl.ds(slots[j] * block, block)
        key_t.append((key_ref[rows, :].astype(jnp.float32) * scaling).T.astype(jnp.bfloat16))
        grads.append(grad_ref[rows, :])
        queries.append(query_ref[rows, :].astype(jnp.float32) * scaling)
        values.append(value_ref[rows, :].astype(jnp.float32))
    grad_queries = [[] for _ in range(blocks)]
    for head in range(2):
        own, _ = lanes_of(head, lane)
        span = slice(head * HEAD_DIM, (head + 1) * HEAD_DIM)
        sides = [
            head_operands(query_ref, key_ref, slots[j], j * block, block, valid_count, head)
            for j in range(blocks)
        ]
        head_values = [jnp.where(own, item, 0.0).astype(jnp.bfloat16) for item in values]
        for i in range(blocks):
            log_row = log_ref[0, head : head + 1, i * block : (i + 1) * block]
            head_grad = jnp.where(own, grads[i].astype(jnp.float32), 0.0).astype(jnp.bfloat16)
            head_query = jnp.where(own, queries[i], 0.0).astype(jnp.bfloat16)
            probs, pushes = [], []
            delta = jnp.zeros((1, block), jnp.float32)
            for j in range(i + 1):
                prob = jnp.exp(rows_by_rows(sides[j][1], sides[i][0]) - log_row)
                push = rows_by_rows(head_values[j], grads[i])
                delta = delta + (prob * push).sum(axis=0, keepdims=True)
                probs.append(prob)
                pushes.append(push)
            grad_query = jnp.zeros((HEAD_DIM, block), jnp.float32)
            for j in range(i + 1):
                slope = (probs[j] * (pushes[j] - delta)).astype(jnp.bfloat16)
                part_value = plain_dot(probs[j].astype(jnp.bfloat16), head_grad)
                part_key = plain_dot(slope, head_query)
                span_rows = slice(j * block, (j + 1) * block)
                if head == 0 and i == j:
                    grad_value[span_rows, :] = part_value
                    grad_key[span_rows, :] = part_key
                else:
                    grad_value[span_rows, :] += part_value
                    grad_key[span_rows, :] += part_key
                grad_query = grad_query + plain_dot(key_t[j][span, :], slope)
            grad_queries[i].append(grad_query)
    for i in range(blocks):
        rows = pl.ds(slots[i] * block, block)
        both = jnp.concatenate(grad_queries[i], axis=0)
        out_ref[0, rows, :] = both.T.astype(out_ref.dtype)
        span_rows = slice(i * block, (i + 1) * block)
        out_ref[1, rows, :] = grad_key[span_rows, :].astype(out_ref.dtype)
        out_ref[2, rows, :] = grad_value[span_rows, :].astype(out_ref.dtype)


def attend(facts, projected, block):
    length, width = projected.shape
    width = width // 3
    pairs = width // LANES
    column = lambda kind: pl.BlockSpec((length, LANES), lambda pair, facts: (0, kind * pairs + pair))
    return pl.pallas_call(
        lambda *refs: attend_kernel(*refs, block=block),
        grid_spec=pltpu.PrefetchScalarGridSpec(
            num_scalar_prefetch=1,
            grid=(pairs,),
            in_specs=[column(0), column(1), column(2)],
            out_specs=[
                pl.BlockSpec((length, LANES), lambda pair, facts: (0, pair)),
                pl.BlockSpec((1, 2, length), lambda pair, facts: (pair, 0, 0)),
            ],
        ),
        out_shape=[
            jax.ShapeDtypeStruct((length, width), jnp.bfloat16),
            jax.ShapeDtypeStruct((pairs, 2, length), jnp.float32),
        ],
        name="attend",
    )(facts, projected, projected, projected)


def attend_back(facts, projected, grad_attended, log_total, block):
    length, width = grad_attended.shape
    pairs = width // LANES
    column = lambda kind: pl.BlockSpec((length, LANES), lambda pair, facts: (0, kind * pairs + pair))
    return pl.pallas_call(
        lambda *refs: attend_back_kernel(*refs, block=block),
        grid_spec=pltpu.PrefetchScalarGridSpec(
            num_scalar_prefetch=1,
            grid=(pairs,),
            in_specs=[
                column(0),
                column(1),
                column(2),
                pl.BlockSpec((length, LANES), lambda pair, facts: (0, pair)),
                pl.BlockSpec((1, 2, length), lambda pair, facts: (pair, 0, 0)),
            ],
            out_specs=pl.BlockSpec((3, length, LANES), lambda pair, facts: (0, 0, pair)),
            scratch_shapes=[
                pltpu.VMEM((length, LANES), jnp.float32),
                pltpu.VMEM((length, LANES), jnp.float32),
            ],
        ),
        out_shape=jax.ShapeDtypeStruct((3, length, width), jnp.bfloat16),
        name="attend_back",
    )(facts, projected, projected, projected, grad_attended, log_total)


def swaps(count, step):
    return [(place, place ^ step) for place in range(count)]


def swap(values, axis, step):
    return lax.ppermute(values, axis, swaps(lax.axis_size(axis), step))


def add_partner(values, axis="tp"):
    low = values.astype(jnp.bfloat16)
    if lax.axis_size(axis) != 2:
        return lax.psum(low, axis).astype(jnp.float32)
    return low.astype(jnp.float32) + swap(low, axis, 1).astype(jnp.float32)


def butterfly(values, axes):
    for axis in axes:
        count = lax.axis_size(axis)
        step = 1
        while step < count:
            values = values + swap(values, axis, step)
            step *= 2
    return values


def to_sequences(blocks, place):
    count = blocks.shape[0]
    pieces = [lax.dynamic_index_in_dim(blocks, place ^ s, 0, keepdims=False) for s in range(count)]
    pieces = [pieces[0]] + [swap(pieces[s], "ctx", s) for s in range(1, count)]
    return jnp.concatenate(pieces, axis=0)


def from_sequences(rows, place, count):
    pieces = jnp.split(rows, count, axis=0)
    pieces = [pieces[0]] + [swap(pieces[s], "ctx", s) for s in range(1, count)]
    result = jnp.zeros((count,) + pieces[0].shape, rows.dtype)
    for s in range(count):
        result = lax.dynamic_update_index_in_dim(result, pieces[s], place ^ s, 0)
    return result


def reduce_over_ctx(owned):
    count = lax.axis_size("ctx")
    rows = owned.shape[0] // count
    if owned.shape[0] % count or rows % 8 or count & (count - 1):
        return lax.psum(owned, "ctx").astype(jnp.float32)
    place = lax.axis_index("ctx")
    parts = owned.reshape((count, rows) + owned.shape[1:])
    total = lax.dynamic_index_in_dim(parts, place, 0, keepdims=False).astype(jnp.float32)
    for s in range(1, count):
        piece = lax.dynamic_index_in_dim(parts, place ^ s, 0, keepdims=False)
        total = total + swap(piece, "ctx", s).astype(jnp.float32)
    total = total.astype(jnp.bfloat16)
    result = jnp.zeros(parts.shape, jnp.bfloat16)
    result = lax.dynamic_update_index_in_dim(result, total, place, 0)
    for s in range(1, count):
        result = lax.dynamic_update_index_in_dim(result, swap(total, "ctx", s), place ^ s, 0)
    return result.reshape(owned.shape).astype(jnp.float32)


def key_blocks_over_ctx(projected, valid_mask, seq_count, block_len):
    inner_width = projected.shape[1] // 3
    ctx_place = lax.axis_index("ctx")
    key_span = 2 * block_len
    key_own = projected[:, inner_width : 2 * inner_width].reshape(seq_count, block_len, inner_width)
    value_own = projected[:, 2 * inner_width :].reshape(seq_count, block_len, inner_width)
    keep_own = valid_mask.astype(jnp.bfloat16)
    keys_all, values_all, keep_all = (
        lax.all_gather(key_own, "ctx", axis=1, tiled=True),
        lax.all_gather(value_own, "ctx", axis=1, tiled=True),
        lax.all_gather(keep_own, "ctx", axis=1, tiled=True),
    )
    seen_limit = (ctx_place + 1) * block_len
    offsets = jnp.arange(key_span, dtype=jnp.int32)

    def key_block(block_index):
        key_start = block_index * key_span
        key_heads = split_heads(lax.dynamic_slice_in_dim(keys_all, key_start, key_span, 1))
        value_heads = split_heads(lax.dynamic_slice_in_dim(values_all, key_start, key_span, 1))
        live_keys = lax.dynamic_slice_in_dim(keep_all, key_start, key_span, 1) > 0.5
        allowed = jnp.logical_and(live_keys, (key_start + offsets)[None, :] < seen_limit)
        return (key_heads, value_heads, allowed[:, None, None, :])

    return key_block


def spread_attend(projected, key_block, seq_count, block_len):
    inner_width = projected.shape[1] // 3
    head_count = inner_width // HEAD_DIM
    scaling = HEAD_DIM ** (-0.5)
    trip_count = lax.axis_index("ctx") // 2 + 1
    query_heads = split_heads(projected[:, :inner_width].reshape(seq_count, block_len, inner_width))

    def attend_step(block_index, carried):
        run_top, run_total, gathered = carried
        key_heads, value_heads, allowed = key_block(block_index)
        raw_scores = scores_of(query_heads, key_heads, allowed, scaling)
        new_top = jnp.maximum(run_top, jnp.max(raw_scores, axis=-1))
        shrink = jnp.exp(run_top - new_top)
        weights_now = jnp.exp(raw_scores - new_top[..., None])
        run_total = run_total * shrink + jnp.sum(weights_now, axis=-1)
        gathered = gathered * jnp.swapaxes(shrink, 1, 2)[..., None] + jnp.einsum(
            "shqk,skhd->sqhd",
            weights_now.astype(jnp.bfloat16),
            value_heads,
            preferred_element_type=jnp.float32,
        )
        return (new_top, run_total, gathered)

    start_top = jnp.full((seq_count, head_count, block_len), MASKED, jnp.float32)
    empty_heads = jnp.zeros((seq_count, block_len, head_count, HEAD_DIM), jnp.float32)
    run_top, run_total, gathered = lax.fori_loop(
        0, trip_count, attend_step, (start_top, jnp.zeros_like(start_top), empty_heads)
    )
    log_total = run_top + jnp.log(run_total)
    attended_exact = gathered / jnp.swapaxes(run_total, 1, 2)[..., None]
    attended = attended_exact.astype(jnp.bfloat16).reshape(seq_count * block_len, inner_width)
    return attended, (attended_exact, log_total)


def spread_attend_back(projected, grad_attended, kept, key_block, seq_count, block_len):
    attended_exact, log_total = kept
    inner_width = projected.shape[1] // 3
    head_count = inner_width // HEAD_DIM
    scaling = HEAD_DIM ** (-0.5)
    ctx_place = lax.axis_index("ctx")
    trip_count = ctx_place // 2 + 1
    key_span = 2 * block_len
    seq_length = block_len * lax.axis_size("ctx")
    row_count = seq_count * block_len
    query_heads = split_heads(projected[:, :inner_width].reshape(seq_count, block_len, inner_width))
    grad_attended = grad_attended.reshape(seq_count, block_len, head_count, HEAD_DIM)
    delta = jnp.swapaxes(jnp.sum(grad_attended.astype(jnp.float32) * attended_exact, axis=-1), 1, 2)
    empty_heads = jnp.zeros((seq_count, block_len, head_count, HEAD_DIM), jnp.float32)

    def back_step(block_index, carried):
        grad_query, spread = carried
        key_heads, value_heads, allowed = key_block(block_index)
        prob_rows = jnp.exp(
            scores_of(query_heads, key_heads, allowed, scaling) - log_total[..., None]
        )
        push = jnp.einsum(
            "sqhd,skhd->shqk", grad_attended, value_heads, preferred_element_type=jnp.float32
        )
        slope = (prob_rows * (push - delta[..., None])).astype(jnp.bfloat16)
        grad_part = (
            jnp.einsum("shqk,skhd->sqhd", slope, key_heads, preferred_element_type=jnp.float32)
            * scaling
        )
        grad_key = (
            jnp.einsum("shqk,sqhd->skhd", slope, query_heads, preferred_element_type=jnp.float32)
            * scaling
        )
        grad_value = jnp.einsum(
            "shqk,sqhd->skhd",
            prob_rows.astype(jnp.bfloat16),
            grad_attended,
            preferred_element_type=jnp.float32,
        )
        piece = jnp.stack(
            [
                grad_key.reshape(seq_count, key_span, inner_width),
                grad_value.reshape(seq_count, key_span, inner_width),
            ],
            axis=2,
        )
        spread = lax.dynamic_update_slice_in_dim(spread, piece, block_index * key_span, 1)
        return (grad_query + grad_part, spread)

    spread_start = jnp.zeros((seq_count, seq_length, 2, inner_width), jnp.float32)
    grad_query, spread = lax.fori_loop(0, trip_count, back_step, (empty_heads, spread_start))
    own_grads = lax.psum_scatter(
        spread.astype(jnp.bfloat16), "ctx", scatter_dimension=1, tiled=True
    ).reshape(row_count, 2, inner_width)
    return jnp.stack(
        [
            grad_query.reshape(row_count, inner_width).astype(jnp.bfloat16),
            own_grads[:, 0],
            own_grads[:, 1],
        ]
    )


def local(
    hidden_in,
    valid_mask,
    teacher,
    qkv_weight,
    qv_bias,
    out_weight,
    out_bias,
    norm1_gain,
    norm1_shift,
    up_weight,
    up_bias,
    down_weight,
    down_bias,
    norm2_gain,
    norm2_shift,
):
    seq_count, block_len, model_width = hidden_in.shape
    ctx_count = lax.axis_size("ctx")
    place = lax.axis_index("ctx")
    inner_width = qkv_weight.shape[2]
    row_count = seq_count * block_len
    whole = (
        seq_count == ctx_count
        and ctx_count & (ctx_count - 1) == 0
        and block_len % LANES == 0
        and inner_width % LANES == 0
    )
    full_qkv, full_out, full_up, full_down = (
        lax.all_gather(qkv_weight.reshape(-1, 3 * inner_width), "fsdp", axis=0, tiled=True),
        lax.all_gather(out_weight, "fsdp", axis=0, tiled=True),
        lax.all_gather(up_weight, "fsdp", axis=0, tiled=True),
        lax.all_gather(down_weight, "fsdp", axis=0, tiled=True),
    )
    local_counts = jnp.sum(valid_mask.astype(jnp.float32), axis=1)
    if whole:
        flat_in = to_sequences(hidden_in, place)
        teacher_rows = to_sequences(teacher, place)
        counts = butterfly(jnp.broadcast_to(local_counts[:, None], (seq_count, LANES)), ("ctx",))
        valid_count = lax.dynamic_slice(counts, (place, 0), (1, 1)).reshape(()).astype(jnp.int32)
        facts = jnp.stack([place, valid_count])
        row_index = jnp.arange(row_count, dtype=jnp.int32)
        positions = ((row_index // block_len) ^ place) * block_len + row_index % block_len
        keep_rows = (positions < valid_count).astype(jnp.float32)[:, None]
    else:
        flat_in = hidden_in.reshape(row_count, model_width)
        teacher_rows = teacher.reshape(row_count, model_width)
        keep_rows = valid_mask.reshape(row_count, 1).astype(jnp.float32)
    full_bias = jnp.concatenate([qv_bias[0], jnp.zeros_like(qv_bias[0]), qv_bias[1]])
    projected = (
        jnp.dot(flat_in, full_qkv, preferred_element_type=jnp.float32) + full_bias
    ).astype(jnp.bfloat16)
    if whole:
        attended, log_total = attend(facts, projected, block_len)
    else:
        key_block = key_blocks_over_ctx(projected, valid_mask, seq_count, block_len)
        attended, kept = spread_attend(projected, key_block, seq_count, block_len)
    attn_branch = add_partner(
        jnp.einsum("te,de->td", attended, full_out, preferred_element_type=jnp.float32)
    )
    resid1 = flat_in.astype(jnp.float32) + attn_branch + out_bias
    normed1, norm1_back = jax.vjp(layer_norm, resid1, norm1_gain, norm1_shift)
    normed1_low = normed1.astype(jnp.bfloat16)
    pre_act = jnp.dot(normed1_low, full_up, preferred_element_type=jnp.float32) + up_bias
    active, gelu_back = jax.vjp(gelu_exact, pre_act)
    active = active.astype(jnp.bfloat16)
    ffn_branch = add_partner(
        jnp.einsum("tf,df->td", active, full_down, preferred_element_type=jnp.float32)
    )
    resid2 = normed1 + ffn_branch + down_bias
    output, norm2_back = jax.vjp(layer_norm, resid2, norm2_gain, norm2_shift)
    layer_out = output.astype(jnp.bfloat16)
    residue = (output - teacher_rows.astype(jnp.float32)) * keep_rows
    squared = jnp.sum(residue * residue)
    grad_resid2, grad_gain2, grad_shift2 = norm2_back(residue)
    grad_down_bias = jnp.sum(grad_resid2, axis=0)
    grad_resid2_low = grad_resid2.astype(jnp.bfloat16)
    grad_active = jnp.dot(grad_resid2_low, full_down, preferred_element_type=jnp.float32)
    grad_down_weight = jnp.einsum(
        "td,tf->df", grad_resid2_low, active, preferred_element_type=jnp.float32
    )
    grad_pre = gelu_back(grad_active)[0].astype(jnp.bfloat16)
    grad_up_bias = jnp.sum(grad_pre.astype(jnp.float32), axis=0)
    grad_up_weight = jnp.einsum(
        "td,tf->df", normed1_low, grad_pre, preferred_element_type=jnp.float32
    )
    grad_normed1 = grad_resid2 + add_partner(
        jnp.einsum("tf,df->td", grad_pre, full_up, preferred_element_type=jnp.float32)
    )
    grad_resid1, grad_gain1, grad_shift1 = norm1_back(grad_normed1)
    grad_out_bias = jnp.sum(grad_resid1, axis=0)
    grad_resid1_low = grad_resid1.astype(jnp.bfloat16)
    grad_attended = jnp.dot(grad_resid1_low, full_out, preferred_element_type=jnp.float32).astype(
        jnp.bfloat16
    )
    grad_out_weight = jnp.einsum(
        "td,te->de", grad_resid1_low, attended, preferred_element_type=jnp.float32
    )
    if whole:
        grad_qkv = attend_back(facts, projected, grad_attended, log_total, block_len)
    else:
        grad_qkv = spread_attend_back(
            projected, grad_attended, kept, key_block, seq_count, block_len
        )
    grad_qv_bias = jnp.sum(grad_qkv[0::2].astype(jnp.float32), axis=1)
    grad_qkv_weight = jnp.concatenate(
        [
            jnp.einsum("td,te->de", flat_in, grad_qkv[kind], preferred_element_type=jnp.float32)
            for kind in range(3)
        ],
        axis=1,
    )
    grad_input = grad_resid1 + add_partner(
        sum(
            jnp.einsum(
                "te,de->td",
                grad_qkv[kind],
                full_qkv[:, kind * inner_width : (kind + 1) * inner_width],
                preferred_element_type=jnp.float32,
            )
            for kind in range(3)
        )
    )
    hidden_width = up_weight.shape[1]
    small = jnp.concatenate(
        [
            grad_out_bias,
            grad_gain1,
            grad_shift1,
            grad_down_bias,
            grad_gain2,
            grad_shift2,
            grad_qv_bias[0],
            grad_qv_bias[1],
            grad_up_bias,
            jnp.full((LANES,), squared),
            jnp.full((LANES,), jnp.sum(local_counts)),
        ]
    )
    small = butterfly(small.reshape(-1, LANES), ("ctx", "fsdp")).reshape(-1)
    vectors = small[: 6 * model_width].reshape(6, model_width)
    place_now = 6 * model_width
    grad_qv_bias = small[place_now : place_now + 2 * inner_width].reshape(2, inner_width)
    place_now += 2 * inner_width
    grad_up_bias = small[place_now : place_now + hidden_width]
    place_now += hidden_width
    squared = small[place_now]
    counted = small[place_now + LANES]
    local_grads = (grad_qkv_weight, grad_out_weight, grad_up_weight, grad_down_weight)
    owned = [
        lax.psum_scatter(item.astype(jnp.bfloat16), "fsdp", scatter_dimension=0, tiled=True)
        for item in local_grads
    ]
    owned = [reduce_over_ctx(item) for item in owned]
    token_total = float(row_count * ctx_count * lax.axis_size("fsdp"))
    ratio = token_total / counted
    loss = squared / (counted * model_width)
    input_grad = grad_input * ratio
    if whole:
        layer_out = from_sequences(layer_out, place, seq_count)
        input_grad = from_sequences(grad_input.astype(jnp.bfloat16), place, seq_count)
        input_grad = input_grad.astype(jnp.float32) * ratio
    else:
        layer_out = layer_out.reshape(seq_count, block_len, model_width)
        input_grad = input_grad.reshape(seq_count, block_len, model_width)
    return (
        layer_out,
        input_grad,
        loss,
        (owned[0] * ratio).reshape(-1, 3, inner_width),
        grad_qv_bias * ratio,
        owned[1] * ratio,
        vectors[0] * ratio,
        vectors[1] * ratio,
        vectors[2] * ratio,
        owned[2] * ratio,
        grad_up_bias * ratio,
        owned[3] * ratio,
        vectors[3] * ratio,
        vectors[4] * ratio,
        vectors[5] * ratio,
    )


def solution(mesh):
    in_specs = (
        P("fsdp", "ctx", None),
        P("fsdp", "ctx"),
        P("fsdp", "ctx", None),
        P("fsdp", None, "tp"),
        P(None, "tp"),
        P("fsdp", "tp"),
        P(),
        P(),
        P(),
        P("fsdp", "tp"),
        P("tp"),
        P("fsdp", "tp"),
        P(),
        P(),
        P(),
    )
    out_specs = (
        P("fsdp", "ctx", None),
        P("fsdp", "ctx", None),
        P(),
        P("fsdp", None, "tp"),
        P(None, "tp"),
        P("fsdp", "tp"),
        P(),
        P(),
        P(),
        P("fsdp", "tp"),
        P("tp"),
        P("fsdp", "tp"),
        P(),
        P(),
        P(),
    )
    return jax.shard_map(local, mesh=mesh, in_specs=in_specs, out_specs=out_specs, check_vma=False)
```

```python
import jax
import jax.numpy as jnp
from jax import lax
from jax.experimental import pallas as pl
from jax.experimental.pallas import tpu as pltpu
from jax.sharding import PartitionSpec as P

HEAD_DIM = 64
NORM_EPS = 1e-05
MASKED = -1e30
LANES = 128


def layer_norm(values_in, gain_vec, shift_vec):
    row_mean = jnp.mean(values_in, axis=-1, keepdims=True)
    centered = values_in - row_mean
    row_var = jnp.mean(centered * centered, axis=-1, keepdims=True)
    return centered * lax.rsqrt(row_var + NORM_EPS) * gain_vec + shift_vec


def gelu_exact(pre_act):
    return jax.nn.gelu(pre_act, approximate=False)


def split_heads(packed):
    return packed.reshape(packed.shape[0], packed.shape[1], packed.shape[2] // HEAD_DIM, HEAD_DIM)


def scores_of(query_heads, key_heads, allowed, scaling):
    raw_scores = (
        jnp.einsum("sqhd,skhd->shqk", query_heads, key_heads, preferred_element_type=jnp.float32)
        * scaling
    )
    return jnp.where(allowed, raw_scores, MASKED)


def rows_by_rows(left, right):
    return lax.dot_general(left, right, (((1,), (1,)), ((), ())), preferred_element_type=jnp.float32)


def plain_dot(left, right):
    return jnp.dot(left, right, preferred_element_type=jnp.float32)


def lanes_of(head, lane):
    own = (lane < HEAD_DIM) if head == 0 else (lane >= HEAD_DIM)
    spare = HEAD_DIM if head == 0 else 0
    return own, lane == spare


def head_operands(query_ref, key_ref, slot, start, block, valid_count, head):
    lane = lax.broadcasted_iota(jnp.int32, (block, LANES), 1)
    own, spare = lanes_of(head, lane)
    position = start + lax.broadcasted_iota(jnp.int32, (block, LANES), 0)
    bias = jnp.where(position < valid_count, 0.0, MASKED)
    rows = pl.ds(slot * block, block)
    query = query_ref[rows, :].astype(jnp.float32) * (HEAD_DIM ** -0.5)
    key = key_ref[rows, :].astype(jnp.float32)
    query_side = jnp.where(spare, 1.0, query).astype(jnp.bfloat16)
    key_side = jnp.where(own, key, jnp.where(spare, bias, 0.0)).astype(jnp.bfloat16)
    return query_side, key_side


def attend_kernel(facts, query_ref, key_ref, value_ref, out_ref, log_ref, *, block):
    valid_count = facts[0]
    blocks = query_ref.shape[0] // block
    slots = list(range(blocks))
    value_t = [
        value_ref[pl.ds(slots[j] * block, block), :].astype(jnp.float32).T.astype(jnp.bfloat16)
        for j in range(blocks)
    ]
    outs = [[] for _ in range(blocks)]
    for head in range(2):
        sides = [
            head_operands(query_ref, key_ref, slots[j], j * block, block, valid_count, head)
            for j in range(blocks)
        ]
        span = slice(head * HEAD_DIM, (head + 1) * HEAD_DIM)
        for i in range(blocks):
            scores = [rows_by_rows(sides[j][1], sides[i][0]) for j in range(i + 1)]
            top = scores[0].max(axis=0, keepdims=True)
            for j in range(1, i + 1):
                top = jnp.maximum(top, scores[j].max(axis=0, keepdims=True))
            total = jnp.zeros_like(top)
            mixed = jnp.zeros((HEAD_DIM, block), jnp.float32)
            for j in range(i + 1):
                weight = jnp.exp(scores[j] - top)
                total = total + weight.sum(axis=0, keepdims=True)
                mixed = mixed + plain_dot(value_t[j][span, :], weight.astype(jnp.bfloat16))
            outs[i].append(mixed / total)
            log_ref[0, head : head + 1, i * block : (i + 1) * block] = top + jnp.log(total)
    for i in range(blocks):
        both = jnp.concatenate(outs[i], axis=0)
        out_ref[pl.ds(slots[i] * block, block), :] = both.T.astype(out_ref.dtype)


def attend_back_kernel(
    facts,
    query_ref,
    key_ref,
    value_ref,
    grad_ref,
    log_ref,
    out_ref,
    stats_ref,
    grad_key,
    grad_value,
    *,
    block,
):
    valid_count = facts[0]
    blocks = query_ref.shape[0] // block
    slots = list(range(blocks))
    scaling = HEAD_DIM ** -0.5
    lane = lax.broadcasted_iota(jnp.int32, (block, LANES), 1)
    key_t, grads, queries, values = [], [], [], []
    for j in range(blocks):
        rows = pl.ds(slots[j] * block, block)
        key_t.append((key_ref[rows, :].astype(jnp.float32) * scaling).T.astype(jnp.bfloat16))
        grads.append(grad_ref[rows, :])
        queries.append(query_ref[rows, :].astype(jnp.float32) * scaling)
        values.append(value_ref[rows, :].astype(jnp.float32))
    grad_queries = [[] for _ in range(blocks)]
    for head in range(2):
        own, _ = lanes_of(head, lane)
        span = slice(head * HEAD_DIM, (head + 1) * HEAD_DIM)
        sides = [
            head_operands(query_ref, key_ref, slots[j], j * block, block, valid_count, head)
            for j in range(blocks)
        ]
        head_values = [jnp.where(own, item, 0.0).astype(jnp.bfloat16) for item in values]
        for i in range(blocks):
            log_row = log_ref[0, head : head + 1, i * block : (i + 1) * block]
            head_grad = jnp.where(own, grads[i].astype(jnp.float32), 0.0).astype(jnp.bfloat16)
            head_query = jnp.where(own, queries[i], 0.0).astype(jnp.bfloat16)
            probs, pushes = [], []
            delta = jnp.zeros((1, block), jnp.float32)
            for j in range(i + 1):
                prob = jnp.exp(rows_by_rows(sides[j][1], sides[i][0]) - log_row)
                push = rows_by_rows(head_values[j], grads[i])
                delta = delta + (prob * push).sum(axis=0, keepdims=True)
                probs.append(prob)
                pushes.append(push)
            grad_query = jnp.zeros((HEAD_DIM, block), jnp.float32)
            for j in range(i + 1):
                slope = (probs[j] * (pushes[j] - delta)).astype(jnp.bfloat16)
                part_value = plain_dot(probs[j].astype(jnp.bfloat16), head_grad)
                part_key = plain_dot(slope, head_query)
                span_rows = slice(j * block, (j + 1) * block)
                if head == 0 and i == j:
                    grad_value[span_rows, :] = part_value
                    grad_key[span_rows, :] = part_key
                else:
                    grad_value[span_rows, :] += part_value
                    grad_key[span_rows, :] += part_key
                grad_query = grad_query + plain_dot(key_t[j][span, :], slope)
            grad_queries[i].append(grad_query)
    totals = jnp.zeros((1, 3 * LANES), jnp.float32)
    for i in range(blocks):
        rows = pl.ds(slots[i] * block, block)
        both = jnp.concatenate(grad_queries[i], axis=0)
        out_ref[rows, :LANES] = both.T.astype(out_ref.dtype)
        span_rows = slice(i * block, (i + 1) * block)
        out_ref[rows, LANES : 2 * LANES] = grad_key[span_rows, :].astype(out_ref.dtype)
        out_ref[rows, 2 * LANES :] = grad_value[span_rows, :].astype(out_ref.dtype)
        totals += jnp.sum(out_ref[rows, :].astype(jnp.float32), axis=0, keepdims=True)
    stats_ref[...] = jnp.broadcast_to(totals, stats_ref.shape)


def attend(facts, projected, block):
    length, width = projected.shape
    pairs = width // (3 * LANES)
    column = lambda kind: pl.BlockSpec((length, LANES), lambda pair, facts: (0, 3 * pair + kind))
    return pl.pallas_call(
        lambda *refs: attend_kernel(*refs, block=block),
        grid_spec=pltpu.PrefetchScalarGridSpec(
            num_scalar_prefetch=1,
            grid=(pairs,),
            in_specs=[column(0), column(1), column(2)],
            out_specs=[
                pl.BlockSpec((length, LANES), lambda pair, facts: (0, pair)),
                pl.BlockSpec((1, 2, length), lambda pair, facts: (pair, 0, 0)),
            ],
        ),
        out_shape=[
            jax.ShapeDtypeStruct((length, pairs * LANES), jnp.bfloat16),
            jax.ShapeDtypeStruct((pairs, 2, length), jnp.float32),
        ],
        name="attend",
    )(facts, projected, projected, projected)


def attend_back(facts, projected, grad_attended, log_total, block):
    length, width = grad_attended.shape
    pairs = width // LANES
    column = lambda kind: pl.BlockSpec((length, LANES), lambda pair, facts: (0, 3 * pair + kind))
    return pl.pallas_call(
        lambda *refs: attend_back_kernel(*refs, block=block),
        grid_spec=pltpu.PrefetchScalarGridSpec(
            num_scalar_prefetch=1,
            grid=(pairs,),
            in_specs=[
                column(0),
                column(1),
                column(2),
                pl.BlockSpec((length, LANES), lambda pair, facts: (0, pair)),
                pl.BlockSpec((1, 2, length), lambda pair, facts: (pair, 0, 0)),
            ],
            out_specs=[
                pl.BlockSpec((length, 3 * LANES), lambda pair, facts: (0, pair)),
                pl.BlockSpec((8, 3 * LANES), lambda pair, facts: (0, pair)),
            ],
            scratch_shapes=[
                pltpu.VMEM((length, LANES), jnp.float32),
                pltpu.VMEM((length, LANES), jnp.float32),
            ],
        ),
        out_shape=[
            jax.ShapeDtypeStruct((length, 3 * width), jnp.bfloat16),
            jax.ShapeDtypeStruct((8, 3 * width), jnp.float32),
        ],
        name="attend_back",
    )(facts, projected, projected, projected, grad_attended, log_total)


def by_pairs(values):
    kinds, width = values.shape[-2:]
    cut = values.reshape(values.shape[:-1] + (width // LANES, LANES))
    return jnp.swapaxes(cut, -3, -2).reshape(values.shape[:-2] + (kinds * width,))


def by_kinds(values, kinds=3):
    width = values.shape[-1] // kinds
    cut = values.reshape(values.shape[:-1] + (width // LANES, kinds, LANES))
    return jnp.swapaxes(cut, -3, -2).reshape(values.shape[:-1] + (kinds, width))


def assemble_kernel(facts, own_ref, *refs, fsdp, count, rows):
    part_refs, out_ref = refs[:count], refs[count]
    place, depth = facts[0], facts[1]
    out_ref[pl.ds(depth * (rows * count), rows * count), :] = own_ref[...]
    for s in range(count):
        for d in range(1, fsdp):
            start = lax.bitwise_xor(depth, jnp.int32(d)) * (rows * count)
            start = start + lax.bitwise_xor(place, jnp.int32(s)) * rows
            out_ref[pl.ds(pl.multiple_of(start, rows), rows), :] = part_refs[s][
                (d - 1) * rows : d * rows, :
            ]


def assemble(places, own, parts):
    fsdp, count = lax.axis_size("fsdp"), len(parts)
    rows = own.shape[0] // count
    width = 3 * LANES if own.shape[1] % (3 * LANES) == 0 else own.shape[1]
    whole_block = lambda shape: pl.BlockSpec((shape[0], width), lambda step, facts: (0, step))
    out_shape = (fsdp * own.shape[0], own.shape[1])
    return pl.pallas_call(
        lambda *refs: assemble_kernel(*refs, fsdp=fsdp, count=count, rows=rows),
        grid_spec=pltpu.PrefetchScalarGridSpec(
            num_scalar_prefetch=1,
            grid=(own.shape[1] // width,),
            in_specs=[whole_block(own.shape)] + [whole_block(item.shape) for item in parts],
            out_specs=whole_block(out_shape),
        ),
        out_shape=jax.ShapeDtypeStruct(out_shape, own.dtype),
        name="assemble",
    )(places, own, *parts)


def swap(values, axis, step):
    pairs = [(place, place ^ step) for place in range(lax.axis_size(axis))]
    return lax.ppermute(values, axis, pairs)


def swap_all(values, axis):
    return [swap(values, axis, step) for step in range(1, lax.axis_size(axis))]


def relay_all(values, axis):
    if lax.axis_size(axis) != 4:
        return swap_all(values, axis)
    first, second = swap(values, axis, 1), swap(values, axis, 2)
    return [first, second, swap(first, axis, 2)]


def swap_each(pieces, axis):
    return [swap(pieces[step], axis, step) for step in range(1, len(pieces))]


def together(*values):
    return lax.optimization_barrier(values)


def wide(values):
    return values.astype(jnp.float32)


def low(values):
    return values.astype(jnp.bfloat16)


def add_partner(values):
    mine = low(values)
    return wide(mine) + wide(swap(mine, "tp", 1))


def add_up(pieces):
    pieces = [wide(item) for item in pieces]
    while len(pieces) > 1:
        pieces = [pieces[i] + pieces[i + 1] for i in range(0, len(pieces), 2)]
    return pieces[0]


def sum_over(values, axis):
    step = 1
    while step < lax.axis_size(axis):
        values = values + swap(values, axis, step)
        step *= 2
    return values


def deal(pieces, axis):
    return lax.all_to_all(pieces, axis, 0, 0)


def own_half(blocks):
    rows = blocks.shape[1] // 2
    return lax.dynamic_slice_in_dim(blocks, lax.axis_index("tp") * rows, rows, 1)


def row_kernel_stats(stats_ref, step, rows):
    @pl.when(step == 0)
    def _():
        stats_ref[...] = jnp.zeros_like(stats_ref)

    for index, row in enumerate(rows):
        stats_ref[index : index + 1, :] += jnp.sum(row, axis=0, keepdims=True)


def normalize(values):
    mean = jnp.mean(values, axis=-1, keepdims=True)
    centered = values - mean
    scale = lax.rsqrt(jnp.mean(centered * centered, axis=-1, keepdims=True) + NORM_EPS)
    return centered * scale, scale


def normalize_back(grads, normal, scale, gain):
    pushed = grads * gain
    mean = jnp.mean(pushed, axis=-1, keepdims=True)
    along = jnp.mean(pushed * normal, axis=-1, keepdims=True)
    return (pushed - mean - normal * along) * scale


def first_norm_kernel(
    hidden_ref, mine_ref, other_ref, bias_ref, gain_ref, shift_ref, normal_ref, scale_ref, low_ref
):
    branch = mine_ref[...].astype(jnp.float32) + other_ref[...].astype(jnp.float32)
    normal, scale = normalize(hidden_ref[...].astype(jnp.float32) + branch + bias_ref[...])
    normal_ref[...] = normal
    scale_ref[...] = scale
    low_ref[...] = (normal * gain_ref[...] + shift_ref[...]).astype(low_ref.dtype)


def second_norm_kernel(
    facts,
    normal_ref,
    gain1_ref,
    shift1_ref,
    mine_ref,
    other_ref,
    bias_ref,
    gain_ref,
    shift_ref,
    own_teacher_ref,
    other_teacher_ref,
    half_ref,
    grad_ref,
    low_ref,
    stats_ref,
):
    step = pl.program_id(0)
    block = normal_ref.shape[0]
    rows = block // 2
    branch = mine_ref[...].astype(jnp.float32) + other_ref[...].astype(jnp.float32)
    normed1 = normal_ref[...] * gain1_ref[...] + shift1_ref[...]
    normal, scale = normalize(normed1 + branch + bias_ref[...])
    output = normal * gain_ref[...] + shift_ref[...]
    first = facts[1] == 0
    half_ref[0] = jnp.where(first, output[:rows], output[rows:]).astype(half_ref.dtype)
    own, other = own_teacher_ref[0], other_teacher_ref[0]
    own, other = own.astype(jnp.float32), other.astype(jnp.float32)
    teacher = jnp.concatenate(
        [jnp.where(first, own, other), jnp.where(first, other, own)], axis=0
    )
    position = step * block + lax.broadcasted_iota(jnp.int32, (block, 1), 0)
    residue = jnp.where(position < facts[0], output - teacher, 0.0)
    grads = normalize_back(residue, normal, scale, gain_ref[...])
    grad_ref[...] = grads
    low_ref[...] = grads.astype(low_ref.dtype)
    row_kernel_stats(stats_ref, step, [grads, residue * normal, residue, residue * residue])


def first_norm_back_kernel(
    facts,
    grad_ref,
    mine_ref,
    other_ref,
    normal_ref,
    scale_ref,
    gain_ref,
    low_ref,
    half_ref,
    stats_ref,
):
    rows = grad_ref.shape[0] // 2
    branch = mine_ref[...].astype(jnp.float32) + other_ref[...].astype(jnp.float32)
    pushed = grad_ref[...] + branch
    normal = normal_ref[...]
    grads = normalize_back(pushed, normal, scale_ref[...], gain_ref[...])
    low_ref[...] = grads.astype(low_ref.dtype)
    half_ref[0] = jnp.where(facts[1] == 0, grads[:rows], grads[rows:])
    row_kernel_stats(stats_ref, pl.program_id(0), [grads, pushed * normal, pushed])


def by_rows(kernel, name, block, operands, results, facts=None, stats=0):
    def spec(shape):
        if len(shape) == 3:
            return pl.BlockSpec((1,) + shape[1:], lambda step, *_: (step, 0, 0))
        if shape[0] == 1:
            return pl.BlockSpec(shape, lambda step, *_: (0, 0))
        return pl.BlockSpec((block, shape[1]), lambda step, *_: (step, 0))

    length = next(item.shape[0] for item in operands if item.ndim == 2 and item.shape[0] > 1)
    out_specs = [spec(item.shape) for item in results]
    if stats:
        results = results + [jax.ShapeDtypeStruct((8, stats), jnp.float32)]
        out_specs.append(pl.BlockSpec((8, stats), lambda step, *_: (0, 0)))
    return pl.pallas_call(
        kernel,
        grid_spec=pltpu.PrefetchScalarGridSpec(
            num_scalar_prefetch=0 if facts is None else 1,
            grid=(length // block,),
            in_specs=[spec(item.shape) for item in operands],
            out_specs=out_specs,
        ),
        out_shape=results,
        name=name,
    )(*([] if facts is None else [facts]), *operands)


def up_kernel(low_ref, weight_ref, bias_ref, active_ref, slope_ref):
    pre = plain_dot(low_ref[...], weight_ref[...]) + bias_ref[...]
    below = 0.5 * (1.0 + lax.erf(pre * (0.5**0.5)))
    active_ref[...] = (pre * below).astype(active_ref.dtype)
    bell = jnp.exp(-0.5 * pre * pre) * 0.3989422804014327
    slope_ref[...] = (below + pre * bell).astype(slope_ref.dtype)


def grad_pre_kernel(low_ref, weight_ref, slope_ref, out_ref, stats_ref):
    grads = plain_dot(low_ref[...], weight_ref[...]) * slope_ref[...].astype(jnp.float32)
    grads = grads.astype(out_ref.dtype)
    out_ref[...] = grads
    row_kernel_stats(stats_ref, pl.program_id(0), [grads.astype(jnp.float32)])


def wide_layer(kernel, name, block, low, weight, operands, count, stats=0):
    length, width = low.shape[0], weight.shape[1]

    def spec(shape):
        if shape[0] == 1:
            return pl.BlockSpec(shape, lambda step: (0, 0))
        return pl.BlockSpec((block, shape[1]), lambda step: (step, 0))

    out_specs = [pl.BlockSpec((block, width), lambda step: (step, 0))] * count
    out_shape = [jax.ShapeDtypeStruct((length, width), jnp.bfloat16)] * count
    if stats:
        out_specs = out_specs + [pl.BlockSpec((8, width), lambda step: (0, 0))]
        out_shape = out_shape + [jax.ShapeDtypeStruct((8, width), jnp.float32)]
    return pl.pallas_call(
        kernel,
        grid=(length // block,),
        in_specs=[spec(low.shape), pl.BlockSpec(weight.shape, lambda step: (0, 0))]
        + [spec(item.shape) for item in operands],
        out_specs=out_specs,
        out_shape=out_shape,
        name=name,
    )(low, weight, *operands)


def pack_kernel(second_ref, first_ref, up_ref, qkv_ref, count_ref, out_ref):
    width = out_ref.shape[1]
    out_ref[...] = jnp.zeros_like(out_ref)
    out_ref[0:4, :] = second_ref[0:4, :]
    out_ref[4:7, :] = first_ref[0:3, :]
    row = 7
    for ref in (up_ref, qkv_ref, count_ref):
        for start in range(0, ref.shape[1], width):
            span = min(width, ref.shape[1] - start)
            out_ref[row : row + 1, :span] = ref[0:1, start : start + span]
            row += 1


def pack(second, first, up, qkv, count):
    width = second.shape[1]
    rows = 7 + sum(-(-item.shape[1] // width) for item in (up, qkv, count))
    return pl.pallas_call(
        pack_kernel,
        out_shape=jax.ShapeDtypeStruct((-(-rows // 8) * 8, width), jnp.float32),
        name="pack",
    )(second, first, up, qkv, count)


def join_kernel(facts, ratio_ref, own_ref, other_ref, out_ref):
    rows = own_ref.shape[1]
    for ref, half in ((own_ref, facts[0]), (other_ref, 1 - facts[0])):
        values = ref[0].astype(jnp.float32) * ratio_ref[0]
        out_ref[0, pl.ds(pl.multiple_of(half * rows, rows), rows), :] = values.astype(out_ref.dtype)


def join_halves(half, ratio=None, dtype=jnp.bfloat16):
    count, rows, width = half.shape
    ratio = jnp.ones((1,), jnp.float32) if ratio is None else ratio.reshape(1)
    return pl.pallas_call(
        join_kernel,
        grid_spec=pltpu.PrefetchScalarGridSpec(
            num_scalar_prefetch=1,
            grid=(count,),
            in_specs=[pl.BlockSpec(memory_space=pltpu.SMEM)]
            + [pl.BlockSpec((1, rows, width), lambda step, facts: (step, 0, 0))] * 2,
            out_specs=pl.BlockSpec((1, 2 * rows, width), lambda step, facts: (step, 0, 0)),
        ),
        out_shape=jax.ShapeDtypeStruct((count, 2 * rows, width), dtype),
        name="join_halves",
    )(lax.axis_index("tp").reshape(1), ratio, half, swap(half, "tp", 1))


def weight_grad_kernel(places, left_ref, right_ref, *refs, fsdp, count):
    total = lax.dot_general(
        left_ref[...],
        right_ref[...],
        (((0,), (0,)), ((), ())),
        preferred_element_type=jnp.float32,
    )
    out_refs, held = refs[:-1], refs[-1]
    held[...] = total.astype(held.dtype)
    rows = held.shape[0] // (fsdp * count)
    for s in range(count):
        for d in range(fsdp):
            start = d * rows * count + lax.bitwise_xor(places[0], jnp.int32(s)) * rows
            out_refs[s][d * rows : (d + 1) * rows, :] = held[
                pl.ds(pl.multiple_of(start, rows), rows), :
            ]


def weight_grad(places, left, right):
    fsdp, count = lax.axis_size("fsdp"), lax.axis_size("ctx")
    tokens, rows = left.shape
    columns = right.shape[1]
    width = max(item for item in range(LANES, 6 * LANES + 1, LANES) if columns % item == 0)
    return pl.pallas_call(
        lambda *refs: weight_grad_kernel(*refs, fsdp=fsdp, count=count),
        grid_spec=pltpu.PrefetchScalarGridSpec(
            num_scalar_prefetch=1,
            grid=(columns // width,),
            in_specs=[
                pl.BlockSpec((tokens, rows), lambda step, places: (0, 0)),
                pl.BlockSpec((tokens, width), lambda step, places: (0, step)),
            ],
            out_specs=[pl.BlockSpec((rows // count, width), lambda step, places: (0, step))]
            * count,
            scratch_shapes=[pltpu.VMEM((rows, width), jnp.bfloat16)],
        ),
        out_shape=[jax.ShapeDtypeStruct((rows // count, columns), jnp.bfloat16)] * count,
        name="weight_grad",
    )(places, left, right)


def place_kernel(places, ratio_ref, *refs):
    part_refs, out_ref = refs[:-1], refs[-1]
    rows = part_refs[0].shape[0]
    ratio = ratio_ref[0]
    for s in range(len(part_refs)):
        start = lax.bitwise_xor(places[0], jnp.int32(s)) * rows
        out_ref[pl.ds(pl.multiple_of(start, rows), rows), :] = (
            part_refs[s][...].astype(jnp.float32) * ratio
        )


def place_rows(places, parts, ratio):
    rows, columns = parts[0].shape
    width = 3 * LANES if columns % (3 * LANES) == 0 else columns
    block = pl.BlockSpec((rows, width), lambda step, places: (0, step))
    return pl.pallas_call(
        place_kernel,
        grid_spec=pltpu.PrefetchScalarGridSpec(
            num_scalar_prefetch=1,
            grid=(columns // width,),
            in_specs=[pl.BlockSpec(memory_space=pltpu.SMEM)] + [block] * len(parts),
            out_specs=pl.BlockSpec((rows * len(parts), width), lambda step, places: (0, step)),
        ),
        out_shape=jax.ShapeDtypeStruct((rows * len(parts), columns), jnp.float32),
        name="place_rows",
    )(places, ratio.reshape(1), *parts)


def whole_local(
    hidden_in,
    valid_mask,
    teacher,
    qkv_weight,
    qv_bias,
    out_weight,
    out_bias,
    norm1_gain,
    norm1_shift,
    up_weight,
    up_bias,
    down_weight,
    down_bias,
    norm2_gain,
    norm2_shift,
):
    seq_count, block_len, model_width = hidden_in.shape
    ctx_count = lax.axis_size("ctx")
    place, depth, core = lax.axis_index("ctx"), lax.axis_index("fsdp"), lax.axis_index("tp")
    inner_width = qkv_weight.shape[2]
    hidden_width = up_weight.shape[1]
    row_count = seq_count * block_len
    shape = hidden_in.shape
    places = jnp.stack([place, depth])
    fsdp_count = lax.axis_size("fsdp")
    row = lambda values: values.reshape(1, -1)
    struct = jax.ShapeDtypeStruct
    part_rows = qkv_weight.shape[0] // ctx_count
    qkv_out = jnp.concatenate([by_pairs(qkv_weight), out_weight], axis=1)
    local_counts = jnp.sum(wide(valid_mask), axis=1)
    weight_rows = swap_all(
        lax.dynamic_slice_in_dim(qkv_out, place * part_rows, part_rows, 0), "fsdp"
    )
    hidden_half = deal(own_half(hidden_in), "ctx")
    full_up = lax.all_gather(up_weight, "fsdp", axis=0, tiled=True)
    full_down = lax.all_gather(down_weight, "fsdp", axis=0, tiled=True)
    weight_rows, hidden_half = together(weight_rows, hidden_half)
    count_rows = jnp.broadcast_to(
        jnp.pad(low(local_counts), (0, qkv_out.shape[1] - seq_count)), (16, qkv_out.shape[1])
    )
    weight_part = jnp.concatenate(weight_rows + [count_rows], axis=0)
    weight_parts = [weight_part] + relay_all(weight_part, "ctx")
    flat_in = join_halves(hidden_half).reshape(row_count, model_width)
    full_bias = by_pairs(jnp.stack([qv_bias[0], jnp.zeros_like(qv_bias[0]), qv_bias[1]]))
    weight_parts, flat_in, teacher_own = together(weight_parts, flat_in, own_half(teacher))
    full_qkv_out = assemble(places, qkv_out, weight_parts)
    full_qkv, full_out = full_qkv_out[:, : 3 * inner_width], full_qkv_out[:, 3 * inner_width :]
    counts = sum(wide(item[-16, :LANES]) for item in weight_parts)
    valid_count = lax.dynamic_index_in_dim(counts, place, 0, keepdims=False).astype(jnp.int32)
    facts = jnp.stack([valid_count, core])
    teacher_half = deal(teacher_own, "ctx")
    projected = low(jnp.dot(flat_in, full_qkv, preferred_element_type=jnp.float32) + full_bias)
    attended, log_total = attend(facts, projected, block_len)
    branch = low(jnp.einsum("te,de->td", attended, full_out, preferred_element_type=jnp.float32))
    normal1, scale1, normed1_low = by_rows(
        first_norm_kernel,
        "first_norm",
        block_len,
        [flat_in, branch, swap(branch, "tp", 1), row(out_bias), row(norm1_gain), row(norm1_shift)],
        [
            struct((row_count, model_width), jnp.float32),
            struct((row_count, 1), jnp.float32),
            struct((row_count, model_width), jnp.bfloat16),
        ],
    )
    normed1_low, teacher_half = together(normed1_low, teacher_half)
    active, slope = wide_layer(
        up_kernel, "up", block_len, normed1_low, full_up, [row(up_bias)], 2
    )
    branch = low(jnp.einsum("tf,df->td", active, full_down, preferred_element_type=jnp.float32))
    layer_half, grad_resid2, grad_resid2_low, stats2 = by_rows(
        second_norm_kernel,
        "second_norm",
        block_len,
        [
            normal1,
            row(norm1_gain),
            row(norm1_shift),
            branch,
            swap(branch, "tp", 1),
            row(down_bias),
            row(norm2_gain),
            row(norm2_shift),
            teacher_half,
            swap(teacher_half, "tp", 1),
        ],
        [
            struct(teacher_half.shape, jnp.bfloat16),
            struct((row_count, model_width), jnp.float32),
            struct((row_count, model_width), jnp.bfloat16),
        ],
        facts=facts,
        stats=model_width,
    )
    grad_down = low(
        jnp.einsum("td,tf->df", grad_resid2_low, active, preferred_element_type=jnp.float32)
    )
    grad_down, grad_resid2_low, layer_half = together(grad_down, grad_resid2_low, layer_half)
    owned_down = lax.psum_scatter(grad_down, "fsdp", scatter_dimension=0, tiled=True)
    grad_pre, stats_up = wide_layer(
        grad_pre_kernel, "grad_pre", block_len, grad_resid2_low, full_down, [slope], 1, hidden_width
    )
    grad_up = low(
        jnp.einsum("td,tf->df", normed1_low, grad_pre, preferred_element_type=jnp.float32)
    )
    grad_pre, grad_up, layer_half = together(grad_pre, grad_up, layer_half)
    owned_up = lax.psum_scatter(grad_up, "fsdp", scatter_dimension=0, tiled=True)
    layer_half = deal(layer_half, "ctx")
    branch = low(jnp.einsum("tf,df->td", grad_pre, full_up, preferred_element_type=jnp.float32))
    grad_resid1_low, grad_half, stats1 = by_rows(
        first_norm_back_kernel,
        "first_norm_back",
        block_len,
        [grad_resid2, branch, swap(branch, "tp", 1), normal1, scale1, row(norm1_gain)],
        [
            struct((row_count, model_width), jnp.bfloat16),
            struct(layer_half.shape, jnp.float32),
        ],
        facts=facts,
        stats=model_width,
    )
    out_pieces = weight_grad(places, grad_resid1_low, attended)
    grad_attended = low(jnp.dot(grad_resid1_low, full_out, preferred_element_type=jnp.float32))
    grad_attended, out_pieces, owned_down, layer_half = together(
        grad_attended, out_pieces, owned_down, layer_half
    )
    down_other = swap(owned_down, "ctx", 1)
    out_sums = swap_each(out_pieces, "ctx")
    grad_qkv, stats_qkv = attend_back(facts, projected, grad_attended, log_total, block_len)
    grad_qkv, down_other, out_sums = together(grad_qkv, down_other, out_sums)
    qkv_pieces = weight_grad(places, flat_in, grad_qkv)
    qkv_pieces, grad_qkv, down_other, out_sums, layer_half = together(
        qkv_pieces, grad_qkv, down_other, out_sums, layer_half
    )
    qkv_sums = swap_each(qkv_pieces, "ctx")
    layer_out = join_halves(layer_half)
    input_part = jnp.einsum("te,de->td", grad_qkv, full_qkv, preferred_element_type=jnp.float32)
    parts = low(input_part).reshape(seq_count, 2, block_len // 2, model_width)
    mine = lax.dynamic_index_in_dim(parts, core, 1, keepdims=False)
    other = swap(lax.dynamic_index_in_dim(parts, 1 - core, 1, keepdims=False), "tp", 1)
    half = low(grad_half + (wide(mine) + wide(other)))
    owned_down = low(wide(owned_down) + wide(down_other))
    down_other = swap(owned_down, "ctx", 2)
    local_count = jnp.broadcast_to(jnp.sum(local_counts), (1, LANES))
    small = pack(stats2, stats1, stats_up, stats_qkv, local_count)
    out_part = add_up([out_pieces[0]] + out_sums)
    qkv_sums, down_other, half, small, out_part, owned_up = together(
        qkv_sums, down_other, half, small, out_part, owned_up
    )
    part = low(jnp.concatenate([add_up([qkv_pieces[0]] + qkv_sums), out_part], axis=1))
    pieces = deal(part.reshape(fsdp_count, -1, part.shape[1]), "fsdp")
    up_other = swap(owned_up, "ctx", 1)
    small = sum_over(small, "ctx")
    pieces, half, small, up_other = together(pieces, half, small, up_other)
    part = low(add_up([pieces[d] for d in range(fsdp_count)]))
    qkv_out_owned = [part] + relay_all(part, "ctx")
    owned_up = low(wide(owned_up) + wide(up_other))
    up_other = swap(owned_up, "ctx", 2)
    input_half = deal(half, "ctx")
    small = sum_over(small, "fsdp")
    at = 7 + -(-hidden_width // model_width)
    counted = small[at + -(-3 * inner_width // model_width), 0]
    ratio = float(row_count * ctx_count * fsdp_count) / counted
    loss = jnp.sum(small[3]) / (counted * model_width)
    scaled = small * ratio
    grad_up_bias = scaled[7:at].reshape(-1)[:hidden_width]
    grad_qv_bias = by_kinds(
        scaled[at : at + -(-3 * inner_width // model_width)].reshape(-1)[: 3 * inner_width]
    )[0::2]
    owned_up = (wide(owned_up) + wide(up_other)) * ratio
    owned_down = (wide(owned_down) + wide(down_other)) * ratio
    owned_qkv_out = place_rows(places, qkv_out_owned, ratio)
    owned_qkv = by_kinds(owned_qkv_out[:, : 3 * inner_width])
    input_grad = join_halves(input_half, ratio, jnp.float32)
    return (
        layer_out,
        input_grad,
        loss,
        owned_qkv,
        grad_qv_bias,
        owned_qkv_out[:, 3 * inner_width :],
        scaled[4],
        scaled[5],
        scaled[6],
        owned_up,
        grad_up_bias,
        owned_down,
        scaled[0],
        scaled[1],
        scaled[2],
    )


def spread_local(
    hidden_in,
    valid_mask,
    teacher,
    qkv_weight,
    qv_bias,
    out_weight,
    out_bias,
    norm1_gain,
    norm1_shift,
    up_weight,
    up_bias,
    down_weight,
    down_bias,
    norm2_gain,
    norm2_shift,
):
    seq_count, block_len, model_width = hidden_in.shape
    ctx_count = lax.axis_size("ctx")
    ctx_place = lax.axis_index("ctx")
    key_span = 2 * block_len
    seq_length = block_len * ctx_count
    row_count = seq_count * block_len
    scaling = HEAD_DIM ** (-0.5)
    full_qkv, full_out, full_up, full_down = (
        lax.all_gather(qkv_weight, "fsdp", axis=0, tiled=True),
        lax.all_gather(out_weight, "fsdp", axis=0, tiled=True),
        lax.all_gather(up_weight, "fsdp", axis=0, tiled=True),
        lax.all_gather(down_weight, "fsdp", axis=0, tiled=True),
    )
    inner_width = full_qkv.shape[2]
    head_count = inner_width // HEAD_DIM
    flat_in = hidden_in.reshape(row_count, model_width)
    full_bias = jnp.stack([qv_bias[0], jnp.zeros_like(qv_bias[0]), qv_bias[1]])
    projected = (
        jnp.einsum("td,dje->tje", flat_in, full_qkv, preferred_element_type=jnp.float32) + full_bias
    ).astype(jnp.bfloat16)
    queries = projected[:, 0].reshape(seq_count, block_len, inner_width)
    key_own = projected[:, 1].reshape(seq_count, block_len, inner_width)
    value_own = projected[:, 2].reshape(seq_count, block_len, inner_width)
    keep_own = valid_mask.astype(jnp.bfloat16)
    keys_all, values_all, keep_all = (
        lax.all_gather(key_own, "ctx", axis=1, tiled=True),
        lax.all_gather(value_own, "ctx", axis=1, tiled=True),
        lax.all_gather(keep_own, "ctx", axis=1, tiled=True),
    )
    query_heads = split_heads(queries)
    seen_limit = (ctx_place + 1) * block_len
    trip_count = ctx_place // 2 + 1
    offsets = jnp.arange(key_span, dtype=jnp.int32)

    def key_block(block_index):
        key_start = block_index * key_span
        key_heads = split_heads(lax.dynamic_slice_in_dim(keys_all, key_start, key_span, 1))
        value_heads = split_heads(lax.dynamic_slice_in_dim(values_all, key_start, key_span, 1))
        live_keys = lax.dynamic_slice_in_dim(keep_all, key_start, key_span, 1) > 0.5
        allowed = jnp.logical_and(live_keys, (key_start + offsets)[None, :] < seen_limit)
        return (key_heads, value_heads, allowed[:, None, None, :])

    def attend_step(block_index, carried):
        run_top, run_total, gathered = carried
        key_heads, value_heads, allowed = key_block(block_index)
        raw_scores = scores_of(query_heads, key_heads, allowed, scaling)
        new_top = jnp.maximum(run_top, jnp.max(raw_scores, axis=-1))
        shrink = jnp.exp(run_top - new_top)
        weights_now = jnp.exp(raw_scores - new_top[..., None])
        run_total = run_total * shrink + jnp.sum(weights_now, axis=-1)
        gathered = gathered * jnp.swapaxes(shrink, 1, 2)[..., None] + jnp.einsum(
            "shqk,skhd->sqhd",
            weights_now.astype(jnp.bfloat16),
            value_heads,
            preferred_element_type=jnp.float32,
        )
        return (new_top, run_total, gathered)

    start_top = jnp.full((seq_count, head_count, block_len), MASKED, jnp.float32)
    empty_heads = jnp.zeros((seq_count, block_len, head_count, HEAD_DIM), jnp.float32)
    run_top, run_total, gathered = lax.fori_loop(
        0, trip_count, attend_step, (start_top, jnp.zeros_like(start_top), empty_heads)
    )
    log_total = run_top + jnp.log(run_total)
    attended_exact = gathered / jnp.swapaxes(run_total, 1, 2)[..., None]
    attended = attended_exact.astype(jnp.bfloat16).reshape(row_count, inner_width)
    attn_branch = lax.psum(
        jnp.einsum("te,de->td", attended, full_out, preferred_element_type=jnp.float32).astype(
            jnp.bfloat16
        ),
        "tp",
    ).astype(jnp.float32)
    resid1 = flat_in.astype(jnp.float32) + attn_branch + out_bias
    normed1, norm1_back = jax.vjp(layer_norm, resid1, norm1_gain, norm1_shift)
    normed1_low = normed1.astype(jnp.bfloat16)
    pre_act = jnp.dot(normed1_low, full_up, preferred_element_type=jnp.float32) + up_bias
    active, gelu_back = jax.vjp(gelu_exact, pre_act)
    active = active.astype(jnp.bfloat16)
    ffn_branch = lax.psum(
        jnp.einsum("tf,df->td", active, full_down, preferred_element_type=jnp.float32).astype(
            jnp.bfloat16
        ),
        "tp",
    ).astype(jnp.float32)
    resid2 = normed1 + ffn_branch + down_bias
    output, norm2_back = jax.vjp(layer_norm, resid2, norm2_gain, norm2_shift)
    layer_out = output.astype(jnp.bfloat16).reshape(seq_count, block_len, model_width)
    keep_rows = valid_mask.reshape(row_count, 1).astype(jnp.float32)
    residue = (output - teacher.reshape(row_count, model_width).astype(jnp.float32)) * keep_rows
    squared = jnp.sum(residue * residue)
    counted = jnp.sum(keep_rows)
    grad_resid2, grad_gain2, grad_shift2 = norm2_back(residue)
    grad_down_bias = jnp.sum(grad_resid2, axis=0)
    grad_resid2_low = grad_resid2.astype(jnp.bfloat16)
    grad_active = jnp.dot(grad_resid2_low, full_down, preferred_element_type=jnp.float32)
    grad_down_weight = jnp.einsum(
        "td,tf->df", grad_resid2_low, active, preferred_element_type=jnp.float32
    )
    grad_pre = gelu_back(grad_active)[0].astype(jnp.bfloat16)
    grad_up_bias = jnp.sum(grad_pre.astype(jnp.float32), axis=0)
    grad_up_weight = jnp.einsum(
        "td,tf->df", normed1_low, grad_pre, preferred_element_type=jnp.float32
    )
    ffn_input_grad = lax.psum(
        jnp.einsum("tf,df->td", grad_pre, full_up, preferred_element_type=jnp.float32).astype(
            jnp.bfloat16
        ),
        "tp",
    ).astype(jnp.float32)
    grad_normed1 = grad_resid2 + ffn_input_grad
    grad_resid1, grad_gain1, grad_shift1 = norm1_back(grad_normed1)
    grad_out_bias = jnp.sum(grad_resid1, axis=0)
    grad_resid1_low = grad_resid1.astype(jnp.bfloat16)
    grad_mixed = jnp.dot(grad_resid1_low, full_out, preferred_element_type=jnp.float32)
    grad_out_weight = jnp.einsum(
        "td,te->de", grad_resid1_low, attended, preferred_element_type=jnp.float32
    )
    grad_attended = grad_mixed.astype(jnp.bfloat16).reshape(
        seq_count, block_len, head_count, HEAD_DIM
    )
    delta = jnp.swapaxes(jnp.sum(grad_attended.astype(jnp.float32) * attended_exact, axis=-1), 1, 2)

    def query_grads(block_index):
        key_heads, value_heads, allowed = key_block(block_index)
        prob_rows = jnp.exp(
            scores_of(query_heads, key_heads, allowed, scaling) - log_total[..., None]
        )
        push = jnp.einsum(
            "sqhd,skhd->shqk", grad_attended, value_heads, preferred_element_type=jnp.float32
        )
        slope = (prob_rows * (push - delta[..., None])).astype(jnp.bfloat16)
        grad_part = (
            jnp.einsum("shqk,skhd->sqhd", slope, key_heads, preferred_element_type=jnp.float32)
            * scaling
        )
        return (prob_rows, slope, grad_part)

    def back_step(block_index, carried):
        grad_query, spread = carried
        prob_rows, slope, grad_part = query_grads(block_index)
        grad_key = (
            jnp.einsum("shqk,sqhd->skhd", slope, query_heads, preferred_element_type=jnp.float32)
            * scaling
        )
        grad_value = jnp.einsum(
            "shqk,sqhd->skhd",
            prob_rows.astype(jnp.bfloat16),
            grad_attended,
            preferred_element_type=jnp.float32,
        )
        piece = jnp.stack(
            [
                grad_key.reshape(seq_count, key_span, inner_width),
                grad_value.reshape(seq_count, key_span, inner_width),
            ],
            axis=2,
        )
        spread = lax.dynamic_update_slice_in_dim(spread, piece, block_index * key_span, 1)
        return (grad_query + grad_part, spread)

    spread_start = jnp.zeros((seq_count, seq_length, 2, inner_width), jnp.float32)
    grad_query, spread = lax.fori_loop(0, trip_count, back_step, (empty_heads, spread_start))
    own_grads = lax.psum_scatter(
        spread.astype(jnp.bfloat16), "ctx", scatter_dimension=1, tiled=True
    ).astype(jnp.float32)
    grad_key_own = own_grads[:, :, 0]
    grad_value_own = own_grads[:, :, 1]
    grad_qkv = jnp.stack(
        [
            grad_query.reshape(row_count, inner_width),
            grad_key_own.reshape(row_count, inner_width),
            grad_value_own.reshape(row_count, inner_width),
        ],
        axis=1,
    ).astype(jnp.bfloat16)
    grad_qv_bias = jnp.sum(grad_qkv[:, 0::2].astype(jnp.float32), axis=0)
    grad_qkv_weight = jnp.einsum(
        "td,tje->dje", flat_in, grad_qkv, preferred_element_type=jnp.float32
    )
    input_part = lax.psum(
        jnp.einsum("tje,dje->td", grad_qkv, full_qkv, preferred_element_type=jnp.float32).astype(
            jnp.bfloat16
        ),
        "tp",
    ).astype(jnp.float32)
    grad_input = grad_resid1 + input_part
    vectors = jnp.stack(
        [grad_out_bias, grad_gain1, grad_shift1, grad_down_bias, grad_gain2, grad_shift2]
    )
    squared, counted, vectors, grad_qv_bias, grad_up_bias = lax.psum(
        (squared, counted, vectors, grad_qv_bias, grad_up_bias), ("fsdp", "ctx")
    )
    local_grads = (grad_qkv_weight, grad_out_weight, grad_up_weight, grad_down_weight)
    owned = (
        lax.psum_scatter(
            local_grads[0].astype(jnp.bfloat16), "fsdp", scatter_dimension=0, tiled=True
        ).astype(jnp.float32),
        lax.psum_scatter(
            local_grads[1].astype(jnp.bfloat16), "fsdp", scatter_dimension=0, tiled=True
        ).astype(jnp.float32),
        lax.psum_scatter(
            local_grads[2].astype(jnp.bfloat16), "fsdp", scatter_dimension=0, tiled=True
        ).astype(jnp.float32),
        lax.psum_scatter(
            local_grads[3].astype(jnp.bfloat16), "fsdp", scatter_dimension=0, tiled=True
        ).astype(jnp.float32),
    )
    owned = (
        lax.psum(owned[0].astype(jnp.bfloat16), "ctx").astype(jnp.float32),
        lax.psum(owned[1].astype(jnp.bfloat16), "ctx").astype(jnp.float32),
        lax.psum(owned[2].astype(jnp.bfloat16), "ctx").astype(jnp.float32),
        lax.psum(owned[3].astype(jnp.bfloat16), "ctx").astype(jnp.float32),
    )
    token_total = float(seq_count * seq_length * lax.axis_size("fsdp"))
    ratio = token_total / counted
    loss = squared / (counted * model_width)
    input_grad = (grad_input * ratio).reshape(seq_count, block_len, model_width)
    return (
        layer_out,
        input_grad,
        loss,
        owned[0] * ratio,
        grad_qv_bias * ratio,
        owned[1] * ratio,
        vectors[0] * ratio,
        vectors[1] * ratio,
        vectors[2] * ratio,
        owned[2] * ratio,
        grad_up_bias * ratio,
        owned[3] * ratio,
        vectors[3] * ratio,
        vectors[4] * ratio,
        vectors[5] * ratio,
    )


def local(hidden_in, *others):
    seq_count, block_len, model_width = hidden_in.shape
    ctx_count, fsdp_count = lax.axis_size("ctx"), lax.axis_size("fsdp")
    rows, inner_width = others[2].shape[0], others[2].shape[2]
    whole = (
        seq_count == ctx_count
        and ctx_count & (ctx_count - 1) == 0
        and fsdp_count & (fsdp_count - 1) == 0
        and lax.axis_size("tp") == 2
        and block_len % LANES == 0
        and others[5].shape[0] >= inner_width
        and inner_width % LANES == 0
        and rows % (16 * ctx_count) == 0
    )
    return (whole_local if whole else spread_local)(hidden_in, *others)


def solution(mesh):
    in_specs = (
        P("fsdp", "ctx", None),
        P("fsdp", "ctx"),
        P("fsdp", "ctx", None),
        P("fsdp", None, "tp"),
        P(None, "tp"),
        P("fsdp", "tp"),
        P(),
        P(),
        P(),
        P("fsdp", "tp"),
        P("tp"),
        P("fsdp", "tp"),
        P(),
        P(),
        P(),
    )
    out_specs = (
        P("fsdp", "ctx", None),
        P("fsdp", "ctx", None),
        P(),
        P("fsdp", None, "tp"),
        P(None, "tp"),
        P("fsdp", "tp"),
        P(),
        P(),
        P(),
        P("fsdp", "tp"),
        P("tp"),
        P("fsdp", "tp"),
        P(),
        P(),
        P(),
    )
    return jax.shard_map(local, mesh=mesh, in_specs=in_specs, out_specs=out_specs, check_vma=False)
```

```python
import jax
import jax.numpy as jnp
from jax import lax
from jax.experimental import pallas as pl
from jax.experimental.pallas import tpu as pltpu
from jax.sharding import PartitionSpec as P

HEAD_DIM = 64
NORM_EPS = 1e-05
MASKED = -1e30
LANES = 128


def layer_norm(values_in, gain_vec, shift_vec):
    row_mean = jnp.mean(values_in, axis=-1, keepdims=True)
    centered = values_in - row_mean
    row_var = jnp.mean(centered * centered, axis=-1, keepdims=True)
    return centered * lax.rsqrt(row_var + NORM_EPS) * gain_vec + shift_vec


def gelu_exact(pre_act):
    return jax.nn.gelu(pre_act, approximate=False)


def split_heads(packed):
    return packed.reshape(packed.shape[0], packed.shape[1], packed.shape[2] // HEAD_DIM, HEAD_DIM)


def scores_of(query_heads, key_heads, allowed, scaling):
    raw_scores = (
        jnp.einsum("sqhd,skhd->shqk", query_heads, key_heads, preferred_element_type=jnp.float32)
        * scaling
    )
    return jnp.where(allowed, raw_scores, MASKED)


def rows_by_rows(left, right):
    return lax.dot_general(left, right, (((1,), (1,)), ((), ())), preferred_element_type=jnp.float32)


def plain_dot(left, right):
    return jnp.dot(left, right, preferred_element_type=jnp.float32)


def lanes_of(head, lane):
    own = (lane < HEAD_DIM) if head == 0 else (lane >= HEAD_DIM)
    spare = HEAD_DIM if head == 0 else 0
    return own, lane == spare


def head_operands(query_ref, key_ref, slot, start, block, valid_count, head):
    lane = lax.broadcasted_iota(jnp.int32, (block, LANES), 1)
    own, spare = lanes_of(head, lane)
    position = start + lax.broadcasted_iota(jnp.int32, (block, LANES), 0)
    bias = jnp.where(position < valid_count, 0.0, MASKED)
    rows = pl.ds(slot * block, block)
    query = query_ref[rows, :].astype(jnp.float32) * (HEAD_DIM ** -0.5)
    key = key_ref[rows, :].astype(jnp.float32)
    query_side = jnp.where(spare, 1.0, query).astype(jnp.bfloat16)
    key_side = jnp.where(own, key, jnp.where(spare, bias, 0.0)).astype(jnp.bfloat16)
    return query_side, key_side


def attend_kernel(facts, query_ref, key_ref, value_ref, out_ref, log_ref, *, block):
    valid_count = facts[0]
    blocks = query_ref.shape[0] // block
    slots = list(range(blocks))
    value_t = [
        value_ref[pl.ds(slots[j] * block, block), :].astype(jnp.float32).T.astype(jnp.bfloat16)
        for j in range(blocks)
    ]
    outs = [[] for _ in range(blocks)]
    for head in range(2):
        sides = [
            head_operands(query_ref, key_ref, slots[j], j * block, block, valid_count, head)
            for j in range(blocks)
        ]
        span = slice(head * HEAD_DIM, (head + 1) * HEAD_DIM)
        for i in range(blocks):
            scores = [rows_by_rows(sides[j][1], sides[i][0]) for j in range(i + 1)]
            top = scores[0].max(axis=0, keepdims=True)
            for j in range(1, i + 1):
                top = jnp.maximum(top, scores[j].max(axis=0, keepdims=True))
            total = jnp.zeros_like(top)
            mixed = jnp.zeros((HEAD_DIM, block), jnp.float32)
            for j in range(i + 1):
                weight = jnp.exp(scores[j] - top)
                total = total + weight.sum(axis=0, keepdims=True)
                mixed = mixed + plain_dot(value_t[j][span, :], weight.astype(jnp.bfloat16))
            outs[i].append(mixed / total)
            log_ref[0, head : head + 1, i * block : (i + 1) * block] = top + jnp.log(total)
    for i in range(blocks):
        both = jnp.concatenate(outs[i], axis=0)
        out_ref[pl.ds(slots[i] * block, block), :] = both.T.astype(out_ref.dtype)


def attend_back_kernel(
    facts,
    query_ref,
    key_ref,
    value_ref,
    grad_ref,
    log_ref,
    out_ref,
    stats_ref,
    grad_key,
    grad_value,
    *,
    block,
):
    valid_count = facts[0]
    blocks = query_ref.shape[0] // block
    slots = list(range(blocks))
    scaling = HEAD_DIM ** -0.5
    lane = lax.broadcasted_iota(jnp.int32, (block, LANES), 1)
    key_t, grads, queries, values = [], [], [], []
    for j in range(blocks):
        rows = pl.ds(slots[j] * block, block)
        key_t.append((key_ref[rows, :].astype(jnp.float32) * scaling).T.astype(jnp.bfloat16))
        grads.append(grad_ref[rows, :])
        queries.append(query_ref[rows, :].astype(jnp.float32) * scaling)
        values.append(value_ref[rows, :].astype(jnp.float32))
    grad_queries = [[] for _ in range(blocks)]
    for head in range(2):
        own, _ = lanes_of(head, lane)
        span = slice(head * HEAD_DIM, (head + 1) * HEAD_DIM)
        sides = [
            head_operands(query_ref, key_ref, slots[j], j * block, block, valid_count, head)
            for j in range(blocks)
        ]
        head_values = [jnp.where(own, item, 0.0).astype(jnp.bfloat16) for item in values]
        for i in range(blocks):
            log_row = log_ref[0, head : head + 1, i * block : (i + 1) * block]
            head_grad = jnp.where(own, grads[i].astype(jnp.float32), 0.0).astype(jnp.bfloat16)
            head_query = jnp.where(own, queries[i], 0.0).astype(jnp.bfloat16)
            probs, pushes = [], []
            delta = jnp.zeros((1, block), jnp.float32)
            for j in range(i + 1):
                prob = jnp.exp(rows_by_rows(sides[j][1], sides[i][0]) - log_row)
                push = rows_by_rows(head_values[j], grads[i])
                delta = delta + (prob * push).sum(axis=0, keepdims=True)
                probs.append(prob)
                pushes.append(push)
            grad_query = jnp.zeros((HEAD_DIM, block), jnp.float32)
            for j in range(i + 1):
                slope = (probs[j] * (pushes[j] - delta)).astype(jnp.bfloat16)
                part_value = plain_dot(probs[j].astype(jnp.bfloat16), head_grad)
                part_key = plain_dot(slope, head_query)
                span_rows = slice(j * block, (j + 1) * block)
                if head == 0 and i == j:
                    grad_value[span_rows, :] = part_value
                    grad_key[span_rows, :] = part_key
                else:
                    grad_value[span_rows, :] += part_value
                    grad_key[span_rows, :] += part_key
                grad_query = grad_query + plain_dot(key_t[j][span, :], slope)
            grad_queries[i].append(grad_query)
    totals = jnp.zeros((1, 3 * LANES), jnp.float32)
    for i in range(blocks):
        rows = pl.ds(slots[i] * block, block)
        both = jnp.concatenate(grad_queries[i], axis=0)
        out_ref[rows, :LANES] = both.T.astype(out_ref.dtype)
        span_rows = slice(i * block, (i + 1) * block)
        out_ref[rows, LANES : 2 * LANES] = grad_key[span_rows, :].astype(out_ref.dtype)
        out_ref[rows, 2 * LANES :] = grad_value[span_rows, :].astype(out_ref.dtype)
        totals += jnp.sum(out_ref[rows, :].astype(jnp.float32), axis=0, keepdims=True)
    stats_ref[...] = jnp.broadcast_to(totals, stats_ref.shape)


def attend(facts, projected, block):
    length, width = projected.shape
    pairs = width // (3 * LANES)
    column = lambda kind: pl.BlockSpec((length, LANES), lambda pair, facts: (0, 3 * pair + kind))
    return pl.pallas_call(
        lambda *refs: attend_kernel(*refs, block=block),
        grid_spec=pltpu.PrefetchScalarGridSpec(
            num_scalar_prefetch=1,
            grid=(pairs,),
            in_specs=[column(0), column(1), column(2)],
            out_specs=[
                pl.BlockSpec((length, LANES), lambda pair, facts: (0, pair)),
                pl.BlockSpec((1, 2, length), lambda pair, facts: (pair, 0, 0)),
            ],
        ),
        out_shape=[
            jax.ShapeDtypeStruct((length, pairs * LANES), jnp.bfloat16),
            jax.ShapeDtypeStruct((pairs, 2, length), jnp.float32),
        ],
        name="attend",
        compiler_params=pltpu.CompilerParams(vmem_limit_bytes=9 << 20),
    )(facts, projected, projected, projected)


def attend_back(facts, projected, grad_attended, log_total, block):
    length, width = grad_attended.shape
    pairs = width // LANES
    column = lambda kind: pl.BlockSpec((length, LANES), lambda pair, facts: (0, 3 * pair + kind))
    return pl.pallas_call(
        lambda *refs: attend_back_kernel(*refs, block=block),
        grid_spec=pltpu.PrefetchScalarGridSpec(
            num_scalar_prefetch=1,
            grid=(pairs,),
            in_specs=[
                column(0),
                column(1),
                column(2),
                pl.BlockSpec((length, LANES), lambda pair, facts: (0, pair)),
                pl.BlockSpec((1, 2, length), lambda pair, facts: (pair, 0, 0)),
            ],
            out_specs=[
                pl.BlockSpec((length, 3 * LANES), lambda pair, facts: (0, pair)),
                pl.BlockSpec((8, 3 * LANES), lambda pair, facts: (0, pair)),
            ],
            scratch_shapes=[
                pltpu.VMEM((length, LANES), jnp.float32),
                pltpu.VMEM((length, LANES), jnp.float32),
            ],
        ),
        out_shape=[
            jax.ShapeDtypeStruct((length, 3 * width), jnp.bfloat16),
            jax.ShapeDtypeStruct((8, 3 * width), jnp.float32),
        ],
        name="attend_back",
        compiler_params=pltpu.CompilerParams(vmem_limit_bytes=12 << 20),
    )(facts, projected, projected, projected, grad_attended, log_total)


def by_pairs(values):
    kinds, width = values.shape[-2:]
    cut = values.reshape(values.shape[:-1] + (width // LANES, LANES))
    return jnp.swapaxes(cut, -3, -2).reshape(values.shape[:-2] + (kinds * width,))


def by_kinds(values, kinds=3):
    width = values.shape[-1] // kinds
    cut = values.reshape(values.shape[:-1] + (width // LANES, kinds, LANES))
    return jnp.swapaxes(cut, -3, -2).reshape(values.shape[:-1] + (kinds, width))


def fill_rows(places, own_ref, part_refs, out_ref):
    count = len(part_refs)
    rows = own_ref.shape[0] // count
    fsdp = out_ref.shape[0] // own_ref.shape[0]
    place, depth = places[0], places[1]
    start = pl.multiple_of(depth * (rows * count), rows)
    out_ref[pl.ds(start, rows * count), :] = own_ref[...]
    for s in range(count):
        for d in range(1, fsdp):
            start = lax.bitwise_xor(depth, jnp.int32(d)) * (rows * count)
            start = start + lax.bitwise_xor(place, jnp.int32(s)) * rows
            out_ref[pl.ds(pl.multiple_of(start, rows), rows), :] = part_refs[s][
                (d - 1) * rows : d * rows, :
            ]


def project_kernel(places, left_ref, bias_ref, own_ref, *refs):
    part_refs, (out_ref, full_ref) = refs[:-2], refs[-2:]

    @pl.when(pl.program_id(0) == 0)
    def _():
        fill_rows(places, own_ref, part_refs, full_ref)

    total = plain_dot(left_ref[...], full_ref[:, : out_ref.shape[1]]) + bias_ref[...]
    out_ref[...] = total.astype(out_ref.dtype)


def up_kernel(places, left_ref, bias_ref, own_ref, *refs):
    part_refs, (active_ref, slope_ref, full_ref) = refs[:-3], refs[-3:]

    @pl.when(pl.program_id(0) == 0)
    def _():
        fill_rows(places, own_ref, part_refs, full_ref)

    pre = plain_dot(left_ref[...], full_ref[...]) + bias_ref[...]
    below = 0.5 * (1.0 + lax.erf(pre * (0.5**0.5)))
    active_ref[...] = (pre * below).astype(active_ref.dtype)
    bell = jnp.exp(-0.5 * pre * pre) * 0.3989422804014327
    slope_ref[...] = (below + pre * bell).astype(slope_ref.dtype)


def down_kernel(places, left_ref, own_ref, part_ref, *refs):
    part_refs, (out_ref, full_ref) = refs[:-2], refs[-2:]
    count = len(part_refs) // 2
    cut = part_refs[0].shape[1]

    @pl.when(pl.program_id(0) == 0)
    def _():
        for index in range(2):
            span = slice(index * cut, (index + 1) * cut)
            fill_rows(
                places,
                own_ref.at[:, span],
                [part_ref.at[:, span]] + list(part_refs[index * count : (index + 1) * count]),
                full_ref.at[:, span],
            )

    out_ref[...] = rows_by_rows(left_ref[...], full_ref[...]).astype(out_ref.dtype)


def gathered_layer(kernel, name, block, places, left, vectors, own, parts, widths, fsdp):
    length = left.shape[0]
    full = (fsdp * own.shape[0], own.shape[1])
    whole = lambda shape: pl.BlockSpec(shape, lambda step, places: (0, 0))
    by_block = lambda width: pl.BlockSpec((block, width), lambda step, places: (step, 0))
    return pl.pallas_call(
        kernel,
        grid_spec=pltpu.PrefetchScalarGridSpec(
            num_scalar_prefetch=1,
            grid=(length // block,),
            in_specs=[by_block(left.shape[1])]
            + [whole(item.shape) for item in vectors + [own] + parts],
            out_specs=[by_block(width) for width in widths] + [whole(full)],
        ),
        out_shape=[jax.ShapeDtypeStruct((length, width), jnp.bfloat16) for width in widths]
        + [jax.ShapeDtypeStruct(full, jnp.bfloat16)],
        name=name,
        compiler_params=pltpu.CompilerParams(vmem_limit_bytes=20 << 20),
    )(places, left, *vectors, own, *parts)


def stack_kernel(*refs):
    row = 0
    for ref in refs[:-1]:
        refs[-1][row : row + ref.shape[0], :] = ref[...]
        row += ref.shape[0]


def stack_rows(pieces):
    rows = sum(item.shape[0] for item in pieces)
    return pl.pallas_call(
        stack_kernel,
        out_shape=jax.ShapeDtypeStruct((rows, pieces[0].shape[1]), pieces[0].dtype),
        name="stack_rows",
        compiler_params=pltpu.CompilerParams(vmem_limit_bytes=4 << 20),
    )(*pieces)


def swap(values, axis, step):
    pairs = [(place, place ^ step) for place in range(lax.axis_size(axis))]
    return lax.ppermute(values, axis, pairs)


def swap_all(values, axis):
    return [swap(values, axis, step) for step in range(1, lax.axis_size(axis))]


def relay_all(values, axis):
    if lax.axis_size(axis) != 4:
        return swap_all(values, axis)
    first, second = swap(values, axis, 1), swap(values, axis, 2)
    return [first, second, swap(first, axis, 2)]


def swap_each(pieces, axis):
    return [swap(pieces[step], axis, step) for step in range(1, len(pieces))]


def together(*values):
    return lax.optimization_barrier(values)


def wide(values):
    return values.astype(jnp.float32)


def low(values):
    return values.astype(jnp.bfloat16)


def add_partner(values):
    mine = low(values)
    return wide(mine) + wide(swap(mine, "tp", 1))


def add_up(pieces):
    pieces = [wide(item) for item in pieces]
    while len(pieces) > 1:
        pieces = [pieces[i] + pieces[i + 1] for i in range(0, len(pieces), 2)]
    return pieces[0]


def sum_over(values, axis):
    step = 1
    while step < lax.axis_size(axis):
        values = values + swap(values, axis, step)
        step *= 2
    return values


def deal(pieces, axis):
    return lax.all_to_all(pieces, axis, 0, 0)


def own_half(blocks):
    rows = blocks.shape[1] // 2
    return lax.dynamic_slice_in_dim(blocks, lax.axis_index("tp") * rows, rows, 1)


def row_kernel_stats(stats_ref, step, rows):
    @pl.when(step == 0)
    def _():
        stats_ref[...] = jnp.zeros_like(stats_ref)

    for index, row in enumerate(rows):
        stats_ref[index : index + 1, :] += jnp.sum(row, axis=0, keepdims=True)


def normalize(values):
    mean = jnp.mean(values, axis=-1, keepdims=True)
    centered = values - mean
    scale = lax.rsqrt(jnp.mean(centered * centered, axis=-1, keepdims=True) + NORM_EPS)
    return centered * scale, scale


def normalize_back(grads, normal, scale, gain):
    pushed = grads * gain
    mean = jnp.mean(pushed, axis=-1, keepdims=True)
    along = jnp.mean(pushed * normal, axis=-1, keepdims=True)
    return (pushed - mean - normal * along) * scale


def first_norm_kernel(
    hidden_ref, mine_ref, other_ref, bias_ref, gain_ref, shift_ref, normal_ref, scale_ref, low_ref
):
    branch = mine_ref[...].astype(jnp.float32) + other_ref[...].astype(jnp.float32)
    normal, scale = normalize(hidden_ref[...].astype(jnp.float32) + branch + bias_ref[...])
    normal_ref[...] = normal
    scale_ref[...] = scale
    low_ref[...] = (normal * gain_ref[...] + shift_ref[...]).astype(low_ref.dtype)


def second_norm_kernel(
    facts,
    normal_ref,
    gain1_ref,
    shift1_ref,
    mine_ref,
    other_ref,
    bias_ref,
    gain_ref,
    shift_ref,
    own_teacher_ref,
    other_teacher_ref,
    half_ref,
    grad_ref,
    low_ref,
    stats_ref,
):
    step = pl.program_id(0)
    block = normal_ref.shape[0]
    rows = block // 2
    branch = mine_ref[...].astype(jnp.float32) + other_ref[...].astype(jnp.float32)
    normed1 = normal_ref[...] * gain1_ref[...] + shift1_ref[...]
    normal, scale = normalize(normed1 + branch + bias_ref[...])
    output = normal * gain_ref[...] + shift_ref[...]
    first = facts[1] == 0
    half_ref[0] = jnp.where(first, output[:rows], output[rows:]).astype(half_ref.dtype)
    own, other = own_teacher_ref[0], other_teacher_ref[0]
    own, other = own.astype(jnp.float32), other.astype(jnp.float32)
    teacher = jnp.concatenate(
        [jnp.where(first, own, other), jnp.where(first, other, own)], axis=0
    )
    position = step * block + lax.broadcasted_iota(jnp.int32, (block, 1), 0)
    residue = jnp.where(position < facts[0], output - teacher, 0.0)
    grads = normalize_back(residue, normal, scale, gain_ref[...])
    grad_ref[...] = grads
    low_ref[...] = grads.astype(low_ref.dtype)
    row_kernel_stats(stats_ref, step, [grads, residue * normal, residue, residue * residue])


def first_norm_back_kernel(
    facts,
    grad_ref,
    mine_ref,
    other_ref,
    normal_ref,
    scale_ref,
    gain_ref,
    low_ref,
    half_ref,
    stats_ref,
):
    rows = grad_ref.shape[0] // 2
    branch = mine_ref[...].astype(jnp.float32) + other_ref[...].astype(jnp.float32)
    pushed = grad_ref[...] + branch
    normal = normal_ref[...]
    grads = normalize_back(pushed, normal, scale_ref[...], gain_ref[...])
    low_ref[...] = grads.astype(low_ref.dtype)
    half_ref[0] = jnp.where(facts[1] == 0, grads[:rows], grads[rows:])
    row_kernel_stats(stats_ref, pl.program_id(0), [grads, pushed * normal, pushed])


def by_rows(kernel, name, block, operands, results, facts=None, stats=0):
    def spec(shape, dealt=False):
        if dealt:
            return pl.BlockSpec((1,) + shape[1:], lambda step, facts: (step ^ facts[2], 0, 0))
        if shape[0] == 1:
            return pl.BlockSpec(shape, lambda step, *_: (0, 0))
        return pl.BlockSpec((block, shape[1]), lambda step, *_: (step, 0))

    length = next(item.shape[0] for item in operands if item.ndim == 2 and item.shape[0] > 1)
    out_specs = [spec(item.shape, item.ndim == 3) for item in results]
    if stats:
        results = results + [jax.ShapeDtypeStruct((8, stats), jnp.float32)]
        out_specs.append(pl.BlockSpec((8, stats), lambda step, *_: (0, 0)))
    return pl.pallas_call(
        kernel,
        grid_spec=pltpu.PrefetchScalarGridSpec(
            num_scalar_prefetch=0 if facts is None else 1,
            grid=(length // block,),
            in_specs=[spec(item.shape, item.ndim == 3) for item in operands],
            out_specs=out_specs,
        ),
        out_shape=results,
        name=name,
        compiler_params=pltpu.CompilerParams(vmem_limit_bytes=20 << 20),
    )(*([] if facts is None else [facts]), *operands)


def grad_pre_kernel(low_ref, weight_ref, slope_ref, out_ref, stats_ref):
    grads = plain_dot(low_ref[...], weight_ref[...]) * slope_ref[...].astype(jnp.float32)
    grads = grads.astype(out_ref.dtype)
    out_ref[...] = grads
    row_kernel_stats(stats_ref, pl.program_id(0), [grads.astype(jnp.float32)])


def wide_layer(kernel, name, block, low, weight, operands, count, stats=0):
    length, width = low.shape[0], weight.shape[1]

    def spec(shape):
        if shape[0] == 1:
            return pl.BlockSpec(shape, lambda step: (0, 0))
        return pl.BlockSpec((block, shape[1]), lambda step: (step, 0))

    out_specs = [pl.BlockSpec((block, width), lambda step: (step, 0))] * count
    out_shape = [jax.ShapeDtypeStruct((length, width), jnp.bfloat16)] * count
    if stats:
        out_specs = out_specs + [pl.BlockSpec((8, width), lambda step: (0, 0))]
        out_shape = out_shape + [jax.ShapeDtypeStruct((8, width), jnp.float32)]
    return pl.pallas_call(
        kernel,
        grid=(length // block,),
        in_specs=[spec(low.shape), pl.BlockSpec(weight.shape, lambda step: (0, 0))]
        + [spec(item.shape) for item in operands],
        out_specs=out_specs,
        out_shape=out_shape,
        name=name,
        compiler_params=pltpu.CompilerParams(vmem_limit_bytes=20 << 20),
    )(low, weight, *operands)


def rows_kernel(left_ref, right_ref, out_ref, *, transposed):
    product = (rows_by_rows if transposed else plain_dot)(left_ref[...], right_ref[...])
    out_ref[...] = product.astype(out_ref.dtype)


def rows_times(left, right, block, transposed):
    length, depth = left.shape
    width = right.shape[0] if transposed else right.shape[1]
    return pl.pallas_call(
        lambda *refs: rows_kernel(*refs, transposed=transposed),
        grid=(length // block,),
        in_specs=[
            pl.BlockSpec((block, depth), lambda step: (step, 0)),
            pl.BlockSpec(right.shape, lambda step: (0, 0)),
        ],
        out_specs=pl.BlockSpec((block, width), lambda step: (step, 0)),
        out_shape=jax.ShapeDtypeStruct((length, width), jnp.bfloat16),
        name="rows_times",
        compiler_params=pltpu.CompilerParams(vmem_limit_bytes=14 << 20),
    )(left, right)


def input_back_kernel(facts, grad_ref, weight_ref, mine_ref, other_ref):
    total = rows_by_rows(grad_ref[...], weight_ref[...]).astype(mine_ref.dtype)
    rows = mine_ref.shape[1]
    first = facts[1] == 0
    mine_ref[0] = jnp.where(first, total[:rows], total[rows:])
    other_ref[0] = jnp.where(first, total[rows:], total[:rows])


def input_back(facts, grads, weight, block):
    length, width = grads.shape
    half = (1, block // 2, weight.shape[0])
    return pl.pallas_call(
        input_back_kernel,
        grid_spec=pltpu.PrefetchScalarGridSpec(
            num_scalar_prefetch=1,
            grid=(length // block,),
            in_specs=[
                pl.BlockSpec((block, width), lambda step, facts: (step, 0)),
                pl.BlockSpec((weight.shape[0], width), lambda step, facts: (0, 0)),
            ],
            out_specs=[pl.BlockSpec(half, lambda step, facts: (step ^ facts[2], 0, 0))] * 2,
        ),
        out_shape=[jax.ShapeDtypeStruct((length // block,) + half[1:], jnp.bfloat16)] * 2,
        name="input_back",
        compiler_params=pltpu.CompilerParams(vmem_limit_bytes=10 << 20),
    )(facts, grads, weight)


def pack_kernel(second_ref, first_ref, up_ref, qkv_ref, count_ref, out_ref):
    width = out_ref.shape[1]
    out_ref[...] = jnp.zeros_like(out_ref)
    out_ref[0:4, :] = second_ref[0:4, :]
    out_ref[4:7, :] = first_ref[0:3, :]
    row = 7
    for ref in (up_ref, qkv_ref, count_ref):
        for start in range(0, ref.shape[1], width):
            span = min(width, ref.shape[1] - start)
            out_ref[row : row + 1, :span] = ref[0:1, start : start + span]
            row += 1


def pack(second, first, up, qkv, count):
    width = second.shape[1]
    rows = 7 + sum(-(-item.shape[1] // width) for item in (up, qkv, count))
    return pl.pallas_call(
        pack_kernel,
        out_shape=jax.ShapeDtypeStruct((-(-rows // 8) * 8, width), jnp.float32),
        name="pack",
        compiler_params=pltpu.CompilerParams(vmem_limit_bytes=2 << 20),
    )(second, first, up, qkv, count)


def join_kernel(facts, ratio_ref, own_ref, other_ref, out_ref):
    rows = own_ref.shape[1]
    for ref, half in ((own_ref, facts[0]), (other_ref, 1 - facts[0])):
        values = ref[0].astype(jnp.float32) * ratio_ref[0]
        out_ref[0, pl.ds(pl.multiple_of(half * rows, rows), rows), :] = values.astype(out_ref.dtype)


def join_halves(half, ratio=None, dtype=jnp.bfloat16, place=0):
    count, rows, width = half.shape
    ratio = jnp.ones((1,), jnp.float32) if ratio is None else ratio.reshape(1)
    return pl.pallas_call(
        join_kernel,
        grid_spec=pltpu.PrefetchScalarGridSpec(
            num_scalar_prefetch=1,
            grid=(count,),
            in_specs=[pl.BlockSpec(memory_space=pltpu.SMEM)]
            + [pl.BlockSpec((1, rows, width), lambda step, facts: (step, 0, 0))] * 2,
            out_specs=pl.BlockSpec(
                (1, 2 * rows, width), lambda step, facts: (step ^ facts[1], 0, 0)
            ),
        ),
        out_shape=jax.ShapeDtypeStruct((count, 2 * rows, width), dtype),
        name="join_halves",
        compiler_params=pltpu.CompilerParams(vmem_limit_bytes=4 << 20),
    )(
        jnp.stack([lax.axis_index("tp"), jnp.asarray(place, jnp.int32)]),
        ratio,
        half,
        swap(half, "tp", 1),
    )


def weight_grad_kernel(places, *refs, chunks, fsdp, count, order):
    kinds = len(chunks)
    left_refs, right_refs = refs[:kinds], refs[kinds : 2 * kinds]
    out_refs, held = refs[2 * kinds : -1], refs[-1]
    step = pl.program_id(0)
    first = 0
    for left_ref, right_ref, chunk in zip(left_refs, right_refs, chunks):

        @pl.when(jnp.logical_and(step >= first, step < first + chunk))
        def _():
            total = lax.dot_general(
                left_ref[...],
                right_ref[...],
                (((0,), (0,)), ((), ())),
                preferred_element_type=jnp.float32,
            )
            held[...] = total.astype(held.dtype)

        first += chunk
    rows = held.shape[0] // (fsdp * count)
    if order == "fsdp":
        own = rows * count
        for half in range(2):
            for index in range(fsdp // 2):
                start = lax.bitwise_xor(places[1], jnp.int32(half + 2 * index)) * own
                out_refs[half][index * own : (index + 1) * own, :] = held[
                    pl.ds(pl.multiple_of(start, own), own), :
                ]
    else:
        steps = list(range(0, fsdp, 2)) + list(range(1, fsdp, 2))
        for s in range(count):
            for index, d in enumerate(steps):
                start = lax.bitwise_xor(places[1], jnp.int32(d)) * (rows * count)
                start = start + lax.bitwise_xor(places[0], jnp.int32(s)) * rows
                out_refs[s][index * rows : (index + 1) * rows, :] = held[
                    pl.ds(pl.multiple_of(start, rows), rows), :
                ]


def weight_grad(places, pairs, order="ctx"):
    fsdp, count = lax.axis_size("fsdp"), lax.axis_size("ctx")
    tokens, rows = pairs[0][0].shape
    columns = [right.shape[1] for _, right in pairs]
    width = max(
        item for item in range(LANES, 6 * LANES + 1, LANES) if not any(c % item for c in columns)
    )
    chunks = [item // width for item in columns]
    firsts = [sum(chunks[:index]) for index in range(len(chunks))]
    pieces = count if order == "ctx" else 2
    right_spec = lambda first, chunk: pl.BlockSpec(
        (tokens, width), lambda step, places: (0, jnp.clip(step - first, 0, chunk - 1))
    )
    return pl.pallas_call(
        lambda *refs: weight_grad_kernel(
            *refs, chunks=chunks, fsdp=fsdp, count=count, order=order
        ),
        grid_spec=pltpu.PrefetchScalarGridSpec(
            num_scalar_prefetch=1,
            grid=(sum(chunks),),
            in_specs=[pl.BlockSpec((tokens, rows), lambda step, places: (0, 0))] * len(pairs)
            + [right_spec(first, chunk) for first, chunk in zip(firsts, chunks)],
            out_specs=[pl.BlockSpec((rows // pieces, width), lambda step, places: (0, step))]
            * pieces,
            scratch_shapes=[pltpu.VMEM((rows, width), jnp.bfloat16)],
        ),
        out_shape=[jax.ShapeDtypeStruct((rows // pieces, sum(columns)), jnp.bfloat16)] * pieces,
        name="weight_grad",
        compiler_params=pltpu.CompilerParams(vmem_limit_bytes=14 << 20),
    )(places, *[left for left, _ in pairs], *[right for _, right in pairs])


def halve(kept, brought):
    rows = kept.shape[0] // 2
    return [
        low(wide(kept[cut]) + wide(brought[cut]))
        for cut in (slice(0, rows), slice(rows, 2 * rows))
    ]


def sum_kernel(*refs):
    part_refs, (kept_ref, sent_ref) = refs[:-2], refs[-2:]
    total = part_refs[0][...].astype(jnp.float32) + part_refs[1][...].astype(jnp.float32)
    for first, second in zip(part_refs[2::2], part_refs[3::2]):
        total = total + (first[...].astype(jnp.float32) + second[...].astype(jnp.float32))
    rows = kept_ref.shape[0]
    kept_ref[...] = total[:rows].astype(kept_ref.dtype)
    sent_ref[...] = total[rows:].astype(sent_ref.dtype)


def sum_and_cut(parts):
    rows, columns = parts[0].shape
    return pl.pallas_call(
        sum_kernel,
        out_shape=[jax.ShapeDtypeStruct((rows // 2, columns), jnp.bfloat16)] * 2,
        name="sum_and_cut",
        compiler_params=pltpu.CompilerParams(vmem_limit_bytes=8 << 20),
    )(*parts)


def place_kernel(places, ratio_ref, *refs, kinds):
    part_refs, (first_ref, second_ref) = refs[:-2], refs[-2:]
    rows = part_refs[0].shape[0]
    width = first_ref.shape[1]
    pairs = width // (kinds * LANES)
    ratio = ratio_ref[0]
    for s in range(len(part_refs)):
        start = lax.bitwise_xor(places[0], jnp.int32(s)) * rows
        start = pl.multiple_of(start, rows)
        second_ref[pl.ds(start, rows), :] = part_refs[s][:, width:].astype(jnp.float32) * ratio
        for kind in range(kinds):
            for pair in range(pairs):
                source = (pair * kinds + kind) * LANES
                target = (kind * pairs + pair) * LANES
                out = part_refs[s][:, source : source + LANES].astype(jnp.float32) * ratio
                first_ref[pl.ds(start, rows), target : target + LANES] = out


def place_rows(places, parts, ratio, width, kinds):
    rows, columns = parts[0].shape
    whole = lambda shape: pl.BlockSpec(shape, lambda step, places: (0, 0))
    shapes = [(rows * len(parts), width), (rows * len(parts), columns - width)]
    return pl.pallas_call(
        lambda *refs: place_kernel(*refs, kinds=kinds),
        grid_spec=pltpu.PrefetchScalarGridSpec(
            num_scalar_prefetch=1,
            grid=(1,),
            in_specs=[pl.BlockSpec(memory_space=pltpu.SMEM)]
            + [whole(item.shape) for item in parts],
            out_specs=[whole(shape) for shape in shapes],
        ),
        out_shape=[jax.ShapeDtypeStruct(shape, jnp.float32) for shape in shapes],
        name="place_rows",
        compiler_params=pltpu.CompilerParams(vmem_limit_bytes=10 << 20),
    )(places, ratio.reshape(1), *parts)


def columns_kernel(first_ref, second_ref, out_ref):
    width = first_ref.shape[1]
    out_ref[:, :width] = first_ref[...]
    out_ref[:, width:] = second_ref[...]


def stack_columns(first, second):
    return pl.pallas_call(
        columns_kernel,
        out_shape=jax.ShapeDtypeStruct(
            (first.shape[0], first.shape[1] + second.shape[1]), first.dtype
        ),
        name="stack_columns",
        compiler_params=pltpu.CompilerParams(vmem_limit_bytes=4 << 20),
    )(first, second)


def whole_local(
    hidden_in,
    valid_mask,
    teacher,
    qkv_weight,
    qv_bias,
    out_weight,
    out_bias,
    norm1_gain,
    norm1_shift,
    up_weight,
    up_bias,
    down_weight,
    down_bias,
    norm2_gain,
    norm2_shift,
):
    seq_count, block_len, model_width = hidden_in.shape
    ctx_count = lax.axis_size("ctx")
    place, depth, core = lax.axis_index("ctx"), lax.axis_index("fsdp"), lax.axis_index("tp")
    inner_width = qkv_weight.shape[2]
    hidden_width = up_weight.shape[1]
    row_count = seq_count * block_len
    shape = hidden_in.shape
    places = jnp.stack([place, depth])
    fsdp_count = lax.axis_size("fsdp")
    row = lambda values: values.reshape(1, -1)
    struct = jax.ShapeDtypeStruct
    part_rows = qkv_weight.shape[0] // ctx_count
    own_part = lambda weight: lax.dynamic_slice_in_dim(weight, place * part_rows, part_rows, 0)
    qkv_out = jnp.concatenate([by_pairs(qkv_weight), out_weight], axis=1)
    local_counts = jnp.sum(wide(valid_mask), axis=1)
    hidden_own, weight_own = together(own_half(hidden_in), own_part(qkv_out))
    weight_rows = swap_all(weight_own, "fsdp")
    hidden_half = deal(hidden_own, "ctx")
    count_rows = jnp.broadcast_to(
        jnp.pad(low(local_counts), (0, qkv_out.shape[1] - seq_count)), (16, qkv_out.shape[1])
    )
    full_bias = row(by_pairs(jnp.stack([qv_bias[0], jnp.zeros_like(qv_bias[0]), qv_bias[1]])))
    teacher_own = own_half(teacher)
    teacher_own = [
        lax.dynamic_index_in_dim(teacher_own, place ^ s, 0, keepdims=False)
        for s in range(ctx_count)
    ]
    weight_rows, hidden_half, count_rows, up_own, down_own, teacher_own, full_bias = together(
        weight_rows,
        hidden_half,
        count_rows,
        own_part(up_weight),
        own_part(down_weight),
        teacher_own,
        full_bias,
    )
    weight_part = stack_rows(weight_rows + [count_rows])
    weight_parts = [weight_part, swap(weight_part, "ctx", 1), swap(weight_part, "ctx", 2)]
    up_rows = [swap(up_own, "fsdp", 1), swap(up_own, "fsdp", 2)]
    weight_parts, up_rows = together(weight_parts, up_rows)
    weight_parts = weight_parts + [swap(weight_parts[1], "ctx", 2)]
    up_rows = up_rows + [swap(up_rows[0], "fsdp", 2)]
    down_rows = [swap(down_own, "fsdp", 1), swap(down_own, "fsdp", 2)]
    flat_in = join_halves(hidden_half).reshape(row_count, model_width)
    weight_parts, flat_in, up_rows, down_rows = together(
        weight_parts, flat_in, up_rows, down_rows
    )
    up_part = stack_rows(up_rows)
    up_parts = [up_part] + swap_all(up_part, "ctx")
    down_rows = down_rows + [swap(down_rows[0], "fsdp", 2)]
    counts = sum(wide(item[-16, :LANES]) for item in weight_parts)
    valid_count = lax.dynamic_index_in_dim(counts, place, 0, keepdims=False).astype(jnp.int32)
    facts = jnp.stack([valid_count, core, place])
    projected, full_qkv_out = gathered_layer(
        project_kernel,
        "project",
        block_len,
        places,
        flat_in,
        [full_bias],
        qkv_out,
        weight_parts,
        [3 * inner_width],
        fsdp_count,
    )
    full_out = full_qkv_out[:, 3 * inner_width :]
    attended, log_total = attend(facts, projected, block_len)
    attended, up_parts, down_rows = together(attended, up_parts, down_rows)
    down_part = stack_rows(down_rows)
    cut = hidden_width // 2
    down_parts = [down_part] + swap_all(down_part[:, :cut], "ctx")
    branch = rows_times(attended, full_out, block_len, True)
    normal1, scale1, normed1_low = by_rows(
        first_norm_kernel,
        "first_norm",
        block_len,
        [flat_in, branch, swap(branch, "tp", 1), row(out_bias), row(norm1_gain), row(norm1_shift)],
        [
            struct((row_count, model_width), jnp.float32),
            struct((row_count, 1), jnp.float32),
            struct((row_count, model_width), jnp.bfloat16),
        ],
    )
    normed1_low, down_parts = together(normed1_low, down_parts)
    down_others = swap_all(down_parts[0][:, cut:], "ctx")
    active, slope, full_up = gathered_layer(
        up_kernel,
        "up",
        block_len,
        places,
        normed1_low,
        [row(up_bias)],
        up_weight,
        up_parts,
        [hidden_width, hidden_width],
        fsdp_count,
    )
    active, down_parts, down_others = together(active, down_parts, down_others)
    teacher_half = stack_rows(
        [teacher_own[0]] + swap_each(teacher_own, "ctx")
    ).reshape(ctx_count, block_len // 2, model_width)
    branch, full_down = gathered_layer(
        down_kernel,
        "down",
        block_len,
        places,
        active,
        [],
        down_weight,
        down_parts[:1] + down_parts[1:] + down_others,
        [model_width],
        fsdp_count,
    )
    layer_half, grad_resid2, grad_resid2_low, stats2 = by_rows(
        second_norm_kernel,
        "second_norm",
        block_len,
        [
            normal1,
            row(norm1_gain),
            row(norm1_shift),
            branch,
            swap(branch, "tp", 1),
            row(down_bias),
            row(norm2_gain),
            row(norm2_shift),
            teacher_half,
            swap(teacher_half, "tp", 1),
        ],
        [
            struct(teacher_half.shape, jnp.bfloat16),
            struct((row_count, model_width), jnp.float32),
            struct((row_count, model_width), jnp.bfloat16),
        ],
        facts=facts,
        stats=model_width,
    )
    down_kept, down_sent = weight_grad(places, [(grad_resid2_low, active)], "fsdp")
    down_kept, down_sent, grad_resid2_low = together(down_kept, down_sent, grad_resid2_low)
    down_brought = swap(down_sent, "fsdp", 1)
    layer_pieces = [layer_half[s] for s in range(ctx_count)]
    layer_pieces = layer_pieces[:1] + swap_each(layer_pieces, "ctx")
    grad_pre, stats_up = wide_layer(
        grad_pre_kernel, "grad_pre", block_len, grad_resid2_low, full_down, [slope], 1, hidden_width
    )
    branch = rows_times(grad_pre, full_up, block_len, True)
    branch, grad_pre, layer_pieces = together(branch, grad_pre, layer_pieces)
    up_pieces = weight_grad(places, [(normed1_low, grad_pre)])
    up_brought = swap_each(up_pieces, "ctx")
    grad_resid1_low, grad_half, stats1 = by_rows(
        first_norm_back_kernel,
        "first_norm_back",
        block_len,
        [grad_resid2, branch, swap(branch, "tp", 1), normal1, scale1, row(norm1_gain)],
        [
            struct((row_count, model_width), jnp.bfloat16),
            struct(layer_half.shape, jnp.float32),
        ],
        facts=facts,
        stats=model_width,
    )
    out_kept, out_sent = weight_grad(places, [(grad_resid1_low, attended)], "fsdp")
    grad_attended = rows_times(grad_resid1_low, full_out, block_len, False)
    out_kept, out_sent, grad_attended = together(out_kept, out_sent, grad_attended)
    out_brought = swap(out_sent, "fsdp", 1)
    grad_qkv, stats_qkv = attend_back(facts, projected, grad_attended, log_total, block_len)
    grad_qkv, up_brought, down_brought, out_brought = together(
        grad_qkv, up_brought, down_brought, out_brought
    )
    last_pieces = weight_grad(places, [(flat_in, grad_qkv)])
    down_kept, down_sent = sum_and_cut([down_kept, down_brought])
    out_kept, out_sent = sum_and_cut([out_kept, out_brought])
    last_pieces, grad_qkv, up_brought, down_sent, out_sent, layer_pieces, stats_qkv = together(
        last_pieces, grad_qkv, up_brought, down_sent, out_sent, layer_pieces, stats_qkv
    )
    last_brought = swap_each(last_pieces, "ctx")
    down_brought = swap(down_sent, "fsdp", 2)
    out_brought = swap(out_sent, "fsdp", 2)
    mine, other = input_back(facts, grad_qkv, full_qkv_out, block_len)
    up_kept, up_sent = sum_and_cut([up_pieces[0]] + up_brought)
    local_count = jnp.broadcast_to(jnp.sum(local_counts), (1, LANES))
    small = pack(stats2, stats1, stats_up, stats_qkv, local_count)
    last_brought, mine, other, down_brought, out_brought, up_sent, small, layer_pieces = together(
        last_brought, mine, other, down_brought, out_brought, up_sent, small, layer_pieces
    )
    last_kept, last_sent = sum_and_cut([last_pieces[0]] + last_brought)
    last_sent, other, down_brought, out_brought, up_sent, small, layer_pieces = together(
        last_sent, other, down_brought, out_brought, up_sent, small, layer_pieces
    )
    last_brought = swap(last_sent, "fsdp", 1)
    up_brought = swap(up_sent, "fsdp", 1)
    other = swap(other, "tp", 1)
    owned_down = low(wide(down_kept) + wide(down_brought))
    down_other = swap(owned_down, "ctx", 1)
    layer_stack = stack_rows(layer_pieces).reshape(layer_half.shape)
    layer_out = join_halves(layer_stack, place=place)
    last_brought, up_brought, other, small, layer_out, out_brought = together(
        last_brought, up_brought, other, small, layer_out, out_brought
    )
    last_kept, last_sent = sum_and_cut([last_kept, last_brought])
    last_sent, up_brought, other, small, out_brought = together(
        last_sent, up_brought, other, small, out_brought
    )
    last_brought = swap(last_sent, "fsdp", 2)
    up_kept, up_sent = sum_and_cut([up_kept, up_brought])
    up_brought = swap(up_sent, "fsdp", 2)
    owned_out = low(wide(out_kept) + wide(out_brought))
    out_other = swap(owned_out, "ctx", 1)
    half = low(grad_half + (wide(mine) + wide(other)))
    small = sum_over(small, "ctx")
    last_brought, up_brought, half, down_other, out_other, small = together(
        last_brought, up_brought, half, down_other, out_other, small
    )
    part = low(wide(last_kept) + wide(last_brought))
    up_part = low(wide(up_kept) + wide(up_brought))
    shared = stack_columns(part, up_part)
    shared, half, down_other, out_other, small = together(
        shared, half, down_other, out_other, small
    )
    shared = [shared, swap(shared, "ctx", 1), swap(shared, "ctx", 2)]
    half_pieces = [half[s] for s in range(ctx_count)]
    half_brought = swap_each(half_pieces, "ctx")
    shared, half_brought, down_other, out_other, small = together(
        shared, half_brought, down_other, out_other, small
    )
    shared = shared + [swap(shared[1], "ctx", 2)]
    owned_down = low(wide(owned_down) + wide(down_other))
    owned_out = low(wide(owned_out) + wide(out_other))
    down_other, out_other = swap(owned_down, "ctx", 2), swap(owned_out, "ctx", 2)
    small = sum_over(small, "fsdp")
    input_half = stack_rows(half_pieces[:1] + half_brought).reshape(half.shape)
    at = 7 + -(-hidden_width // model_width)
    counted = small[at + -(-3 * inner_width // model_width), 0]
    ratio = float(row_count * ctx_count * fsdp_count) / counted
    loss = jnp.sum(small[3]) / (counted * model_width)
    scaled = small * ratio
    input_grad = join_halves(input_half, ratio, jnp.float32, place)
    shared, down_other, out_other, input_grad, scaled = together(
        shared, down_other, out_other, input_grad, scaled
    )
    owned_qkv, owned_up = place_rows(places, shared, ratio, 3 * inner_width, 3)
    owned_qkv = owned_qkv.reshape(qkv_weight.shape)
    owned_down = (wide(owned_down) + wide(down_other)) * ratio
    owned_out = (wide(owned_out) + wide(out_other)) * ratio
    grad_up_bias = scaled[7:at].reshape(-1)[:hidden_width]
    grad_qv_bias = by_kinds(
        scaled[at : at + -(-3 * inner_width // model_width)].reshape(-1)[: 3 * inner_width]
    )[0::2]
    return (
        layer_out,
        input_grad,
        loss,
        owned_qkv,
        grad_qv_bias,
        owned_out,
        scaled[4],
        scaled[5],
        scaled[6],
        owned_up,
        grad_up_bias,
        owned_down,
        scaled[0],
        scaled[1],
        scaled[2],
    )


def spread_local(
    hidden_in,
    valid_mask,
    teacher,
    qkv_weight,
    qv_bias,
    out_weight,
    out_bias,
    norm1_gain,
    norm1_shift,
    up_weight,
    up_bias,
    down_weight,
    down_bias,
    norm2_gain,
    norm2_shift,
):
    seq_count, block_len, model_width = hidden_in.shape
    ctx_count = lax.axis_size("ctx")
    ctx_place = lax.axis_index("ctx")
    key_span = 2 * block_len
    seq_length = block_len * ctx_count
    row_count = seq_count * block_len
    scaling = HEAD_DIM ** (-0.5)
    full_qkv, full_out, full_up, full_down = (
        lax.all_gather(qkv_weight, "fsdp", axis=0, tiled=True),
        lax.all_gather(out_weight, "fsdp", axis=0, tiled=True),
        lax.all_gather(up_weight, "fsdp", axis=0, tiled=True),
        lax.all_gather(down_weight, "fsdp", axis=0, tiled=True),
    )
    inner_width = full_qkv.shape[2]
    head_count = inner_width // HEAD_DIM
    flat_in = hidden_in.reshape(row_count, model_width)
    full_bias = jnp.stack([qv_bias[0], jnp.zeros_like(qv_bias[0]), qv_bias[1]])
    projected = (
        jnp.einsum("td,dje->tje", flat_in, full_qkv, preferred_element_type=jnp.float32) + full_bias
    ).astype(jnp.bfloat16)
    queries = projected[:, 0].reshape(seq_count, block_len, inner_width)
    key_own = projected[:, 1].reshape(seq_count, block_len, inner_width)
    value_own = projected[:, 2].reshape(seq_count, block_len, inner_width)
    keep_own = valid_mask.astype(jnp.bfloat16)
    keys_all, values_all, keep_all = (
        lax.all_gather(key_own, "ctx", axis=1, tiled=True),
        lax.all_gather(value_own, "ctx", axis=1, tiled=True),
        lax.all_gather(keep_own, "ctx", axis=1, tiled=True),
    )
    query_heads = split_heads(queries)
    seen_limit = (ctx_place + 1) * block_len
    trip_count = ctx_place // 2 + 1
    offsets = jnp.arange(key_span, dtype=jnp.int32)

    def key_block(block_index):
        key_start = block_index * key_span
        key_heads = split_heads(lax.dynamic_slice_in_dim(keys_all, key_start, key_span, 1))
        value_heads = split_heads(lax.dynamic_slice_in_dim(values_all, key_start, key_span, 1))
        live_keys = lax.dynamic_slice_in_dim(keep_all, key_start, key_span, 1) > 0.5
        allowed = jnp.logical_and(live_keys, (key_start + offsets)[None, :] < seen_limit)
        return (key_heads, value_heads, allowed[:, None, None, :])

    def attend_step(block_index, carried):
        run_top, run_total, gathered = carried
        key_heads, value_heads, allowed = key_block(block_index)
        raw_scores = scores_of(query_heads, key_heads, allowed, scaling)
        new_top = jnp.maximum(run_top, jnp.max(raw_scores, axis=-1))
        shrink = jnp.exp(run_top - new_top)
        weights_now = jnp.exp(raw_scores - new_top[..., None])
        run_total = run_total * shrink + jnp.sum(weights_now, axis=-1)
        gathered = gathered * jnp.swapaxes(shrink, 1, 2)[..., None] + jnp.einsum(
            "shqk,skhd->sqhd",
            weights_now.astype(jnp.bfloat16),
            value_heads,
            preferred_element_type=jnp.float32,
        )
        return (new_top, run_total, gathered)

    start_top = jnp.full((seq_count, head_count, block_len), MASKED, jnp.float32)
    empty_heads = jnp.zeros((seq_count, block_len, head_count, HEAD_DIM), jnp.float32)
    run_top, run_total, gathered = lax.fori_loop(
        0, trip_count, attend_step, (start_top, jnp.zeros_like(start_top), empty_heads)
    )
    log_total = run_top + jnp.log(run_total)
    attended_exact = gathered / jnp.swapaxes(run_total, 1, 2)[..., None]
    attended = attended_exact.astype(jnp.bfloat16).reshape(row_count, inner_width)
    attn_branch = lax.psum(
        jnp.einsum("te,de->td", attended, full_out, preferred_element_type=jnp.float32).astype(
            jnp.bfloat16
        ),
        "tp",
    ).astype(jnp.float32)
    resid1 = flat_in.astype(jnp.float32) + attn_branch + out_bias
    normed1, norm1_back = jax.vjp(layer_norm, resid1, norm1_gain, norm1_shift)
    normed1_low = normed1.astype(jnp.bfloat16)
    pre_act = jnp.dot(normed1_low, full_up, preferred_element_type=jnp.float32) + up_bias
    active, gelu_back = jax.vjp(gelu_exact, pre_act)
    active = active.astype(jnp.bfloat16)
    ffn_branch = lax.psum(
        jnp.einsum("tf,df->td", active, full_down, preferred_element_type=jnp.float32).astype(
            jnp.bfloat16
        ),
        "tp",
    ).astype(jnp.float32)
    resid2 = normed1 + ffn_branch + down_bias
    output, norm2_back = jax.vjp(layer_norm, resid2, norm2_gain, norm2_shift)
    layer_out = output.astype(jnp.bfloat16).reshape(seq_count, block_len, model_width)
    keep_rows = valid_mask.reshape(row_count, 1).astype(jnp.float32)
    residue = (output - teacher.reshape(row_count, model_width).astype(jnp.float32)) * keep_rows
    squared = jnp.sum(residue * residue)
    counted = jnp.sum(keep_rows)
    grad_resid2, grad_gain2, grad_shift2 = norm2_back(residue)
    grad_down_bias = jnp.sum(grad_resid2, axis=0)
    grad_resid2_low = grad_resid2.astype(jnp.bfloat16)
    grad_active = jnp.dot(grad_resid2_low, full_down, preferred_element_type=jnp.float32)
    grad_down_weight = jnp.einsum(
        "td,tf->df", grad_resid2_low, active, preferred_element_type=jnp.float32
    )
    grad_pre = gelu_back(grad_active)[0].astype(jnp.bfloat16)
    grad_up_bias = jnp.sum(grad_pre.astype(jnp.float32), axis=0)
    grad_up_weight = jnp.einsum(
        "td,tf->df", normed1_low, grad_pre, preferred_element_type=jnp.float32
    )
    ffn_input_grad = lax.psum(
        jnp.einsum("tf,df->td", grad_pre, full_up, preferred_element_type=jnp.float32).astype(
            jnp.bfloat16
        ),
        "tp",
    ).astype(jnp.float32)
    grad_normed1 = grad_resid2 + ffn_input_grad
    grad_resid1, grad_gain1, grad_shift1 = norm1_back(grad_normed1)
    grad_out_bias = jnp.sum(grad_resid1, axis=0)
    grad_resid1_low = grad_resid1.astype(jnp.bfloat16)
    grad_mixed = jnp.dot(grad_resid1_low, full_out, preferred_element_type=jnp.float32)
    grad_out_weight = jnp.einsum(
        "td,te->de", grad_resid1_low, attended, preferred_element_type=jnp.float32
    )
    grad_attended = grad_mixed.astype(jnp.bfloat16).reshape(
        seq_count, block_len, head_count, HEAD_DIM
    )
    delta = jnp.swapaxes(jnp.sum(grad_attended.astype(jnp.float32) * attended_exact, axis=-1), 1, 2)

    def query_grads(block_index):
        key_heads, value_heads, allowed = key_block(block_index)
        prob_rows = jnp.exp(
            scores_of(query_heads, key_heads, allowed, scaling) - log_total[..., None]
        )
        push = jnp.einsum(
            "sqhd,skhd->shqk", grad_attended, value_heads, preferred_element_type=jnp.float32
        )
        slope = (prob_rows * (push - delta[..., None])).astype(jnp.bfloat16)
        grad_part = (
            jnp.einsum("shqk,skhd->sqhd", slope, key_heads, preferred_element_type=jnp.float32)
            * scaling
        )
        return (prob_rows, slope, grad_part)

    def back_step(block_index, carried):
        grad_query, spread = carried
        prob_rows, slope, grad_part = query_grads(block_index)
        grad_key = (
            jnp.einsum("shqk,sqhd->skhd", slope, query_heads, preferred_element_type=jnp.float32)
            * scaling
        )
        grad_value = jnp.einsum(
            "shqk,sqhd->skhd",
            prob_rows.astype(jnp.bfloat16),
            grad_attended,
            preferred_element_type=jnp.float32,
        )
        piece = jnp.stack(
            [
                grad_key.reshape(seq_count, key_span, inner_width),
                grad_value.reshape(seq_count, key_span, inner_width),
            ],
            axis=2,
        )
        spread = lax.dynamic_update_slice_in_dim(spread, piece, block_index * key_span, 1)
        return (grad_query + grad_part, spread)

    spread_start = jnp.zeros((seq_count, seq_length, 2, inner_width), jnp.float32)
    grad_query, spread = lax.fori_loop(0, trip_count, back_step, (empty_heads, spread_start))
    own_grads = lax.psum_scatter(
        spread.astype(jnp.bfloat16), "ctx", scatter_dimension=1, tiled=True
    ).astype(jnp.float32)
    grad_key_own = own_grads[:, :, 0]
    grad_value_own = own_grads[:, :, 1]
    grad_qkv = jnp.stack(
        [
            grad_query.reshape(row_count, inner_width),
            grad_key_own.reshape(row_count, inner_width),
            grad_value_own.reshape(row_count, inner_width),
        ],
        axis=1,
    ).astype(jnp.bfloat16)
    grad_qv_bias = jnp.sum(grad_qkv[:, 0::2].astype(jnp.float32), axis=0)
    grad_qkv_weight = jnp.einsum(
        "td,tje->dje", flat_in, grad_qkv, preferred_element_type=jnp.float32
    )
    input_part = lax.psum(
        jnp.einsum("tje,dje->td", grad_qkv, full_qkv, preferred_element_type=jnp.float32).astype(
            jnp.bfloat16
        ),
        "tp",
    ).astype(jnp.float32)
    grad_input = grad_resid1 + input_part
    vectors = jnp.stack(
        [grad_out_bias, grad_gain1, grad_shift1, grad_down_bias, grad_gain2, grad_shift2]
    )
    squared, counted, vectors, grad_qv_bias, grad_up_bias = lax.psum(
        (squared, counted, vectors, grad_qv_bias, grad_up_bias), ("fsdp", "ctx")
    )
    local_grads = (grad_qkv_weight, grad_out_weight, grad_up_weight, grad_down_weight)
    owned = (
        lax.psum_scatter(
            local_grads[0].astype(jnp.bfloat16), "fsdp", scatter_dimension=0, tiled=True
        ).astype(jnp.float32),
        lax.psum_scatter(
            local_grads[1].astype(jnp.bfloat16), "fsdp", scatter_dimension=0, tiled=True
        ).astype(jnp.float32),
        lax.psum_scatter(
            local_grads[2].astype(jnp.bfloat16), "fsdp", scatter_dimension=0, tiled=True
        ).astype(jnp.float32),
        lax.psum_scatter(
            local_grads[3].astype(jnp.bfloat16), "fsdp", scatter_dimension=0, tiled=True
        ).astype(jnp.float32),
    )
    owned = (
        lax.psum(owned[0].astype(jnp.bfloat16), "ctx").astype(jnp.float32),
        lax.psum(owned[1].astype(jnp.bfloat16), "ctx").astype(jnp.float32),
        lax.psum(owned[2].astype(jnp.bfloat16), "ctx").astype(jnp.float32),
        lax.psum(owned[3].astype(jnp.bfloat16), "ctx").astype(jnp.float32),
    )
    token_total = float(seq_count * seq_length * lax.axis_size("fsdp"))
    ratio = token_total / counted
    loss = squared / (counted * model_width)
    input_grad = (grad_input * ratio).reshape(seq_count, block_len, model_width)
    return (
        layer_out,
        input_grad,
        loss,
        owned[0] * ratio,
        grad_qv_bias * ratio,
        owned[1] * ratio,
        vectors[0] * ratio,
        vectors[1] * ratio,
        vectors[2] * ratio,
        owned[2] * ratio,
        grad_up_bias * ratio,
        owned[3] * ratio,
        vectors[3] * ratio,
        vectors[4] * ratio,
        vectors[5] * ratio,
    )


def local(hidden_in, *others):
    seq_count, block_len, model_width = hidden_in.shape
    ctx_count, fsdp_count = lax.axis_size("ctx"), lax.axis_size("fsdp")
    rows, inner_width = others[2].shape[0], others[2].shape[2]
    whole = (
        seq_count == ctx_count
        and ctx_count & (ctx_count - 1) == 0
        and fsdp_count == 4
        and lax.axis_size("tp") == 2
        and block_len % LANES == 0
        and others[5].shape[0] >= inner_width
        and inner_width % LANES == 0
        and rows % (16 * ctx_count) == 0
    )
    return (whole_local if whole else spread_local)(hidden_in, *others)


def solution(mesh):
    in_specs = (
        P("fsdp", "ctx", None),
        P("fsdp", "ctx"),
        P("fsdp", "ctx", None),
        P("fsdp", None, "tp"),
        P(None, "tp"),
        P("fsdp", "tp"),
        P(),
        P(),
        P(),
        P("fsdp", "tp"),
        P("tp"),
        P("fsdp", "tp"),
        P(),
        P(),
        P(),
    )
    out_specs = (
        P("fsdp", "ctx", None),
        P("fsdp", "ctx", None),
        P(),
        P("fsdp", None, "tp"),
        P(None, "tp"),
        P("fsdp", "tp"),
        P(),
        P(),
        P(),
        P("fsdp", "tp"),
        P("tp"),
        P("fsdp", "tp"),
        P(),
        P(),
        P(),
    )
    return jax.shard_map(local, mesh=mesh, in_specs=in_specs, out_specs=out_specs, check_vma=False)
```

```python
import jax
import jax.numpy as jnp
from jax import lax
from jax.experimental import pallas as pl
from jax.experimental.pallas import tpu as pltpu
from jax.sharding import PartitionSpec as P

HEAD_DIM = 64
NORM_EPS = 1e-05
MASKED = -1e30
LANES = 128


def layer_norm(values_in, gain_vec, shift_vec):
    row_mean = jnp.mean(values_in, axis=-1, keepdims=True)
    centered = values_in - row_mean
    row_var = jnp.mean(centered * centered, axis=-1, keepdims=True)
    return centered * lax.rsqrt(row_var + NORM_EPS) * gain_vec + shift_vec


def gelu_exact(pre_act):
    return jax.nn.gelu(pre_act, approximate=False)


def split_heads(packed):
    return packed.reshape(packed.shape[0], packed.shape[1], packed.shape[2] // HEAD_DIM, HEAD_DIM)


def scores_of(query_heads, key_heads, allowed, scaling):
    raw_scores = (
        jnp.einsum("sqhd,skhd->shqk", query_heads, key_heads, preferred_element_type=jnp.float32)
        * scaling
    )
    return jnp.where(allowed, raw_scores, MASKED)


def rows_by_rows(left, right):
    return lax.dot_general(left, right, (((1,), (1,)), ((), ())), preferred_element_type=jnp.float32)


def plain_dot(left, right):
    return jnp.dot(left, right, preferred_element_type=jnp.float32)


def lanes_of(head, lane):
    own = (lane < HEAD_DIM) if head == 0 else (lane >= HEAD_DIM)
    spare = HEAD_DIM if head == 0 else 0
    return own, lane == spare


def head_operands(query_ref, key_ref, slot, start, block, valid_count, head):
    lane = lax.broadcasted_iota(jnp.int32, (block, LANES), 1)
    own, spare = lanes_of(head, lane)
    position = start + lax.broadcasted_iota(jnp.int32, (block, LANES), 0)
    bias = jnp.where(position < valid_count, 0.0, MASKED)
    rows = pl.ds(slot * block, block)
    query = query_ref[rows, :].astype(jnp.float32) * (HEAD_DIM ** -0.5)
    key = key_ref[rows, :].astype(jnp.float32)
    query_side = jnp.where(spare, 1.0, query).astype(jnp.bfloat16)
    key_side = jnp.where(own, key, jnp.where(spare, bias, 0.0)).astype(jnp.bfloat16)
    return query_side, key_side


def attend_kernel(facts, query_ref, key_ref, value_ref, out_ref, log_ref, *, block):
    valid_count = facts[0]
    blocks = query_ref.shape[0] // block
    slots = list(range(blocks))
    value_t = [
        value_ref[pl.ds(slots[j] * block, block), :].astype(jnp.float32).T.astype(jnp.bfloat16)
        for j in range(blocks)
    ]
    outs = [[] for _ in range(blocks)]
    for head in range(2):
        sides = [
            head_operands(query_ref, key_ref, slots[j], j * block, block, valid_count, head)
            for j in range(blocks)
        ]
        span = slice(head * HEAD_DIM, (head + 1) * HEAD_DIM)
        for i in range(blocks):
            scores = [rows_by_rows(sides[j][1], sides[i][0]) for j in range(i + 1)]
            top = scores[0].max(axis=0, keepdims=True)
            for j in range(1, i + 1):
                top = jnp.maximum(top, scores[j].max(axis=0, keepdims=True))
            total = jnp.zeros_like(top)
            mixed = jnp.zeros((HEAD_DIM, block), jnp.float32)
            for j in range(i + 1):
                weight = jnp.exp(scores[j] - top)
                total = total + weight.sum(axis=0, keepdims=True)
                mixed = mixed + plain_dot(value_t[j][span, :], weight.astype(jnp.bfloat16))
            outs[i].append(mixed / total)
            log_ref[0, head : head + 1, i * block : (i + 1) * block] = top + jnp.log(total)
    for i in range(blocks):
        both = jnp.concatenate(outs[i], axis=0)
        out_ref[pl.ds(slots[i] * block, block), :] = both.T.astype(out_ref.dtype)


def attend_back_kernel(
    facts,
    query_ref,
    key_ref,
    value_ref,
    grad_ref,
    log_ref,
    out_ref,
    stats_ref,
    grad_key,
    grad_value,
    *,
    block,
):
    valid_count = facts[0]
    blocks = query_ref.shape[0] // block
    slots = list(range(blocks))
    scaling = HEAD_DIM ** -0.5
    lane = lax.broadcasted_iota(jnp.int32, (block, LANES), 1)
    key_t, grads, queries, values = [], [], [], []
    for j in range(blocks):
        rows = pl.ds(slots[j] * block, block)
        key_t.append((key_ref[rows, :].astype(jnp.float32) * scaling).T.astype(jnp.bfloat16))
        grads.append(grad_ref[rows, :])
        queries.append(query_ref[rows, :].astype(jnp.float32) * scaling)
        values.append(value_ref[rows, :].astype(jnp.float32))
    grad_queries = [[] for _ in range(blocks)]
    for head in range(2):
        own, _ = lanes_of(head, lane)
        span = slice(head * HEAD_DIM, (head + 1) * HEAD_DIM)
        sides = [
            head_operands(query_ref, key_ref, slots[j], j * block, block, valid_count, head)
            for j in range(blocks)
        ]
        head_values = [jnp.where(own, item, 0.0).astype(jnp.bfloat16) for item in values]
        for i in range(blocks):
            log_row = log_ref[0, head : head + 1, i * block : (i + 1) * block]
            head_grad = jnp.where(own, grads[i].astype(jnp.float32), 0.0).astype(jnp.bfloat16)
            head_query = jnp.where(own, queries[i], 0.0).astype(jnp.bfloat16)
            probs, pushes = [], []
            delta = jnp.zeros((1, block), jnp.float32)
            for j in range(i + 1):
                prob = jnp.exp(rows_by_rows(sides[j][1], sides[i][0]) - log_row)
                push = rows_by_rows(head_values[j], grads[i])
                delta = delta + (prob * push).sum(axis=0, keepdims=True)
                probs.append(prob)
                pushes.append(push)
            grad_query = jnp.zeros((HEAD_DIM, block), jnp.float32)
            for j in range(i + 1):
                slope = (probs[j] * (pushes[j] - delta)).astype(jnp.bfloat16)
                part_value = plain_dot(probs[j].astype(jnp.bfloat16), head_grad)
                part_key = plain_dot(slope, head_query)
                span_rows = slice(j * block, (j + 1) * block)
                if head == 0 and i == j:
                    grad_value[span_rows, :] = part_value
                    grad_key[span_rows, :] = part_key
                else:
                    grad_value[span_rows, :] += part_value
                    grad_key[span_rows, :] += part_key
                grad_query = grad_query + plain_dot(key_t[j][span, :], slope)
            grad_queries[i].append(grad_query)
    totals = jnp.zeros((1, 3 * LANES), jnp.float32)
    for i in range(blocks):
        rows = pl.ds(slots[i] * block, block)
        both = jnp.concatenate(grad_queries[i], axis=0)
        out_ref[rows, :LANES] = both.T.astype(out_ref.dtype)
        span_rows = slice(i * block, (i + 1) * block)
        out_ref[rows, LANES : 2 * LANES] = grad_key[span_rows, :].astype(out_ref.dtype)
        out_ref[rows, 2 * LANES :] = grad_value[span_rows, :].astype(out_ref.dtype)
        totals += jnp.sum(out_ref[rows, :].astype(jnp.float32), axis=0, keepdims=True)
    stats_ref[...] = jnp.broadcast_to(totals, stats_ref.shape)


def attend(facts, projected, block):
    length, width = projected.shape
    pairs = width // (3 * LANES)
    column = lambda kind: pl.BlockSpec((length, LANES), lambda pair, facts: (0, 3 * pair + kind))
    return pl.pallas_call(
        lambda *refs: attend_kernel(*refs, block=block),
        grid_spec=pltpu.PrefetchScalarGridSpec(
            num_scalar_prefetch=1,
            grid=(pairs,),
            in_specs=[column(0), column(1), column(2)],
            out_specs=[
                pl.BlockSpec((length, LANES), lambda pair, facts: (0, pair)),
                pl.BlockSpec((1, 2, length), lambda pair, facts: (pair, 0, 0)),
            ],
        ),
        out_shape=[
            jax.ShapeDtypeStruct((length, pairs * LANES), jnp.bfloat16),
            jax.ShapeDtypeStruct((pairs, 2, length), jnp.float32),
        ],
        name="attend",
        compiler_params=pltpu.CompilerParams(vmem_limit_bytes=9 << 20),
    )(facts, projected, projected, projected)


def attend_back(facts, projected, grad_attended, log_total, block):
    length, width = grad_attended.shape
    pairs = width // LANES
    column = lambda kind: pl.BlockSpec((length, LANES), lambda pair, facts: (0, 3 * pair + kind))
    return pl.pallas_call(
        lambda *refs: attend_back_kernel(*refs, block=block),
        grid_spec=pltpu.PrefetchScalarGridSpec(
            num_scalar_prefetch=1,
            grid=(pairs,),
            in_specs=[
                column(0),
                column(1),
                column(2),
                pl.BlockSpec((length, LANES), lambda pair, facts: (0, pair)),
                pl.BlockSpec((1, 2, length), lambda pair, facts: (pair, 0, 0)),
            ],
            out_specs=[
                pl.BlockSpec((length, 3 * LANES), lambda pair, facts: (0, pair)),
                pl.BlockSpec((8, 3 * LANES), lambda pair, facts: (0, pair)),
            ],
            scratch_shapes=[
                pltpu.VMEM((length, LANES), jnp.float32),
                pltpu.VMEM((length, LANES), jnp.float32),
            ],
        ),
        out_shape=[
            jax.ShapeDtypeStruct((length, 3 * width), jnp.bfloat16),
            jax.ShapeDtypeStruct((8, 3 * width), jnp.float32),
        ],
        name="attend_back",
        compiler_params=pltpu.CompilerParams(vmem_limit_bytes=12 << 20),
    )(facts, projected, projected, projected, grad_attended, log_total)


def by_pairs(values):
    kinds, width = values.shape[-2:]
    cut = values.reshape(values.shape[:-1] + (width // LANES, LANES))
    return jnp.swapaxes(cut, -3, -2).reshape(values.shape[:-2] + (kinds * width,))


def by_kinds(values, kinds=3):
    width = values.shape[-1] // kinds
    cut = values.reshape(values.shape[:-1] + (width // LANES, kinds, LANES))
    return jnp.swapaxes(cut, -3, -2).reshape(values.shape[:-1] + (kinds, width))


def fill_rows(places, own_ref, part_refs, out_ref):
    count = len(part_refs)
    rows = own_ref.shape[0] // count
    fsdp = out_ref.shape[0] // own_ref.shape[0]
    place, depth = places[0], places[1]
    start = pl.multiple_of(depth * (rows * count), rows)
    out_ref[pl.ds(start, rows * count), :] = own_ref[...]
    for s in range(count):
        for d in range(1, fsdp):
            start = lax.bitwise_xor(depth, jnp.int32(d)) * (rows * count)
            start = start + lax.bitwise_xor(place, jnp.int32(s)) * rows
            out_ref[pl.ds(pl.multiple_of(start, rows), rows), :] = part_refs[s][
                (d - 1) * rows : d * rows, :
            ]


def project_kernel(places, left_ref, bias_ref, own_ref, *refs):
    part_refs, (out_ref, full_ref) = refs[:-2], refs[-2:]

    @pl.when(pl.program_id(0) == 0)
    def _():
        fill_rows(places, own_ref, part_refs, full_ref)

    total = plain_dot(left_ref[...], full_ref[:, : out_ref.shape[1]]) + bias_ref[...]
    out_ref[...] = total.astype(out_ref.dtype)


def up_kernel(places, left_ref, bias_ref, own_ref, *refs):
    part_refs, (active_ref, slope_ref, full_ref) = refs[:-3], refs[-3:]

    @pl.when(pl.program_id(0) == 0)
    def _():
        fill_rows(places, own_ref, part_refs, full_ref)

    pre = plain_dot(left_ref[...], full_ref[...]) + bias_ref[...]
    below = 0.5 * (1.0 + lax.erf(pre * (0.5**0.5)))
    active_ref[...] = (pre * below).astype(active_ref.dtype)
    bell = jnp.exp(-0.5 * pre * pre) * 0.3989422804014327
    slope_ref[...] = (below + pre * bell).astype(slope_ref.dtype)


def down_kernel(places, left_ref, own_ref, *refs):
    part_refs, (out_ref, full_ref) = refs[:-2], refs[-2:]

    @pl.when(pl.program_id(0) == 0)
    def _():
        fill_rows(places, own_ref, part_refs, full_ref)

    out_ref[...] = rows_by_rows(left_ref[...], full_ref[...]).astype(out_ref.dtype)


def gathered_layer(kernel, name, block, places, left, vectors, own, parts, widths, fsdp):
    length = left.shape[0]
    full = (fsdp * own.shape[0], own.shape[1])
    whole = lambda shape: pl.BlockSpec(shape, lambda step, places: (0, 0))
    by_block = lambda width: pl.BlockSpec((block, width), lambda step, places: (step, 0))
    return pl.pallas_call(
        kernel,
        grid_spec=pltpu.PrefetchScalarGridSpec(
            num_scalar_prefetch=1,
            grid=(length // block,),
            in_specs=[by_block(left.shape[1])]
            + [whole(item.shape) for item in vectors + [own] + parts],
            out_specs=[by_block(width) for width in widths] + [whole(full)],
        ),
        out_shape=[jax.ShapeDtypeStruct((length, width), jnp.bfloat16) for width in widths]
        + [jax.ShapeDtypeStruct(full, jnp.bfloat16)],
        name=name,
        compiler_params=pltpu.CompilerParams(vmem_limit_bytes=20 << 20),
    )(places, left, *vectors, own, *parts)


def stack_kernel(*refs):
    row = 0
    for ref in refs[:-1]:
        refs[-1][row : row + ref.shape[0], :] = ref[...]
        row += ref.shape[0]


def stack_rows(pieces):
    rows = sum(item.shape[0] for item in pieces)
    return pl.pallas_call(
        stack_kernel,
        out_shape=jax.ShapeDtypeStruct((rows, pieces[0].shape[1]), pieces[0].dtype),
        name="stack_rows",
        compiler_params=pltpu.CompilerParams(vmem_limit_bytes=4 << 20),
    )(*pieces)


def swap(values, axis, step):
    pairs = [(place, place ^ step) for place in range(lax.axis_size(axis))]
    return lax.ppermute(values, axis, pairs)


def swap_all(values, axis):
    return [swap(values, axis, step) for step in range(1, lax.axis_size(axis))]


def relay_all(values, axis):
    if lax.axis_size(axis) != 4:
        return swap_all(values, axis)
    first, second = swap(values, axis, 1), swap(values, axis, 2)
    return [first, second, swap(first, axis, 2)]


def swap_each(pieces, axis):
    return [swap(pieces[step], axis, step) for step in range(1, len(pieces))]


def together(*values):
    return lax.optimization_barrier(values)


def wide(values):
    return values.astype(jnp.float32)


def low(values):
    return values.astype(jnp.bfloat16)


def add_partner(values):
    mine = low(values)
    return wide(mine) + wide(swap(mine, "tp", 1))


def add_up(pieces):
    pieces = [wide(item) for item in pieces]
    while len(pieces) > 1:
        pieces = [pieces[i] + pieces[i + 1] for i in range(0, len(pieces), 2)]
    return pieces[0]


def sum_over(values, axis):
    step = 1
    while step < lax.axis_size(axis):
        values = values + swap(values, axis, step)
        step *= 2
    return values


def deal(pieces, axis):
    return lax.all_to_all(pieces, axis, 0, 0)


def own_half(blocks):
    rows = blocks.shape[1] // 2
    return lax.dynamic_slice_in_dim(blocks, lax.axis_index("tp") * rows, rows, 1)


def row_kernel_stats(stats_ref, step, rows):
    @pl.when(step == 0)
    def _():
        stats_ref[...] = jnp.zeros_like(stats_ref)

    for index, row in enumerate(rows):
        stats_ref[index : index + 1, :] += jnp.sum(row, axis=0, keepdims=True)


def normalize(values):
    mean = jnp.mean(values, axis=-1, keepdims=True)
    centered = values - mean
    scale = lax.rsqrt(jnp.mean(centered * centered, axis=-1, keepdims=True) + NORM_EPS)
    return centered * scale, scale


def normalize_back(grads, normal, scale, gain):
    pushed = grads * gain
    mean = jnp.mean(pushed, axis=-1, keepdims=True)
    along = jnp.mean(pushed * normal, axis=-1, keepdims=True)
    return (pushed - mean - normal * along) * scale


def first_norm_kernel(
    hidden_ref, mine_ref, other_ref, bias_ref, gain_ref, shift_ref, normal_ref, scale_ref, low_ref
):
    branch = mine_ref[...].astype(jnp.float32) + other_ref[...].astype(jnp.float32)
    normal, scale = normalize(hidden_ref[...].astype(jnp.float32) + branch + bias_ref[...])
    normal_ref[...] = normal
    scale_ref[...] = scale
    low_ref[...] = (normal * gain_ref[...] + shift_ref[...]).astype(low_ref.dtype)


def second_norm_kernel(
    facts,
    normal_ref,
    gain1_ref,
    shift1_ref,
    mine_ref,
    other_ref,
    bias_ref,
    gain_ref,
    shift_ref,
    own_teacher_ref,
    other_teacher_ref,
    half_ref,
    grad_ref,
    low_ref,
    stats_ref,
):
    step = pl.program_id(0)
    block = normal_ref.shape[0]
    rows = block // 2
    branch = mine_ref[...].astype(jnp.float32) + other_ref[...].astype(jnp.float32)
    normed1 = normal_ref[...] * gain1_ref[...] + shift1_ref[...]
    normal, scale = normalize(normed1 + branch + bias_ref[...])
    output = normal * gain_ref[...] + shift_ref[...]
    first = facts[1] == 0
    half_ref[0] = jnp.where(first, output[:rows], output[rows:]).astype(half_ref.dtype)
    own, other = own_teacher_ref[0], other_teacher_ref[0]
    own, other = own.astype(jnp.float32), other.astype(jnp.float32)
    teacher = jnp.concatenate(
        [jnp.where(first, own, other), jnp.where(first, other, own)], axis=0
    )
    position = step * block + lax.broadcasted_iota(jnp.int32, (block, 1), 0)
    residue = jnp.where(position < facts[0], output - teacher, 0.0)
    grads = normalize_back(residue, normal, scale, gain_ref[...])
    grad_ref[...] = grads
    low_ref[...] = grads.astype(low_ref.dtype)
    row_kernel_stats(stats_ref, step, [grads, residue * normal, residue, residue * residue])


def first_norm_back_kernel(
    facts,
    grad_ref,
    mine_ref,
    other_ref,
    normal_ref,
    scale_ref,
    gain_ref,
    low_ref,
    half_ref,
    stats_ref,
):
    rows = grad_ref.shape[0] // 2
    branch = mine_ref[...].astype(jnp.float32) + other_ref[...].astype(jnp.float32)
    pushed = grad_ref[...] + branch
    normal = normal_ref[...]
    grads = normalize_back(pushed, normal, scale_ref[...], gain_ref[...])
    low_ref[...] = grads.astype(low_ref.dtype)
    half_ref[0] = jnp.where(facts[1] == 0, grads[:rows], grads[rows:])
    row_kernel_stats(stats_ref, pl.program_id(0), [grads, pushed * normal, pushed])


def by_rows(kernel, name, block, operands, results, facts=None, stats=0):
    def spec(shape, dealt=False):
        if dealt:
            return pl.BlockSpec((1,) + shape[1:], lambda step, facts: (step ^ facts[2], 0, 0))
        if shape[0] == 1:
            return pl.BlockSpec(shape, lambda step, *_: (0, 0))
        return pl.BlockSpec((block, shape[1]), lambda step, *_: (step, 0))

    length = next(item.shape[0] for item in operands if item.ndim == 2 and item.shape[0] > 1)
    out_specs = [spec(item.shape, item.ndim == 3) for item in results]
    if stats:
        results = results + [jax.ShapeDtypeStruct((8, stats), jnp.float32)]
        out_specs.append(pl.BlockSpec((8, stats), lambda step, *_: (0, 0)))
    return pl.pallas_call(
        kernel,
        grid_spec=pltpu.PrefetchScalarGridSpec(
            num_scalar_prefetch=0 if facts is None else 1,
            grid=(length // block,),
            in_specs=[spec(item.shape, item.ndim == 3) for item in operands],
            out_specs=out_specs,
        ),
        out_shape=results,
        name=name,
        compiler_params=pltpu.CompilerParams(vmem_limit_bytes=20 << 20),
    )(*([] if facts is None else [facts]), *operands)


def grad_pre_kernel(low_ref, weight_ref, slope_ref, out_ref, stats_ref):
    grads = plain_dot(low_ref[...], weight_ref[...]) * slope_ref[...].astype(jnp.float32)
    grads = grads.astype(out_ref.dtype)
    out_ref[...] = grads
    row_kernel_stats(stats_ref, pl.program_id(0), [grads.astype(jnp.float32)])


def wide_layer(kernel, name, block, low, weight, operands, count, stats=0):
    length, width = low.shape[0], weight.shape[1]

    def spec(shape):
        if shape[0] == 1:
            return pl.BlockSpec(shape, lambda step: (0, 0))
        return pl.BlockSpec((block, shape[1]), lambda step: (step, 0))

    out_specs = [pl.BlockSpec((block, width), lambda step: (step, 0))] * count
    out_shape = [jax.ShapeDtypeStruct((length, width), jnp.bfloat16)] * count
    if stats:
        out_specs = out_specs + [pl.BlockSpec((8, width), lambda step: (0, 0))]
        out_shape = out_shape + [jax.ShapeDtypeStruct((8, width), jnp.float32)]
    return pl.pallas_call(
        kernel,
        grid=(length // block,),
        in_specs=[spec(low.shape), pl.BlockSpec(weight.shape, lambda step: (0, 0))]
        + [spec(item.shape) for item in operands],
        out_specs=out_specs,
        out_shape=out_shape,
        name=name,
        compiler_params=pltpu.CompilerParams(vmem_limit_bytes=20 << 20),
    )(low, weight, *operands)


def rows_kernel(left_ref, right_ref, out_ref, *, transposed):
    product = (rows_by_rows if transposed else plain_dot)(left_ref[...], right_ref[...])
    out_ref[...] = product.astype(out_ref.dtype)


def rows_times(left, right, block, transposed):
    length, depth = left.shape
    width = right.shape[0] if transposed else right.shape[1]
    return pl.pallas_call(
        lambda *refs: rows_kernel(*refs, transposed=transposed),
        grid=(length // block,),
        in_specs=[
            pl.BlockSpec((block, depth), lambda step: (step, 0)),
            pl.BlockSpec(right.shape, lambda step: (0, 0)),
        ],
        out_specs=pl.BlockSpec((block, width), lambda step: (step, 0)),
        out_shape=jax.ShapeDtypeStruct((length, width), jnp.bfloat16),
        name="rows_times",
        compiler_params=pltpu.CompilerParams(vmem_limit_bytes=14 << 20),
    )(left, right)


def input_back_kernel(facts, grad_ref, weight_ref, mine_ref, other_ref):
    total = rows_by_rows(grad_ref[...], weight_ref[...]).astype(mine_ref.dtype)
    rows = mine_ref.shape[1]
    first = facts[1] == 0
    mine_ref[0] = jnp.where(first, total[:rows], total[rows:])
    other_ref[0] = jnp.where(first, total[rows:], total[:rows])


def input_back(facts, grads, weight, block):
    length, width = grads.shape
    half = (1, block // 2, weight.shape[0])
    return pl.pallas_call(
        input_back_kernel,
        grid_spec=pltpu.PrefetchScalarGridSpec(
            num_scalar_prefetch=1,
            grid=(length // block,),
            in_specs=[
                pl.BlockSpec((block, width), lambda step, facts: (step, 0)),
                pl.BlockSpec((weight.shape[0], width), lambda step, facts: (0, 0)),
            ],
            out_specs=[pl.BlockSpec(half, lambda step, facts: (step ^ facts[2], 0, 0))] * 2,
        ),
        out_shape=[jax.ShapeDtypeStruct((length // block,) + half[1:], jnp.bfloat16)] * 2,
        name="input_back",
        compiler_params=pltpu.CompilerParams(vmem_limit_bytes=10 << 20),
    )(facts, grads, weight)


def pack_kernel(second_ref, first_ref, up_ref, qkv_ref, count_ref, out_ref):
    width = out_ref.shape[1]
    out_ref[...] = jnp.zeros_like(out_ref)
    out_ref[0:4, :] = second_ref[0:4, :]
    out_ref[4:7, :] = first_ref[0:3, :]
    row = 7
    for ref in (up_ref, qkv_ref, count_ref):
        for start in range(0, ref.shape[1], width):
            span = min(width, ref.shape[1] - start)
            out_ref[row : row + 1, :span] = ref[0:1, start : start + span]
            row += 1


def pack(second, first, up, qkv, count):
    width = second.shape[1]
    rows = 7 + sum(-(-item.shape[1] // width) for item in (up, qkv, count))
    return pl.pallas_call(
        pack_kernel,
        out_shape=jax.ShapeDtypeStruct((-(-rows // 8) * 8, width), jnp.float32),
        name="pack",
        compiler_params=pltpu.CompilerParams(vmem_limit_bytes=2 << 20),
    )(second, first, up, qkv, count)


def join_kernel(facts, ratio_ref, own_ref, other_ref, out_ref):
    rows = own_ref.shape[1]
    for ref, half in ((own_ref, facts[0]), (other_ref, 1 - facts[0])):
        values = ref[0].astype(jnp.float32) * ratio_ref[0]
        out_ref[0, pl.ds(pl.multiple_of(half * rows, rows), rows), :] = values.astype(out_ref.dtype)


def join_halves(half, ratio=None, dtype=jnp.bfloat16, place=0):
    count, rows, width = half.shape
    ratio = jnp.ones((1,), jnp.float32) if ratio is None else ratio.reshape(1)
    return pl.pallas_call(
        join_kernel,
        grid_spec=pltpu.PrefetchScalarGridSpec(
            num_scalar_prefetch=1,
            grid=(count,),
            in_specs=[pl.BlockSpec(memory_space=pltpu.SMEM)]
            + [pl.BlockSpec((1, rows, width), lambda step, facts: (step, 0, 0))] * 2,
            out_specs=pl.BlockSpec(
                (1, 2 * rows, width), lambda step, facts: (step ^ facts[1], 0, 0)
            ),
        ),
        out_shape=jax.ShapeDtypeStruct((count, 2 * rows, width), dtype),
        name="join_halves",
        compiler_params=pltpu.CompilerParams(vmem_limit_bytes=4 << 20),
    )(
        jnp.stack([lax.axis_index("tp"), jnp.asarray(place, jnp.int32)]),
        ratio,
        half,
        swap(half, "tp", 1),
    )


def weight_grad_kernel(places, *refs, chunks, fsdp, count, order):
    kinds = len(chunks)
    left_refs, right_refs = refs[:kinds], refs[kinds : 2 * kinds]
    out_refs, held = refs[2 * kinds : -1], refs[-1]
    step = pl.program_id(0)
    first = 0
    for left_ref, right_ref, chunk in zip(left_refs, right_refs, chunks):

        @pl.when(jnp.logical_and(step >= first, step < first + chunk))
        def _():
            total = lax.dot_general(
                left_ref[...],
                right_ref[...],
                (((0,), (0,)), ((), ())),
                preferred_element_type=jnp.float32,
            )
            held[...] = total.astype(held.dtype)

        first += chunk
    rows = held.shape[0] // (fsdp * count)
    if order == "fsdp":
        own = rows * count
        for half in range(2):
            for index in range(fsdp // 2):
                start = lax.bitwise_xor(places[1], jnp.int32(half + 2 * index)) * own
                out_refs[half][index * own : (index + 1) * own, :] = held[
                    pl.ds(pl.multiple_of(start, own), own), :
                ]
    else:
        steps = list(range(0, fsdp, 2)) + list(range(1, fsdp, 2))
        for s in range(count):
            for index, d in enumerate(steps):
                start = lax.bitwise_xor(places[1], jnp.int32(d)) * (rows * count)
                start = start + lax.bitwise_xor(places[0], jnp.int32(s)) * rows
                out_refs[s][index * rows : (index + 1) * rows, :] = held[
                    pl.ds(pl.multiple_of(start, rows), rows), :
                ]


def weight_grad(places, pairs, order="ctx"):
    fsdp, count = lax.axis_size("fsdp"), lax.axis_size("ctx")
    tokens, rows = pairs[0][0].shape
    columns = [right.shape[1] for _, right in pairs]
    width = max(
        item for item in range(LANES, 6 * LANES + 1, LANES) if not any(c % item for c in columns)
    )
    chunks = [item // width for item in columns]
    firsts = [sum(chunks[:index]) for index in range(len(chunks))]
    pieces = count if order == "ctx" else 2
    right_spec = lambda first, chunk: pl.BlockSpec(
        (tokens, width), lambda step, places: (0, jnp.clip(step - first, 0, chunk - 1))
    )
    return pl.pallas_call(
        lambda *refs: weight_grad_kernel(
            *refs, chunks=chunks, fsdp=fsdp, count=count, order=order
        ),
        grid_spec=pltpu.PrefetchScalarGridSpec(
            num_scalar_prefetch=1,
            grid=(sum(chunks),),
            in_specs=[pl.BlockSpec((tokens, rows), lambda step, places: (0, 0))] * len(pairs)
            + [right_spec(first, chunk) for first, chunk in zip(firsts, chunks)],
            out_specs=[pl.BlockSpec((rows // pieces, width), lambda step, places: (0, step))]
            * pieces,
            scratch_shapes=[pltpu.VMEM((rows, width), jnp.bfloat16)],
        ),
        out_shape=[jax.ShapeDtypeStruct((rows // pieces, sum(columns)), jnp.bfloat16)] * pieces,
        name="weight_grad",
        compiler_params=pltpu.CompilerParams(vmem_limit_bytes=14 << 20),
    )(places, *[left for left, _ in pairs], *[right for _, right in pairs])


def halve(kept, brought):
    rows = kept.shape[0] // 2
    return [
        low(wide(kept[cut]) + wide(brought[cut]))
        for cut in (slice(0, rows), slice(rows, 2 * rows))
    ]


def sum_kernel(*refs):
    part_refs, (kept_ref, sent_ref) = refs[:-2], refs[-2:]
    total = part_refs[0][...].astype(jnp.float32) + part_refs[1][...].astype(jnp.float32)
    for first, second in zip(part_refs[2::2], part_refs[3::2]):
        total = total + (first[...].astype(jnp.float32) + second[...].astype(jnp.float32))
    rows = kept_ref.shape[0]
    kept_ref[...] = total[:rows].astype(kept_ref.dtype)
    sent_ref[...] = total[rows:].astype(sent_ref.dtype)


def sum_and_cut(parts):
    rows, columns = parts[0].shape
    return pl.pallas_call(
        sum_kernel,
        out_shape=[jax.ShapeDtypeStruct((rows // 2, columns), jnp.bfloat16)] * 2,
        name="sum_and_cut",
        compiler_params=pltpu.CompilerParams(vmem_limit_bytes=8 << 20),
    )(*parts)


def place_kernel(places, ratio_ref, *refs, kinds):
    part_refs, out_ref = refs[:-1], refs[-1]
    rows, columns = part_refs[0].shape
    pairs = columns // (kinds * LANES)
    ratio = ratio_ref[0]
    for s in range(len(part_refs)):
        start = lax.bitwise_xor(places[0], jnp.int32(s)) * rows
        start = pl.multiple_of(start, rows)
        for kind in range(kinds):
            for pair in range(pairs):
                source = (pair * kinds + kind) * LANES
                target = (kind * pairs + pair) * LANES
                out_ref[pl.ds(start, rows), target : target + LANES] = (
                    part_refs[s][:, source : source + LANES].astype(jnp.float32) * ratio
                )


def place_rows(places, parts, ratio, kinds=1):
    rows, columns = parts[0].shape
    block = pl.BlockSpec((rows, columns), lambda step, places: (0, 0))
    return pl.pallas_call(
        lambda *refs: place_kernel(*refs, kinds=kinds),
        grid_spec=pltpu.PrefetchScalarGridSpec(
            num_scalar_prefetch=1,
            grid=(1,),
            in_specs=[pl.BlockSpec(memory_space=pltpu.SMEM)] + [block] * len(parts),
            out_specs=pl.BlockSpec((rows * len(parts), columns), lambda step, places: (0, 0)),
        ),
        out_shape=jax.ShapeDtypeStruct((rows * len(parts), columns), jnp.float32),
        name="place_rows",
        compiler_params=pltpu.CompilerParams(vmem_limit_bytes=6 << 20),
    )(places, ratio.reshape(1), *parts)


def whole_local(
    hidden_in,
    valid_mask,
    teacher,
    qkv_weight,
    qv_bias,
    out_weight,
    out_bias,
    norm1_gain,
    norm1_shift,
    up_weight,
    up_bias,
    down_weight,
    down_bias,
    norm2_gain,
    norm2_shift,
):
    seq_count, block_len, model_width = hidden_in.shape
    ctx_count = lax.axis_size("ctx")
    place, depth, core = lax.axis_index("ctx"), lax.axis_index("fsdp"), lax.axis_index("tp")
    inner_width = qkv_weight.shape[2]
    hidden_width = up_weight.shape[1]
    row_count = seq_count * block_len
    shape = hidden_in.shape
    places = jnp.stack([place, depth])
    fsdp_count = lax.axis_size("fsdp")
    row = lambda values: values.reshape(1, -1)
    struct = jax.ShapeDtypeStruct
    part_rows = qkv_weight.shape[0] // ctx_count
    own_part = lambda weight: lax.dynamic_slice_in_dim(weight, place * part_rows, part_rows, 0)
    qkv_out = jnp.concatenate([by_pairs(qkv_weight), out_weight], axis=1)
    local_counts = jnp.sum(wide(valid_mask), axis=1)
    hidden_own, weight_own = together(own_half(hidden_in), own_part(qkv_out))
    weight_rows = swap_all(weight_own, "fsdp")
    hidden_half = deal(hidden_own, "ctx")
    count_rows = jnp.broadcast_to(
        jnp.pad(low(local_counts), (0, qkv_out.shape[1] - seq_count)), (16, qkv_out.shape[1])
    )
    full_bias = row(by_pairs(jnp.stack([qv_bias[0], jnp.zeros_like(qv_bias[0]), qv_bias[1]])))
    teacher_own = own_half(teacher)
    teacher_own = [
        lax.dynamic_index_in_dim(teacher_own, place ^ s, 0, keepdims=False)
        for s in range(ctx_count)
    ]
    weight_rows, hidden_half, count_rows, up_own, down_own, teacher_own, full_bias = together(
        weight_rows,
        hidden_half,
        count_rows,
        own_part(up_weight),
        own_part(down_weight),
        teacher_own,
        full_bias,
    )
    weight_part = stack_rows(weight_rows + [count_rows])
    weight_parts = [weight_part] + swap_all(weight_part, "ctx")
    up_rows = relay_all(up_own, "fsdp")
    flat_in = join_halves(hidden_half).reshape(row_count, model_width)
    weight_parts, flat_in, up_rows, down_own = together(
        weight_parts, flat_in, up_rows, down_own
    )
    up_part = stack_rows(up_rows)
    up_parts = [up_part] + swap_all(up_part, "ctx")
    down_rows = relay_all(down_own, "fsdp")
    counts = sum(wide(item[-16, :LANES]) for item in weight_parts)
    valid_count = lax.dynamic_index_in_dim(counts, place, 0, keepdims=False).astype(jnp.int32)
    facts = jnp.stack([valid_count, core, place])
    projected, full_qkv_out = gathered_layer(
        project_kernel,
        "project",
        block_len,
        places,
        flat_in,
        [full_bias],
        qkv_out,
        weight_parts,
        [3 * inner_width],
        fsdp_count,
    )
    full_out = full_qkv_out[:, 3 * inner_width :]
    attended, log_total = attend(facts, projected, block_len)
    attended, up_parts, down_rows = together(attended, up_parts, down_rows)
    down_part = stack_rows(down_rows)
    down_parts = [down_part] + swap_all(down_part, "ctx")
    branch = rows_times(attended, full_out, block_len, True)
    normal1, scale1, normed1_low = by_rows(
        first_norm_kernel,
        "first_norm",
        block_len,
        [flat_in, branch, swap(branch, "tp", 1), row(out_bias), row(norm1_gain), row(norm1_shift)],
        [
            struct((row_count, model_width), jnp.float32),
            struct((row_count, 1), jnp.float32),
            struct((row_count, model_width), jnp.bfloat16),
        ],
    )
    active, slope, full_up = gathered_layer(
        up_kernel,
        "up",
        block_len,
        places,
        normed1_low,
        [row(up_bias)],
        up_weight,
        up_parts,
        [hidden_width, hidden_width],
        fsdp_count,
    )
    active, down_parts = together(active, down_parts)
    teacher_half = stack_rows(
        [teacher_own[0]] + swap_each(teacher_own, "ctx")
    ).reshape(ctx_count, block_len // 2, model_width)
    branch, full_down = gathered_layer(
        down_kernel,
        "down",
        block_len,
        places,
        active,
        [],
        down_weight,
        down_parts,
        [model_width],
        fsdp_count,
    )
    layer_half, grad_resid2, grad_resid2_low, stats2 = by_rows(
        second_norm_kernel,
        "second_norm",
        block_len,
        [
            normal1,
            row(norm1_gain),
            row(norm1_shift),
            branch,
            swap(branch, "tp", 1),
            row(down_bias),
            row(norm2_gain),
            row(norm2_shift),
            teacher_half,
            swap(teacher_half, "tp", 1),
        ],
        [
            struct(teacher_half.shape, jnp.bfloat16),
            struct((row_count, model_width), jnp.float32),
            struct((row_count, model_width), jnp.bfloat16),
        ],
        facts=facts,
        stats=model_width,
    )
    down_kept, down_sent = weight_grad(places, [(grad_resid2_low, active)], "fsdp")
    down_kept, down_sent, grad_resid2_low = together(down_kept, down_sent, grad_resid2_low)
    down_brought = swap(down_sent, "fsdp", 1)
    layer_pieces = [layer_half[s] for s in range(ctx_count)]
    layer_pieces = layer_pieces[:1] + swap_each(layer_pieces, "ctx")
    grad_pre, stats_up = wide_layer(
        grad_pre_kernel, "grad_pre", block_len, grad_resid2_low, full_down, [slope], 1, hidden_width
    )
    branch = rows_times(grad_pre, full_up, block_len, True)
    branch, grad_pre, layer_pieces = together(branch, grad_pre, layer_pieces)
    up_pieces = weight_grad(places, [(normed1_low, grad_pre)])
    up_brought = swap_each(up_pieces, "ctx")
    grad_resid1_low, grad_half, stats1 = by_rows(
        first_norm_back_kernel,
        "first_norm_back",
        block_len,
        [grad_resid2, branch, swap(branch, "tp", 1), normal1, scale1, row(norm1_gain)],
        [
            struct((row_count, model_width), jnp.bfloat16),
            struct(layer_half.shape, jnp.float32),
        ],
        facts=facts,
        stats=model_width,
    )
    out_kept, out_sent = weight_grad(places, [(grad_resid1_low, attended)], "fsdp")
    grad_attended = rows_times(grad_resid1_low, full_out, block_len, False)
    out_kept, out_sent, grad_attended = together(out_kept, out_sent, grad_attended)
    out_brought = swap(out_sent, "fsdp", 1)
    grad_qkv, stats_qkv = attend_back(facts, projected, grad_attended, log_total, block_len)
    grad_qkv, down_brought, out_brought = together(grad_qkv, down_brought, out_brought)
    last_pieces = weight_grad(places, [(flat_in, grad_qkv)])
    down_kept, down_sent = sum_and_cut([down_kept, down_brought])
    out_kept, out_sent = sum_and_cut([out_kept, out_brought])
    last_pieces, grad_qkv, down_sent, out_sent, layer_pieces, stats_qkv = together(
        last_pieces, grad_qkv, down_sent, out_sent, layer_pieces, stats_qkv
    )
    last_brought = swap_each(last_pieces, "ctx")
    down_brought = swap(down_sent, "fsdp", 2)
    mine, other = input_back(facts, grad_qkv, full_qkv_out, block_len)
    up_kept, up_sent = sum_and_cut([up_pieces[0]] + up_brought)
    local_count = jnp.broadcast_to(jnp.sum(local_counts), (1, LANES))
    small = pack(stats2, stats1, stats_up, stats_qkv, local_count)
    last_brought, mine, other, up_sent, out_sent, small, layer_pieces = together(
        last_brought, mine, other, up_sent, out_sent, small, layer_pieces
    )
    last_kept, last_sent = sum_and_cut([last_pieces[0]] + last_brought)
    last_sent, other, down_brought, up_sent, out_sent, small, layer_pieces = together(
        last_sent, other, down_brought, up_sent, out_sent, small, layer_pieces
    )
    last_brought = swap(last_sent, "fsdp", 1)
    other = swap(other, "tp", 1)
    owned_down = low(wide(down_kept) + wide(down_brought))
    down_other = swap(owned_down, "ctx", 1)
    last_brought, other, up_sent, out_sent, small, layer_pieces = together(
        last_brought, other, up_sent, out_sent, small, layer_pieces
    )
    last_kept, last_sent = sum_and_cut([last_kept, last_brought])
    half = low(grad_half + (wide(mine) + wide(other)))
    last_sent, half, up_sent, out_sent, small, layer_pieces = together(
        last_sent, half, up_sent, out_sent, small, layer_pieces
    )
    last_brought = swap(last_sent, "fsdp", 2)
    up_brought = swap(up_sent, "fsdp", 1)
    half_pieces = [half[s] for s in range(ctx_count)]
    half_brought = swap_each(half_pieces, "ctx")
    layer_stack = stack_rows(layer_pieces).reshape(layer_half.shape)
    last_brought, up_brought, down_other, out_sent, small, layer_stack = together(
        last_brought, up_brought, down_other, out_sent, small, layer_stack
    )
    part = low(wide(last_kept) + wide(last_brought))
    up_kept, up_sent = sum_and_cut([up_kept, up_brought])
    owned_down = low(wide(owned_down) + wide(down_other))
    part, up_sent, owned_down, out_sent, small, layer_stack = together(
        part, up_sent, owned_down, out_sent, small, layer_stack
    )
    shared = [part, swap(part, "ctx", 1), swap(part, "ctx", 2)]
    up_brought = swap(up_sent, "fsdp", 2)
    out_brought = swap(out_sent, "fsdp", 2)
    down_other = swap(owned_down, "ctx", 2)
    layer_out = join_halves(layer_stack, place=place)
    shared, up_brought, half_brought, out_brought, small, layer_out = together(
        shared, up_brought, half_brought, out_brought, small, layer_out
    )
    up_part = low(wide(up_kept) + wide(up_brought))
    owned_out = low(wide(out_kept) + wide(out_brought))
    up_part, owned_out, shared, small = together(up_part, owned_out, shared, small)
    shared = shared + [swap(shared[1], "ctx", 2)]
    up_shared = [up_part, swap(up_part, "ctx", 1), swap(up_part, "ctx", 2)]
    out_other = swap(owned_out, "ctx", 1)
    input_half = stack_rows(half_pieces[:1] + half_brought).reshape(half.shape)
    small = sum_over(small, "ctx")
    up_shared, input_half, out_other, small = together(up_shared, input_half, out_other, small)
    up_shared = up_shared + [swap(up_shared[1], "ctx", 2)]
    owned_out = low(wide(owned_out) + wide(out_other))
    out_other = swap(owned_out, "ctx", 2)
    small = sum_over(small, "fsdp")
    at = 7 + -(-hidden_width // model_width)
    counted = small[at + -(-3 * inner_width // model_width), 0]
    ratio = float(row_count * ctx_count * fsdp_count) / counted
    loss = jnp.sum(small[3]) / (counted * model_width)
    scaled = small * ratio
    input_grad = join_halves(input_half, ratio, jnp.float32, place)
    owned_qkv = place_rows(places, shared, ratio, 3)
    owned_qkv, up_shared, down_other, out_other, input_grad, scaled = together(
        owned_qkv, up_shared, down_other, out_other, input_grad, scaled
    )
    owned_qkv = owned_qkv.reshape(qkv_weight.shape)
    owned_up = place_rows(places, up_shared, ratio)
    owned_down = (wide(owned_down) + wide(down_other)) * ratio
    owned_out = (wide(owned_out) + wide(out_other)) * ratio
    grad_up_bias = scaled[7:at].reshape(-1)[:hidden_width]
    grad_qv_bias = by_kinds(
        scaled[at : at + -(-3 * inner_width // model_width)].reshape(-1)[: 3 * inner_width]
    )[0::2]
    return (
        layer_out,
        input_grad,
        loss,
        owned_qkv,
        grad_qv_bias,
        owned_out,
        scaled[4],
        scaled[5],
        scaled[6],
        owned_up,
        grad_up_bias,
        owned_down,
        scaled[0],
        scaled[1],
        scaled[2],
    )


def spread_local(
    hidden_in,
    valid_mask,
    teacher,
    qkv_weight,
    qv_bias,
    out_weight,
    out_bias,
    norm1_gain,
    norm1_shift,
    up_weight,
    up_bias,
    down_weight,
    down_bias,
    norm2_gain,
    norm2_shift,
):
    seq_count, block_len, model_width = hidden_in.shape
    ctx_count = lax.axis_size("ctx")
    ctx_place = lax.axis_index("ctx")
    key_span = 2 * block_len
    seq_length = block_len * ctx_count
    row_count = seq_count * block_len
    scaling = HEAD_DIM ** (-0.5)
    full_qkv, full_out, full_up, full_down = (
        lax.all_gather(qkv_weight, "fsdp", axis=0, tiled=True),
        lax.all_gather(out_weight, "fsdp", axis=0, tiled=True),
        lax.all_gather(up_weight, "fsdp", axis=0, tiled=True),
        lax.all_gather(down_weight, "fsdp", axis=0, tiled=True),
    )
    inner_width = full_qkv.shape[2]
    head_count = inner_width // HEAD_DIM
    flat_in = hidden_in.reshape(row_count, model_width)
    full_bias = jnp.stack([qv_bias[0], jnp.zeros_like(qv_bias[0]), qv_bias[1]])
    projected = (
        jnp.einsum("td,dje->tje", flat_in, full_qkv, preferred_element_type=jnp.float32) + full_bias
    ).astype(jnp.bfloat16)
    queries = projected[:, 0].reshape(seq_count, block_len, inner_width)
    key_own = projected[:, 1].reshape(seq_count, block_len, inner_width)
    value_own = projected[:, 2].reshape(seq_count, block_len, inner_width)
    keep_own = valid_mask.astype(jnp.bfloat16)
    keys_all, values_all, keep_all = (
        lax.all_gather(key_own, "ctx", axis=1, tiled=True),
        lax.all_gather(value_own, "ctx", axis=1, tiled=True),
        lax.all_gather(keep_own, "ctx", axis=1, tiled=True),
    )
    query_heads = split_heads(queries)
    seen_limit = (ctx_place + 1) * block_len
    trip_count = ctx_place // 2 + 1
    offsets = jnp.arange(key_span, dtype=jnp.int32)

    def key_block(block_index):
        key_start = block_index * key_span
        key_heads = split_heads(lax.dynamic_slice_in_dim(keys_all, key_start, key_span, 1))
        value_heads = split_heads(lax.dynamic_slice_in_dim(values_all, key_start, key_span, 1))
        live_keys = lax.dynamic_slice_in_dim(keep_all, key_start, key_span, 1) > 0.5
        allowed = jnp.logical_and(live_keys, (key_start + offsets)[None, :] < seen_limit)
        return (key_heads, value_heads, allowed[:, None, None, :])

    def attend_step(block_index, carried):
        run_top, run_total, gathered = carried
        key_heads, value_heads, allowed = key_block(block_index)
        raw_scores = scores_of(query_heads, key_heads, allowed, scaling)
        new_top = jnp.maximum(run_top, jnp.max(raw_scores, axis=-1))
        shrink = jnp.exp(run_top - new_top)
        weights_now = jnp.exp(raw_scores - new_top[..., None])
        run_total = run_total * shrink + jnp.sum(weights_now, axis=-1)
        gathered = gathered * jnp.swapaxes(shrink, 1, 2)[..., None] + jnp.einsum(
            "shqk,skhd->sqhd",
            weights_now.astype(jnp.bfloat16),
            value_heads,
            preferred_element_type=jnp.float32,
        )
        return (new_top, run_total, gathered)

    start_top = jnp.full((seq_count, head_count, block_len), MASKED, jnp.float32)
    empty_heads = jnp.zeros((seq_count, block_len, head_count, HEAD_DIM), jnp.float32)
    run_top, run_total, gathered = lax.fori_loop(
        0, trip_count, attend_step, (start_top, jnp.zeros_like(start_top), empty_heads)
    )
    log_total = run_top + jnp.log(run_total)
    attended_exact = gathered / jnp.swapaxes(run_total, 1, 2)[..., None]
    attended = attended_exact.astype(jnp.bfloat16).reshape(row_count, inner_width)
    attn_branch = lax.psum(
        jnp.einsum("te,de->td", attended, full_out, preferred_element_type=jnp.float32).astype(
            jnp.bfloat16
        ),
        "tp",
    ).astype(jnp.float32)
    resid1 = flat_in.astype(jnp.float32) + attn_branch + out_bias
    normed1, norm1_back = jax.vjp(layer_norm, resid1, norm1_gain, norm1_shift)
    normed1_low = normed1.astype(jnp.bfloat16)
    pre_act = jnp.dot(normed1_low, full_up, preferred_element_type=jnp.float32) + up_bias
    active, gelu_back = jax.vjp(gelu_exact, pre_act)
    active = active.astype(jnp.bfloat16)
    ffn_branch = lax.psum(
        jnp.einsum("tf,df->td", active, full_down, preferred_element_type=jnp.float32).astype(
            jnp.bfloat16
        ),
        "tp",
    ).astype(jnp.float32)
    resid2 = normed1 + ffn_branch + down_bias
    output, norm2_back = jax.vjp(layer_norm, resid2, norm2_gain, norm2_shift)
    layer_out = output.astype(jnp.bfloat16).reshape(seq_count, block_len, model_width)
    keep_rows = valid_mask.reshape(row_count, 1).astype(jnp.float32)
    residue = (output - teacher.reshape(row_count, model_width).astype(jnp.float32)) * keep_rows
    squared = jnp.sum(residue * residue)
    counted = jnp.sum(keep_rows)
    grad_resid2, grad_gain2, grad_shift2 = norm2_back(residue)
    grad_down_bias = jnp.sum(grad_resid2, axis=0)
    grad_resid2_low = grad_resid2.astype(jnp.bfloat16)
    grad_active = jnp.dot(grad_resid2_low, full_down, preferred_element_type=jnp.float32)
    grad_down_weight = jnp.einsum(
        "td,tf->df", grad_resid2_low, active, preferred_element_type=jnp.float32
    )
    grad_pre = gelu_back(grad_active)[0].astype(jnp.bfloat16)
    grad_up_bias = jnp.sum(grad_pre.astype(jnp.float32), axis=0)
    grad_up_weight = jnp.einsum(
        "td,tf->df", normed1_low, grad_pre, preferred_element_type=jnp.float32
    )
    ffn_input_grad = lax.psum(
        jnp.einsum("tf,df->td", grad_pre, full_up, preferred_element_type=jnp.float32).astype(
            jnp.bfloat16
        ),
        "tp",
    ).astype(jnp.float32)
    grad_normed1 = grad_resid2 + ffn_input_grad
    grad_resid1, grad_gain1, grad_shift1 = norm1_back(grad_normed1)
    grad_out_bias = jnp.sum(grad_resid1, axis=0)
    grad_resid1_low = grad_resid1.astype(jnp.bfloat16)
    grad_mixed = jnp.dot(grad_resid1_low, full_out, preferred_element_type=jnp.float32)
    grad_out_weight = jnp.einsum(
        "td,te->de", grad_resid1_low, attended, preferred_element_type=jnp.float32
    )
    grad_attended = grad_mixed.astype(jnp.bfloat16).reshape(
        seq_count, block_len, head_count, HEAD_DIM
    )
    delta = jnp.swapaxes(jnp.sum(grad_attended.astype(jnp.float32) * attended_exact, axis=-1), 1, 2)

    def query_grads(block_index):
        key_heads, value_heads, allowed = key_block(block_index)
        prob_rows = jnp.exp(
            scores_of(query_heads, key_heads, allowed, scaling) - log_total[..., None]
        )
        push = jnp.einsum(
            "sqhd,skhd->shqk", grad_attended, value_heads, preferred_element_type=jnp.float32
        )
        slope = (prob_rows * (push - delta[..., None])).astype(jnp.bfloat16)
        grad_part = (
            jnp.einsum("shqk,skhd->sqhd", slope, key_heads, preferred_element_type=jnp.float32)
            * scaling
        )
        return (prob_rows, slope, grad_part)

    def back_step(block_index, carried):
        grad_query, spread = carried
        prob_rows, slope, grad_part = query_grads(block_index)
        grad_key = (
            jnp.einsum("shqk,sqhd->skhd", slope, query_heads, preferred_element_type=jnp.float32)
            * scaling
        )
        grad_value = jnp.einsum(
            "shqk,sqhd->skhd",
            prob_rows.astype(jnp.bfloat16),
            grad_attended,
            preferred_element_type=jnp.float32,
        )
        piece = jnp.stack(
            [
                grad_key.reshape(seq_count, key_span, inner_width),
                grad_value.reshape(seq_count, key_span, inner_width),
            ],
            axis=2,
        )
        spread = lax.dynamic_update_slice_in_dim(spread, piece, block_index * key_span, 1)
        return (grad_query + grad_part, spread)

    spread_start = jnp.zeros((seq_count, seq_length, 2, inner_width), jnp.float32)
    grad_query, spread = lax.fori_loop(0, trip_count, back_step, (empty_heads, spread_start))
    own_grads = lax.psum_scatter(
        spread.astype(jnp.bfloat16), "ctx", scatter_dimension=1, tiled=True
    ).astype(jnp.float32)
    grad_key_own = own_grads[:, :, 0]
    grad_value_own = own_grads[:, :, 1]
    grad_qkv = jnp.stack(
        [
            grad_query.reshape(row_count, inner_width),
            grad_key_own.reshape(row_count, inner_width),
            grad_value_own.reshape(row_count, inner_width),
        ],
        axis=1,
    ).astype(jnp.bfloat16)
    grad_qv_bias = jnp.sum(grad_qkv[:, 0::2].astype(jnp.float32), axis=0)
    grad_qkv_weight = jnp.einsum(
        "td,tje->dje", flat_in, grad_qkv, preferred_element_type=jnp.float32
    )
    input_part = lax.psum(
        jnp.einsum("tje,dje->td", grad_qkv, full_qkv, preferred_element_type=jnp.float32).astype(
            jnp.bfloat16
        ),
        "tp",
    ).astype(jnp.float32)
    grad_input = grad_resid1 + input_part
    vectors = jnp.stack(
        [grad_out_bias, grad_gain1, grad_shift1, grad_down_bias, grad_gain2, grad_shift2]
    )
    squared, counted, vectors, grad_qv_bias, grad_up_bias = lax.psum(
        (squared, counted, vectors, grad_qv_bias, grad_up_bias), ("fsdp", "ctx")
    )
    local_grads = (grad_qkv_weight, grad_out_weight, grad_up_weight, grad_down_weight)
    owned = (
        lax.psum_scatter(
            local_grads[0].astype(jnp.bfloat16), "fsdp", scatter_dimension=0, tiled=True
        ).astype(jnp.float32),
        lax.psum_scatter(
            local_grads[1].astype(jnp.bfloat16), "fsdp", scatter_dimension=0, tiled=True
        ).astype(jnp.float32),
        lax.psum_scatter(
            local_grads[2].astype(jnp.bfloat16), "fsdp", scatter_dimension=0, tiled=True
        ).astype(jnp.float32),
        lax.psum_scatter(
            local_grads[3].astype(jnp.bfloat16), "fsdp", scatter_dimension=0, tiled=True
        ).astype(jnp.float32),
    )
    owned = (
        lax.psum(owned[0].astype(jnp.bfloat16), "ctx").astype(jnp.float32),
        lax.psum(owned[1].astype(jnp.bfloat16), "ctx").astype(jnp.float32),
        lax.psum(owned[2].astype(jnp.bfloat16), "ctx").astype(jnp.float32),
        lax.psum(owned[3].astype(jnp.bfloat16), "ctx").astype(jnp.float32),
    )
    token_total = float(seq_count * seq_length * lax.axis_size("fsdp"))
    ratio = token_total / counted
    loss = squared / (counted * model_width)
    input_grad = (grad_input * ratio).reshape(seq_count, block_len, model_width)
    return (
        layer_out,
        input_grad,
        loss,
        owned[0] * ratio,
        grad_qv_bias * ratio,
        owned[1] * ratio,
        vectors[0] * ratio,
        vectors[1] * ratio,
        vectors[2] * ratio,
        owned[2] * ratio,
        grad_up_bias * ratio,
        owned[3] * ratio,
        vectors[3] * ratio,
        vectors[4] * ratio,
        vectors[5] * ratio,
    )


def local(hidden_in, *others):
    seq_count, block_len, model_width = hidden_in.shape
    ctx_count, fsdp_count = lax.axis_size("ctx"), lax.axis_size("fsdp")
    rows, inner_width = others[2].shape[0], others[2].shape[2]
    whole = (
        seq_count == ctx_count
        and ctx_count & (ctx_count - 1) == 0
        and fsdp_count == 4
        and lax.axis_size("tp") == 2
        and block_len % LANES == 0
        and others[5].shape[0] >= inner_width
        and inner_width % LANES == 0
        and rows % (16 * ctx_count) == 0
    )
    return (whole_local if whole else spread_local)(hidden_in, *others)


def solution(mesh):
    in_specs = (
        P("fsdp", "ctx", None),
        P("fsdp", "ctx"),
        P("fsdp", "ctx", None),
        P("fsdp", None, "tp"),
        P(None, "tp"),
        P("fsdp", "tp"),
        P(),
        P(),
        P(),
        P("fsdp", "tp"),
        P("tp"),
        P("fsdp", "tp"),
        P(),
        P(),
        P(),
    )
    out_specs = (
        P("fsdp", "ctx", None),
        P("fsdp", "ctx", None),
        P(),
        P("fsdp", None, "tp"),
        P(None, "tp"),
        P("fsdp", "tp"),
        P(),
        P(),
        P(),
        P("fsdp", "tp"),
        P("tp"),
        P("fsdp", "tp"),
        P(),
        P(),
        P(),
    )
    return jax.shard_map(local, mesh=mesh, in_specs=in_specs, out_specs=out_specs, check_vma=False)
```

```python
import jax
import jax.numpy as jnp
from jax import lax
from jax.experimental import pallas as pl
from jax.experimental.pallas import tpu as pltpu
from jax.sharding import PartitionSpec as P

HEAD_DIM = 64
NORM_EPS = 1e-05
MASKED = -1e30
LANES = 128


def layer_norm(values_in, gain_vec, shift_vec):
    row_mean = jnp.mean(values_in, axis=-1, keepdims=True)
    centered = values_in - row_mean
    row_var = jnp.mean(centered * centered, axis=-1, keepdims=True)
    return centered * lax.rsqrt(row_var + NORM_EPS) * gain_vec + shift_vec


def gelu_exact(pre_act):
    return jax.nn.gelu(pre_act, approximate=False)


def split_heads(packed):
    return packed.reshape(packed.shape[0], packed.shape[1], packed.shape[2] // HEAD_DIM, HEAD_DIM)


def scores_of(query_heads, key_heads, allowed, scaling):
    raw_scores = (
        jnp.einsum("sqhd,skhd->shqk", query_heads, key_heads, preferred_element_type=jnp.float32)
        * scaling
    )
    return jnp.where(allowed, raw_scores, MASKED)


def rows_by_rows(left, right):
    return lax.dot_general(left, right, (((1,), (1,)), ((), ())), preferred_element_type=jnp.float32)


def plain_dot(left, right):
    return jnp.dot(left, right, preferred_element_type=jnp.float32)


def lanes_of(head, lane):
    own = (lane < HEAD_DIM) if head == 0 else (lane >= HEAD_DIM)
    spare = HEAD_DIM if head == 0 else 0
    return own, lane == spare


def head_operands(query_ref, key_ref, slot, start, block, valid_count, head):
    lane = lax.broadcasted_iota(jnp.int32, (block, LANES), 1)
    own, spare = lanes_of(head, lane)
    position = start + lax.broadcasted_iota(jnp.int32, (block, LANES), 0)
    bias = jnp.where(position < valid_count, 0.0, MASKED)
    rows = pl.ds(slot * block, block)
    query = query_ref[rows, :].astype(jnp.float32) * (HEAD_DIM ** -0.5)
    key = key_ref[rows, :].astype(jnp.float32)
    query_side = jnp.where(spare, 1.0, query).astype(jnp.bfloat16)
    key_side = jnp.where(own, key, jnp.where(spare, bias, 0.0)).astype(jnp.bfloat16)
    return query_side, key_side


def attend_kernel(facts, query_ref, key_ref, value_ref, out_ref, log_ref, *, block):
    valid_count = facts[0]
    blocks = query_ref.shape[0] // block
    slots = list(range(blocks))
    value_t = [
        value_ref[pl.ds(slots[j] * block, block), :].astype(jnp.float32).T.astype(jnp.bfloat16)
        for j in range(blocks)
    ]
    outs = [[] for _ in range(blocks)]
    for head in range(2):
        sides = [
            head_operands(query_ref, key_ref, slots[j], j * block, block, valid_count, head)
            for j in range(blocks)
        ]
        span = slice(head * HEAD_DIM, (head + 1) * HEAD_DIM)
        for i in range(blocks):
            scores = [rows_by_rows(sides[j][1], sides[i][0]) for j in range(i + 1)]
            top = scores[0].max(axis=0, keepdims=True)
            for j in range(1, i + 1):
                top = jnp.maximum(top, scores[j].max(axis=0, keepdims=True))
            total = jnp.zeros_like(top)
            mixed = jnp.zeros((HEAD_DIM, block), jnp.float32)
            for j in range(i + 1):
                weight = jnp.exp(scores[j] - top)
                total = total + weight.sum(axis=0, keepdims=True)
                mixed = mixed + plain_dot(value_t[j][span, :], weight.astype(jnp.bfloat16))
            outs[i].append(mixed / total)
            log_ref[0, head : head + 1, i * block : (i + 1) * block] = top + jnp.log(total)
    for i in range(blocks):
        both = jnp.concatenate(outs[i], axis=0)
        out_ref[pl.ds(slots[i] * block, block), :] = both.T.astype(out_ref.dtype)


def attend_back_kernel(
    facts,
    query_ref,
    key_ref,
    value_ref,
    grad_ref,
    log_ref,
    out_ref,
    stats_ref,
    grad_key,
    grad_value,
    *,
    block,
):
    valid_count = facts[0]
    blocks = query_ref.shape[0] // block
    slots = list(range(blocks))
    scaling = HEAD_DIM ** -0.5
    lane = lax.broadcasted_iota(jnp.int32, (block, LANES), 1)
    key_t, grads, queries, values = [], [], [], []
    for j in range(blocks):
        rows = pl.ds(slots[j] * block, block)
        key_t.append((key_ref[rows, :].astype(jnp.float32) * scaling).T.astype(jnp.bfloat16))
        grads.append(grad_ref[rows, :])
        queries.append(query_ref[rows, :].astype(jnp.float32) * scaling)
        values.append(value_ref[rows, :].astype(jnp.float32))
    grad_queries = [[] for _ in range(blocks)]
    for head in range(2):
        own, _ = lanes_of(head, lane)
        span = slice(head * HEAD_DIM, (head + 1) * HEAD_DIM)
        sides = [
            head_operands(query_ref, key_ref, slots[j], j * block, block, valid_count, head)
            for j in range(blocks)
        ]
        head_values = [jnp.where(own, item, 0.0).astype(jnp.bfloat16) for item in values]
        for i in range(blocks):
            log_row = log_ref[0, head : head + 1, i * block : (i + 1) * block]
            head_grad = jnp.where(own, grads[i].astype(jnp.float32), 0.0).astype(jnp.bfloat16)
            head_query = jnp.where(own, queries[i], 0.0).astype(jnp.bfloat16)
            probs, pushes = [], []
            delta = jnp.zeros((1, block), jnp.float32)
            for j in range(i + 1):
                prob = jnp.exp(rows_by_rows(sides[j][1], sides[i][0]) - log_row)
                push = rows_by_rows(head_values[j], grads[i])
                delta = delta + (prob * push).sum(axis=0, keepdims=True)
                probs.append(prob)
                pushes.append(push)
            grad_query = jnp.zeros((HEAD_DIM, block), jnp.float32)
            for j in range(i + 1):
                slope = (probs[j] * (pushes[j] - delta)).astype(jnp.bfloat16)
                part_value = plain_dot(probs[j].astype(jnp.bfloat16), head_grad)
                part_key = plain_dot(slope, head_query)
                span_rows = slice(j * block, (j + 1) * block)
                if head == 0 and i == j:
                    grad_value[span_rows, :] = part_value
                    grad_key[span_rows, :] = part_key
                else:
                    grad_value[span_rows, :] += part_value
                    grad_key[span_rows, :] += part_key
                grad_query = grad_query + plain_dot(key_t[j][span, :], slope)
            grad_queries[i].append(grad_query)
    totals = jnp.zeros((1, 3 * LANES), jnp.float32)
    for i in range(blocks):
        rows = pl.ds(slots[i] * block, block)
        both = jnp.concatenate(grad_queries[i], axis=0)
        out_ref[rows, :LANES] = both.T.astype(out_ref.dtype)
        span_rows = slice(i * block, (i + 1) * block)
        out_ref[rows, LANES : 2 * LANES] = grad_key[span_rows, :].astype(out_ref.dtype)
        out_ref[rows, 2 * LANES :] = grad_value[span_rows, :].astype(out_ref.dtype)
        totals += jnp.sum(out_ref[rows, :].astype(jnp.float32), axis=0, keepdims=True)
    stats_ref[...] = jnp.broadcast_to(totals, stats_ref.shape)


def attend(facts, projected, block):
    length, width = projected.shape
    pairs = width // (3 * LANES)
    column = lambda kind: pl.BlockSpec((length, LANES), lambda pair, facts: (0, 3 * pair + kind))
    return pl.pallas_call(
        lambda *refs: attend_kernel(*refs, block=block),
        grid_spec=pltpu.PrefetchScalarGridSpec(
            num_scalar_prefetch=1,
            grid=(pairs,),
            in_specs=[column(0), column(1), column(2)],
            out_specs=[
                pl.BlockSpec((length, LANES), lambda pair, facts: (0, pair)),
                pl.BlockSpec((1, 2, length), lambda pair, facts: (pair, 0, 0)),
            ],
        ),
        out_shape=[
            jax.ShapeDtypeStruct((length, pairs * LANES), jnp.bfloat16),
            jax.ShapeDtypeStruct((pairs, 2, length), jnp.float32),
        ],
        name="attend",
        compiler_params=pltpu.CompilerParams(vmem_limit_bytes=9 << 20),
    )(facts, projected, projected, projected)


def attend_back(facts, projected, grad_attended, log_total, block):
    length, width = grad_attended.shape
    pairs = width // LANES
    column = lambda kind: pl.BlockSpec((length, LANES), lambda pair, facts: (0, 3 * pair + kind))
    return pl.pallas_call(
        lambda *refs: attend_back_kernel(*refs, block=block),
        grid_spec=pltpu.PrefetchScalarGridSpec(
            num_scalar_prefetch=1,
            grid=(pairs,),
            in_specs=[
                column(0),
                column(1),
                column(2),
                pl.BlockSpec((length, LANES), lambda pair, facts: (0, pair)),
                pl.BlockSpec((1, 2, length), lambda pair, facts: (pair, 0, 0)),
            ],
            out_specs=[
                pl.BlockSpec((length, 3 * LANES), lambda pair, facts: (0, pair)),
                pl.BlockSpec((8, 3 * LANES), lambda pair, facts: (0, pair)),
            ],
            scratch_shapes=[
                pltpu.VMEM((length, LANES), jnp.float32),
                pltpu.VMEM((length, LANES), jnp.float32),
            ],
        ),
        out_shape=[
            jax.ShapeDtypeStruct((length, 3 * width), jnp.bfloat16),
            jax.ShapeDtypeStruct((8, 3 * width), jnp.float32),
        ],
        name="attend_back",
        compiler_params=pltpu.CompilerParams(vmem_limit_bytes=12 << 20),
    )(facts, projected, projected, projected, grad_attended, log_total)


def by_pairs(values):
    kinds, width = values.shape[-2:]
    cut = values.reshape(values.shape[:-1] + (width // LANES, LANES))
    return jnp.swapaxes(cut, -3, -2).reshape(values.shape[:-2] + (kinds * width,))


def by_kinds(values, kinds=3):
    width = values.shape[-1] // kinds
    cut = values.reshape(values.shape[:-1] + (width // LANES, kinds, LANES))
    return jnp.swapaxes(cut, -3, -2).reshape(values.shape[:-1] + (kinds, width))


def fill_rows(places, own_ref, part_refs, out_ref):
    count = len(part_refs)
    rows = own_ref.shape[0] // count
    fsdp = out_ref.shape[0] // own_ref.shape[0]
    place, depth = places[0], places[1]
    start = pl.multiple_of(depth * (rows * count), rows)
    out_ref[pl.ds(start, rows * count), :] = own_ref[...]
    for s in range(count):
        for d in range(1, fsdp):
            start = lax.bitwise_xor(depth, jnp.int32(d)) * (rows * count)
            start = start + lax.bitwise_xor(place, jnp.int32(s)) * rows
            out_ref[pl.ds(pl.multiple_of(start, rows), rows), :] = part_refs[s][
                (d - 1) * rows : d * rows, :
            ]


def project_kernel(places, left_ref, bias_ref, own_ref, *refs):
    part_refs, (out_ref, full_ref) = refs[:-2], refs[-2:]

    @pl.when(pl.program_id(0) == 0)
    def _():
        fill_rows(places, own_ref, part_refs, full_ref)

    total = plain_dot(left_ref[...], full_ref[:, : out_ref.shape[1]]) + bias_ref[...]
    out_ref[...] = total.astype(out_ref.dtype)


def up_kernel(places, left_ref, bias_ref, own_ref, *refs):
    part_refs, (active_ref, slope_ref, full_ref) = refs[:-3], refs[-3:]

    @pl.when(pl.program_id(0) == 0)
    def _():
        fill_rows(places, own_ref, part_refs, full_ref)

    pre = plain_dot(left_ref[...], full_ref[...]) + bias_ref[...]
    below = 0.5 * (1.0 + lax.erf(pre * (0.5**0.5)))
    active_ref[...] = (pre * below).astype(active_ref.dtype)
    bell = jnp.exp(-0.5 * pre * pre) * 0.3989422804014327
    slope_ref[...] = (below + pre * bell).astype(slope_ref.dtype)


def down_kernel(places, left_ref, own_ref, *refs):
    part_refs, (out_ref, full_ref) = refs[:-2], refs[-2:]

    @pl.when(pl.program_id(0) == 0)
    def _():
        fill_rows(places, own_ref, part_refs, full_ref)

    out_ref[...] = rows_by_rows(left_ref[...], full_ref[...]).astype(out_ref.dtype)


def gathered_layer(kernel, name, block, places, left, vectors, own, parts, widths, fsdp):
    length = left.shape[0]
    full = (fsdp * own.shape[0], own.shape[1])
    whole = lambda shape: pl.BlockSpec(shape, lambda step, places: (0, 0))
    by_block = lambda width: pl.BlockSpec((block, width), lambda step, places: (step, 0))
    return pl.pallas_call(
        kernel,
        grid_spec=pltpu.PrefetchScalarGridSpec(
            num_scalar_prefetch=1,
            grid=(length // block,),
            in_specs=[by_block(left.shape[1])]
            + [whole(item.shape) for item in vectors + [own] + parts],
            out_specs=[by_block(width) for width in widths] + [whole(full)],
        ),
        out_shape=[jax.ShapeDtypeStruct((length, width), jnp.bfloat16) for width in widths]
        + [jax.ShapeDtypeStruct(full, jnp.bfloat16)],
        name=name,
        compiler_params=pltpu.CompilerParams(vmem_limit_bytes=20 << 20),
    )(places, left, *vectors, own, *parts)


def stack_kernel(*refs):
    row = 0
    for ref in refs[:-1]:
        refs[-1][row : row + ref.shape[0], :] = ref[...]
        row += ref.shape[0]


def stack_rows(pieces):
    rows = sum(item.shape[0] for item in pieces)
    return pl.pallas_call(
        stack_kernel,
        out_shape=jax.ShapeDtypeStruct((rows, pieces[0].shape[1]), pieces[0].dtype),
        name="stack_rows",
        compiler_params=pltpu.CompilerParams(vmem_limit_bytes=4 << 20),
    )(*pieces)


def swap(values, axis, step):
    pairs = [(place, place ^ step) for place in range(lax.axis_size(axis))]
    return lax.ppermute(values, axis, pairs)


def swap_all(values, axis):
    return [swap(values, axis, step) for step in range(1, lax.axis_size(axis))]


def relay_all(values, axis):
    if lax.axis_size(axis) != 4:
        return swap_all(values, axis)
    first, second = swap(values, axis, 1), swap(values, axis, 2)
    return [first, second, swap(first, axis, 2)]


def swap_each(pieces, axis):
    return [swap(pieces[step], axis, step) for step in range(1, len(pieces))]


def together(*values):
    return lax.optimization_barrier(values)


def wide(values):
    return values.astype(jnp.float32)


def low(values):
    return values.astype(jnp.bfloat16)


def add_partner(values):
    mine = low(values)
    return wide(mine) + wide(swap(mine, "tp", 1))


def add_up(pieces):
    pieces = [wide(item) for item in pieces]
    while len(pieces) > 1:
        pieces = [pieces[i] + pieces[i + 1] for i in range(0, len(pieces), 2)]
    return pieces[0]


def sum_over(values, axis):
    step = 1
    while step < lax.axis_size(axis):
        values = values + swap(values, axis, step)
        step *= 2
    return values


def deal(pieces, axis):
    return lax.all_to_all(pieces, axis, 0, 0)


def own_half(blocks):
    rows = blocks.shape[1] // 2
    return lax.dynamic_slice_in_dim(blocks, lax.axis_index("tp") * rows, rows, 1)


def row_kernel_stats(stats_ref, step, rows):
    @pl.when(step == 0)
    def _():
        stats_ref[...] = jnp.zeros_like(stats_ref)

    for index, row in enumerate(rows):
        stats_ref[index : index + 1, :] += jnp.sum(row, axis=0, keepdims=True)


def normalize(values):
    mean = jnp.mean(values, axis=-1, keepdims=True)
    centered = values - mean
    scale = lax.rsqrt(jnp.mean(centered * centered, axis=-1, keepdims=True) + NORM_EPS)
    return centered * scale, scale


def normalize_back(grads, normal, scale, gain):
    pushed = grads * gain
    mean = jnp.mean(pushed, axis=-1, keepdims=True)
    along = jnp.mean(pushed * normal, axis=-1, keepdims=True)
    return (pushed - mean - normal * along) * scale


def first_norm_kernel(
    hidden_ref, mine_ref, other_ref, bias_ref, gain_ref, shift_ref, normal_ref, scale_ref, low_ref
):
    branch = mine_ref[...].astype(jnp.float32) + other_ref[...].astype(jnp.float32)
    normal, scale = normalize(hidden_ref[...].astype(jnp.float32) + branch + bias_ref[...])
    normal_ref[...] = normal
    scale_ref[...] = scale
    low_ref[...] = (normal * gain_ref[...] + shift_ref[...]).astype(low_ref.dtype)


def second_norm_kernel(
    facts,
    normal_ref,
    gain1_ref,
    shift1_ref,
    mine_ref,
    other_ref,
    bias_ref,
    gain_ref,
    shift_ref,
    own_teacher_ref,
    other_teacher_ref,
    half_ref,
    grad_ref,
    low_ref,
    stats_ref,
):
    step = pl.program_id(0)
    block = normal_ref.shape[0]
    rows = block // 2
    branch = mine_ref[...].astype(jnp.float32) + other_ref[...].astype(jnp.float32)
    normed1 = normal_ref[...] * gain1_ref[...] + shift1_ref[...]
    normal, scale = normalize(normed1 + branch + bias_ref[...])
    output = normal * gain_ref[...] + shift_ref[...]
    first = facts[1] == 0
    half_ref[0] = jnp.where(first, output[:rows], output[rows:]).astype(half_ref.dtype)
    own, other = own_teacher_ref[0], other_teacher_ref[0]
    own, other = own.astype(jnp.float32), other.astype(jnp.float32)
    teacher = jnp.concatenate(
        [jnp.where(first, own, other), jnp.where(first, other, own)], axis=0
    )
    position = step * block + lax.broadcasted_iota(jnp.int32, (block, 1), 0)
    residue = jnp.where(position < facts[0], output - teacher, 0.0)
    grads = normalize_back(residue, normal, scale, gain_ref[...])
    grad_ref[...] = grads
    low_ref[...] = grads.astype(low_ref.dtype)
    row_kernel_stats(stats_ref, step, [grads, residue * normal, residue, residue * residue])


def first_norm_back_kernel(
    facts,
    grad_ref,
    mine_ref,
    other_ref,
    normal_ref,
    scale_ref,
    gain_ref,
    low_ref,
    half_ref,
    stats_ref,
):
    rows = grad_ref.shape[0] // 2
    branch = mine_ref[...].astype(jnp.float32) + other_ref[...].astype(jnp.float32)
    pushed = grad_ref[...] + branch
    normal = normal_ref[...]
    grads = normalize_back(pushed, normal, scale_ref[...], gain_ref[...])
    low_ref[...] = grads.astype(low_ref.dtype)
    half_ref[0] = jnp.where(facts[1] == 0, grads[:rows], grads[rows:])
    row_kernel_stats(stats_ref, pl.program_id(0), [grads, pushed * normal, pushed])


def by_rows(kernel, name, block, operands, results, facts=None, stats=0):
    def spec(shape, dealt=False):
        if dealt:
            return pl.BlockSpec((1,) + shape[1:], lambda step, facts: (step ^ facts[2], 0, 0))
        if shape[0] == 1:
            return pl.BlockSpec(shape, lambda step, *_: (0, 0))
        return pl.BlockSpec((block, shape[1]), lambda step, *_: (step, 0))

    length = next(item.shape[0] for item in operands if item.ndim == 2 and item.shape[0] > 1)
    out_specs = [spec(item.shape, item.ndim == 3) for item in results]
    if stats:
        results = results + [jax.ShapeDtypeStruct((8, stats), jnp.float32)]
        out_specs.append(pl.BlockSpec((8, stats), lambda step, *_: (0, 0)))
    return pl.pallas_call(
        kernel,
        grid_spec=pltpu.PrefetchScalarGridSpec(
            num_scalar_prefetch=0 if facts is None else 1,
            grid=(length // block,),
            in_specs=[spec(item.shape, item.ndim == 3) for item in operands],
            out_specs=out_specs,
        ),
        out_shape=results,
        name=name,
        compiler_params=pltpu.CompilerParams(vmem_limit_bytes=20 << 20),
    )(*([] if facts is None else [facts]), *operands)


def grad_pre_kernel(low_ref, weight_ref, slope_ref, out_ref, stats_ref):
    grads = plain_dot(low_ref[...], weight_ref[...]) * slope_ref[...].astype(jnp.float32)
    grads = grads.astype(out_ref.dtype)
    out_ref[...] = grads
    row_kernel_stats(stats_ref, pl.program_id(0), [grads.astype(jnp.float32)])


def wide_layer(kernel, name, block, low, weight, operands, count, stats=0):
    length, width = low.shape[0], weight.shape[1]

    def spec(shape):
        if shape[0] == 1:
            return pl.BlockSpec(shape, lambda step: (0, 0))
        return pl.BlockSpec((block, shape[1]), lambda step: (step, 0))

    out_specs = [pl.BlockSpec((block, width), lambda step: (step, 0))] * count
    out_shape = [jax.ShapeDtypeStruct((length, width), jnp.bfloat16)] * count
    if stats:
        out_specs = out_specs + [pl.BlockSpec((8, width), lambda step: (0, 0))]
        out_shape = out_shape + [jax.ShapeDtypeStruct((8, width), jnp.float32)]
    return pl.pallas_call(
        kernel,
        grid=(length // block,),
        in_specs=[spec(low.shape), pl.BlockSpec(weight.shape, lambda step: (0, 0))]
        + [spec(item.shape) for item in operands],
        out_specs=out_specs,
        out_shape=out_shape,
        name=name,
        compiler_params=pltpu.CompilerParams(vmem_limit_bytes=20 << 20),
    )(low, weight, *operands)


def rows_kernel(left_ref, right_ref, out_ref, *, transposed):
    product = (rows_by_rows if transposed else plain_dot)(left_ref[...], right_ref[...])
    out_ref[...] = product.astype(out_ref.dtype)


def rows_times(left, right, block, transposed):
    length, depth = left.shape
    width = right.shape[0] if transposed else right.shape[1]
    return pl.pallas_call(
        lambda *refs: rows_kernel(*refs, transposed=transposed),
        grid=(length // block,),
        in_specs=[
            pl.BlockSpec((block, depth), lambda step: (step, 0)),
            pl.BlockSpec(right.shape, lambda step: (0, 0)),
        ],
        out_specs=pl.BlockSpec((block, width), lambda step: (step, 0)),
        out_shape=jax.ShapeDtypeStruct((length, width), jnp.bfloat16),
        name="rows_times",
        compiler_params=pltpu.CompilerParams(vmem_limit_bytes=14 << 20),
    )(left, right)


def pick_kernel(seat, in_ref, out_ref):
    out_ref[...] = in_ref[...]


def pick_halves(seat, blocks):
    count, rows, width = blocks.shape
    half = (1, rows // 2, width)
    return pl.pallas_call(
        pick_kernel,
        grid_spec=pltpu.PrefetchScalarGridSpec(
            num_scalar_prefetch=1,
            grid=(count,),
            in_specs=[pl.BlockSpec(half, lambda step, seat: (step ^ seat[1], seat[0], 0))],
            out_specs=pl.BlockSpec(half, lambda step, seat: (step, 0, 0)),
        ),
        out_shape=jax.ShapeDtypeStruct((count,) + half[1:], blocks.dtype),
        name="pick_halves",
        compiler_params=pltpu.CompilerParams(vmem_limit_bytes=4 << 20),
    )(seat, blocks)


def input_back_kernel(facts, grad_ref, weight_ref, mine_ref, other_ref):
    total = rows_by_rows(grad_ref[...], weight_ref[...]).astype(mine_ref.dtype)
    rows = mine_ref.shape[1]
    first = facts[1] == 0
    mine_ref[0] = jnp.where(first, total[:rows], total[rows:])
    other_ref[0] = jnp.where(first, total[rows:], total[:rows])


def input_back(facts, grads, weight, block):
    length, width = grads.shape
    half = (1, block // 2, weight.shape[0])
    return pl.pallas_call(
        input_back_kernel,
        grid_spec=pltpu.PrefetchScalarGridSpec(
            num_scalar_prefetch=1,
            grid=(length // block,),
            in_specs=[
                pl.BlockSpec((block, width), lambda step, facts: (step, 0)),
                pl.BlockSpec((weight.shape[0], width), lambda step, facts: (0, 0)),
            ],
            out_specs=[pl.BlockSpec(half, lambda step, facts: (step ^ facts[2], 0, 0))] * 2,
        ),
        out_shape=[jax.ShapeDtypeStruct((length // block,) + half[1:], jnp.bfloat16)] * 2,
        name="input_back",
        compiler_params=pltpu.CompilerParams(vmem_limit_bytes=10 << 20),
    )(facts, grads, weight)


def pack_kernel(second_ref, first_ref, up_ref, qkv_ref, count_ref, out_ref):
    width = out_ref.shape[1]
    out_ref[...] = jnp.zeros_like(out_ref)
    out_ref[0:4, :] = second_ref[0:4, :]
    out_ref[4:7, :] = first_ref[0:3, :]
    row = 7
    for ref in (up_ref, qkv_ref, count_ref):
        for start in range(0, ref.shape[1], width):
            span = min(width, ref.shape[1] - start)
            out_ref[row : row + 1, :span] = ref[0:1, start : start + span]
            row += 1


def pack(second, first, up, qkv, count):
    width = second.shape[1]
    rows = 7 + sum(-(-item.shape[1] // width) for item in (up, qkv, count))
    return pl.pallas_call(
        pack_kernel,
        out_shape=jax.ShapeDtypeStruct((-(-rows // 8) * 8, width), jnp.float32),
        name="pack",
        compiler_params=pltpu.CompilerParams(vmem_limit_bytes=2 << 20),
    )(second, first, up, qkv, count)


def join_kernel(facts, ratio_ref, own_ref, other_ref, out_ref):
    rows = own_ref.shape[1]
    for ref, half in ((own_ref, facts[0]), (other_ref, 1 - facts[0])):
        values = ref[0].astype(jnp.float32) * ratio_ref[0]
        out_ref[0, pl.ds(pl.multiple_of(half * rows, rows), rows), :] = values.astype(out_ref.dtype)


def join_halves(seat, half, ratio=None, dtype=jnp.bfloat16):
    count, rows, width = half.shape
    ratio = jnp.ones((1,), jnp.float32) if ratio is None else ratio.reshape(1)
    return pl.pallas_call(
        join_kernel,
        grid_spec=pltpu.PrefetchScalarGridSpec(
            num_scalar_prefetch=1,
            grid=(count,),
            in_specs=[pl.BlockSpec(memory_space=pltpu.SMEM)]
            + [pl.BlockSpec((1, rows, width), lambda step, facts: (step, 0, 0))] * 2,
            out_specs=pl.BlockSpec(
                (1, 2 * rows, width), lambda step, facts: (step ^ facts[1], 0, 0)
            ),
        ),
        out_shape=jax.ShapeDtypeStruct((count, 2 * rows, width), dtype),
        name="join_halves",
        compiler_params=pltpu.CompilerParams(vmem_limit_bytes=4 << 20),
    )(seat, ratio, half, swap(half, "tp", 1))


def weight_grad_kernel(places, *refs, chunks, fsdp, count, order):
    kinds = len(chunks)
    left_refs, right_refs = refs[:kinds], refs[kinds : 2 * kinds]
    out_refs, held = refs[2 * kinds : -1], refs[-1]
    step = pl.program_id(0)
    first = 0
    for left_ref, right_ref, chunk in zip(left_refs, right_refs, chunks):

        @pl.when(jnp.logical_and(step >= first, step < first + chunk))
        def _():
            total = lax.dot_general(
                left_ref[...],
                right_ref[...],
                (((0,), (0,)), ((), ())),
                preferred_element_type=jnp.float32,
            )
            held[...] = total.astype(held.dtype)

        first += chunk
    rows = held.shape[0] // (fsdp * count)
    if order == "fsdp":
        own = rows * count
        for half in range(2):
            for index in range(fsdp // 2):
                start = lax.bitwise_xor(places[1], jnp.int32(half + 2 * index)) * own
                out_refs[half][index * own : (index + 1) * own, :] = held[
                    pl.ds(pl.multiple_of(start, own), own), :
                ]
    else:
        steps = list(range(0, fsdp, 2)) + list(range(1, fsdp, 2))
        for s in range(count):
            for index, d in enumerate(steps):
                start = lax.bitwise_xor(places[1], jnp.int32(d)) * (rows * count)
                start = start + lax.bitwise_xor(places[0], jnp.int32(s)) * rows
                out_refs[s][index * rows : (index + 1) * rows, :] = held[
                    pl.ds(pl.multiple_of(start, rows), rows), :
                ]


def weight_grad(places, pairs, order="ctx"):
    fsdp, count = lax.axis_size("fsdp"), lax.axis_size("ctx")
    tokens, rows = pairs[0][0].shape
    columns = [right.shape[1] for _, right in pairs]
    width = max(
        item for item in range(LANES, 6 * LANES + 1, LANES) if not any(c % item for c in columns)
    )
    chunks = [item // width for item in columns]
    firsts = [sum(chunks[:index]) for index in range(len(chunks))]
    pieces = count if order == "ctx" else 2
    right_spec = lambda first, chunk: pl.BlockSpec(
        (tokens, width), lambda step, places: (0, jnp.clip(step - first, 0, chunk - 1))
    )
    return pl.pallas_call(
        lambda *refs: weight_grad_kernel(
            *refs, chunks=chunks, fsdp=fsdp, count=count, order=order
        ),
        grid_spec=pltpu.PrefetchScalarGridSpec(
            num_scalar_prefetch=1,
            grid=(sum(chunks),),
            in_specs=[pl.BlockSpec((tokens, rows), lambda step, places: (0, 0))] * len(pairs)
            + [right_spec(first, chunk) for first, chunk in zip(firsts, chunks)],
            out_specs=[pl.BlockSpec((rows // pieces, width), lambda step, places: (0, step))]
            * pieces,
            scratch_shapes=[pltpu.VMEM((rows, width), jnp.bfloat16)],
        ),
        out_shape=[jax.ShapeDtypeStruct((rows // pieces, sum(columns)), jnp.bfloat16)] * pieces,
        name="weight_grad",
        compiler_params=pltpu.CompilerParams(vmem_limit_bytes=14 << 20),
    )(places, *[left for left, _ in pairs], *[right for _, right in pairs])


def halve(kept, brought):
    rows = kept.shape[0] // 2
    return [
        low(wide(kept[cut]) + wide(brought[cut]))
        for cut in (slice(0, rows), slice(rows, 2 * rows))
    ]


def sum_kernel(*refs):
    part_refs, (kept_ref, sent_ref) = refs[:-2], refs[-2:]
    total = part_refs[0][...].astype(jnp.float32) + part_refs[1][...].astype(jnp.float32)
    for first, second in zip(part_refs[2::2], part_refs[3::2]):
        total = total + (first[...].astype(jnp.float32) + second[...].astype(jnp.float32))
    rows = kept_ref.shape[0]
    kept_ref[...] = total[:rows].astype(kept_ref.dtype)
    sent_ref[...] = total[rows:].astype(sent_ref.dtype)


def sum_and_cut(parts):
    rows, columns = parts[0].shape
    return pl.pallas_call(
        sum_kernel,
        out_shape=[jax.ShapeDtypeStruct((rows // 2, columns), jnp.bfloat16)] * 2,
        name="sum_and_cut",
        compiler_params=pltpu.CompilerParams(vmem_limit_bytes=8 << 20),
    )(*parts)


def place_kernel(places, ratio_ref, *refs, kinds):
    part_refs, out_ref = refs[:-1], refs[-1]
    rows, columns = part_refs[0].shape
    pairs = columns // (kinds * LANES)
    ratio = ratio_ref[0]
    for s in range(len(part_refs)):
        start = lax.bitwise_xor(places[0], jnp.int32(s)) * rows
        start = pl.multiple_of(start, rows)
        for kind in range(kinds):
            for pair in range(pairs):
                source = (pair * kinds + kind) * LANES
                target = (kind * pairs + pair) * LANES
                out_ref[pl.ds(start, rows), target : target + LANES] = (
                    part_refs[s][:, source : source + LANES].astype(jnp.float32) * ratio
                )


def place_rows(places, parts, ratio, kinds=1):
    rows, columns = parts[0].shape
    block = pl.BlockSpec((rows, columns), lambda step, places: (0, 0))
    return pl.pallas_call(
        lambda *refs: place_kernel(*refs, kinds=kinds),
        grid_spec=pltpu.PrefetchScalarGridSpec(
            num_scalar_prefetch=1,
            grid=(1,),
            in_specs=[pl.BlockSpec(memory_space=pltpu.SMEM)] + [block] * len(parts),
            out_specs=pl.BlockSpec((rows * len(parts), columns), lambda step, places: (0, 0)),
        ),
        out_shape=jax.ShapeDtypeStruct((rows * len(parts), columns), jnp.float32),
        name="place_rows",
        compiler_params=pltpu.CompilerParams(vmem_limit_bytes=6 << 20),
    )(places, ratio.reshape(1), *parts)


def whole_local(
    hidden_in,
    valid_mask,
    teacher,
    qkv_weight,
    qv_bias,
    out_weight,
    out_bias,
    norm1_gain,
    norm1_shift,
    up_weight,
    up_bias,
    down_weight,
    down_bias,
    norm2_gain,
    norm2_shift,
):
    seq_count, block_len, model_width = hidden_in.shape
    ctx_count = lax.axis_size("ctx")
    place, depth, core = lax.axis_index("ctx"), lax.axis_index("fsdp"), lax.axis_index("tp")
    inner_width = qkv_weight.shape[2]
    hidden_width = up_weight.shape[1]
    row_count = seq_count * block_len
    shape = hidden_in.shape
    places = jnp.stack([place, depth])
    seat = jnp.stack([core, place])
    lane = jnp.arange(LANES, dtype=jnp.int32)
    chosen = wide(lane == place)
    seat_rows = wide(jnp.where(lane == 0, seat[:, None], 0))
    fsdp_count = lax.axis_size("fsdp")
    row = lambda values: values.reshape(1, -1)
    struct = jax.ShapeDtypeStruct
    part_rows = qkv_weight.shape[0] // ctx_count
    own_part = lambda weight: lax.dynamic_slice_in_dim(weight, place * part_rows, part_rows, 0)
    qkv_out = jnp.concatenate([by_pairs(qkv_weight), out_weight], axis=1)
    local_counts = jnp.sum(wide(valid_mask), axis=1)
    hidden_own, weight_own = together(own_half(hidden_in), own_part(qkv_out))
    weight_rows = swap_all(weight_own, "fsdp")
    hidden_half = deal(hidden_own, "ctx")
    count_rows = jnp.broadcast_to(
        jnp.pad(low(local_counts), (0, qkv_out.shape[1] - seq_count)), (16, qkv_out.shape[1])
    )
    full_bias = row(by_pairs(jnp.stack([qv_bias[0], jnp.zeros_like(qv_bias[0]), qv_bias[1]])))
    teacher_own = pick_halves(seat, teacher)
    (
        places,
        seat,
        chosen,
        seat_rows,
        weight_rows,
        hidden_half,
        count_rows,
        up_own,
        down_own,
        teacher_own,
        full_bias,
    ) = together(
        places,
        seat,
        chosen,
        seat_rows,
        weight_rows,
        hidden_half,
        count_rows,
        own_part(up_weight),
        own_part(down_weight),
        teacher_own,
        full_bias,
    )
    weight_part = stack_rows(weight_rows + [count_rows])
    weight_parts = [weight_part] + swap_all(weight_part, "ctx")
    up_rows = relay_all(up_own, "fsdp")
    flat_in = join_halves(seat * jnp.array([1, 0], jnp.int32), hidden_half).reshape(row_count, model_width)
    weight_parts, flat_in, up_rows, down_own = together(
        weight_parts, flat_in, up_rows, down_own
    )
    up_part = stack_rows(up_rows)
    up_parts = [up_part] + swap_all(up_part, "ctx")
    down_rows = [swap(down_own, "fsdp", 1), swap(down_own, "fsdp", 2)]
    counts = sum(wide(item[-16, :LANES]) for item in weight_parts)
    facts = jnp.sum(jnp.concatenate([(counts * chosen)[None], seat_rows]), axis=1)
    facts = facts.astype(jnp.int32)
    projected, full_qkv_out = gathered_layer(
        project_kernel,
        "project",
        block_len,
        places,
        flat_in,
        [full_bias],
        qkv_out,
        weight_parts,
        [3 * inner_width],
        fsdp_count,
    )
    projected, down_first = together(projected, down_rows[0])
    down_rows = [down_first, down_rows[1], swap(down_first, "fsdp", 2)]
    full_out = full_qkv_out[:, 3 * inner_width :]
    attended, log_total = attend(facts, projected, block_len)
    attended, up_parts, down_rows = together(attended, up_parts, down_rows)
    down_part = stack_rows(down_rows)
    down_parts = [down_part] + swap_all(down_part, "ctx")
    branch = rows_times(attended, full_out, block_len, True)
    normal1, scale1, normed1_low = by_rows(
        first_norm_kernel,
        "first_norm",
        block_len,
        [flat_in, branch, swap(branch, "tp", 1), row(out_bias), row(norm1_gain), row(norm1_shift)],
        [
            struct((row_count, model_width), jnp.float32),
            struct((row_count, 1), jnp.float32),
            struct((row_count, model_width), jnp.bfloat16),
        ],
    )
    active, slope, full_up = gathered_layer(
        up_kernel,
        "up",
        block_len,
        places,
        normed1_low,
        [row(up_bias)],
        up_weight,
        up_parts,
        [hidden_width, hidden_width],
        fsdp_count,
    )
    active, down_parts = together(active, down_parts)
    teacher_half = stack_rows(
        [teacher_own[0]] + swap_each([teacher_own[s] for s in range(ctx_count)], "ctx")
    ).reshape(ctx_count, block_len // 2, model_width)
    branch, full_down = gathered_layer(
        down_kernel,
        "down",
        block_len,
        places,
        active,
        [],
        down_weight,
        down_parts,
        [model_width],
        fsdp_count,
    )
    layer_half, grad_resid2, grad_resid2_low, stats2 = by_rows(
        second_norm_kernel,
        "second_norm",
        block_len,
        [
            normal1,
            row(norm1_gain),
            row(norm1_shift),
            branch,
            swap(branch, "tp", 1),
            row(down_bias),
            row(norm2_gain),
            row(norm2_shift),
            teacher_half,
            swap(teacher_half, "tp", 1),
        ],
        [
            struct(teacher_half.shape, jnp.bfloat16),
            struct((row_count, model_width), jnp.float32),
            struct((row_count, model_width), jnp.bfloat16),
        ],
        facts=facts,
        stats=model_width,
    )
    down_kept, down_sent = weight_grad(places, [(grad_resid2_low, active)], "fsdp")
    down_kept, down_sent, grad_resid2_low = together(down_kept, down_sent, grad_resid2_low)
    down_brought = swap(down_sent, "fsdp", 1)
    layer_pieces = [layer_half[s] for s in range(ctx_count)]
    layer_pieces = layer_pieces[:1] + swap_each(layer_pieces, "ctx")
    grad_pre, stats_up = wide_layer(
        grad_pre_kernel, "grad_pre", block_len, grad_resid2_low, full_down, [slope], 1, hidden_width
    )
    branch = rows_times(grad_pre, full_up, block_len, True)
    branch, grad_pre, layer_pieces = together(branch, grad_pre, layer_pieces)
    layer_out = join_halves(seat, stack_rows(layer_pieces).reshape(layer_half.shape))
    up_pieces = weight_grad(places, [(normed1_low, grad_pre)])
    up_brought = swap_each(up_pieces, "ctx")
    grad_resid1_low, grad_half, stats1 = by_rows(
        first_norm_back_kernel,
        "first_norm_back",
        block_len,
        [grad_resid2, branch, swap(branch, "tp", 1), normal1, scale1, row(norm1_gain)],
        [
            struct((row_count, model_width), jnp.bfloat16),
            struct(layer_half.shape, jnp.float32),
        ],
        facts=facts,
        stats=model_width,
    )
    out_kept, out_sent = weight_grad(places, [(grad_resid1_low, attended)], "fsdp")
    grad_attended = rows_times(grad_resid1_low, full_out, block_len, False)
    out_kept, out_sent, grad_attended, layer_out = together(
        out_kept, out_sent, grad_attended, layer_out
    )
    out_brought = swap(out_sent, "fsdp", 1)
    grad_qkv, stats_qkv = attend_back(facts, projected, grad_attended, log_total, block_len)
    grad_qkv, down_brought, out_brought = together(grad_qkv, down_brought, out_brought)
    local_count = jnp.broadcast_to(jnp.sum(local_counts), (1, LANES))
    small = pack(stats2, stats1, stats_up, stats_qkv, local_count)
    small_other = swap(small, "ctx", 1)
    last_pieces = weight_grad(places, [(flat_in, grad_qkv)])
    down_kept, down_sent = sum_and_cut([down_kept, down_brought])
    out_kept, out_sent = sum_and_cut([out_kept, out_brought])
    last_pieces, grad_qkv, down_sent, out_sent, small_other = together(
        last_pieces, grad_qkv, down_sent, out_sent, small_other
    )
    last_brought = swap_each(last_pieces, "ctx")
    down_brought = swap(down_sent, "fsdp", 2)
    mine, other = input_back(facts, grad_qkv, full_qkv_out, block_len)
    up_kept, up_sent = sum_and_cut([up_pieces[0]] + up_brought)
    small = small + small_other
    small_other = swap(small, "ctx", 2)
    last_brought, mine, other, up_sent, out_sent, small, small_other = together(
        last_brought, mine, other, up_sent, out_sent, small, small_other
    )
    last_kept, last_sent = sum_and_cut([last_pieces[0]] + last_brought)
    last_sent, other, down_brought, up_sent, out_sent, small, small_other = together(
        last_sent, other, down_brought, up_sent, out_sent, small, small_other
    )
    last_brought = swap(last_sent, "fsdp", 1)
    other = swap(other, "tp", 1)
    owned_down = low(wide(down_kept) + wide(down_brought))
    down_other = swap(owned_down, "ctx", 1)
    small = small + small_other
    small_other = swap(small, "fsdp", 1)
    last_brought, other, up_sent, out_sent, small, small_other = together(
        last_brought, other, up_sent, out_sent, small, small_other
    )
    last_kept, last_sent = sum_and_cut([last_kept, last_brought])
    half = low(grad_half + (wide(mine) + wide(other)))
    small = small + small_other
    last_sent, half, up_sent, out_sent, small = together(
        last_sent, half, up_sent, out_sent, small
    )
    last_brought = swap(last_sent, "fsdp", 2)
    up_brought = swap(up_sent, "fsdp", 1)
    half_pieces = [half[s] for s in range(ctx_count)]
    half_brought = [half_pieces[0], swap(half_pieces[1], "ctx", 1)]
    small_other = swap(small, "fsdp", 2)
    last_brought, up_brought, down_other, out_sent, small_other, half_pieces = together(
        last_brought, up_brought, down_other, out_sent, small_other, half_pieces
    )
    part = low(wide(last_kept) + wide(last_brought))
    up_kept, up_sent = sum_and_cut([up_kept, up_brought])
    owned_down = low(wide(owned_down) + wide(down_other))
    small = small + small_other
    part, up_sent, owned_down, out_sent, small, half_pieces = together(
        part, up_sent, owned_down, out_sent, small, half_pieces
    )
    shared = [part, swap(part, "ctx", 1), swap(part, "ctx", 2)]
    up_brought = swap(up_sent, "fsdp", 2)
    out_brought = swap(out_sent, "fsdp", 2)
    down_other = swap(owned_down, "ctx", 2)
    shared, up_brought, out_brought, half_pieces, down_other = together(
        shared, up_brought, out_brought, half_pieces, down_other
    )
    up_part = low(wide(up_kept) + wide(up_brought))
    owned_out = low(wide(out_kept) + wide(out_brought))
    up_part, owned_out, shared, half_pieces = together(up_part, owned_out, shared, half_pieces)
    shared = shared + [swap(shared[1], "ctx", 2)]
    up_shared = [up_part, swap(up_part, "ctx", 1), swap(up_part, "ctx", 2)]
    half_brought = half_brought + [swap(half_pieces[s], "ctx", s) for s in range(2, ctx_count)]
    up_shared, half_brought, owned_out = together(up_shared, half_brought, owned_out)
    up_shared = up_shared + [swap(up_shared[1], "ctx", 2)]
    input_half = stack_rows(half_brought).reshape(half.shape)
    out_other = swap(owned_out, "ctx", 1)
    owned_out, out_other, input_half, up_shared = together(
        owned_out, out_other, input_half, up_shared
    )
    owned_out = low(wide(owned_out) + wide(out_other))
    out_other = swap(owned_out, "ctx", 2)
    at = 7 + -(-hidden_width // model_width)
    last_row = at + -(-3 * inner_width // model_width)
    counted = small[last_row : last_row + 1, :1]
    ratio = float(row_count * ctx_count * fsdp_count) / counted
    loss = jnp.sum(small[3:4], axis=1, keepdims=True) / (counted * model_width)
    scaled = small * ratio
    input_grad = join_halves(seat, input_half, ratio, jnp.float32)
    owned_qkv = place_rows(places, shared, ratio, 3)
    owned_qkv, up_shared, down_other, out_other, input_grad, scaled = together(
        owned_qkv, up_shared, down_other, out_other, input_grad, scaled
    )
    owned_qkv = owned_qkv.reshape(qkv_weight.shape)
    owned_up = place_rows(places, up_shared, ratio)
    owned_down = (wide(owned_down) + wide(down_other)) * ratio
    owned_out = (wide(owned_out) + wide(out_other)) * ratio
    grad_up_bias = scaled[7:at].reshape(-1)[:hidden_width]
    grad_qv_bias = by_kinds(
        scaled[at : at + -(-3 * inner_width // model_width)].reshape(-1)[: 3 * inner_width]
    )[0::2]
    return (
        layer_out,
        input_grad,
        loss.reshape(()),
        owned_qkv,
        grad_qv_bias,
        owned_out,
        scaled[4],
        scaled[5],
        scaled[6],
        owned_up,
        grad_up_bias,
        owned_down,
        scaled[0],
        scaled[1],
        scaled[2],
    )


def spread_local(
    hidden_in,
    valid_mask,
    teacher,
    qkv_weight,
    qv_bias,
    out_weight,
    out_bias,
    norm1_gain,
    norm1_shift,
    up_weight,
    up_bias,
    down_weight,
    down_bias,
    norm2_gain,
    norm2_shift,
):
    seq_count, block_len, model_width = hidden_in.shape
    ctx_count = lax.axis_size("ctx")
    ctx_place = lax.axis_index("ctx")
    key_span = 2 * block_len
    seq_length = block_len * ctx_count
    row_count = seq_count * block_len
    scaling = HEAD_DIM ** (-0.5)
    full_qkv, full_out, full_up, full_down = (
        lax.all_gather(qkv_weight, "fsdp", axis=0, tiled=True),
        lax.all_gather(out_weight, "fsdp", axis=0, tiled=True),
        lax.all_gather(up_weight, "fsdp", axis=0, tiled=True),
        lax.all_gather(down_weight, "fsdp", axis=0, tiled=True),
    )
    inner_width = full_qkv.shape[2]
    head_count = inner_width // HEAD_DIM
    flat_in = hidden_in.reshape(row_count, model_width)
    full_bias = jnp.stack([qv_bias[0], jnp.zeros_like(qv_bias[0]), qv_bias[1]])
    projected = (
        jnp.einsum("td,dje->tje", flat_in, full_qkv, preferred_element_type=jnp.float32) + full_bias
    ).astype(jnp.bfloat16)
    queries = projected[:, 0].reshape(seq_count, block_len, inner_width)
    key_own = projected[:, 1].reshape(seq_count, block_len, inner_width)
    value_own = projected[:, 2].reshape(seq_count, block_len, inner_width)
    keep_own = valid_mask.astype(jnp.bfloat16)
    keys_all, values_all, keep_all = (
        lax.all_gather(key_own, "ctx", axis=1, tiled=True),
        lax.all_gather(value_own, "ctx", axis=1, tiled=True),
        lax.all_gather(keep_own, "ctx", axis=1, tiled=True),
    )
    query_heads = split_heads(queries)
    seen_limit = (ctx_place + 1) * block_len
    trip_count = ctx_place // 2 + 1
    offsets = jnp.arange(key_span, dtype=jnp.int32)

    def key_block(block_index):
        key_start = block_index * key_span
        key_heads = split_heads(lax.dynamic_slice_in_dim(keys_all, key_start, key_span, 1))
        value_heads = split_heads(lax.dynamic_slice_in_dim(values_all, key_start, key_span, 1))
        live_keys = lax.dynamic_slice_in_dim(keep_all, key_start, key_span, 1) > 0.5
        allowed = jnp.logical_and(live_keys, (key_start + offsets)[None, :] < seen_limit)
        return (key_heads, value_heads, allowed[:, None, None, :])

    def attend_step(block_index, carried):
        run_top, run_total, gathered = carried
        key_heads, value_heads, allowed = key_block(block_index)
        raw_scores = scores_of(query_heads, key_heads, allowed, scaling)
        new_top = jnp.maximum(run_top, jnp.max(raw_scores, axis=-1))
        shrink = jnp.exp(run_top - new_top)
        weights_now = jnp.exp(raw_scores - new_top[..., None])
        run_total = run_total * shrink + jnp.sum(weights_now, axis=-1)
        gathered = gathered * jnp.swapaxes(shrink, 1, 2)[..., None] + jnp.einsum(
            "shqk,skhd->sqhd",
            weights_now.astype(jnp.bfloat16),
            value_heads,
            preferred_element_type=jnp.float32,
        )
        return (new_top, run_total, gathered)

    start_top = jnp.full((seq_count, head_count, block_len), MASKED, jnp.float32)
    empty_heads = jnp.zeros((seq_count, block_len, head_count, HEAD_DIM), jnp.float32)
    run_top, run_total, gathered = lax.fori_loop(
        0, trip_count, attend_step, (start_top, jnp.zeros_like(start_top), empty_heads)
    )
    log_total = run_top + jnp.log(run_total)
    attended_exact = gathered / jnp.swapaxes(run_total, 1, 2)[..., None]
    attended = attended_exact.astype(jnp.bfloat16).reshape(row_count, inner_width)
    attn_branch = lax.psum(
        jnp.einsum("te,de->td", attended, full_out, preferred_element_type=jnp.float32).astype(
            jnp.bfloat16
        ),
        "tp",
    ).astype(jnp.float32)
    resid1 = flat_in.astype(jnp.float32) + attn_branch + out_bias
    normed1, norm1_back = jax.vjp(layer_norm, resid1, norm1_gain, norm1_shift)
    normed1_low = normed1.astype(jnp.bfloat16)
    pre_act = jnp.dot(normed1_low, full_up, preferred_element_type=jnp.float32) + up_bias
    active, gelu_back = jax.vjp(gelu_exact, pre_act)
    active = active.astype(jnp.bfloat16)
    ffn_branch = lax.psum(
        jnp.einsum("tf,df->td", active, full_down, preferred_element_type=jnp.float32).astype(
            jnp.bfloat16
        ),
        "tp",
    ).astype(jnp.float32)
    resid2 = normed1 + ffn_branch + down_bias
    output, norm2_back = jax.vjp(layer_norm, resid2, norm2_gain, norm2_shift)
    layer_out = output.astype(jnp.bfloat16).reshape(seq_count, block_len, model_width)
    keep_rows = valid_mask.reshape(row_count, 1).astype(jnp.float32)
    residue = (output - teacher.reshape(row_count, model_width).astype(jnp.float32)) * keep_rows
    squared = jnp.sum(residue * residue)
    counted = jnp.sum(keep_rows)
    grad_resid2, grad_gain2, grad_shift2 = norm2_back(residue)
    grad_down_bias = jnp.sum(grad_resid2, axis=0)
    grad_resid2_low = grad_resid2.astype(jnp.bfloat16)
    grad_active = jnp.dot(grad_resid2_low, full_down, preferred_element_type=jnp.float32)
    grad_down_weight = jnp.einsum(
        "td,tf->df", grad_resid2_low, active, preferred_element_type=jnp.float32
    )
    grad_pre = gelu_back(grad_active)[0].astype(jnp.bfloat16)
    grad_up_bias = jnp.sum(grad_pre.astype(jnp.float32), axis=0)
    grad_up_weight = jnp.einsum(
        "td,tf->df", normed1_low, grad_pre, preferred_element_type=jnp.float32
    )
    ffn_input_grad = lax.psum(
        jnp.einsum("tf,df->td", grad_pre, full_up, preferred_element_type=jnp.float32).astype(
            jnp.bfloat16
        ),
        "tp",
    ).astype(jnp.float32)
    grad_normed1 = grad_resid2 + ffn_input_grad
    grad_resid1, grad_gain1, grad_shift1 = norm1_back(grad_normed1)
    grad_out_bias = jnp.sum(grad_resid1, axis=0)
    grad_resid1_low = grad_resid1.astype(jnp.bfloat16)
    grad_mixed = jnp.dot(grad_resid1_low, full_out, preferred_element_type=jnp.float32)
    grad_out_weight = jnp.einsum(
        "td,te->de", grad_resid1_low, attended, preferred_element_type=jnp.float32
    )
    grad_attended = grad_mixed.astype(jnp.bfloat16).reshape(
        seq_count, block_len, head_count, HEAD_DIM
    )
    delta = jnp.swapaxes(jnp.sum(grad_attended.astype(jnp.float32) * attended_exact, axis=-1), 1, 2)

    def query_grads(block_index):
        key_heads, value_heads, allowed = key_block(block_index)
        prob_rows = jnp.exp(
            scores_of(query_heads, key_heads, allowed, scaling) - log_total[..., None]
        )
        push = jnp.einsum(
            "sqhd,skhd->shqk", grad_attended, value_heads, preferred_element_type=jnp.float32
        )
        slope = (prob_rows * (push - delta[..., None])).astype(jnp.bfloat16)
        grad_part = (
            jnp.einsum("shqk,skhd->sqhd", slope, key_heads, preferred_element_type=jnp.float32)
            * scaling
        )
        return (prob_rows, slope, grad_part)

    def back_step(block_index, carried):
        grad_query, spread = carried
        prob_rows, slope, grad_part = query_grads(block_index)
        grad_key = (
            jnp.einsum("shqk,sqhd->skhd", slope, query_heads, preferred_element_type=jnp.float32)
            * scaling
        )
        grad_value = jnp.einsum(
            "shqk,sqhd->skhd",
            prob_rows.astype(jnp.bfloat16),
            grad_attended,
            preferred_element_type=jnp.float32,
        )
        piece = jnp.stack(
            [
                grad_key.reshape(seq_count, key_span, inner_width),
                grad_value.reshape(seq_count, key_span, inner_width),
            ],
            axis=2,
        )
        spread = lax.dynamic_update_slice_in_dim(spread, piece, block_index * key_span, 1)
        return (grad_query + grad_part, spread)

    spread_start = jnp.zeros((seq_count, seq_length, 2, inner_width), jnp.float32)
    grad_query, spread = lax.fori_loop(0, trip_count, back_step, (empty_heads, spread_start))
    own_grads = lax.psum_scatter(
        spread.astype(jnp.bfloat16), "ctx", scatter_dimension=1, tiled=True
    ).astype(jnp.float32)
    grad_key_own = own_grads[:, :, 0]
    grad_value_own = own_grads[:, :, 1]
    grad_qkv = jnp.stack(
        [
            grad_query.reshape(row_count, inner_width),
            grad_key_own.reshape(row_count, inner_width),
            grad_value_own.reshape(row_count, inner_width),
        ],
        axis=1,
    ).astype(jnp.bfloat16)
    grad_qv_bias = jnp.sum(grad_qkv[:, 0::2].astype(jnp.float32), axis=0)
    grad_qkv_weight = jnp.einsum(
        "td,tje->dje", flat_in, grad_qkv, preferred_element_type=jnp.float32
    )
    input_part = lax.psum(
        jnp.einsum("tje,dje->td", grad_qkv, full_qkv, preferred_element_type=jnp.float32).astype(
            jnp.bfloat16
        ),
        "tp",
    ).astype(jnp.float32)
    grad_input = grad_resid1 + input_part
    vectors = jnp.stack(
        [grad_out_bias, grad_gain1, grad_shift1, grad_down_bias, grad_gain2, grad_shift2]
    )
    squared, counted, vectors, grad_qv_bias, grad_up_bias = lax.psum(
        (squared, counted, vectors, grad_qv_bias, grad_up_bias), ("fsdp", "ctx")
    )
    local_grads = (grad_qkv_weight, grad_out_weight, grad_up_weight, grad_down_weight)
    owned = (
        lax.psum_scatter(
            local_grads[0].astype(jnp.bfloat16), "fsdp", scatter_dimension=0, tiled=True
        ).astype(jnp.float32),
        lax.psum_scatter(
            local_grads[1].astype(jnp.bfloat16), "fsdp", scatter_dimension=0, tiled=True
        ).astype(jnp.float32),
        lax.psum_scatter(
            local_grads[2].astype(jnp.bfloat16), "fsdp", scatter_dimension=0, tiled=True
        ).astype(jnp.float32),
        lax.psum_scatter(
            local_grads[3].astype(jnp.bfloat16), "fsdp", scatter_dimension=0, tiled=True
        ).astype(jnp.float32),
    )
    owned = (
        lax.psum(owned[0].astype(jnp.bfloat16), "ctx").astype(jnp.float32),
        lax.psum(owned[1].astype(jnp.bfloat16), "ctx").astype(jnp.float32),
        lax.psum(owned[2].astype(jnp.bfloat16), "ctx").astype(jnp.float32),
        lax.psum(owned[3].astype(jnp.bfloat16), "ctx").astype(jnp.float32),
    )
    token_total = float(seq_count * seq_length * lax.axis_size("fsdp"))
    ratio = token_total / counted
    loss = squared / (counted * model_width)
    input_grad = (grad_input * ratio).reshape(seq_count, block_len, model_width)
    return (
        layer_out,
        input_grad,
        loss,
        owned[0] * ratio,
        grad_qv_bias * ratio,
        owned[1] * ratio,
        vectors[0] * ratio,
        vectors[1] * ratio,
        vectors[2] * ratio,
        owned[2] * ratio,
        grad_up_bias * ratio,
        owned[3] * ratio,
        vectors[3] * ratio,
        vectors[4] * ratio,
        vectors[5] * ratio,
    )


def local(hidden_in, *others):
    seq_count, block_len, model_width = hidden_in.shape
    ctx_count, fsdp_count = lax.axis_size("ctx"), lax.axis_size("fsdp")
    rows, inner_width = others[2].shape[0], others[2].shape[2]
    whole = (
        seq_count == ctx_count
        and ctx_count & (ctx_count - 1) == 0
        and fsdp_count == 4
        and lax.axis_size("tp") == 2
        and block_len % LANES == 0
        and others[5].shape[0] >= inner_width
        and inner_width % LANES == 0
        and rows % (16 * ctx_count) == 0
    )
    return (whole_local if whole else spread_local)(hidden_in, *others)


def solution(mesh):
    in_specs = (
        P("fsdp", "ctx", None),
        P("fsdp", "ctx"),
        P("fsdp", "ctx", None),
        P("fsdp", None, "tp"),
        P(None, "tp"),
        P("fsdp", "tp"),
        P(),
        P(),
        P(),
        P("fsdp", "tp"),
        P("tp"),
        P("fsdp", "tp"),
        P(),
        P(),
        P(),
    )
    out_specs = (
        P("fsdp", "ctx", None),
        P("fsdp", "ctx", None),
        P(),
        P("fsdp", None, "tp"),
        P(None, "tp"),
        P("fsdp", "tp"),
        P(),
        P(),
        P(),
        P("fsdp", "tp"),
        P("tp"),
        P("fsdp", "tp"),
        P(),
        P(),
        P(),
    )
    return jax.shard_map(local, mesh=mesh, in_specs=in_specs, out_specs=out_specs, check_vma=False)
```

```python
import jax
import jax.numpy as jnp
from jax import lax
from jax.experimental import pallas as pl
from jax.experimental.pallas import tpu as pltpu
from jax.sharding import PartitionSpec as P

HEAD_DIM = 64
NORM_EPS = 1e-05
MASKED = -1e30
LANES = 128


def layer_norm(values_in, gain_vec, shift_vec):
    row_mean = jnp.mean(values_in, axis=-1, keepdims=True)
    centered = values_in - row_mean
    row_var = jnp.mean(centered * centered, axis=-1, keepdims=True)
    return centered * lax.rsqrt(row_var + NORM_EPS) * gain_vec + shift_vec


def gelu_exact(pre_act):
    return jax.nn.gelu(pre_act, approximate=False)


def split_heads(packed):
    return packed.reshape(packed.shape[0], packed.shape[1], packed.shape[2] // HEAD_DIM, HEAD_DIM)


def scores_of(query_heads, key_heads, allowed, scaling):
    raw_scores = (
        jnp.einsum("sqhd,skhd->shqk", query_heads, key_heads, preferred_element_type=jnp.float32)
        * scaling
    )
    return jnp.where(allowed, raw_scores, MASKED)


def rows_by_rows(left, right):
    return lax.dot_general(left, right, (((1,), (1,)), ((), ())), preferred_element_type=jnp.float32)


def plain_dot(left, right):
    return jnp.dot(left, right, preferred_element_type=jnp.float32)


def lanes_of(head, lane):
    own = (lane < HEAD_DIM) if head == 0 else (lane >= HEAD_DIM)
    spare = HEAD_DIM if head == 0 else 0
    return own, lane == spare


def head_operands(query_ref, key_ref, slot, start, block, valid_count, head):
    lane = lax.broadcasted_iota(jnp.int32, (block, LANES), 1)
    own, spare = lanes_of(head, lane)
    position = start + lax.broadcasted_iota(jnp.int32, (block, LANES), 0)
    bias = jnp.where(position < valid_count, 0.0, MASKED)
    rows = pl.ds(slot * block, block)
    query = query_ref[rows, :].astype(jnp.float32) * (HEAD_DIM ** -0.5)
    key = key_ref[rows, :].astype(jnp.float32)
    query_side = jnp.where(spare, 1.0, query).astype(jnp.bfloat16)
    key_side = jnp.where(own, key, jnp.where(spare, bias, 0.0)).astype(jnp.bfloat16)
    return query_side, key_side


def attend_kernel(facts, query_ref, key_ref, value_ref, out_ref, log_ref, *, block):
    valid_count = facts[0]
    blocks = query_ref.shape[0] // block
    slots = list(range(blocks))
    value_t = [
        value_ref[pl.ds(slots[j] * block, block), :].astype(jnp.float32).T.astype(jnp.bfloat16)
        for j in range(blocks)
    ]
    outs = [[] for _ in range(blocks)]
    for head in range(2):
        sides = [
            head_operands(query_ref, key_ref, slots[j], j * block, block, valid_count, head)
            for j in range(blocks)
        ]
        span = slice(head * HEAD_DIM, (head + 1) * HEAD_DIM)
        for i in range(blocks):
            scores = [rows_by_rows(sides[j][1], sides[i][0]) for j in range(i + 1)]
            top = scores[0].max(axis=0, keepdims=True)
            for j in range(1, i + 1):
                top = jnp.maximum(top, scores[j].max(axis=0, keepdims=True))
            total = jnp.zeros_like(top)
            mixed = jnp.zeros((HEAD_DIM, block), jnp.float32)
            for j in range(i + 1):
                weight = jnp.exp(scores[j] - top)
                total = total + weight.sum(axis=0, keepdims=True)
                mixed = mixed + plain_dot(value_t[j][span, :], weight.astype(jnp.bfloat16))
            outs[i].append(mixed / total)
            log_ref[0, head : head + 1, i * block : (i + 1) * block] = top + jnp.log(total)
    for i in range(blocks):
        both = jnp.concatenate(outs[i], axis=0)
        out_ref[pl.ds(slots[i] * block, block), :] = both.T.astype(out_ref.dtype)


def attend_back_kernel(
    facts,
    query_ref,
    key_ref,
    value_ref,
    grad_ref,
    log_ref,
    out_ref,
    stats_ref,
    grad_key,
    grad_value,
    *,
    block,
):
    valid_count = facts[0]
    blocks = query_ref.shape[0] // block
    slots = list(range(blocks))
    scaling = HEAD_DIM ** -0.5
    lane = lax.broadcasted_iota(jnp.int32, (block, LANES), 1)
    key_t, grads, queries, values = [], [], [], []
    for j in range(blocks):
        rows = pl.ds(slots[j] * block, block)
        key_t.append((key_ref[rows, :].astype(jnp.float32) * scaling).T.astype(jnp.bfloat16))
        grads.append(grad_ref[rows, :])
        queries.append(query_ref[rows, :].astype(jnp.float32) * scaling)
        values.append(value_ref[rows, :].astype(jnp.float32))
    grad_queries = [[] for _ in range(blocks)]
    for head in range(2):
        own, _ = lanes_of(head, lane)
        span = slice(head * HEAD_DIM, (head + 1) * HEAD_DIM)
        sides = [
            head_operands(query_ref, key_ref, slots[j], j * block, block, valid_count, head)
            for j in range(blocks)
        ]
        head_values = [jnp.where(own, item, 0.0).astype(jnp.bfloat16) for item in values]
        for i in range(blocks):
            log_row = log_ref[0, head : head + 1, i * block : (i + 1) * block]
            head_grad = jnp.where(own, grads[i].astype(jnp.float32), 0.0).astype(jnp.bfloat16)
            head_query = jnp.where(own, queries[i], 0.0).astype(jnp.bfloat16)
            probs, pushes = [], []
            delta = jnp.zeros((1, block), jnp.float32)
            for j in range(i + 1):
                prob = jnp.exp(rows_by_rows(sides[j][1], sides[i][0]) - log_row)
                push = rows_by_rows(head_values[j], grads[i])
                delta = delta + (prob * push).sum(axis=0, keepdims=True)
                probs.append(prob)
                pushes.append(push)
            grad_query = jnp.zeros((HEAD_DIM, block), jnp.float32)
            for j in range(i + 1):
                slope = (probs[j] * (pushes[j] - delta)).astype(jnp.bfloat16)
                part_value = plain_dot(probs[j].astype(jnp.bfloat16), head_grad)
                part_key = plain_dot(slope, head_query)
                span_rows = slice(j * block, (j + 1) * block)
                if head == 0 and i == j:
                    grad_value[span_rows, :] = part_value
                    grad_key[span_rows, :] = part_key
                else:
                    grad_value[span_rows, :] += part_value
                    grad_key[span_rows, :] += part_key
                grad_query = grad_query + plain_dot(key_t[j][span, :], slope)
            grad_queries[i].append(grad_query)
    totals = jnp.zeros((1, 3 * LANES), jnp.float32)
    for i in range(blocks):
        rows = pl.ds(slots[i] * block, block)
        both = jnp.concatenate(grad_queries[i], axis=0)
        out_ref[rows, :LANES] = both.T.astype(out_ref.dtype)
        span_rows = slice(i * block, (i + 1) * block)
        out_ref[rows, LANES : 2 * LANES] = grad_key[span_rows, :].astype(out_ref.dtype)
        out_ref[rows, 2 * LANES :] = grad_value[span_rows, :].astype(out_ref.dtype)
        totals += jnp.sum(out_ref[rows, :].astype(jnp.float32), axis=0, keepdims=True)
    stats_ref[...] = jnp.broadcast_to(totals, stats_ref.shape)


def attend(facts, projected, block):
    length, width = projected.shape
    pairs = width // (3 * LANES)
    column = lambda kind: pl.BlockSpec((length, LANES), lambda pair, facts: (0, 3 * pair + kind))
    return pl.pallas_call(
        lambda *refs: attend_kernel(*refs, block=block),
        grid_spec=pltpu.PrefetchScalarGridSpec(
            num_scalar_prefetch=1,
            grid=(pairs,),
            in_specs=[column(0), column(1), column(2)],
            out_specs=[
                pl.BlockSpec((length, LANES), lambda pair, facts: (0, pair)),
                pl.BlockSpec((1, 2, length), lambda pair, facts: (pair, 0, 0)),
            ],
        ),
        out_shape=[
            jax.ShapeDtypeStruct((length, pairs * LANES), jnp.bfloat16),
            jax.ShapeDtypeStruct((pairs, 2, length), jnp.float32),
        ],
        name="attend",
        compiler_params=pltpu.CompilerParams(vmem_limit_bytes=9 << 20),
    )(facts, projected, projected, projected)


def attend_back(facts, projected, grad_attended, log_total, block):
    length, width = grad_attended.shape
    pairs = width // LANES
    column = lambda kind: pl.BlockSpec((length, LANES), lambda pair, facts: (0, 3 * pair + kind))
    return pl.pallas_call(
        lambda *refs: attend_back_kernel(*refs, block=block),
        grid_spec=pltpu.PrefetchScalarGridSpec(
            num_scalar_prefetch=1,
            grid=(pairs,),
            in_specs=[
                column(0),
                column(1),
                column(2),
                pl.BlockSpec((length, LANES), lambda pair, facts: (0, pair)),
                pl.BlockSpec((1, 2, length), lambda pair, facts: (pair, 0, 0)),
            ],
            out_specs=[
                pl.BlockSpec((length, 3 * LANES), lambda pair, facts: (0, pair)),
                pl.BlockSpec((8, 3 * LANES), lambda pair, facts: (0, pair)),
            ],
            scratch_shapes=[
                pltpu.VMEM((length, LANES), jnp.float32),
                pltpu.VMEM((length, LANES), jnp.float32),
            ],
        ),
        out_shape=[
            jax.ShapeDtypeStruct((length, 3 * width), jnp.bfloat16),
            jax.ShapeDtypeStruct((8, 3 * width), jnp.float32),
        ],
        name="attend_back",
        compiler_params=pltpu.CompilerParams(vmem_limit_bytes=12 << 20),
    )(facts, projected, projected, projected, grad_attended, log_total)


def by_pairs(values):
    kinds, width = values.shape[-2:]
    cut = values.reshape(values.shape[:-1] + (width // LANES, LANES))
    return jnp.swapaxes(cut, -3, -2).reshape(values.shape[:-2] + (kinds * width,))


def by_kinds(values, kinds=3):
    width = values.shape[-1] // kinds
    cut = values.reshape(values.shape[:-1] + (width // LANES, kinds, LANES))
    return jnp.swapaxes(cut, -3, -2).reshape(values.shape[:-1] + (kinds, width))


def fill_rows(places, own_ref, part_refs, out_ref):
    count = len(part_refs)
    rows = own_ref.shape[0] // count
    fsdp = out_ref.shape[0] // own_ref.shape[0]
    place, depth = places[0], places[1]
    start = pl.multiple_of(depth * (rows * count), rows)
    out_ref[pl.ds(start, rows * count), :] = own_ref[...]
    for s in range(count):
        for d in range(1, fsdp):
            start = lax.bitwise_xor(depth, jnp.int32(d)) * (rows * count)
            start = start + lax.bitwise_xor(place, jnp.int32(s)) * rows
            out_ref[pl.ds(pl.multiple_of(start, rows), rows), :] = part_refs[s][
                (d - 1) * rows : d * rows, :
            ]


def project_kernel(places, left_ref, bias_ref, own_ref, *refs):
    part_refs, (out_ref, full_ref) = refs[:-2], refs[-2:]

    @pl.when(pl.program_id(0) == 0)
    def _():
        fill_rows(places, own_ref, part_refs, full_ref)

    total = plain_dot(left_ref[...], full_ref[:, : out_ref.shape[1]]) + bias_ref[...]
    out_ref[...] = total.astype(out_ref.dtype)


def up_kernel(places, left_ref, bias_ref, own_ref, *refs):
    part_refs, (active_ref, slope_ref, full_ref) = refs[:-3], refs[-3:]

    @pl.when(pl.program_id(0) == 0)
    def _():
        fill_rows(places, own_ref, part_refs, full_ref)

    pre = plain_dot(left_ref[...], full_ref[...]) + bias_ref[...]
    below = 0.5 * (1.0 + lax.erf(pre * (0.5**0.5)))
    active_ref[...] = (pre * below).astype(active_ref.dtype)
    bell = jnp.exp(-0.5 * pre * pre) * 0.3989422804014327
    slope_ref[...] = (below + pre * bell).astype(slope_ref.dtype)


def down_kernel(places, left_ref, own_ref, *refs):
    part_refs, (out_ref, full_ref) = refs[:-2], refs[-2:]

    @pl.when(pl.program_id(0) == 0)
    def _():
        fill_rows(places, own_ref, part_refs, full_ref)

    out_ref[...] = rows_by_rows(left_ref[...], full_ref[...]).astype(out_ref.dtype)


def gathered_layer(kernel, name, block, places, left, vectors, own, parts, widths, fsdp):
    length = left.shape[0]
    full = (fsdp * own.shape[0], own.shape[1])
    whole = lambda shape: pl.BlockSpec(shape, lambda step, places: (0, 0))
    by_block = lambda width: pl.BlockSpec((block, width), lambda step, places: (step, 0))
    return pl.pallas_call(
        kernel,
        grid_spec=pltpu.PrefetchScalarGridSpec(
            num_scalar_prefetch=1,
            grid=(length // block,),
            in_specs=[by_block(left.shape[1])]
            + [whole(item.shape) for item in vectors + [own] + parts],
            out_specs=[by_block(width) for width in widths] + [whole(full)],
        ),
        out_shape=[jax.ShapeDtypeStruct((length, width), jnp.bfloat16) for width in widths]
        + [jax.ShapeDtypeStruct(full, jnp.bfloat16)],
        name=name,
        compiler_params=pltpu.CompilerParams(vmem_limit_bytes=20 << 20),
    )(places, left, *vectors, own, *parts)


def stack_kernel(*refs):
    row = 0
    for ref in refs[:-1]:
        refs[-1][row : row + ref.shape[0], :] = ref[...]
        row += ref.shape[0]


def stack_rows(pieces):
    rows = sum(item.shape[0] for item in pieces)
    return pl.pallas_call(
        stack_kernel,
        out_shape=jax.ShapeDtypeStruct((rows, pieces[0].shape[1]), pieces[0].dtype),
        name="stack_rows",
        compiler_params=pltpu.CompilerParams(vmem_limit_bytes=4 << 20),
    )(*pieces)


def swap(values, axis, step):
    pairs = [(place, place ^ step) for place in range(lax.axis_size(axis))]
    return lax.ppermute(values, axis, pairs)


def swap_all(values, axis):
    return [swap(values, axis, step) for step in range(1, lax.axis_size(axis))]


def relay_all(values, axis):
    if lax.axis_size(axis) != 4:
        return swap_all(values, axis)
    first, second = swap(values, axis, 1), swap(values, axis, 2)
    return [first, second, swap(first, axis, 2)]


def swap_each(pieces, axis):
    return [swap(pieces[step], axis, step) for step in range(1, len(pieces))]


def together(*values):
    return lax.optimization_barrier(values)


def wide(values):
    return values.astype(jnp.float32)


def low(values):
    return values.astype(jnp.bfloat16)


def add_partner(values):
    mine = low(values)
    return wide(mine) + wide(swap(mine, "tp", 1))


def add_up(pieces):
    pieces = [wide(item) for item in pieces]
    while len(pieces) > 1:
        pieces = [pieces[i] + pieces[i + 1] for i in range(0, len(pieces), 2)]
    return pieces[0]


def sum_over(values, axis):
    step = 1
    while step < lax.axis_size(axis):
        values = values + swap(values, axis, step)
        step *= 2
    return values


def deal(pieces, axis):
    return lax.all_to_all(pieces, axis, 0, 0)


def own_half(blocks):
    rows = blocks.shape[1] // 2
    return lax.dynamic_slice_in_dim(blocks, lax.axis_index("tp") * rows, rows, 1)


def row_kernel_stats(stats_ref, step, rows):
    @pl.when(step == 0)
    def _():
        stats_ref[...] = jnp.zeros_like(stats_ref)

    for index, row in enumerate(rows):
        stats_ref[index : index + 1, :] += jnp.sum(row, axis=0, keepdims=True)


def normalize(values):
    mean = jnp.mean(values, axis=-1, keepdims=True)
    centered = values - mean
    scale = lax.rsqrt(jnp.mean(centered * centered, axis=-1, keepdims=True) + NORM_EPS)
    return centered * scale, scale


def normalize_back(grads, normal, scale, gain):
    pushed = grads * gain
    mean = jnp.mean(pushed, axis=-1, keepdims=True)
    along = jnp.mean(pushed * normal, axis=-1, keepdims=True)
    return (pushed - mean - normal * along) * scale


def first_norm_kernel(
    hidden_ref, mine_ref, other_ref, bias_ref, gain_ref, shift_ref, normal_ref, scale_ref, low_ref
):
    branch = mine_ref[...].astype(jnp.float32) + other_ref[...].astype(jnp.float32)
    normal, scale = normalize(hidden_ref[...].astype(jnp.float32) + branch + bias_ref[...])
    normal_ref[...] = normal
    scale_ref[...] = scale
    low_ref[...] = (normal * gain_ref[...] + shift_ref[...]).astype(low_ref.dtype)


def second_norm_kernel(
    facts,
    normal_ref,
    gain1_ref,
    shift1_ref,
    mine_ref,
    other_ref,
    bias_ref,
    gain_ref,
    shift_ref,
    own_teacher_ref,
    other_teacher_ref,
    half_ref,
    grad_ref,
    low_ref,
    stats_ref,
):
    step = pl.program_id(0)
    block = normal_ref.shape[0]
    rows = block // 2
    branch = mine_ref[...].astype(jnp.float32) + other_ref[...].astype(jnp.float32)
    normed1 = normal_ref[...] * gain1_ref[...] + shift1_ref[...]
    normal, scale = normalize(normed1 + branch + bias_ref[...])
    output = normal * gain_ref[...] + shift_ref[...]
    first = facts[1] == 0
    half_ref[0] = jnp.where(first, output[:rows], output[rows:]).astype(half_ref.dtype)
    own, other = own_teacher_ref[0], other_teacher_ref[0]
    own, other = own.astype(jnp.float32), other.astype(jnp.float32)
    teacher = jnp.concatenate(
        [jnp.where(first, own, other), jnp.where(first, other, own)], axis=0
    )
    position = step * block + lax.broadcasted_iota(jnp.int32, (block, 1), 0)
    residue = jnp.where(position < facts[0], output - teacher, 0.0)
    grads = normalize_back(residue, normal, scale, gain_ref[...])
    grad_ref[...] = grads
    low_ref[...] = grads.astype(low_ref.dtype)
    row_kernel_stats(stats_ref, step, [grads, residue * normal, residue, residue * residue])


def first_norm_back_kernel(
    facts,
    grad_ref,
    mine_ref,
    other_ref,
    normal_ref,
    scale_ref,
    gain_ref,
    low_ref,
    half_ref,
    stats_ref,
):
    rows = grad_ref.shape[0] // 2
    branch = mine_ref[...].astype(jnp.float32) + other_ref[...].astype(jnp.float32)
    pushed = grad_ref[...] + branch
    normal = normal_ref[...]
    grads = normalize_back(pushed, normal, scale_ref[...], gain_ref[...])
    low_ref[...] = grads.astype(low_ref.dtype)
    half_ref[0] = jnp.where(facts[1] == 0, grads[:rows], grads[rows:])
    row_kernel_stats(stats_ref, pl.program_id(0), [grads, pushed * normal, pushed])


def by_rows(kernel, name, block, operands, results, facts=None, stats=0):
    def spec(shape, dealt=False):
        if dealt:
            return pl.BlockSpec((1,) + shape[1:], lambda step, facts: (step ^ facts[2], 0, 0))
        if shape[0] == 1:
            return pl.BlockSpec(shape, lambda step, *_: (0, 0))
        return pl.BlockSpec((block, shape[1]), lambda step, *_: (step, 0))

    length = next(item.shape[0] for item in operands if item.ndim == 2 and item.shape[0] > 1)
    out_specs = [spec(item.shape, item.ndim == 3) for item in results]
    if stats:
        results = results + [jax.ShapeDtypeStruct((8, stats), jnp.float32)]
        out_specs.append(pl.BlockSpec((8, stats), lambda step, *_: (0, 0)))
    return pl.pallas_call(
        kernel,
        grid_spec=pltpu.PrefetchScalarGridSpec(
            num_scalar_prefetch=0 if facts is None else 1,
            grid=(length // block,),
            in_specs=[spec(item.shape, item.ndim == 3) for item in operands],
            out_specs=out_specs,
        ),
        out_shape=results,
        name=name,
        compiler_params=pltpu.CompilerParams(vmem_limit_bytes=20 << 20),
    )(*([] if facts is None else [facts]), *operands)


def grad_pre_kernel(low_ref, weight_ref, slope_ref, out_ref, stats_ref):
    grads = plain_dot(low_ref[...], weight_ref[...]) * slope_ref[...].astype(jnp.float32)
    grads = grads.astype(out_ref.dtype)
    out_ref[...] = grads
    row_kernel_stats(stats_ref, pl.program_id(0), [grads.astype(jnp.float32)])


def wide_layer(kernel, name, block, low, weight, operands, count, stats=0):
    length, width = low.shape[0], weight.shape[1]

    def spec(shape):
        if shape[0] == 1:
            return pl.BlockSpec(shape, lambda step: (0, 0))
        return pl.BlockSpec((block, shape[1]), lambda step: (step, 0))

    out_specs = [pl.BlockSpec((block, width), lambda step: (step, 0))] * count
    out_shape = [jax.ShapeDtypeStruct((length, width), jnp.bfloat16)] * count
    if stats:
        out_specs = out_specs + [pl.BlockSpec((8, width), lambda step: (0, 0))]
        out_shape = out_shape + [jax.ShapeDtypeStruct((8, width), jnp.float32)]
    return pl.pallas_call(
        kernel,
        grid=(length // block,),
        in_specs=[spec(low.shape), pl.BlockSpec(weight.shape, lambda step: (0, 0))]
        + [spec(item.shape) for item in operands],
        out_specs=out_specs,
        out_shape=out_shape,
        name=name,
        compiler_params=pltpu.CompilerParams(vmem_limit_bytes=20 << 20),
    )(low, weight, *operands)


def rows_kernel(left_ref, right_ref, out_ref, *, transposed):
    product = (rows_by_rows if transposed else plain_dot)(left_ref[...], right_ref[...])
    out_ref[...] = product.astype(out_ref.dtype)


def rows_times(left, right, block, transposed):
    length, depth = left.shape
    width = right.shape[0] if transposed else right.shape[1]
    return pl.pallas_call(
        lambda *refs: rows_kernel(*refs, transposed=transposed),
        grid=(length // block,),
        in_specs=[
            pl.BlockSpec((block, depth), lambda step: (step, 0)),
            pl.BlockSpec(right.shape, lambda step: (0, 0)),
        ],
        out_specs=pl.BlockSpec((block, width), lambda step: (step, 0)),
        out_shape=jax.ShapeDtypeStruct((length, width), jnp.bfloat16),
        name="rows_times",
        compiler_params=pltpu.CompilerParams(vmem_limit_bytes=14 << 20),
    )(left, right)


def pick_kernel(seat, in_ref, out_ref):
    out_ref[...] = in_ref[...]


def pick_halves(seat, blocks):
    count, rows, width = blocks.shape
    half = (1, rows // 2, width)
    return pl.pallas_call(
        pick_kernel,
        grid_spec=pltpu.PrefetchScalarGridSpec(
            num_scalar_prefetch=1,
            grid=(count,),
            in_specs=[pl.BlockSpec(half, lambda step, seat: (step ^ seat[1], seat[0], 0))],
            out_specs=pl.BlockSpec(half, lambda step, seat: (step, 0, 0)),
        ),
        out_shape=jax.ShapeDtypeStruct((count,) + half[1:], blocks.dtype),
        name="pick_halves",
        compiler_params=pltpu.CompilerParams(vmem_limit_bytes=4 << 20),
    )(seat, blocks)


def input_back_kernel(facts, grad_ref, weight_ref, mine_ref, other_ref):
    total = rows_by_rows(grad_ref[...], weight_ref[...]).astype(mine_ref.dtype)
    rows = mine_ref.shape[1]
    first = facts[1] == 0
    mine_ref[0] = jnp.where(first, total[:rows], total[rows:])
    other_ref[0] = jnp.where(first, total[rows:], total[:rows])


def input_back(facts, grads, weight, block):
    length, width = grads.shape
    half = (1, block // 2, weight.shape[0])
    return pl.pallas_call(
        input_back_kernel,
        grid_spec=pltpu.PrefetchScalarGridSpec(
            num_scalar_prefetch=1,
            grid=(length // block,),
            in_specs=[
                pl.BlockSpec((block, width), lambda step, facts: (step, 0)),
                pl.BlockSpec((weight.shape[0], width), lambda step, facts: (0, 0)),
            ],
            out_specs=[pl.BlockSpec(half, lambda step, facts: (step ^ facts[2], 0, 0))] * 2,
        ),
        out_shape=[jax.ShapeDtypeStruct((length // block,) + half[1:], jnp.bfloat16)] * 2,
        name="input_back",
        compiler_params=pltpu.CompilerParams(vmem_limit_bytes=10 << 20),
    )(facts, grads, weight)


def pack_kernel(second_ref, first_ref, up_ref, qkv_ref, count_ref, out_ref):
    width = out_ref.shape[1]
    out_ref[...] = jnp.zeros_like(out_ref)
    out_ref[0:4, :] = second_ref[0:4, :]
    out_ref[4:7, :] = first_ref[0:3, :]
    row = 7
    for ref in (up_ref, qkv_ref, count_ref):
        for start in range(0, ref.shape[1], width):
            span = min(width, ref.shape[1] - start)
            out_ref[row : row + 1, :span] = ref[0:1, start : start + span]
            row += 1


def pack(second, first, up, qkv, count):
    width = second.shape[1]
    rows = 7 + sum(-(-item.shape[1] // width) for item in (up, qkv, count))
    return pl.pallas_call(
        pack_kernel,
        out_shape=jax.ShapeDtypeStruct((-(-rows // 8) * 8, width), jnp.float32),
        name="pack",
        compiler_params=pltpu.CompilerParams(vmem_limit_bytes=2 << 20),
    )(second, first, up, qkv, count)


def join_kernel(facts, ratio_ref, own_ref, other_ref, out_ref):
    rows = own_ref.shape[1]
    for ref, half in ((own_ref, facts[0]), (other_ref, 1 - facts[0])):
        values = ref[0].astype(jnp.float32) * ratio_ref[0]
        out_ref[0, pl.ds(pl.multiple_of(half * rows, rows), rows), :] = values.astype(out_ref.dtype)


def join_halves(seat, half, ratio=None, dtype=jnp.bfloat16):
    count, rows, width = half.shape
    ratio = jnp.ones((1,), jnp.float32) if ratio is None else ratio.reshape(1)
    return pl.pallas_call(
        join_kernel,
        grid_spec=pltpu.PrefetchScalarGridSpec(
            num_scalar_prefetch=1,
            grid=(count,),
            in_specs=[pl.BlockSpec(memory_space=pltpu.SMEM)]
            + [pl.BlockSpec((1, rows, width), lambda step, facts: (step, 0, 0))] * 2,
            out_specs=pl.BlockSpec(
                (1, 2 * rows, width), lambda step, facts: (step ^ facts[1], 0, 0)
            ),
        ),
        out_shape=jax.ShapeDtypeStruct((count, 2 * rows, width), dtype),
        name="join_halves",
        compiler_params=pltpu.CompilerParams(vmem_limit_bytes=4 << 20),
    )(seat, ratio, half, swap(half, "tp", 1))


def weight_grad_kernel(places, *refs, chunks, fsdp, count, order):
    kinds = len(chunks)
    left_refs, right_refs = refs[:kinds], refs[kinds : 2 * kinds]
    out_refs, held = refs[2 * kinds : -1], refs[-1]
    step = pl.program_id(0)
    first = 0
    for left_ref, right_ref, chunk in zip(left_refs, right_refs, chunks):

        @pl.when(jnp.logical_and(step >= first, step < first + chunk))
        def _():
            total = lax.dot_general(
                left_ref[...],
                right_ref[...],
                (((0,), (0,)), ((), ())),
                preferred_element_type=jnp.float32,
            )
            held[...] = total.astype(held.dtype)

        first += chunk
    rows = held.shape[0] // (fsdp * count)
    if order == "fsdp":
        own = rows * count
        for half in range(2):
            for index in range(fsdp // 2):
                start = lax.bitwise_xor(places[1], jnp.int32(half + 2 * index)) * own
                out_refs[half][index * own : (index + 1) * own, :] = held[
                    pl.ds(pl.multiple_of(start, own), own), :
                ]
    else:
        steps = list(range(0, fsdp, 2)) + list(range(1, fsdp, 2))
        for s in range(count):
            for index, d in enumerate(steps):
                start = lax.bitwise_xor(places[1], jnp.int32(d)) * (rows * count)
                start = start + lax.bitwise_xor(places[0], jnp.int32(s)) * rows
                out_refs[s][index * rows : (index + 1) * rows, :] = held[
                    pl.ds(pl.multiple_of(start, rows), rows), :
                ]


def weight_grad(places, pairs, order="ctx"):
    fsdp, count = lax.axis_size("fsdp"), lax.axis_size("ctx")
    tokens, rows = pairs[0][0].shape
    columns = [right.shape[1] for _, right in pairs]
    width = max(
        item for item in range(LANES, 6 * LANES + 1, LANES) if not any(c % item for c in columns)
    )
    chunks = [item // width for item in columns]
    firsts = [sum(chunks[:index]) for index in range(len(chunks))]
    pieces = count if order == "ctx" else 2
    right_spec = lambda first, chunk: pl.BlockSpec(
        (tokens, width), lambda step, places: (0, jnp.clip(step - first, 0, chunk - 1))
    )
    return pl.pallas_call(
        lambda *refs: weight_grad_kernel(
            *refs, chunks=chunks, fsdp=fsdp, count=count, order=order
        ),
        grid_spec=pltpu.PrefetchScalarGridSpec(
            num_scalar_prefetch=1,
            grid=(sum(chunks),),
            in_specs=[pl.BlockSpec((tokens, rows), lambda step, places: (0, 0))] * len(pairs)
            + [right_spec(first, chunk) for first, chunk in zip(firsts, chunks)],
            out_specs=[pl.BlockSpec((rows // pieces, width), lambda step, places: (0, step))]
            * pieces,
            scratch_shapes=[pltpu.VMEM((rows, width), jnp.bfloat16)],
        ),
        out_shape=[jax.ShapeDtypeStruct((rows // pieces, sum(columns)), jnp.bfloat16)] * pieces,
        name="weight_grad",
        compiler_params=pltpu.CompilerParams(vmem_limit_bytes=14 << 20),
    )(places, *[left for left, _ in pairs], *[right for _, right in pairs])


def halve(kept, brought):
    rows = kept.shape[0] // 2
    return [
        low(wide(kept[cut]) + wide(brought[cut]))
        for cut in (slice(0, rows), slice(rows, 2 * rows))
    ]


def sum_kernel(*refs):
    part_refs, (kept_ref, sent_ref) = refs[:-2], refs[-2:]
    total = part_refs[0][...].astype(jnp.float32) + part_refs[1][...].astype(jnp.float32)
    for first, second in zip(part_refs[2::2], part_refs[3::2]):
        total = total + (first[...].astype(jnp.float32) + second[...].astype(jnp.float32))
    rows = kept_ref.shape[0]
    kept_ref[...] = total[:rows].astype(kept_ref.dtype)
    sent_ref[...] = total[rows:].astype(sent_ref.dtype)


def sum_and_cut(parts):
    rows, columns = parts[0].shape
    return pl.pallas_call(
        sum_kernel,
        out_shape=[jax.ShapeDtypeStruct((rows // 2, columns), jnp.bfloat16)] * 2,
        name="sum_and_cut",
        compiler_params=pltpu.CompilerParams(vmem_limit_bytes=8 << 20),
    )(*parts)


def join_rows_kernel(ratio_ref, *refs):
    out_ref, start = refs[-1], 0
    for first, second in zip(refs[0:-1:2], refs[1:-1:2]):
        total = first[...].astype(jnp.float32) + second[...].astype(jnp.float32)
        out_ref[start : start + first.shape[0], :] = total * ratio_ref[0]
        start += first.shape[0]


def join_rows(pairs, ratio):
    rows = sum(first.shape[0] for first, _ in pairs)
    operands = [item for pair in pairs for item in pair]
    vmem = pl.BlockSpec(memory_space=pltpu.VMEM)
    return pl.pallas_call(
        join_rows_kernel,
        in_specs=[pl.BlockSpec(memory_space=pltpu.SMEM)] + [vmem] * len(operands),
        out_specs=vmem,
        out_shape=jax.ShapeDtypeStruct((rows, operands[0].shape[1]), jnp.float32),
        name="join_rows",
        compiler_params=pltpu.CompilerParams(vmem_limit_bytes=8 << 20),
    )(ratio.reshape(1), *operands)


def place_kernel(places, ratio_ref, *refs, kinds):
    part_refs, out_ref = refs[:-1], refs[-1]
    rows, columns = part_refs[0].shape
    pairs = columns // (kinds * LANES)
    ratio = ratio_ref[0]
    for s in range(len(part_refs)):
        start = lax.bitwise_xor(places[0], jnp.int32(s)) * rows
        start = pl.multiple_of(start, rows)
        for kind in range(kinds):
            for pair in range(pairs):
                source = (pair * kinds + kind) * LANES
                target = (kind * pairs + pair) * LANES
                out_ref[pl.ds(start, rows), target : target + LANES] = (
                    part_refs[s][:, source : source + LANES].astype(jnp.float32) * ratio
                )


def place_rows(places, parts, ratio, kinds=1):
    rows, columns = parts[0].shape
    block = pl.BlockSpec((rows, columns), lambda step, places: (0, 0))
    return pl.pallas_call(
        lambda *refs: place_kernel(*refs, kinds=kinds),
        grid_spec=pltpu.PrefetchScalarGridSpec(
            num_scalar_prefetch=1,
            grid=(1,),
            in_specs=[pl.BlockSpec(memory_space=pltpu.SMEM)] + [block] * len(parts),
            out_specs=pl.BlockSpec((rows * len(parts), columns), lambda step, places: (0, 0)),
        ),
        out_shape=jax.ShapeDtypeStruct((rows * len(parts), columns), jnp.float32),
        name="place_rows",
        compiler_params=pltpu.CompilerParams(vmem_limit_bytes=6 << 20),
    )(places, ratio.reshape(1), *parts)


def whole_local(
    hidden_in,
    valid_mask,
    teacher,
    qkv_weight,
    qv_bias,
    out_weight,
    out_bias,
    norm1_gain,
    norm1_shift,
    up_weight,
    up_bias,
    down_weight,
    down_bias,
    norm2_gain,
    norm2_shift,
):
    seq_count, block_len, model_width = hidden_in.shape
    ctx_count = lax.axis_size("ctx")
    place, depth, core = lax.axis_index("ctx"), lax.axis_index("fsdp"), lax.axis_index("tp")
    inner_width = qkv_weight.shape[2]
    hidden_width = up_weight.shape[1]
    row_count = seq_count * block_len
    shape = hidden_in.shape
    places = jnp.stack([place, depth])
    seat = jnp.stack([core, place])
    lane = jnp.arange(LANES, dtype=jnp.int32)
    chosen = wide(lane == place)
    seat_rows = wide(jnp.where(lane == 0, seat[:, None], 0))
    fsdp_count = lax.axis_size("fsdp")
    row = lambda values: values.reshape(1, -1)
    struct = jax.ShapeDtypeStruct
    part_rows = qkv_weight.shape[0] // ctx_count
    own_part = lambda weight: lax.dynamic_slice_in_dim(weight, place * part_rows, part_rows, 0)
    qkv_out = jnp.concatenate([by_pairs(qkv_weight), out_weight], axis=1)
    local_counts = jnp.sum(wide(valid_mask), axis=1)
    hidden_own, weight_own = together(own_half(hidden_in), own_part(qkv_out))
    weight_rows = swap_all(weight_own, "fsdp")
    hidden_half = deal(hidden_own, "ctx")
    count_rows = jnp.broadcast_to(
        jnp.pad(low(local_counts), (0, qkv_out.shape[1] - seq_count)), (16, qkv_out.shape[1])
    )
    full_bias = row(by_pairs(jnp.stack([qv_bias[0], jnp.zeros_like(qv_bias[0]), qv_bias[1]])))
    teacher_own = pick_halves(seat, teacher)
    (
        places,
        seat,
        chosen,
        seat_rows,
        weight_rows,
        hidden_half,
        count_rows,
        up_own,
        down_own,
        teacher_own,
        full_bias,
    ) = together(
        places,
        seat,
        chosen,
        seat_rows,
        weight_rows,
        hidden_half,
        count_rows,
        own_part(up_weight),
        own_part(down_weight),
        teacher_own,
        full_bias,
    )
    weight_part = stack_rows(weight_rows + [count_rows])
    weight_parts = [weight_part] + swap_all(weight_part, "ctx")
    up_rows = relay_all(up_own, "fsdp")
    flat_in = join_halves(seat * jnp.array([1, 0], jnp.int32), hidden_half).reshape(row_count, model_width)
    weight_parts, flat_in, up_rows, down_own = together(
        weight_parts, flat_in, up_rows, down_own
    )
    up_part = stack_rows(up_rows)
    up_parts = [up_part] + swap_all(up_part, "ctx")
    down_rows = [swap(down_own, "fsdp", 1), swap(down_own, "fsdp", 2)]
    counts = sum(wide(item[-16, :LANES]) for item in weight_parts)
    facts = jnp.sum(jnp.concatenate([(counts * chosen)[None], seat_rows]), axis=1)
    facts = facts.astype(jnp.int32)
    projected, full_qkv_out = gathered_layer(
        project_kernel,
        "project",
        block_len,
        places,
        flat_in,
        [full_bias],
        qkv_out,
        weight_parts,
        [3 * inner_width],
        fsdp_count,
    )
    projected, down_first = together(projected, down_rows[0])
    down_rows = [down_first, down_rows[1], swap(down_first, "fsdp", 2)]
    full_out = full_qkv_out[:, 3 * inner_width :]
    attended, log_total = attend(facts, projected, block_len)
    attended, up_parts, down_rows = together(attended, up_parts, down_rows)
    down_part = stack_rows(down_rows)
    down_parts = [down_part] + swap_all(down_part, "ctx")
    branch = rows_times(attended, full_out, block_len, True)
    normal1, scale1, normed1_low = by_rows(
        first_norm_kernel,
        "first_norm",
        block_len,
        [flat_in, branch, swap(branch, "tp", 1), row(out_bias), row(norm1_gain), row(norm1_shift)],
        [
            struct((row_count, model_width), jnp.float32),
            struct((row_count, 1), jnp.float32),
            struct((row_count, model_width), jnp.bfloat16),
        ],
    )
    active, slope, full_up = gathered_layer(
        up_kernel,
        "up",
        block_len,
        places,
        normed1_low,
        [row(up_bias)],
        up_weight,
        up_parts,
        [hidden_width, hidden_width],
        fsdp_count,
    )
    active, down_parts = together(active, down_parts)
    teacher_half = stack_rows(
        [teacher_own[0]] + swap_each([teacher_own[s] for s in range(ctx_count)], "ctx")
    ).reshape(ctx_count, block_len // 2, model_width)
    branch, full_down = gathered_layer(
        down_kernel,
        "down",
        block_len,
        places,
        active,
        [],
        down_weight,
        down_parts,
        [model_width],
        fsdp_count,
    )
    layer_half, grad_resid2, grad_resid2_low, stats2 = by_rows(
        second_norm_kernel,
        "second_norm",
        block_len,
        [
            normal1,
            row(norm1_gain),
            row(norm1_shift),
            branch,
            swap(branch, "tp", 1),
            row(down_bias),
            row(norm2_gain),
            row(norm2_shift),
            teacher_half,
            swap(teacher_half, "tp", 1),
        ],
        [
            struct(teacher_half.shape, jnp.bfloat16),
            struct((row_count, model_width), jnp.float32),
            struct((row_count, model_width), jnp.bfloat16),
        ],
        facts=facts,
        stats=model_width,
    )
    down_kept, down_sent = weight_grad(places, [(grad_resid2_low, active)], "fsdp")
    down_kept, down_sent, grad_resid2_low = together(down_kept, down_sent, grad_resid2_low)
    down_brought = swap(down_sent, "fsdp", 1)
    layer_pieces = [layer_half[s] for s in range(ctx_count)]
    layer_pieces = layer_pieces[:1] + swap_each(layer_pieces, "ctx")
    grad_pre, stats_up = wide_layer(
        grad_pre_kernel, "grad_pre", block_len, grad_resid2_low, full_down, [slope], 1, hidden_width
    )
    branch = rows_times(grad_pre, full_up, block_len, True)
    branch, grad_pre, layer_pieces = together(branch, grad_pre, layer_pieces)
    layer_out = join_halves(seat, stack_rows(layer_pieces).reshape(layer_half.shape))
    up_pieces = weight_grad(places, [(normed1_low, grad_pre)])
    up_brought = swap_each(up_pieces, "ctx")
    grad_resid1_low, grad_half, stats1 = by_rows(
        first_norm_back_kernel,
        "first_norm_back",
        block_len,
        [grad_resid2, branch, swap(branch, "tp", 1), normal1, scale1, row(norm1_gain)],
        [
            struct((row_count, model_width), jnp.bfloat16),
            struct(layer_half.shape, jnp.float32),
        ],
        facts=facts,
        stats=model_width,
    )
    out_kept, out_sent = weight_grad(places, [(grad_resid1_low, attended)], "fsdp")
    grad_attended = rows_times(grad_resid1_low, full_out, block_len, False)
    out_kept, out_sent, grad_attended, layer_out = together(
        out_kept, out_sent, grad_attended, layer_out
    )
    out_brought = swap(out_sent, "fsdp", 1)
    grad_qkv, stats_qkv = attend_back(facts, projected, grad_attended, log_total, block_len)
    grad_qkv, down_brought, out_brought = together(grad_qkv, down_brought, out_brought)
    local_count = jnp.broadcast_to(jnp.sum(local_counts), (1, LANES))
    small = pack(stats2, stats1, stats_up, stats_qkv, local_count)
    small_other = swap(small, "ctx", 1)
    last_pieces = weight_grad(places, [(flat_in, grad_qkv)])
    down_kept, down_sent = sum_and_cut([down_kept, down_brought])
    out_kept, out_sent = sum_and_cut([out_kept, out_brought])
    last_pieces, grad_qkv, down_sent, out_sent, small_other = together(
        last_pieces, grad_qkv, down_sent, out_sent, small_other
    )
    last_brought = swap_each(last_pieces, "ctx")
    down_brought = swap(down_sent, "fsdp", 2)
    mine, other = input_back(facts, grad_qkv, full_qkv_out, block_len)
    up_kept, up_sent = sum_and_cut([up_pieces[0]] + up_brought)
    small = small + small_other
    small_other = swap(small, "ctx", 2)
    last_brought, mine, other, up_sent, out_sent, small, small_other = together(
        last_brought, mine, other, up_sent, out_sent, small, small_other
    )
    last_kept, last_sent = sum_and_cut([last_pieces[0]] + last_brought)
    last_sent, other, down_brought, up_sent, out_sent, small, small_other = together(
        last_sent, other, down_brought, up_sent, out_sent, small, small_other
    )
    last_brought = swap(last_sent, "fsdp", 1)
    other = swap(other, "tp", 1)
    cut = down_kept.shape[0] // 2
    owned_down = [
        low(wide(down_kept[span]) + wide(down_brought[span]))
        for span in (slice(0, cut), slice(cut, 2 * cut))
    ]
    down_other = [swap(owned_down[0], "ctx", 1), swap(owned_down[1], "ctx", 2)]
    small = small + small_other
    small_other = swap(small, "fsdp", 1)
    last_brought, other, up_sent, out_sent, small, small_other = together(
        last_brought, other, up_sent, out_sent, small, small_other
    )
    last_kept, last_sent = sum_and_cut([last_kept, last_brought])
    half = low(grad_half + (wide(mine) + wide(other)))
    small = small + small_other
    last_sent, half, up_sent, out_sent, small = together(
        last_sent, half, up_sent, out_sent, small
    )
    last_brought = swap(last_sent, "fsdp", 2)
    up_brought = swap(up_sent, "fsdp", 1)
    half_pieces = [half[s] for s in range(ctx_count)]
    half_brought = [half_pieces[0], swap(half_pieces[1], "ctx", 1)]
    small_other = swap(small, "fsdp", 2)
    out_brought = swap(out_sent, "fsdp", 2)
    last_brought, up_brought, down_other, out_brought, small_other, half_pieces = together(
        last_brought, up_brought, down_other, out_brought, small_other, half_pieces
    )
    part = low(wide(last_kept) + wide(last_brought))
    up_kept, up_sent = sum_and_cut([up_kept, up_brought])
    owned_down = [low(wide(mine) + wide(other)) for mine, other in zip(owned_down, down_other)]
    small = small + small_other
    part, up_sent, owned_down, out_brought, small, half_pieces = together(
        part, up_sent, owned_down, out_brought, small, half_pieces
    )
    shared = [part, swap(part, "ctx", 1), swap(part, "ctx", 2)]
    up_brought = swap(up_sent, "fsdp", 2)
    down_other = [swap(owned_down[0], "ctx", 2), swap(owned_down[1], "ctx", 1)]
    shared, up_brought, out_brought, half_pieces, down_other = together(
        shared, up_brought, out_brought, half_pieces, down_other
    )
    up_part = low(wide(up_kept) + wide(up_brought))
    owned_out = low(wide(out_kept) + wide(out_brought))
    up_part, owned_out, shared, half_pieces = together(up_part, owned_out, shared, half_pieces)
    shared = shared + [swap(shared[1], "ctx", 2)]
    up_shared = [up_part, swap(up_part, "ctx", 1), swap(up_part, "ctx", 2)]
    half_brought = half_brought + [swap(half_pieces[s], "ctx", s) for s in range(2, ctx_count)]
    up_shared, shared, half_brought, owned_out = together(
        up_shared, shared, half_brought, owned_out
    )
    up_shared = up_shared + [swap(up_shared[1], "ctx", 2)]
    input_half = stack_rows(half_brought).reshape(half.shape)
    out_other = swap(owned_out, "ctx", 1)
    owned_out, out_other, input_half, up_shared = together(
        owned_out, out_other, input_half, up_shared
    )
    owned_out = low(wide(owned_out) + wide(out_other))
    out_other = swap(owned_out, "ctx", 2)
    at = 7 + -(-hidden_width // model_width)
    last_row = at + -(-3 * inner_width // model_width)
    counted = small[last_row : last_row + 1, :1]
    ratio = float(row_count * ctx_count * fsdp_count) / counted
    loss = jnp.sum(small[3:4], axis=1, keepdims=True) / (counted * model_width)
    scaled = small * ratio
    input_grad = join_halves(seat, input_half, ratio, jnp.float32)
    owned_qkv = place_rows(places, shared, ratio, 3)
    owned_down = join_rows(list(zip(owned_down, down_other)), ratio)
    owned_up = place_rows(places, up_shared, ratio)
    owned_qkv, owned_up, owned_down, out_other, input_grad, scaled = together(
        owned_qkv, owned_up, owned_down, out_other, input_grad, scaled
    )
    owned_qkv = owned_qkv.reshape(qkv_weight.shape)
    owned_out = (wide(owned_out) + wide(out_other)) * ratio
    grad_up_bias = scaled[7:at].reshape(-1)[:hidden_width]
    grad_qv_bias = by_kinds(
        scaled[at : at + -(-3 * inner_width // model_width)].reshape(-1)[: 3 * inner_width]
    )[0::2]
    return (
        layer_out,
        input_grad,
        loss.reshape(()),
        owned_qkv,
        grad_qv_bias,
        owned_out,
        scaled[4],
        scaled[5],
        scaled[6],
        owned_up,
        grad_up_bias,
        owned_down,
        scaled[0],
        scaled[1],
        scaled[2],
    )


def spread_local(
    hidden_in,
    valid_mask,
    teacher,
    qkv_weight,
    qv_bias,
    out_weight,
    out_bias,
    norm1_gain,
    norm1_shift,
    up_weight,
    up_bias,
    down_weight,
    down_bias,
    norm2_gain,
    norm2_shift,
):
    seq_count, block_len, model_width = hidden_in.shape
    ctx_count = lax.axis_size("ctx")
    ctx_place = lax.axis_index("ctx")
    key_span = 2 * block_len
    seq_length = block_len * ctx_count
    row_count = seq_count * block_len
    scaling = HEAD_DIM ** (-0.5)
    full_qkv, full_out, full_up, full_down = (
        lax.all_gather(qkv_weight, "fsdp", axis=0, tiled=True),
        lax.all_gather(out_weight, "fsdp", axis=0, tiled=True),
        lax.all_gather(up_weight, "fsdp", axis=0, tiled=True),
        lax.all_gather(down_weight, "fsdp", axis=0, tiled=True),
    )
    inner_width = full_qkv.shape[2]
    head_count = inner_width // HEAD_DIM
    flat_in = hidden_in.reshape(row_count, model_width)
    full_bias = jnp.stack([qv_bias[0], jnp.zeros_like(qv_bias[0]), qv_bias[1]])
    projected = (
        jnp.einsum("td,dje->tje", flat_in, full_qkv, preferred_element_type=jnp.float32) + full_bias
    ).astype(jnp.bfloat16)
    queries = projected[:, 0].reshape(seq_count, block_len, inner_width)
    key_own = projected[:, 1].reshape(seq_count, block_len, inner_width)
    value_own = projected[:, 2].reshape(seq_count, block_len, inner_width)
    keep_own = valid_mask.astype(jnp.bfloat16)
    keys_all, values_all, keep_all = (
        lax.all_gather(key_own, "ctx", axis=1, tiled=True),
        lax.all_gather(value_own, "ctx", axis=1, tiled=True),
        lax.all_gather(keep_own, "ctx", axis=1, tiled=True),
    )
    query_heads = split_heads(queries)
    seen_limit = (ctx_place + 1) * block_len
    trip_count = ctx_place // 2 + 1
    offsets = jnp.arange(key_span, dtype=jnp.int32)

    def key_block(block_index):
        key_start = block_index * key_span
        key_heads = split_heads(lax.dynamic_slice_in_dim(keys_all, key_start, key_span, 1))
        value_heads = split_heads(lax.dynamic_slice_in_dim(values_all, key_start, key_span, 1))
        live_keys = lax.dynamic_slice_in_dim(keep_all, key_start, key_span, 1) > 0.5
        allowed = jnp.logical_and(live_keys, (key_start + offsets)[None, :] < seen_limit)
        return (key_heads, value_heads, allowed[:, None, None, :])

    def attend_step(block_index, carried):
        run_top, run_total, gathered = carried
        key_heads, value_heads, allowed = key_block(block_index)
        raw_scores = scores_of(query_heads, key_heads, allowed, scaling)
        new_top = jnp.maximum(run_top, jnp.max(raw_scores, axis=-1))
        shrink = jnp.exp(run_top - new_top)
        weights_now = jnp.exp(raw_scores - new_top[..., None])
        run_total = run_total * shrink + jnp.sum(weights_now, axis=-1)
        gathered = gathered * jnp.swapaxes(shrink, 1, 2)[..., None] + jnp.einsum(
            "shqk,skhd->sqhd",
            weights_now.astype(jnp.bfloat16),
            value_heads,
            preferred_element_type=jnp.float32,
        )
        return (new_top, run_total, gathered)

    start_top = jnp.full((seq_count, head_count, block_len), MASKED, jnp.float32)
    empty_heads = jnp.zeros((seq_count, block_len, head_count, HEAD_DIM), jnp.float32)
    run_top, run_total, gathered = lax.fori_loop(
        0, trip_count, attend_step, (start_top, jnp.zeros_like(start_top), empty_heads)
    )
    log_total = run_top + jnp.log(run_total)
    attended_exact = gathered / jnp.swapaxes(run_total, 1, 2)[..., None]
    attended = attended_exact.astype(jnp.bfloat16).reshape(row_count, inner_width)
    attn_branch = lax.psum(
        jnp.einsum("te,de->td", attended, full_out, preferred_element_type=jnp.float32).astype(
            jnp.bfloat16
        ),
        "tp",
    ).astype(jnp.float32)
    resid1 = flat_in.astype(jnp.float32) + attn_branch + out_bias
    normed1, norm1_back = jax.vjp(layer_norm, resid1, norm1_gain, norm1_shift)
    normed1_low = normed1.astype(jnp.bfloat16)
    pre_act = jnp.dot(normed1_low, full_up, preferred_element_type=jnp.float32) + up_bias
    active, gelu_back = jax.vjp(gelu_exact, pre_act)
    active = active.astype(jnp.bfloat16)
    ffn_branch = lax.psum(
        jnp.einsum("tf,df->td", active, full_down, preferred_element_type=jnp.float32).astype(
            jnp.bfloat16
        ),
        "tp",
    ).astype(jnp.float32)
    resid2 = normed1 + ffn_branch + down_bias
    output, norm2_back = jax.vjp(layer_norm, resid2, norm2_gain, norm2_shift)
    layer_out = output.astype(jnp.bfloat16).reshape(seq_count, block_len, model_width)
    keep_rows = valid_mask.reshape(row_count, 1).astype(jnp.float32)
    residue = (output - teacher.reshape(row_count, model_width).astype(jnp.float32)) * keep_rows
    squared = jnp.sum(residue * residue)
    counted = jnp.sum(keep_rows)
    grad_resid2, grad_gain2, grad_shift2 = norm2_back(residue)
    grad_down_bias = jnp.sum(grad_resid2, axis=0)
    grad_resid2_low = grad_resid2.astype(jnp.bfloat16)
    grad_active = jnp.dot(grad_resid2_low, full_down, preferred_element_type=jnp.float32)
    grad_down_weight = jnp.einsum(
        "td,tf->df", grad_resid2_low, active, preferred_element_type=jnp.float32
    )
    grad_pre = gelu_back(grad_active)[0].astype(jnp.bfloat16)
    grad_up_bias = jnp.sum(grad_pre.astype(jnp.float32), axis=0)
    grad_up_weight = jnp.einsum(
        "td,tf->df", normed1_low, grad_pre, preferred_element_type=jnp.float32
    )
    ffn_input_grad = lax.psum(
        jnp.einsum("tf,df->td", grad_pre, full_up, preferred_element_type=jnp.float32).astype(
            jnp.bfloat16
        ),
        "tp",
    ).astype(jnp.float32)
    grad_normed1 = grad_resid2 + ffn_input_grad
    grad_resid1, grad_gain1, grad_shift1 = norm1_back(grad_normed1)
    grad_out_bias = jnp.sum(grad_resid1, axis=0)
    grad_resid1_low = grad_resid1.astype(jnp.bfloat16)
    grad_mixed = jnp.dot(grad_resid1_low, full_out, preferred_element_type=jnp.float32)
    grad_out_weight = jnp.einsum(
        "td,te->de", grad_resid1_low, attended, preferred_element_type=jnp.float32
    )
    grad_attended = grad_mixed.astype(jnp.bfloat16).reshape(
        seq_count, block_len, head_count, HEAD_DIM
    )
    delta = jnp.swapaxes(jnp.sum(grad_attended.astype(jnp.float32) * attended_exact, axis=-1), 1, 2)

    def query_grads(block_index):
        key_heads, value_heads, allowed = key_block(block_index)
        prob_rows = jnp.exp(
            scores_of(query_heads, key_heads, allowed, scaling) - log_total[..., None]
        )
        push = jnp.einsum(
            "sqhd,skhd->shqk", grad_attended, value_heads, preferred_element_type=jnp.float32
        )
        slope = (prob_rows * (push - delta[..., None])).astype(jnp.bfloat16)
        grad_part = (
            jnp.einsum("shqk,skhd->sqhd", slope, key_heads, preferred_element_type=jnp.float32)
            * scaling
        )
        return (prob_rows, slope, grad_part)

    def back_step(block_index, carried):
        grad_query, spread = carried
        prob_rows, slope, grad_part = query_grads(block_index)
        grad_key = (
            jnp.einsum("shqk,sqhd->skhd", slope, query_heads, preferred_element_type=jnp.float32)
            * scaling
        )
        grad_value = jnp.einsum(
            "shqk,sqhd->skhd",
            prob_rows.astype(jnp.bfloat16),
            grad_attended,
            preferred_element_type=jnp.float32,
        )
        piece = jnp.stack(
            [
                grad_key.reshape(seq_count, key_span, inner_width),
                grad_value.reshape(seq_count, key_span, inner_width),
            ],
            axis=2,
        )
        spread = lax.dynamic_update_slice_in_dim(spread, piece, block_index * key_span, 1)
        return (grad_query + grad_part, spread)

    spread_start = jnp.zeros((seq_count, seq_length, 2, inner_width), jnp.float32)
    grad_query, spread = lax.fori_loop(0, trip_count, back_step, (empty_heads, spread_start))
    own_grads = lax.psum_scatter(
        spread.astype(jnp.bfloat16), "ctx", scatter_dimension=1, tiled=True
    ).astype(jnp.float32)
    grad_key_own = own_grads[:, :, 0]
    grad_value_own = own_grads[:, :, 1]
    grad_qkv = jnp.stack(
        [
            grad_query.reshape(row_count, inner_width),
            grad_key_own.reshape(row_count, inner_width),
            grad_value_own.reshape(row_count, inner_width),
        ],
        axis=1,
    ).astype(jnp.bfloat16)
    grad_qv_bias = jnp.sum(grad_qkv[:, 0::2].astype(jnp.float32), axis=0)
    grad_qkv_weight = jnp.einsum(
        "td,tje->dje", flat_in, grad_qkv, preferred_element_type=jnp.float32
    )
    input_part = lax.psum(
        jnp.einsum("tje,dje->td", grad_qkv, full_qkv, preferred_element_type=jnp.float32).astype(
            jnp.bfloat16
        ),
        "tp",
    ).astype(jnp.float32)
    grad_input = grad_resid1 + input_part
    vectors = jnp.stack(
        [grad_out_bias, grad_gain1, grad_shift1, grad_down_bias, grad_gain2, grad_shift2]
    )
    squared, counted, vectors, grad_qv_bias, grad_up_bias = lax.psum(
        (squared, counted, vectors, grad_qv_bias, grad_up_bias), ("fsdp", "ctx")
    )
    local_grads = (grad_qkv_weight, grad_out_weight, grad_up_weight, grad_down_weight)
    owned = (
        lax.psum_scatter(
            local_grads[0].astype(jnp.bfloat16), "fsdp", scatter_dimension=0, tiled=True
        ).astype(jnp.float32),
        lax.psum_scatter(
            local_grads[1].astype(jnp.bfloat16), "fsdp", scatter_dimension=0, tiled=True
        ).astype(jnp.float32),
        lax.psum_scatter(
            local_grads[2].astype(jnp.bfloat16), "fsdp", scatter_dimension=0, tiled=True
        ).astype(jnp.float32),
        lax.psum_scatter(
            local_grads[3].astype(jnp.bfloat16), "fsdp", scatter_dimension=0, tiled=True
        ).astype(jnp.float32),
    )
    owned = (
        lax.psum(owned[0].astype(jnp.bfloat16), "ctx").astype(jnp.float32),
        lax.psum(owned[1].astype(jnp.bfloat16), "ctx").astype(jnp.float32),
        lax.psum(owned[2].astype(jnp.bfloat16), "ctx").astype(jnp.float32),
        lax.psum(owned[3].astype(jnp.bfloat16), "ctx").astype(jnp.float32),
    )
    token_total = float(seq_count * seq_length * lax.axis_size("fsdp"))
    ratio = token_total / counted
    loss = squared / (counted * model_width)
    input_grad = (grad_input * ratio).reshape(seq_count, block_len, model_width)
    return (
        layer_out,
        input_grad,
        loss,
        owned[0] * ratio,
        grad_qv_bias * ratio,
        owned[1] * ratio,
        vectors[0] * ratio,
        vectors[1] * ratio,
        vectors[2] * ratio,
        owned[2] * ratio,
        grad_up_bias * ratio,
        owned[3] * ratio,
        vectors[3] * ratio,
        vectors[4] * ratio,
        vectors[5] * ratio,
    )


def local(hidden_in, *others):
    seq_count, block_len, model_width = hidden_in.shape
    ctx_count, fsdp_count = lax.axis_size("ctx"), lax.axis_size("fsdp")
    rows, inner_width = others[2].shape[0], others[2].shape[2]
    whole = (
        seq_count == ctx_count
        and ctx_count & (ctx_count - 1) == 0
        and fsdp_count == 4
        and lax.axis_size("tp") == 2
        and block_len % LANES == 0
        and others[5].shape[0] >= inner_width
        and inner_width % LANES == 0
        and rows % (16 * ctx_count) == 0
    )
    return (whole_local if whole else spread_local)(hidden_in, *others)


def solution(mesh):
    in_specs = (
        P("fsdp", "ctx", None),
        P("fsdp", "ctx"),
        P("fsdp", "ctx", None),
        P("fsdp", None, "tp"),
        P(None, "tp"),
        P("fsdp", "tp"),
        P(),
        P(),
        P(),
        P("fsdp", "tp"),
        P("tp"),
        P("fsdp", "tp"),
        P(),
        P(),
        P(),
    )
    out_specs = (
        P("fsdp", "ctx", None),
        P("fsdp", "ctx", None),
        P(),
        P("fsdp", None, "tp"),
        P(None, "tp"),
        P("fsdp", "tp"),
        P(),
        P(),
        P(),
        P("fsdp", "tp"),
        P("tp"),
        P("fsdp", "tp"),
        P(),
        P(),
        P(),
    )
    return jax.shard_map(local, mesh=mesh, in_specs=in_specs, out_specs=out_specs, check_vma=False)
```

```python
import jax
import jax.numpy as jnp
from jax import lax
from jax.experimental import pallas as pl
from jax.experimental.pallas import tpu as pltpu
from jax.sharding import PartitionSpec as P

HEAD_DIM = 64
NORM_EPS = 1e-05
MASKED = -1e30
LANES = 128


def layer_norm(values_in, gain_vec, shift_vec):
    row_mean = jnp.mean(values_in, axis=-1, keepdims=True)
    centered = values_in - row_mean
    row_var = jnp.mean(centered * centered, axis=-1, keepdims=True)
    return centered * lax.rsqrt(row_var + NORM_EPS) * gain_vec + shift_vec


def gelu_exact(pre_act):
    return jax.nn.gelu(pre_act, approximate=False)


def split_heads(packed):
    return packed.reshape(packed.shape[0], packed.shape[1], packed.shape[2] // HEAD_DIM, HEAD_DIM)


def scores_of(query_heads, key_heads, allowed, scaling):
    raw_scores = (
        jnp.einsum("sqhd,skhd->shqk", query_heads, key_heads, preferred_element_type=jnp.float32)
        * scaling
    )
    return jnp.where(allowed, raw_scores, MASKED)


def rows_by_rows(left, right):
    return lax.dot_general(left, right, (((1,), (1,)), ((), ())), preferred_element_type=jnp.float32)


def plain_dot(left, right):
    return jnp.dot(left, right, preferred_element_type=jnp.float32)


def lanes_of(head, lane):
    own = (lane < HEAD_DIM) if head == 0 else (lane >= HEAD_DIM)
    spare = HEAD_DIM if head == 0 else 0
    return own, lane == spare


def head_operands(query_ref, key_ref, slot, start, block, valid_count, head):
    lane = lax.broadcasted_iota(jnp.int32, (block, LANES), 1)
    own, spare = lanes_of(head, lane)
    position = start + lax.broadcasted_iota(jnp.int32, (block, LANES), 0)
    bias = jnp.where(position < valid_count, 0.0, MASKED)
    rows = pl.ds(slot * block, block)
    query = query_ref[rows, :].astype(jnp.float32) * (HEAD_DIM ** -0.5)
    key = key_ref[rows, :].astype(jnp.float32)
    query_side = jnp.where(spare, 1.0, query).astype(jnp.bfloat16)
    key_side = jnp.where(own, key, jnp.where(spare, bias, 0.0)).astype(jnp.bfloat16)
    return query_side, key_side


def attend_kernel(facts, query_ref, key_ref, value_ref, out_ref, log_ref, *, block):
    valid_count = facts[0]
    blocks = query_ref.shape[0] // block
    slots = list(range(blocks))
    value_t = [
        value_ref[pl.ds(slots[j] * block, block), :].astype(jnp.float32).T.astype(jnp.bfloat16)
        for j in range(blocks)
    ]
    outs = [[] for _ in range(blocks)]
    for head in range(2):
        sides = [
            head_operands(query_ref, key_ref, slots[j], j * block, block, valid_count, head)
            for j in range(blocks)
        ]
        span = slice(head * HEAD_DIM, (head + 1) * HEAD_DIM)
        for i in range(blocks):
            scores = [rows_by_rows(sides[j][1], sides[i][0]) for j in range(i + 1)]
            top = scores[0].max(axis=0, keepdims=True)
            for j in range(1, i + 1):
                top = jnp.maximum(top, scores[j].max(axis=0, keepdims=True))
            total = jnp.zeros_like(top)
            mixed = jnp.zeros((HEAD_DIM, block), jnp.float32)
            for j in range(i + 1):
                weight = jnp.exp(scores[j] - top)
                total = total + weight.sum(axis=0, keepdims=True)
                mixed = mixed + plain_dot(value_t[j][span, :], weight.astype(jnp.bfloat16))
            outs[i].append(mixed / total)
            log_ref[0, head : head + 1, i * block : (i + 1) * block] = top + jnp.log(total)
    for i in range(blocks):
        both = jnp.concatenate(outs[i], axis=0)
        out_ref[pl.ds(slots[i] * block, block), :] = both.T.astype(out_ref.dtype)


def attend_back_kernel(
    facts,
    query_ref,
    key_ref,
    value_ref,
    grad_ref,
    log_ref,
    out_ref,
    stats_ref,
    grad_key,
    grad_value,
    *,
    block,
):
    valid_count = facts[0]
    blocks = query_ref.shape[0] // block
    slots = list(range(blocks))
    scaling = HEAD_DIM ** -0.5
    lane = lax.broadcasted_iota(jnp.int32, (block, LANES), 1)
    key_t, grads, queries, values = [], [], [], []
    for j in range(blocks):
        rows = pl.ds(slots[j] * block, block)
        key_t.append((key_ref[rows, :].astype(jnp.float32) * scaling).T.astype(jnp.bfloat16))
        grads.append(grad_ref[rows, :])
        queries.append(query_ref[rows, :].astype(jnp.float32) * scaling)
        values.append(value_ref[rows, :].astype(jnp.float32))
    grad_queries = [[] for _ in range(blocks)]
    for head in range(2):
        own, _ = lanes_of(head, lane)
        span = slice(head * HEAD_DIM, (head + 1) * HEAD_DIM)
        sides = [
            head_operands(query_ref, key_ref, slots[j], j * block, block, valid_count, head)
            for j in range(blocks)
        ]
        head_values = [jnp.where(own, item, 0.0).astype(jnp.bfloat16) for item in values]
        for i in range(blocks):
            log_row = log_ref[0, head : head + 1, i * block : (i + 1) * block]
            head_grad = jnp.where(own, grads[i].astype(jnp.float32), 0.0).astype(jnp.bfloat16)
            head_query = jnp.where(own, queries[i], 0.0).astype(jnp.bfloat16)
            probs, pushes = [], []
            delta = jnp.zeros((1, block), jnp.float32)
            for j in range(i + 1):
                prob = jnp.exp(rows_by_rows(sides[j][1], sides[i][0]) - log_row)
                push = rows_by_rows(head_values[j], grads[i])
                delta = delta + (prob * push).sum(axis=0, keepdims=True)
                probs.append(prob)
                pushes.append(push)
            grad_query = jnp.zeros((HEAD_DIM, block), jnp.float32)
            for j in range(i + 1):
                slope = (probs[j] * (pushes[j] - delta)).astype(jnp.bfloat16)
                part_value = plain_dot(probs[j].astype(jnp.bfloat16), head_grad)
                part_key = plain_dot(slope, head_query)
                span_rows = slice(j * block, (j + 1) * block)
                if head == 0 and i == j:
                    grad_value[span_rows, :] = part_value
                    grad_key[span_rows, :] = part_key
                else:
                    grad_value[span_rows, :] += part_value
                    grad_key[span_rows, :] += part_key
                grad_query = grad_query + plain_dot(key_t[j][span, :], slope)
            grad_queries[i].append(grad_query)
    totals = jnp.zeros((1, 3 * LANES), jnp.float32)
    for i in range(blocks):
        rows = pl.ds(slots[i] * block, block)
        both = jnp.concatenate(grad_queries[i], axis=0)
        out_ref[rows, :LANES] = both.T.astype(out_ref.dtype)
        span_rows = slice(i * block, (i + 1) * block)
        out_ref[rows, LANES : 2 * LANES] = grad_key[span_rows, :].astype(out_ref.dtype)
        out_ref[rows, 2 * LANES :] = grad_value[span_rows, :].astype(out_ref.dtype)
        totals += jnp.sum(out_ref[rows, :].astype(jnp.float32), axis=0, keepdims=True)
    stats_ref[...] = jnp.broadcast_to(totals, stats_ref.shape)


def attend(facts, projected, block):
    length, width = projected.shape
    pairs = width // (3 * LANES)
    column = lambda kind: pl.BlockSpec((length, LANES), lambda pair, facts: (0, 3 * pair + kind))
    return pl.pallas_call(
        lambda *refs: attend_kernel(*refs, block=block),
        grid_spec=pltpu.PrefetchScalarGridSpec(
            num_scalar_prefetch=1,
            grid=(pairs,),
            in_specs=[column(0), column(1), column(2)],
            out_specs=[
                pl.BlockSpec((length, LANES), lambda pair, facts: (0, pair)),
                pl.BlockSpec((1, 2, length), lambda pair, facts: (pair, 0, 0)),
            ],
        ),
        out_shape=[
            jax.ShapeDtypeStruct((length, pairs * LANES), jnp.bfloat16),
            jax.ShapeDtypeStruct((pairs, 2, length), jnp.float32),
        ],
        name="attend",
        compiler_params=pltpu.CompilerParams(vmem_limit_bytes=9 << 20),
    )(facts, projected, projected, projected)


def attend_back(facts, projected, grad_attended, log_total, block):
    length, width = grad_attended.shape
    pairs = width // LANES
    column = lambda kind: pl.BlockSpec((length, LANES), lambda pair, facts: (0, 3 * pair + kind))
    return pl.pallas_call(
        lambda *refs: attend_back_kernel(*refs, block=block),
        grid_spec=pltpu.PrefetchScalarGridSpec(
            num_scalar_prefetch=1,
            grid=(pairs,),
            in_specs=[
                column(0),
                column(1),
                column(2),
                pl.BlockSpec((length, LANES), lambda pair, facts: (0, pair)),
                pl.BlockSpec((1, 2, length), lambda pair, facts: (pair, 0, 0)),
            ],
            out_specs=[
                pl.BlockSpec((length, 3 * LANES), lambda pair, facts: (0, pair)),
                pl.BlockSpec((8, 3 * LANES), lambda pair, facts: (0, pair)),
            ],
            scratch_shapes=[
                pltpu.VMEM((length, LANES), jnp.float32),
                pltpu.VMEM((length, LANES), jnp.float32),
            ],
        ),
        out_shape=[
            jax.ShapeDtypeStruct((length, 3 * width), jnp.bfloat16),
            jax.ShapeDtypeStruct((8, 3 * width), jnp.float32),
        ],
        name="attend_back",
        compiler_params=pltpu.CompilerParams(vmem_limit_bytes=12 << 20),
    )(facts, projected, projected, projected, grad_attended, log_total)


def by_pairs(values):
    kinds, width = values.shape[-2:]
    cut = values.reshape(values.shape[:-1] + (width // LANES, LANES))
    return jnp.swapaxes(cut, -3, -2).reshape(values.shape[:-2] + (kinds * width,))


def by_kinds(values, kinds=3):
    width = values.shape[-1] // kinds
    cut = values.reshape(values.shape[:-1] + (width // LANES, kinds, LANES))
    return jnp.swapaxes(cut, -3, -2).reshape(values.shape[:-1] + (kinds, width))


def fill_rows(places, own_ref, part_refs, out_ref):
    count = len(part_refs)
    rows = own_ref.shape[0] // count
    fsdp = out_ref.shape[0] // own_ref.shape[0]
    place, depth = places[0], places[1]
    start = pl.multiple_of(depth * (rows * count), rows)
    out_ref[pl.ds(start, rows * count), :] = own_ref[...]
    for s in range(count):
        for d in range(1, fsdp):
            start = lax.bitwise_xor(depth, jnp.int32(d)) * (rows * count)
            start = start + lax.bitwise_xor(place, jnp.int32(s)) * rows
            out_ref[pl.ds(pl.multiple_of(start, rows), rows), :] = part_refs[s][
                (d - 1) * rows : d * rows, :
            ]


def project_kernel(places, left_ref, bias_ref, own_ref, *refs):
    part_refs, (out_ref, full_ref) = refs[:-2], refs[-2:]

    @pl.when(pl.program_id(0) == 0)
    def _():
        fill_rows(places, own_ref, part_refs, full_ref)

    total = plain_dot(left_ref[...], full_ref[:, : out_ref.shape[1]]) + bias_ref[...]
    out_ref[...] = total.astype(out_ref.dtype)


def up_kernel(places, left_ref, bias_ref, own_ref, *refs):
    part_refs, (active_ref, slope_ref, full_ref) = refs[:-3], refs[-3:]

    @pl.when(pl.program_id(0) == 0)
    def _():
        fill_rows(places, own_ref, part_refs, full_ref)

    pre = plain_dot(left_ref[...], full_ref[...]) + bias_ref[...]
    below = 0.5 * (1.0 + lax.erf(pre * (0.5**0.5)))
    active_ref[...] = (pre * below).astype(active_ref.dtype)
    bell = jnp.exp(-0.5 * pre * pre) * 0.3989422804014327
    slope_ref[...] = (below + pre * bell).astype(slope_ref.dtype)


def down_kernel(places, left_ref, own_ref, *refs):
    part_refs, (out_ref, full_ref) = refs[:-2], refs[-2:]

    @pl.when(pl.program_id(0) == 0)
    def _():
        fill_rows(places, own_ref, part_refs, full_ref)

    out_ref[...] = rows_by_rows(left_ref[...], full_ref[...]).astype(out_ref.dtype)


def gathered_layer(kernel, name, block, places, left, vectors, own, parts, widths, fsdp):
    length = left.shape[0]
    full = (fsdp * own.shape[0], own.shape[1])
    whole = lambda shape: pl.BlockSpec(shape, lambda step, places: (0, 0))
    by_block = lambda width: pl.BlockSpec((block, width), lambda step, places: (step, 0))
    return pl.pallas_call(
        kernel,
        grid_spec=pltpu.PrefetchScalarGridSpec(
            num_scalar_prefetch=1,
            grid=(length // block,),
            in_specs=[by_block(left.shape[1])]
            + [whole(item.shape) for item in vectors + [own] + parts],
            out_specs=[by_block(width) for width in widths] + [whole(full)],
        ),
        out_shape=[jax.ShapeDtypeStruct((length, width), jnp.bfloat16) for width in widths]
        + [jax.ShapeDtypeStruct(full, jnp.bfloat16)],
        name=name,
        compiler_params=pltpu.CompilerParams(vmem_limit_bytes=20 << 20),
    )(places, left, *vectors, own, *parts)


def stack_kernel(*refs):
    row = 0
    for ref in refs[:-1]:
        refs[-1][row : row + ref.shape[0], :] = ref[...]
        row += ref.shape[0]


def stack_rows(pieces):
    rows = sum(item.shape[0] for item in pieces)
    return pl.pallas_call(
        stack_kernel,
        out_shape=jax.ShapeDtypeStruct((rows, pieces[0].shape[1]), pieces[0].dtype),
        name="stack_rows",
        compiler_params=pltpu.CompilerParams(vmem_limit_bytes=4 << 20),
    )(*pieces)


def swap(values, axis, step):
    pairs = [(place, place ^ step) for place in range(lax.axis_size(axis))]
    return lax.ppermute(values, axis, pairs)


def swap_all(values, axis):
    return [swap(values, axis, step) for step in range(1, lax.axis_size(axis))]


def relay_all(values, axis):
    if lax.axis_size(axis) != 4:
        return swap_all(values, axis)
    first, second = swap(values, axis, 1), swap(values, axis, 2)
    return [first, second, swap(first, axis, 2)]


def swap_each(pieces, axis):
    return [swap(pieces[step], axis, step) for step in range(1, len(pieces))]


def together(*values):
    return lax.optimization_barrier(values)


def wide(values):
    return values.astype(jnp.float32)


def low(values):
    return values.astype(jnp.bfloat16)


def add_partner(values):
    mine = low(values)
    return wide(mine) + wide(swap(mine, "tp", 1))


def add_up(pieces):
    pieces = [wide(item) for item in pieces]
    while len(pieces) > 1:
        pieces = [pieces[i] + pieces[i + 1] for i in range(0, len(pieces), 2)]
    return pieces[0]


def sum_over(values, axis):
    step = 1
    while step < lax.axis_size(axis):
        values = values + swap(values, axis, step)
        step *= 2
    return values


def deal(pieces, axis):
    return lax.all_to_all(pieces, axis, 0, 0)


def own_half(blocks):
    rows = blocks.shape[1] // 2
    return lax.dynamic_slice_in_dim(blocks, lax.axis_index("tp") * rows, rows, 1)


def row_kernel_stats(stats_ref, step, rows):
    @pl.when(step == 0)
    def _():
        stats_ref[...] = jnp.zeros_like(stats_ref)

    for index, row in enumerate(rows):
        stats_ref[index : index + 1, :] += jnp.sum(row, axis=0, keepdims=True)


def normalize(values):
    mean = jnp.mean(values, axis=-1, keepdims=True)
    centered = values - mean
    scale = lax.rsqrt(jnp.mean(centered * centered, axis=-1, keepdims=True) + NORM_EPS)
    return centered * scale, scale


def normalize_back(grads, normal, scale, gain):
    pushed = grads * gain
    mean = jnp.mean(pushed, axis=-1, keepdims=True)
    along = jnp.mean(pushed * normal, axis=-1, keepdims=True)
    return (pushed - mean - normal * along) * scale


def first_norm_kernel(
    hidden_ref, mine_ref, other_ref, bias_ref, gain_ref, shift_ref, normal_ref, scale_ref, low_ref
):
    branch = mine_ref[...].astype(jnp.float32) + other_ref[...].astype(jnp.float32)
    normal, scale = normalize(hidden_ref[...].astype(jnp.float32) + branch + bias_ref[...])
    normal_ref[...] = normal
    scale_ref[...] = scale
    low_ref[...] = (normal * gain_ref[...] + shift_ref[...]).astype(low_ref.dtype)


def second_norm_kernel(
    facts,
    normal_ref,
    gain1_ref,
    shift1_ref,
    mine_ref,
    other_ref,
    bias_ref,
    gain_ref,
    shift_ref,
    own_teacher_ref,
    other_teacher_ref,
    half_ref,
    grad_ref,
    low_ref,
    stats_ref,
):
    step = pl.program_id(0)
    block = normal_ref.shape[0]
    rows = block // 2
    branch = mine_ref[...].astype(jnp.float32) + other_ref[...].astype(jnp.float32)
    normed1 = normal_ref[...] * gain1_ref[...] + shift1_ref[...]
    normal, scale = normalize(normed1 + branch + bias_ref[...])
    output = normal * gain_ref[...] + shift_ref[...]
    first = facts[1] == 0
    half_ref[0] = jnp.where(first, output[:rows], output[rows:]).astype(half_ref.dtype)
    own, other = own_teacher_ref[0], other_teacher_ref[0]
    own, other = own.astype(jnp.float32), other.astype(jnp.float32)
    teacher = jnp.concatenate(
        [jnp.where(first, own, other), jnp.where(first, other, own)], axis=0
    )
    position = step * block + lax.broadcasted_iota(jnp.int32, (block, 1), 0)
    residue = jnp.where(position < facts[0], output - teacher, 0.0)
    grads = normalize_back(residue, normal, scale, gain_ref[...])
    grad_ref[...] = grads
    low_ref[...] = grads.astype(low_ref.dtype)
    row_kernel_stats(stats_ref, step, [grads, residue * normal, residue, residue * residue])


def first_norm_back_kernel(
    facts,
    grad_ref,
    mine_ref,
    other_ref,
    normal_ref,
    scale_ref,
    gain_ref,
    low_ref,
    half_ref,
    stats_ref,
):
    rows = grad_ref.shape[0] // 2
    branch = mine_ref[...].astype(jnp.float32) + other_ref[...].astype(jnp.float32)
    pushed = grad_ref[...] + branch
    normal = normal_ref[...]
    grads = normalize_back(pushed, normal, scale_ref[...], gain_ref[...])
    low_ref[...] = grads.astype(low_ref.dtype)
    half_ref[0] = jnp.where(facts[1] == 0, grads[:rows], grads[rows:])
    row_kernel_stats(stats_ref, pl.program_id(0), [grads, pushed * normal, pushed])


def by_rows(kernel, name, block, operands, results, facts=None, stats=0):
    def spec(shape, dealt=False):
        if dealt:
            return pl.BlockSpec((1,) + shape[1:], lambda step, facts: (step ^ facts[2], 0, 0))
        if shape[0] == 1:
            return pl.BlockSpec(shape, lambda step, *_: (0, 0))
        return pl.BlockSpec((block, shape[1]), lambda step, *_: (step, 0))

    length = next(item.shape[0] for item in operands if item.ndim == 2 and item.shape[0] > 1)
    out_specs = [spec(item.shape, item.ndim == 3) for item in results]
    if stats:
        results = results + [jax.ShapeDtypeStruct((8, stats), jnp.float32)]
        out_specs.append(pl.BlockSpec((8, stats), lambda step, *_: (0, 0)))
    return pl.pallas_call(
        kernel,
        grid_spec=pltpu.PrefetchScalarGridSpec(
            num_scalar_prefetch=0 if facts is None else 1,
            grid=(length // block,),
            in_specs=[spec(item.shape, item.ndim == 3) for item in operands],
            out_specs=out_specs,
        ),
        out_shape=results,
        name=name,
        compiler_params=pltpu.CompilerParams(vmem_limit_bytes=20 << 20),
    )(*([] if facts is None else [facts]), *operands)


def grad_pre_kernel(low_ref, weight_ref, slope_ref, out_ref, stats_ref):
    grads = plain_dot(low_ref[...], weight_ref[...]) * slope_ref[...].astype(jnp.float32)
    grads = grads.astype(out_ref.dtype)
    out_ref[...] = grads
    row_kernel_stats(stats_ref, pl.program_id(0), [grads.astype(jnp.float32)])


def wide_layer(kernel, name, block, low, weight, operands, count, stats=0):
    length, width = low.shape[0], weight.shape[1]

    def spec(shape):
        if shape[0] == 1:
            return pl.BlockSpec(shape, lambda step: (0, 0))
        return pl.BlockSpec((block, shape[1]), lambda step: (step, 0))

    out_specs = [pl.BlockSpec((block, width), lambda step: (step, 0))] * count
    out_shape = [jax.ShapeDtypeStruct((length, width), jnp.bfloat16)] * count
    if stats:
        out_specs = out_specs + [pl.BlockSpec((8, width), lambda step: (0, 0))]
        out_shape = out_shape + [jax.ShapeDtypeStruct((8, width), jnp.float32)]
    return pl.pallas_call(
        kernel,
        grid=(length // block,),
        in_specs=[spec(low.shape), pl.BlockSpec(weight.shape, lambda step: (0, 0))]
        + [spec(item.shape) for item in operands],
        out_specs=out_specs,
        out_shape=out_shape,
        name=name,
        compiler_params=pltpu.CompilerParams(vmem_limit_bytes=20 << 20),
    )(low, weight, *operands)


def rows_kernel(left_ref, right_ref, out_ref, *, transposed):
    product = (rows_by_rows if transposed else plain_dot)(left_ref[...], right_ref[...])
    out_ref[...] = product.astype(out_ref.dtype)


def rows_times(left, right, block, transposed):
    length, depth = left.shape
    width = right.shape[0] if transposed else right.shape[1]
    return pl.pallas_call(
        lambda *refs: rows_kernel(*refs, transposed=transposed),
        grid=(length // block,),
        in_specs=[
            pl.BlockSpec((block, depth), lambda step: (step, 0)),
            pl.BlockSpec(right.shape, lambda step: (0, 0)),
        ],
        out_specs=pl.BlockSpec((block, width), lambda step: (step, 0)),
        out_shape=jax.ShapeDtypeStruct((length, width), jnp.bfloat16),
        name="rows_times",
        compiler_params=pltpu.CompilerParams(vmem_limit_bytes=14 << 20),
    )(left, right)


def pick_kernel(seat, in_ref, out_ref):
    out_ref[...] = in_ref[...]


def pick_halves(seat, blocks):
    count, rows, width = blocks.shape
    half = (1, rows // 2, width)
    return pl.pallas_call(
        pick_kernel,
        grid_spec=pltpu.PrefetchScalarGridSpec(
            num_scalar_prefetch=1,
            grid=(count,),
            in_specs=[pl.BlockSpec(half, lambda step, seat: (step ^ seat[1], seat[0], 0))],
            out_specs=pl.BlockSpec(half, lambda step, seat: (step, 0, 0)),
        ),
        out_shape=jax.ShapeDtypeStruct((count,) + half[1:], blocks.dtype),
        name="pick_halves",
        compiler_params=pltpu.CompilerParams(vmem_limit_bytes=4 << 20),
    )(seat, blocks)


def input_back_kernel(facts, grad_ref, weight_ref, mine_ref, other_ref):
    total = rows_by_rows(grad_ref[...], weight_ref[...]).astype(mine_ref.dtype)
    rows = mine_ref.shape[1]
    first = facts[1] == 0
    mine_ref[0] = jnp.where(first, total[:rows], total[rows:])
    other_ref[0] = jnp.where(first, total[rows:], total[:rows])


def input_back(facts, grads, weight, block):
    length, width = grads.shape
    half = (1, block // 2, weight.shape[0])
    return pl.pallas_call(
        input_back_kernel,
        grid_spec=pltpu.PrefetchScalarGridSpec(
            num_scalar_prefetch=1,
            grid=(length // block,),
            in_specs=[
                pl.BlockSpec((block, width), lambda step, facts: (step, 0)),
                pl.BlockSpec((weight.shape[0], width), lambda step, facts: (0, 0)),
            ],
            out_specs=[pl.BlockSpec(half, lambda step, facts: (step ^ facts[2], 0, 0))] * 2,
        ),
        out_shape=[jax.ShapeDtypeStruct((length // block,) + half[1:], jnp.bfloat16)] * 2,
        name="input_back",
        compiler_params=pltpu.CompilerParams(vmem_limit_bytes=10 << 20),
    )(facts, grads, weight)


def pack_kernel(second_ref, first_ref, up_ref, qkv_ref, count_ref, out_ref):
    width = out_ref.shape[1]
    out_ref[...] = jnp.zeros_like(out_ref)
    out_ref[0:4, :] = second_ref[0:4, :]
    out_ref[4:7, :] = first_ref[0:3, :]
    row = 7
    for ref in (up_ref, qkv_ref, count_ref):
        for start in range(0, ref.shape[1], width):
            span = min(width, ref.shape[1] - start)
            out_ref[row : row + 1, :span] = ref[0:1, start : start + span]
            row += 1


def pack(second, first, up, qkv, count):
    width = second.shape[1]
    rows = 7 + sum(-(-item.shape[1] // width) for item in (up, qkv, count))
    return pl.pallas_call(
        pack_kernel,
        out_shape=jax.ShapeDtypeStruct((-(-rows // 8) * 8, width), jnp.float32),
        name="pack",
        compiler_params=pltpu.CompilerParams(vmem_limit_bytes=2 << 20),
    )(second, first, up, qkv, count)


def join_kernel(facts, ratio_ref, own_ref, other_ref, out_ref):
    rows = own_ref.shape[1]
    for ref, half in ((own_ref, facts[0]), (other_ref, 1 - facts[0])):
        values = ref[0].astype(jnp.float32) * ratio_ref[0]
        out_ref[0, pl.ds(pl.multiple_of(half * rows, rows), rows), :] = values.astype(out_ref.dtype)


def join_halves(seat, half, ratio=None, dtype=jnp.bfloat16):
    count, rows, width = half.shape
    ratio = jnp.ones((1,), jnp.float32) if ratio is None else ratio.reshape(1)
    return pl.pallas_call(
        join_kernel,
        grid_spec=pltpu.PrefetchScalarGridSpec(
            num_scalar_prefetch=1,
            grid=(count,),
            in_specs=[pl.BlockSpec(memory_space=pltpu.SMEM)]
            + [pl.BlockSpec((1, rows, width), lambda step, facts: (step, 0, 0))] * 2,
            out_specs=pl.BlockSpec(
                (1, 2 * rows, width), lambda step, facts: (step ^ facts[1], 0, 0)
            ),
        ),
        out_shape=jax.ShapeDtypeStruct((count, 2 * rows, width), dtype),
        name="join_halves",
        compiler_params=pltpu.CompilerParams(vmem_limit_bytes=4 << 20),
    )(seat, ratio, half, swap(half, "tp", 1))


def weight_grad_kernel(places, *refs, chunks, fsdp, count, order):
    kinds = len(chunks)
    left_refs, right_refs = refs[:kinds], refs[kinds : 2 * kinds]
    out_refs, held = refs[2 * kinds : -1], refs[-1]
    step = pl.program_id(0)
    first = 0
    for left_ref, right_ref, chunk in zip(left_refs, right_refs, chunks):

        @pl.when(jnp.logical_and(step >= first, step < first + chunk))
        def _():
            total = lax.dot_general(
                left_ref[...],
                right_ref[...],
                (((0,), (0,)), ((), ())),
                preferred_element_type=jnp.float32,
            )
            held[...] = total.astype(held.dtype)

        first += chunk
    rows = held.shape[0] // (fsdp * count)
    if order == "fsdp":
        own = rows * count
        for half in range(2):
            for index in range(fsdp // 2):
                start = lax.bitwise_xor(places[1], jnp.int32(half + 2 * index)) * own
                out_refs[half][index * own : (index + 1) * own, :] = held[
                    pl.ds(pl.multiple_of(start, own), own), :
                ]
    else:
        steps = list(range(0, fsdp, 2)) + list(range(1, fsdp, 2))
        for s in range(count):
            for index, d in enumerate(steps):
                start = lax.bitwise_xor(places[1], jnp.int32(d)) * (rows * count)
                start = start + lax.bitwise_xor(places[0], jnp.int32(s)) * rows
                out_refs[s][index * rows : (index + 1) * rows, :] = held[
                    pl.ds(pl.multiple_of(start, rows), rows), :
                ]


def weight_grad(places, pairs, order="ctx"):
    fsdp, count = lax.axis_size("fsdp"), lax.axis_size("ctx")
    tokens, rows = pairs[0][0].shape
    columns = [right.shape[1] for _, right in pairs]
    width = max(
        item for item in range(LANES, 6 * LANES + 1, LANES) if not any(c % item for c in columns)
    )
    chunks = [item // width for item in columns]
    firsts = [sum(chunks[:index]) for index in range(len(chunks))]
    pieces = count if order == "ctx" else 2
    right_spec = lambda first, chunk: pl.BlockSpec(
        (tokens, width), lambda step, places: (0, jnp.clip(step - first, 0, chunk - 1))
    )
    return pl.pallas_call(
        lambda *refs: weight_grad_kernel(
            *refs, chunks=chunks, fsdp=fsdp, count=count, order=order
        ),
        grid_spec=pltpu.PrefetchScalarGridSpec(
            num_scalar_prefetch=1,
            grid=(sum(chunks),),
            in_specs=[pl.BlockSpec((tokens, rows), lambda step, places: (0, 0))] * len(pairs)
            + [right_spec(first, chunk) for first, chunk in zip(firsts, chunks)],
            out_specs=[pl.BlockSpec((rows // pieces, width), lambda step, places: (0, step))]
            * pieces,
            scratch_shapes=[pltpu.VMEM((rows, width), jnp.bfloat16)],
        ),
        out_shape=[jax.ShapeDtypeStruct((rows // pieces, sum(columns)), jnp.bfloat16)] * pieces,
        name="weight_grad",
        compiler_params=pltpu.CompilerParams(vmem_limit_bytes=14 << 20),
    )(places, *[left for left, _ in pairs], *[right for _, right in pairs])


def halve(kept, brought):
    rows = kept.shape[0] // 2
    return [
        low(wide(kept[cut]) + wide(brought[cut]))
        for cut in (slice(0, rows), slice(rows, 2 * rows))
    ]


def sum_kernel(*refs):
    part_refs, (kept_ref, sent_ref) = refs[:-2], refs[-2:]
    total = part_refs[0][...].astype(jnp.float32) + part_refs[1][...].astype(jnp.float32)
    for first, second in zip(part_refs[2::2], part_refs[3::2]):
        total = total + (first[...].astype(jnp.float32) + second[...].astype(jnp.float32))
    rows = kept_ref.shape[0]
    kept_ref[...] = total[:rows].astype(kept_ref.dtype)
    sent_ref[...] = total[rows:].astype(sent_ref.dtype)


def sum_and_cut(parts):
    rows, columns = parts[0].shape
    return pl.pallas_call(
        sum_kernel,
        out_shape=[jax.ShapeDtypeStruct((rows // 2, columns), jnp.bfloat16)] * 2,
        name="sum_and_cut",
        compiler_params=pltpu.CompilerParams(vmem_limit_bytes=8 << 20),
    )(*parts)


def join_rows_kernel(ratio_ref, *refs):
    out_ref, start = refs[-1], 0
    for first, second in zip(refs[0:-1:2], refs[1:-1:2]):
        total = first[...].astype(jnp.float32) + second[...].astype(jnp.float32)
        out_ref[start : start + first.shape[0], :] = total * ratio_ref[0]
        start += first.shape[0]


def join_rows(pairs, ratio):
    rows = sum(first.shape[0] for first, _ in pairs)
    operands = [item for pair in pairs for item in pair]
    vmem = pl.BlockSpec(memory_space=pltpu.VMEM)
    return pl.pallas_call(
        join_rows_kernel,
        in_specs=[pl.BlockSpec(memory_space=pltpu.SMEM)] + [vmem] * len(operands),
        out_specs=vmem,
        out_shape=jax.ShapeDtypeStruct((rows, operands[0].shape[1]), jnp.float32),
        name="join_rows",
        compiler_params=pltpu.CompilerParams(vmem_limit_bytes=8 << 20),
    )(ratio.reshape(1), *operands)


def place_kernel(places, ratio_ref, *refs, kinds):
    part_refs, out_ref = refs[:-1], refs[-1]
    rows, columns = part_refs[0].shape
    pairs = columns // (kinds * LANES)
    ratio = ratio_ref[0]
    for s in range(len(part_refs)):
        start = lax.bitwise_xor(places[0], jnp.int32(s)) * rows
        start = pl.multiple_of(start, rows)
        for kind in range(kinds):
            for pair in range(pairs):
                source = (pair * kinds + kind) * LANES
                target = (kind * pairs + pair) * LANES
                out_ref[pl.ds(start, rows), target : target + LANES] = (
                    part_refs[s][:, source : source + LANES].astype(jnp.float32) * ratio
                )


def place_rows(places, parts, ratio, kinds=1):
    rows, columns = parts[0].shape
    block = pl.BlockSpec((rows, columns), lambda step, places: (0, 0))
    return pl.pallas_call(
        lambda *refs: place_kernel(*refs, kinds=kinds),
        grid_spec=pltpu.PrefetchScalarGridSpec(
            num_scalar_prefetch=1,
            grid=(1,),
            in_specs=[pl.BlockSpec(memory_space=pltpu.SMEM)] + [block] * len(parts),
            out_specs=pl.BlockSpec((rows * len(parts), columns), lambda step, places: (0, 0)),
        ),
        out_shape=jax.ShapeDtypeStruct((rows * len(parts), columns), jnp.float32),
        name="place_rows",
        compiler_params=pltpu.CompilerParams(vmem_limit_bytes=6 << 20),
    )(places, ratio.reshape(1), *parts)


def whole_local(
    hidden_in,
    valid_mask,
    teacher,
    qkv_weight,
    qv_bias,
    out_weight,
    out_bias,
    norm1_gain,
    norm1_shift,
    up_weight,
    up_bias,
    down_weight,
    down_bias,
    norm2_gain,
    norm2_shift,
):
    seq_count, block_len, model_width = hidden_in.shape
    ctx_count = lax.axis_size("ctx")
    place, depth, core = lax.axis_index("ctx"), lax.axis_index("fsdp"), lax.axis_index("tp")
    inner_width = qkv_weight.shape[2]
    hidden_width = up_weight.shape[1]
    row_count = seq_count * block_len
    shape = hidden_in.shape
    places = jnp.stack([place, depth])
    seat = jnp.stack([core, place])
    lane = jnp.arange(LANES, dtype=jnp.int32)
    chosen = wide(lane == place)
    seat_rows = wide(jnp.where(lane == 0, seat[:, None], 0))
    fsdp_count = lax.axis_size("fsdp")
    row = lambda values: values.reshape(1, -1)
    struct = jax.ShapeDtypeStruct
    part_rows = qkv_weight.shape[0] // ctx_count
    own_part = lambda weight: lax.dynamic_slice_in_dim(weight, place * part_rows, part_rows, 0)
    qkv_out = jnp.concatenate([by_pairs(qkv_weight), out_weight], axis=1)
    local_counts = jnp.sum(wide(valid_mask), axis=1)
    hidden_own, weight_own = together(own_half(hidden_in), own_part(qkv_out))
    weight_rows = swap_all(weight_own, "fsdp")
    hidden_half = deal(hidden_own, "ctx")
    count_rows = jnp.broadcast_to(
        jnp.pad(low(local_counts), (0, qkv_out.shape[1] - seq_count)), (16, qkv_out.shape[1])
    )
    full_bias = row(by_pairs(jnp.stack([qv_bias[0], jnp.zeros_like(qv_bias[0]), qv_bias[1]])))
    teacher_own = pick_halves(seat, teacher)
    (
        places,
        seat,
        chosen,
        seat_rows,
        weight_rows,
        hidden_half,
        count_rows,
        up_own,
        down_own,
        teacher_own,
        full_bias,
    ) = together(
        places,
        seat,
        chosen,
        seat_rows,
        weight_rows,
        hidden_half,
        count_rows,
        own_part(up_weight),
        own_part(down_weight),
        teacher_own,
        full_bias,
    )
    weight_part = stack_rows(weight_rows + [count_rows])
    weight_parts = [weight_part] + swap_all(weight_part, "ctx")
    up_rows = relay_all(up_own, "fsdp")
    flat_in = join_halves(seat * jnp.array([1, 0], jnp.int32), hidden_half).reshape(row_count, model_width)
    weight_parts, flat_in, up_rows, down_own = together(
        weight_parts, flat_in, up_rows, down_own
    )
    up_part = stack_rows(up_rows)
    up_parts = [up_part] + swap_all(up_part, "ctx")
    down_rows = [swap(down_own, "fsdp", 1), swap(down_own, "fsdp", 2)]
    counts = sum(wide(item[-16, :LANES]) for item in weight_parts)
    facts = jnp.sum(jnp.concatenate([(counts * chosen)[None], seat_rows]), axis=1)
    facts = facts.astype(jnp.int32)
    projected, full_qkv_out = gathered_layer(
        project_kernel,
        "project",
        block_len,
        places,
        flat_in,
        [full_bias],
        qkv_out,
        weight_parts,
        [3 * inner_width],
        fsdp_count,
    )
    projected, down_first = together(projected, down_rows[0])
    down_rows = [down_first, down_rows[1], swap(down_first, "fsdp", 2)]
    full_out = full_qkv_out[:, 3 * inner_width :]
    attended, log_total = attend(facts, projected, block_len)
    attended, up_parts, down_rows = together(attended, up_parts, down_rows)
    down_part = stack_rows(down_rows)
    down_parts = [down_part] + swap_all(down_part, "ctx")
    branch = rows_times(attended, full_out, block_len, True)
    normal1, scale1, normed1_low = by_rows(
        first_norm_kernel,
        "first_norm",
        block_len,
        [flat_in, branch, swap(branch, "tp", 1), row(out_bias), row(norm1_gain), row(norm1_shift)],
        [
            struct((row_count, model_width), jnp.float32),
            struct((row_count, 1), jnp.float32),
            struct((row_count, model_width), jnp.bfloat16),
        ],
    )
    active, slope, full_up = gathered_layer(
        up_kernel,
        "up",
        block_len,
        places,
        normed1_low,
        [row(up_bias)],
        up_weight,
        up_parts,
        [hidden_width, hidden_width],
        fsdp_count,
    )
    active, down_parts = together(active, down_parts)
    teacher_pieces = [teacher_own[s] for s in range(ctx_count)]
    teacher_pieces = teacher_pieces[:1] + swap_each(teacher_pieces, "ctx")
    branch, full_down = gathered_layer(
        down_kernel,
        "down",
        block_len,
        places,
        active,
        [],
        down_weight,
        down_parts,
        [model_width],
        fsdp_count,
    )
    branch, teacher_pieces = together(branch, teacher_pieces)
    teacher_half = stack_rows(teacher_pieces).reshape(ctx_count, block_len // 2, model_width)
    layer_half, grad_resid2, grad_resid2_low, stats2 = by_rows(
        second_norm_kernel,
        "second_norm",
        block_len,
        [
            normal1,
            row(norm1_gain),
            row(norm1_shift),
            branch,
            swap(branch, "tp", 1),
            row(down_bias),
            row(norm2_gain),
            row(norm2_shift),
            teacher_half,
            swap(teacher_half, "tp", 1),
        ],
        [
            struct(teacher_half.shape, jnp.bfloat16),
            struct((row_count, model_width), jnp.float32),
            struct((row_count, model_width), jnp.bfloat16),
        ],
        facts=facts,
        stats=model_width,
    )
    down_kept, down_sent = weight_grad(places, [(grad_resid2_low, active)], "fsdp")
    down_kept, down_sent, grad_resid2_low = together(down_kept, down_sent, grad_resid2_low)
    down_brought = swap(down_sent, "fsdp", 1)
    layer_pieces = [layer_half[s] for s in range(ctx_count)]
    layer_pieces = layer_pieces[:1] + swap_each(layer_pieces, "ctx")
    grad_pre, stats_up = wide_layer(
        grad_pre_kernel, "grad_pre", block_len, grad_resid2_low, full_down, [slope], 1, hidden_width
    )
    branch = rows_times(grad_pre, full_up, block_len, True)
    branch, grad_pre, layer_pieces = together(branch, grad_pre, layer_pieces)
    layer_out = join_halves(seat, stack_rows(layer_pieces).reshape(layer_half.shape))
    up_pieces = weight_grad(places, [(normed1_low, grad_pre)])
    up_brought = swap_each(up_pieces, "ctx")
    grad_resid1_low, grad_half, stats1 = by_rows(
        first_norm_back_kernel,
        "first_norm_back",
        block_len,
        [grad_resid2, branch, swap(branch, "tp", 1), normal1, scale1, row(norm1_gain)],
        [
            struct((row_count, model_width), jnp.bfloat16),
            struct(layer_half.shape, jnp.float32),
        ],
        facts=facts,
        stats=model_width,
    )
    out_kept, out_sent = weight_grad(places, [(grad_resid1_low, attended)], "fsdp")
    grad_attended = rows_times(grad_resid1_low, full_out, block_len, False)
    out_kept, out_sent, grad_attended, layer_out = together(
        out_kept, out_sent, grad_attended, layer_out
    )
    out_brought = swap(out_sent, "fsdp", 1)
    grad_qkv, stats_qkv = attend_back(facts, projected, grad_attended, log_total, block_len)
    grad_qkv, down_brought, out_brought = together(grad_qkv, down_brought, out_brought)
    local_count = jnp.broadcast_to(jnp.sum(local_counts), (1, LANES))
    small = pack(stats2, stats1, stats_up, stats_qkv, local_count)
    small_other = swap(small, "ctx", 1)
    last_pieces = weight_grad(places, [(flat_in, grad_qkv)])
    down_kept, down_sent = sum_and_cut([down_kept, down_brought])
    out_kept, out_sent = sum_and_cut([out_kept, out_brought])
    last_pieces, grad_qkv, down_sent, out_sent, small_other = together(
        last_pieces, grad_qkv, down_sent, out_sent, small_other
    )
    last_brought = swap_each(last_pieces, "ctx")
    down_brought = swap(down_sent, "fsdp", 2)
    mine, other = input_back(facts, grad_qkv, full_qkv_out, block_len)
    up_kept, up_sent = sum_and_cut([up_pieces[0]] + up_brought)
    small = small + small_other
    small_other = swap(small, "ctx", 2)
    last_brought, mine, other, up_sent, out_sent, small, small_other = together(
        last_brought, mine, other, up_sent, out_sent, small, small_other
    )
    last_kept, last_sent = sum_and_cut([last_pieces[0]] + last_brought)
    last_sent, other, down_brought, up_sent, out_sent, small, small_other = together(
        last_sent, other, down_brought, up_sent, out_sent, small, small_other
    )
    last_brought = swap(last_sent, "fsdp", 1)
    other = swap(other, "tp", 1)
    cut = down_kept.shape[0] // 2
    owned_down = [
        low(wide(down_kept[span]) + wide(down_brought[span]))
        for span in (slice(0, cut), slice(cut, 2 * cut))
    ]
    down_other = [swap(owned_down[0], "ctx", 1), swap(owned_down[1], "ctx", 2)]
    small = small + small_other
    small_other = swap(small, "fsdp", 1)
    last_brought, other, up_sent, out_sent, small, small_other = together(
        last_brought, other, up_sent, out_sent, small, small_other
    )
    last_kept, last_sent = sum_and_cut([last_kept, last_brought])
    half = low(grad_half + (wide(mine) + wide(other)))
    small = small + small_other
    last_sent, half, up_sent, out_sent, small = together(
        last_sent, half, up_sent, out_sent, small
    )
    last_brought = swap(last_sent, "fsdp", 2)
    up_brought = swap(up_sent, "fsdp", 1)
    half_pieces = [half[s] for s in range(ctx_count)]
    half_brought = [half_pieces[0], swap(half_pieces[1], "ctx", 1)]
    small_other = swap(small, "fsdp", 2)
    out_brought = swap(out_sent, "fsdp", 2)
    last_brought, up_brought, down_other, out_brought, small_other, half_pieces = together(
        last_brought, up_brought, down_other, out_brought, small_other, half_pieces
    )
    part = low(wide(last_kept) + wide(last_brought))
    up_kept, up_sent = sum_and_cut([up_kept, up_brought])
    owned_down = [low(wide(mine) + wide(other)) for mine, other in zip(owned_down, down_other)]
    small = small + small_other
    part, up_sent, owned_down, out_brought, small, half_pieces = together(
        part, up_sent, owned_down, out_brought, small, half_pieces
    )
    shared = [part, swap(part, "ctx", 1), swap(part, "ctx", 2)]
    up_brought = swap(up_sent, "fsdp", 2)
    down_other = [swap(owned_down[0], "ctx", 2), swap(owned_down[1], "ctx", 1)]
    shared, up_brought, out_brought, half_pieces, down_other = together(
        shared, up_brought, out_brought, half_pieces, down_other
    )
    up_part = low(wide(up_kept) + wide(up_brought))
    owned_out = low(wide(out_kept) + wide(out_brought))
    up_part, owned_out, shared, half_pieces = together(up_part, owned_out, shared, half_pieces)
    shared = shared + [swap(shared[1], "ctx", 2)]
    up_shared = [up_part, swap(up_part, "ctx", 1), swap(up_part, "ctx", 2)]
    half_brought = half_brought + [swap(half_pieces[s], "ctx", s) for s in range(2, ctx_count)]
    up_shared, shared, half_brought, owned_out = together(
        up_shared, shared, half_brought, owned_out
    )
    up_shared = up_shared + [swap(up_shared[1], "ctx", 2)]
    input_half = stack_rows(half_brought).reshape(half.shape)
    out_other = swap(owned_out, "ctx", 1)
    owned_out, out_other, input_half, up_shared = together(
        owned_out, out_other, input_half, up_shared
    )
    owned_out = low(wide(owned_out) + wide(out_other))
    out_other = swap(owned_out, "ctx", 2)
    at = 7 + -(-hidden_width // model_width)
    last_row = at + -(-3 * inner_width // model_width)
    counted = small[last_row : last_row + 1, :1]
    ratio = float(row_count * ctx_count * fsdp_count) / counted
    loss = jnp.sum(small[3:4], axis=1, keepdims=True) / (counted * model_width)
    scaled = small * ratio
    input_grad = join_halves(seat, input_half, ratio, jnp.float32)
    owned_qkv = place_rows(places, shared, ratio, 3)
    owned_down = join_rows(list(zip(owned_down, down_other)), ratio)
    owned_up = place_rows(places, up_shared, ratio)
    owned_qkv, owned_up, owned_down, out_other, input_grad, scaled = together(
        owned_qkv, owned_up, owned_down, out_other, input_grad, scaled
    )
    owned_qkv = owned_qkv.reshape(qkv_weight.shape)
    owned_out = (wide(owned_out) + wide(out_other)) * ratio
    grad_up_bias = scaled[7:at].reshape(-1)[:hidden_width]
    grad_qv_bias = by_kinds(
        scaled[at : at + -(-3 * inner_width // model_width)].reshape(-1)[: 3 * inner_width]
    )[0::2]
    return (
        layer_out,
        input_grad,
        loss.reshape(()),
        owned_qkv,
        grad_qv_bias,
        owned_out,
        scaled[4],
        scaled[5],
        scaled[6],
        owned_up,
        grad_up_bias,
        owned_down,
        scaled[0],
        scaled[1],
        scaled[2],
    )


def spread_local(
    hidden_in,
    valid_mask,
    teacher,
    qkv_weight,
    qv_bias,
    out_weight,
    out_bias,
    norm1_gain,
    norm1_shift,
    up_weight,
    up_bias,
    down_weight,
    down_bias,
    norm2_gain,
    norm2_shift,
):
    seq_count, block_len, model_width = hidden_in.shape
    ctx_count = lax.axis_size("ctx")
    ctx_place = lax.axis_index("ctx")
    key_span = 2 * block_len
    seq_length = block_len * ctx_count
    row_count = seq_count * block_len
    scaling = HEAD_DIM ** (-0.5)
    full_qkv, full_out, full_up, full_down = (
        lax.all_gather(qkv_weight, "fsdp", axis=0, tiled=True),
        lax.all_gather(out_weight, "fsdp", axis=0, tiled=True),
        lax.all_gather(up_weight, "fsdp", axis=0, tiled=True),
        lax.all_gather(down_weight, "fsdp", axis=0, tiled=True),
    )
    inner_width = full_qkv.shape[2]
    head_count = inner_width // HEAD_DIM
    flat_in = hidden_in.reshape(row_count, model_width)
    full_bias = jnp.stack([qv_bias[0], jnp.zeros_like(qv_bias[0]), qv_bias[1]])
    projected = (
        jnp.einsum("td,dje->tje", flat_in, full_qkv, preferred_element_type=jnp.float32) + full_bias
    ).astype(jnp.bfloat16)
    queries = projected[:, 0].reshape(seq_count, block_len, inner_width)
    key_own = projected[:, 1].reshape(seq_count, block_len, inner_width)
    value_own = projected[:, 2].reshape(seq_count, block_len, inner_width)
    keep_own = valid_mask.astype(jnp.bfloat16)
    keys_all, values_all, keep_all = (
        lax.all_gather(key_own, "ctx", axis=1, tiled=True),
        lax.all_gather(value_own, "ctx", axis=1, tiled=True),
        lax.all_gather(keep_own, "ctx", axis=1, tiled=True),
    )
    query_heads = split_heads(queries)
    seen_limit = (ctx_place + 1) * block_len
    trip_count = ctx_place // 2 + 1
    offsets = jnp.arange(key_span, dtype=jnp.int32)

    def key_block(block_index):
        key_start = block_index * key_span
        key_heads = split_heads(lax.dynamic_slice_in_dim(keys_all, key_start, key_span, 1))
        value_heads = split_heads(lax.dynamic_slice_in_dim(values_all, key_start, key_span, 1))
        live_keys = lax.dynamic_slice_in_dim(keep_all, key_start, key_span, 1) > 0.5
        allowed = jnp.logical_and(live_keys, (key_start + offsets)[None, :] < seen_limit)
        return (key_heads, value_heads, allowed[:, None, None, :])

    def attend_step(block_index, carried):
        run_top, run_total, gathered = carried
        key_heads, value_heads, allowed = key_block(block_index)
        raw_scores = scores_of(query_heads, key_heads, allowed, scaling)
        new_top = jnp.maximum(run_top, jnp.max(raw_scores, axis=-1))
        shrink = jnp.exp(run_top - new_top)
        weights_now = jnp.exp(raw_scores - new_top[..., None])
        run_total = run_total * shrink + jnp.sum(weights_now, axis=-1)
        gathered = gathered * jnp.swapaxes(shrink, 1, 2)[..., None] + jnp.einsum(
            "shqk,skhd->sqhd",
            weights_now.astype(jnp.bfloat16),
            value_heads,
            preferred_element_type=jnp.float32,
        )
        return (new_top, run_total, gathered)

    start_top = jnp.full((seq_count, head_count, block_len), MASKED, jnp.float32)
    empty_heads = jnp.zeros((seq_count, block_len, head_count, HEAD_DIM), jnp.float32)
    run_top, run_total, gathered = lax.fori_loop(
        0, trip_count, attend_step, (start_top, jnp.zeros_like(start_top), empty_heads)
    )
    log_total = run_top + jnp.log(run_total)
    attended_exact = gathered / jnp.swapaxes(run_total, 1, 2)[..., None]
    attended = attended_exact.astype(jnp.bfloat16).reshape(row_count, inner_width)
    attn_branch = lax.psum(
        jnp.einsum("te,de->td", attended, full_out, preferred_element_type=jnp.float32).astype(
            jnp.bfloat16
        ),
        "tp",
    ).astype(jnp.float32)
    resid1 = flat_in.astype(jnp.float32) + attn_branch + out_bias
    normed1, norm1_back = jax.vjp(layer_norm, resid1, norm1_gain, norm1_shift)
    normed1_low = normed1.astype(jnp.bfloat16)
    pre_act = jnp.dot(normed1_low, full_up, preferred_element_type=jnp.float32) + up_bias
    active, gelu_back = jax.vjp(gelu_exact, pre_act)
    active = active.astype(jnp.bfloat16)
    ffn_branch = lax.psum(
        jnp.einsum("tf,df->td", active, full_down, preferred_element_type=jnp.float32).astype(
            jnp.bfloat16
        ),
        "tp",
    ).astype(jnp.float32)
    resid2 = normed1 + ffn_branch + down_bias
    output, norm2_back = jax.vjp(layer_norm, resid2, norm2_gain, norm2_shift)
    layer_out = output.astype(jnp.bfloat16).reshape(seq_count, block_len, model_width)
    keep_rows = valid_mask.reshape(row_count, 1).astype(jnp.float32)
    residue = (output - teacher.reshape(row_count, model_width).astype(jnp.float32)) * keep_rows
    squared = jnp.sum(residue * residue)
    counted = jnp.sum(keep_rows)
    grad_resid2, grad_gain2, grad_shift2 = norm2_back(residue)
    grad_down_bias = jnp.sum(grad_resid2, axis=0)
    grad_resid2_low = grad_resid2.astype(jnp.bfloat16)
    grad_active = jnp.dot(grad_resid2_low, full_down, preferred_element_type=jnp.float32)
    grad_down_weight = jnp.einsum(
        "td,tf->df", grad_resid2_low, active, preferred_element_type=jnp.float32
    )
    grad_pre = gelu_back(grad_active)[0].astype(jnp.bfloat16)
    grad_up_bias = jnp.sum(grad_pre.astype(jnp.float32), axis=0)
    grad_up_weight = jnp.einsum(
        "td,tf->df", normed1_low, grad_pre, preferred_element_type=jnp.float32
    )
    ffn_input_grad = lax.psum(
        jnp.einsum("tf,df->td", grad_pre, full_up, preferred_element_type=jnp.float32).astype(
            jnp.bfloat16
        ),
        "tp",
    ).astype(jnp.float32)
    grad_normed1 = grad_resid2 + ffn_input_grad
    grad_resid1, grad_gain1, grad_shift1 = norm1_back(grad_normed1)
    grad_out_bias = jnp.sum(grad_resid1, axis=0)
    grad_resid1_low = grad_resid1.astype(jnp.bfloat16)
    grad_mixed = jnp.dot(grad_resid1_low, full_out, preferred_element_type=jnp.float32)
    grad_out_weight = jnp.einsum(
        "td,te->de", grad_resid1_low, attended, preferred_element_type=jnp.float32
    )
    grad_attended = grad_mixed.astype(jnp.bfloat16).reshape(
        seq_count, block_len, head_count, HEAD_DIM
    )
    delta = jnp.swapaxes(jnp.sum(grad_attended.astype(jnp.float32) * attended_exact, axis=-1), 1, 2)

    def query_grads(block_index):
        key_heads, value_heads, allowed = key_block(block_index)
        prob_rows = jnp.exp(
            scores_of(query_heads, key_heads, allowed, scaling) - log_total[..., None]
        )
        push = jnp.einsum(
            "sqhd,skhd->shqk", grad_attended, value_heads, preferred_element_type=jnp.float32
        )
        slope = (prob_rows * (push - delta[..., None])).astype(jnp.bfloat16)
        grad_part = (
            jnp.einsum("shqk,skhd->sqhd", slope, key_heads, preferred_element_type=jnp.float32)
            * scaling
        )
        return (prob_rows, slope, grad_part)

    def back_step(block_index, carried):
        grad_query, spread = carried
        prob_rows, slope, grad_part = query_grads(block_index)
        grad_key = (
            jnp.einsum("shqk,sqhd->skhd", slope, query_heads, preferred_element_type=jnp.float32)
            * scaling
        )
        grad_value = jnp.einsum(
            "shqk,sqhd->skhd",
            prob_rows.astype(jnp.bfloat16),
            grad_attended,
            preferred_element_type=jnp.float32,
        )
        piece = jnp.stack(
            [
                grad_key.reshape(seq_count, key_span, inner_width),
                grad_value.reshape(seq_count, key_span, inner_width),
            ],
            axis=2,
        )
        spread = lax.dynamic_update_slice_in_dim(spread, piece, block_index * key_span, 1)
        return (grad_query + grad_part, spread)

    spread_start = jnp.zeros((seq_count, seq_length, 2, inner_width), jnp.float32)
    grad_query, spread = lax.fori_loop(0, trip_count, back_step, (empty_heads, spread_start))
    own_grads = lax.psum_scatter(
        spread.astype(jnp.bfloat16), "ctx", scatter_dimension=1, tiled=True
    ).astype(jnp.float32)
    grad_key_own = own_grads[:, :, 0]
    grad_value_own = own_grads[:, :, 1]
    grad_qkv = jnp.stack(
        [
            grad_query.reshape(row_count, inner_width),
            grad_key_own.reshape(row_count, inner_width),
            grad_value_own.reshape(row_count, inner_width),
        ],
        axis=1,
    ).astype(jnp.bfloat16)
    grad_qv_bias = jnp.sum(grad_qkv[:, 0::2].astype(jnp.float32), axis=0)
    grad_qkv_weight = jnp.einsum(
        "td,tje->dje", flat_in, grad_qkv, preferred_element_type=jnp.float32
    )
    input_part = lax.psum(
        jnp.einsum("tje,dje->td", grad_qkv, full_qkv, preferred_element_type=jnp.float32).astype(
            jnp.bfloat16
        ),
        "tp",
    ).astype(jnp.float32)
    grad_input = grad_resid1 + input_part
    vectors = jnp.stack(
        [grad_out_bias, grad_gain1, grad_shift1, grad_down_bias, grad_gain2, grad_shift2]
    )
    squared, counted, vectors, grad_qv_bias, grad_up_bias = lax.psum(
        (squared, counted, vectors, grad_qv_bias, grad_up_bias), ("fsdp", "ctx")
    )
    local_grads = (grad_qkv_weight, grad_out_weight, grad_up_weight, grad_down_weight)
    owned = (
        lax.psum_scatter(
            local_grads[0].astype(jnp.bfloat16), "fsdp", scatter_dimension=0, tiled=True
        ).astype(jnp.float32),
        lax.psum_scatter(
            local_grads[1].astype(jnp.bfloat16), "fsdp", scatter_dimension=0, tiled=True
        ).astype(jnp.float32),
        lax.psum_scatter(
            local_grads[2].astype(jnp.bfloat16), "fsdp", scatter_dimension=0, tiled=True
        ).astype(jnp.float32),
        lax.psum_scatter(
            local_grads[3].astype(jnp.bfloat16), "fsdp", scatter_dimension=0, tiled=True
        ).astype(jnp.float32),
    )
    owned = (
        lax.psum(owned[0].astype(jnp.bfloat16), "ctx").astype(jnp.float32),
        lax.psum(owned[1].astype(jnp.bfloat16), "ctx").astype(jnp.float32),
        lax.psum(owned[2].astype(jnp.bfloat16), "ctx").astype(jnp.float32),
        lax.psum(owned[3].astype(jnp.bfloat16), "ctx").astype(jnp.float32),
    )
    token_total = float(seq_count * seq_length * lax.axis_size("fsdp"))
    ratio = token_total / counted
    loss = squared / (counted * model_width)
    input_grad = (grad_input * ratio).reshape(seq_count, block_len, model_width)
    return (
        layer_out,
        input_grad,
        loss,
        owned[0] * ratio,
        grad_qv_bias * ratio,
        owned[1] * ratio,
        vectors[0] * ratio,
        vectors[1] * ratio,
        vectors[2] * ratio,
        owned[2] * ratio,
        grad_up_bias * ratio,
        owned[3] * ratio,
        vectors[3] * ratio,
        vectors[4] * ratio,
        vectors[5] * ratio,
    )


def local(hidden_in, *others):
    seq_count, block_len, model_width = hidden_in.shape
    ctx_count, fsdp_count = lax.axis_size("ctx"), lax.axis_size("fsdp")
    rows, inner_width = others[2].shape[0], others[2].shape[2]
    whole = (
        seq_count == ctx_count
        and ctx_count & (ctx_count - 1) == 0
        and fsdp_count == 4
        and lax.axis_size("tp") == 2
        and block_len % LANES == 0
        and others[5].shape[0] >= inner_width
        and inner_width % LANES == 0
        and rows % (16 * ctx_count) == 0
    )
    return (whole_local if whole else spread_local)(hidden_in, *others)


def solution(mesh):
    in_specs = (
        P("fsdp", "ctx", None),
        P("fsdp", "ctx"),
        P("fsdp", "ctx", None),
        P("fsdp", None, "tp"),
        P(None, "tp"),
        P("fsdp", "tp"),
        P(),
        P(),
        P(),
        P("fsdp", "tp"),
        P("tp"),
        P("fsdp", "tp"),
        P(),
        P(),
        P(),
    )
    out_specs = (
        P("fsdp", "ctx", None),
        P("fsdp", "ctx", None),
        P(),
        P("fsdp", None, "tp"),
        P(None, "tp"),
        P("fsdp", "tp"),
        P(),
        P(),
        P(),
        P("fsdp", "tp"),
        P("tp"),
        P("fsdp", "tp"),
        P(),
        P(),
        P(),
    )
    return jax.shard_map(local, mesh=mesh, in_specs=in_specs, out_specs=out_specs, check_vma=False)
```

```python
import jax
import jax.numpy as jnp
from jax import lax
from jax.experimental import pallas as pl
from jax.experimental.pallas import tpu as pltpu
from jax.sharding import PartitionSpec as P

HEAD_DIM = 64
NORM_EPS = 1e-05
MASKED = -1e30
LANES = 128


def layer_norm(values_in, gain_vec, shift_vec):
    row_mean = jnp.mean(values_in, axis=-1, keepdims=True)
    centered = values_in - row_mean
    row_var = jnp.mean(centered * centered, axis=-1, keepdims=True)
    return centered * lax.rsqrt(row_var + NORM_EPS) * gain_vec + shift_vec


def gelu_exact(pre_act):
    return jax.nn.gelu(pre_act, approximate=False)


def split_heads(packed):
    return packed.reshape(packed.shape[0], packed.shape[1], packed.shape[2] // HEAD_DIM, HEAD_DIM)


def scores_of(query_heads, key_heads, allowed, scaling):
    raw_scores = (
        jnp.einsum("sqhd,skhd->shqk", query_heads, key_heads, preferred_element_type=jnp.float32)
        * scaling
    )
    return jnp.where(allowed, raw_scores, MASKED)


def rows_by_rows(left, right):
    return lax.dot_general(left, right, (((1,), (1,)), ((), ())), preferred_element_type=jnp.float32)


def plain_dot(left, right):
    return jnp.dot(left, right, preferred_element_type=jnp.float32)


def lanes_of(head, lane):
    own = (lane < HEAD_DIM) if head == 0 else (lane >= HEAD_DIM)
    spare = HEAD_DIM if head == 0 else 0
    return own, lane == spare


def head_operands(query_ref, key_ref, slot, start, block, valid_count, head):
    lane = lax.broadcasted_iota(jnp.int32, (block, LANES), 1)
    own, spare = lanes_of(head, lane)
    position = start + lax.broadcasted_iota(jnp.int32, (block, LANES), 0)
    bias = jnp.where(position < valid_count, 0.0, MASKED)
    rows = pl.ds(slot * block, block)
    query = query_ref[rows, :].astype(jnp.float32) * (HEAD_DIM ** -0.5)
    key = key_ref[rows, :].astype(jnp.float32)
    query_side = jnp.where(spare, 1.0, query).astype(jnp.bfloat16)
    key_side = jnp.where(own, key, jnp.where(spare, bias, 0.0)).astype(jnp.bfloat16)
    return query_side, key_side


def attend_kernel(facts, query_ref, key_ref, value_ref, out_ref, log_ref, *, block):
    valid_count = facts[0]
    blocks = query_ref.shape[0] // block
    slots = list(range(blocks))
    value_t = [
        value_ref[pl.ds(slots[j] * block, block), :].astype(jnp.float32).T.astype(jnp.bfloat16)
        for j in range(blocks)
    ]
    outs = [[] for _ in range(blocks)]
    for head in range(2):
        sides = [
            head_operands(query_ref, key_ref, slots[j], j * block, block, valid_count, head)
            for j in range(blocks)
        ]
        span = slice(head * HEAD_DIM, (head + 1) * HEAD_DIM)
        for i in range(blocks):
            scores = [rows_by_rows(sides[j][1], sides[i][0]) for j in range(i + 1)]
            top = scores[0].max(axis=0, keepdims=True)
            for j in range(1, i + 1):
                top = jnp.maximum(top, scores[j].max(axis=0, keepdims=True))
            total = jnp.zeros_like(top)
            mixed = jnp.zeros((HEAD_DIM, block), jnp.float32)
            for j in range(i + 1):
                weight = jnp.exp(scores[j] - top)
                total = total + weight.sum(axis=0, keepdims=True)
                mixed = mixed + plain_dot(value_t[j][span, :], weight.astype(jnp.bfloat16))
            outs[i].append(mixed / total)
            log_ref[0, head : head + 1, i * block : (i + 1) * block] = top + jnp.log(total)
    for i in range(blocks):
        both = jnp.concatenate(outs[i], axis=0)
        out_ref[pl.ds(slots[i] * block, block), :] = both.T.astype(out_ref.dtype)


def attend_back_kernel(
    facts,
    query_ref,
    key_ref,
    value_ref,
    grad_ref,
    log_ref,
    out_ref,
    stats_ref,
    grad_key,
    grad_value,
    *,
    block,
):
    valid_count = facts[0]
    blocks = query_ref.shape[0] // block
    slots = list(range(blocks))
    scaling = HEAD_DIM ** -0.5
    lane = lax.broadcasted_iota(jnp.int32, (block, LANES), 1)
    key_t, grads, queries, values = [], [], [], []
    for j in range(blocks):
        rows = pl.ds(slots[j] * block, block)
        key_t.append((key_ref[rows, :].astype(jnp.float32) * scaling).T.astype(jnp.bfloat16))
        grads.append(grad_ref[rows, :])
        queries.append(query_ref[rows, :].astype(jnp.float32) * scaling)
        values.append(value_ref[rows, :].astype(jnp.float32))
    grad_queries = [[] for _ in range(blocks)]
    for head in range(2):
        own, _ = lanes_of(head, lane)
        span = slice(head * HEAD_DIM, (head + 1) * HEAD_DIM)
        sides = [
            head_operands(query_ref, key_ref, slots[j], j * block, block, valid_count, head)
            for j in range(blocks)
        ]
        head_values = [jnp.where(own, item, 0.0).astype(jnp.bfloat16) for item in values]
        for i in range(blocks):
            log_row = log_ref[0, head : head + 1, i * block : (i + 1) * block]
            head_grad = jnp.where(own, grads[i].astype(jnp.float32), 0.0).astype(jnp.bfloat16)
            head_query = jnp.where(own, queries[i], 0.0).astype(jnp.bfloat16)
            probs, pushes = [], []
            delta = jnp.zeros((1, block), jnp.float32)
            for j in range(i + 1):
                prob = jnp.exp(rows_by_rows(sides[j][1], sides[i][0]) - log_row)
                push = rows_by_rows(head_values[j], grads[i])
                delta = delta + (prob * push).sum(axis=0, keepdims=True)
                probs.append(prob)
                pushes.append(push)
            grad_query = jnp.zeros((HEAD_DIM, block), jnp.float32)
            for j in range(i + 1):
                slope = (probs[j] * (pushes[j] - delta)).astype(jnp.bfloat16)
                part_value = plain_dot(probs[j].astype(jnp.bfloat16), head_grad)
                part_key = plain_dot(slope, head_query)
                span_rows = slice(j * block, (j + 1) * block)
                if head == 0 and i == j:
                    grad_value[span_rows, :] = part_value
                    grad_key[span_rows, :] = part_key
                else:
                    grad_value[span_rows, :] += part_value
                    grad_key[span_rows, :] += part_key
                grad_query = grad_query + plain_dot(key_t[j][span, :], slope)
            grad_queries[i].append(grad_query)
    totals = jnp.zeros((1, 3 * LANES), jnp.float32)
    for i in range(blocks):
        rows = pl.ds(slots[i] * block, block)
        both = jnp.concatenate(grad_queries[i], axis=0)
        out_ref[rows, :LANES] = both.T.astype(out_ref.dtype)
        span_rows = slice(i * block, (i + 1) * block)
        out_ref[rows, LANES : 2 * LANES] = grad_key[span_rows, :].astype(out_ref.dtype)
        out_ref[rows, 2 * LANES :] = grad_value[span_rows, :].astype(out_ref.dtype)
        totals += jnp.sum(out_ref[rows, :].astype(jnp.float32), axis=0, keepdims=True)
    stats_ref[...] = jnp.broadcast_to(totals, stats_ref.shape)


def attend(facts, projected, block):
    length, width = projected.shape
    pairs = width // (3 * LANES)
    column = lambda kind: pl.BlockSpec((length, LANES), lambda pair, facts: (0, 3 * pair + kind))
    return pl.pallas_call(
        lambda *refs: attend_kernel(*refs, block=block),
        grid_spec=pltpu.PrefetchScalarGridSpec(
            num_scalar_prefetch=1,
            grid=(pairs,),
            in_specs=[column(0), column(1), column(2)],
            out_specs=[
                pl.BlockSpec((length, LANES), lambda pair, facts: (0, pair)),
                pl.BlockSpec((1, 2, length), lambda pair, facts: (pair, 0, 0)),
            ],
        ),
        out_shape=[
            jax.ShapeDtypeStruct((length, pairs * LANES), jnp.bfloat16),
            jax.ShapeDtypeStruct((pairs, 2, length), jnp.float32),
        ],
        name="attend",
        compiler_params=pltpu.CompilerParams(vmem_limit_bytes=9 << 20),
    )(facts, projected, projected, projected)


def attend_back(facts, projected, grad_attended, log_total, block):
    length, width = grad_attended.shape
    pairs = width // LANES
    column = lambda kind: pl.BlockSpec((length, LANES), lambda pair, facts: (0, 3 * pair + kind))
    return pl.pallas_call(
        lambda *refs: attend_back_kernel(*refs, block=block),
        grid_spec=pltpu.PrefetchScalarGridSpec(
            num_scalar_prefetch=1,
            grid=(pairs,),
            in_specs=[
                column(0),
                column(1),
                column(2),
                pl.BlockSpec((length, LANES), lambda pair, facts: (0, pair)),
                pl.BlockSpec((1, 2, length), lambda pair, facts: (pair, 0, 0)),
            ],
            out_specs=[
                pl.BlockSpec((length, 3 * LANES), lambda pair, facts: (0, pair)),
                pl.BlockSpec((8, 3 * LANES), lambda pair, facts: (0, pair)),
            ],
            scratch_shapes=[
                pltpu.VMEM((length, LANES), jnp.float32),
                pltpu.VMEM((length, LANES), jnp.float32),
            ],
        ),
        out_shape=[
            jax.ShapeDtypeStruct((length, 3 * width), jnp.bfloat16),
            jax.ShapeDtypeStruct((8, 3 * width), jnp.float32),
        ],
        name="attend_back",
        compiler_params=pltpu.CompilerParams(vmem_limit_bytes=12 << 20),
    )(facts, projected, projected, projected, grad_attended, log_total)


def by_pairs(values):
    kinds, width = values.shape[-2:]
    cut = values.reshape(values.shape[:-1] + (width // LANES, LANES))
    return jnp.swapaxes(cut, -3, -2).reshape(values.shape[:-2] + (kinds * width,))


def by_kinds(values, kinds=3):
    width = values.shape[-1] // kinds
    cut = values.reshape(values.shape[:-1] + (width // LANES, kinds, LANES))
    return jnp.swapaxes(cut, -3, -2).reshape(values.shape[:-1] + (kinds, width))


def fill_rows(places, own_ref, part_refs, out_ref):
    count = len(part_refs)
    rows = own_ref.shape[0] // count
    fsdp = out_ref.shape[0] // own_ref.shape[0]
    place, depth = places[0], places[1]
    start = pl.multiple_of(depth * (rows * count), rows)
    out_ref[pl.ds(start, rows * count), :] = own_ref[...]
    for s in range(count):
        for d in range(1, fsdp):
            start = lax.bitwise_xor(depth, jnp.int32(d)) * (rows * count)
            start = start + lax.bitwise_xor(place, jnp.int32(s)) * rows
            out_ref[pl.ds(pl.multiple_of(start, rows), rows), :] = part_refs[s][
                (d - 1) * rows : d * rows, :
            ]


def project_kernel(places, left_ref, bias_ref, own_ref, *refs):
    part_refs, (out_ref, full_ref) = refs[:-2], refs[-2:]

    @pl.when(pl.program_id(0) == 0)
    def _():
        fill_rows(places, own_ref, part_refs, full_ref)

    total = plain_dot(left_ref[...], full_ref[:, : out_ref.shape[1]]) + bias_ref[...]
    out_ref[...] = total.astype(out_ref.dtype)


def up_kernel(places, left_ref, bias_ref, own_ref, *refs):
    part_refs, (active_ref, slope_ref, full_ref) = refs[:-3], refs[-3:]

    @pl.when(pl.program_id(0) == 0)
    def _():
        fill_rows(places, own_ref, part_refs, full_ref)

    pre = plain_dot(left_ref[...], full_ref[...]) + bias_ref[...]
    below = 0.5 * (1.0 + lax.erf(pre * (0.5**0.5)))
    active_ref[...] = (pre * below).astype(active_ref.dtype)
    bell = jnp.exp(-0.5 * pre * pre) * 0.3989422804014327
    slope_ref[...] = (below + pre * bell).astype(slope_ref.dtype)


def down_kernel(places, left_ref, own_ref, *refs):
    part_refs, (out_ref, full_ref) = refs[:-2], refs[-2:]

    @pl.when(pl.program_id(0) == 0)
    def _():
        fill_rows(places, own_ref, part_refs, full_ref)

    out_ref[...] = rows_by_rows(left_ref[...], full_ref[...]).astype(out_ref.dtype)


def gathered_layer(kernel, name, block, places, left, vectors, own, parts, widths, fsdp):
    length = left.shape[0]
    full = (fsdp * own.shape[0], own.shape[1])
    whole = lambda shape: pl.BlockSpec(shape, lambda step, places: (0, 0))
    by_block = lambda width: pl.BlockSpec((block, width), lambda step, places: (step, 0))
    return pl.pallas_call(
        kernel,
        grid_spec=pltpu.PrefetchScalarGridSpec(
            num_scalar_prefetch=1,
            grid=(length // block,),
            in_specs=[by_block(left.shape[1])]
            + [whole(item.shape) for item in vectors + [own] + parts],
            out_specs=[by_block(width) for width in widths] + [whole(full)],
        ),
        out_shape=[jax.ShapeDtypeStruct((length, width), jnp.bfloat16) for width in widths]
        + [jax.ShapeDtypeStruct(full, jnp.bfloat16)],
        name=name,
        compiler_params=pltpu.CompilerParams(vmem_limit_bytes=20 << 20),
    )(places, left, *vectors, own, *parts)


def stack_kernel(*refs):
    row = 0
    for ref in refs[:-1]:
        refs[-1][row : row + ref.shape[0], :] = ref[...]
        row += ref.shape[0]


def stack_rows(pieces):
    rows = sum(item.shape[0] for item in pieces)
    return pl.pallas_call(
        stack_kernel,
        out_shape=jax.ShapeDtypeStruct((rows, pieces[0].shape[1]), pieces[0].dtype),
        name="stack_rows",
        compiler_params=pltpu.CompilerParams(vmem_limit_bytes=4 << 20),
    )(*pieces)


def swap(values, axis, step):
    pairs = [(place, place ^ step) for place in range(lax.axis_size(axis))]
    return lax.ppermute(values, axis, pairs)


def swap_all(values, axis):
    return [swap(values, axis, step) for step in range(1, lax.axis_size(axis))]


def relay_all(values, axis):
    if lax.axis_size(axis) != 4:
        return swap_all(values, axis)
    first, second = swap(values, axis, 1), swap(values, axis, 2)
    return [first, second, swap(first, axis, 2)]


def swap_each(pieces, axis):
    return [swap(pieces[step], axis, step) for step in range(1, len(pieces))]


def together(*values):
    return lax.optimization_barrier(values)


def wide(values):
    return values.astype(jnp.float32)


def low(values):
    return values.astype(jnp.bfloat16)


def add_partner(values):
    mine = low(values)
    return wide(mine) + wide(swap(mine, "tp", 1))


def add_up(pieces):
    pieces = [wide(item) for item in pieces]
    while len(pieces) > 1:
        pieces = [pieces[i] + pieces[i + 1] for i in range(0, len(pieces), 2)]
    return pieces[0]


def sum_over(values, axis):
    step = 1
    while step < lax.axis_size(axis):
        values = values + swap(values, axis, step)
        step *= 2
    return values


def deal(pieces, axis):
    return lax.all_to_all(pieces, axis, 0, 0)


def own_half(blocks):
    rows = blocks.shape[1] // 2
    return lax.dynamic_slice_in_dim(blocks, lax.axis_index("tp") * rows, rows, 1)


def row_kernel_stats(stats_ref, step, rows):
    @pl.when(step == 0)
    def _():
        stats_ref[...] = jnp.zeros_like(stats_ref)

    for index, row in enumerate(rows):
        stats_ref[index : index + 1, :] += jnp.sum(row, axis=0, keepdims=True)


def normalize(values):
    mean = jnp.mean(values, axis=-1, keepdims=True)
    centered = values - mean
    scale = lax.rsqrt(jnp.mean(centered * centered, axis=-1, keepdims=True) + NORM_EPS)
    return centered * scale, scale


def normalize_back(grads, normal, scale, gain):
    pushed = grads * gain
    mean = jnp.mean(pushed, axis=-1, keepdims=True)
    along = jnp.mean(pushed * normal, axis=-1, keepdims=True)
    return (pushed - mean - normal * along) * scale


def first_norm_kernel(
    hidden_ref, mine_ref, other_ref, bias_ref, gain_ref, shift_ref, normal_ref, scale_ref, low_ref
):
    branch = mine_ref[...].astype(jnp.float32) + other_ref[...].astype(jnp.float32)
    normal, scale = normalize(hidden_ref[...].astype(jnp.float32) + branch + bias_ref[...])
    normal_ref[...] = normal
    scale_ref[...] = scale
    low_ref[...] = (normal * gain_ref[...] + shift_ref[...]).astype(low_ref.dtype)


def second_norm_kernel(
    facts,
    normal_ref,
    gain1_ref,
    shift1_ref,
    mine_ref,
    other_ref,
    bias_ref,
    gain_ref,
    shift_ref,
    own_teacher_ref,
    other_teacher_ref,
    half_ref,
    grad_ref,
    low_ref,
    stats_ref,
):
    step = pl.program_id(0)
    block = normal_ref.shape[0]
    rows = block // 2
    branch = mine_ref[...].astype(jnp.float32) + other_ref[...].astype(jnp.float32)
    normed1 = normal_ref[...] * gain1_ref[...] + shift1_ref[...]
    normal, scale = normalize(normed1 + branch + bias_ref[...])
    output = normal * gain_ref[...] + shift_ref[...]
    first = facts[1] == 0
    half_ref[0] = jnp.where(first, output[:rows], output[rows:]).astype(half_ref.dtype)
    own, other = own_teacher_ref[0], other_teacher_ref[0]
    own, other = own.astype(jnp.float32), other.astype(jnp.float32)
    teacher = jnp.concatenate(
        [jnp.where(first, own, other), jnp.where(first, other, own)], axis=0
    )
    position = step * block + lax.broadcasted_iota(jnp.int32, (block, 1), 0)
    residue = jnp.where(position < facts[0], output - teacher, 0.0)
    grads = normalize_back(residue, normal, scale, gain_ref[...])
    grad_ref[...] = grads
    low_ref[...] = grads.astype(low_ref.dtype)
    row_kernel_stats(stats_ref, step, [grads, residue * normal, residue, residue * residue])


def first_norm_back_kernel(
    facts,
    grad_ref,
    mine_ref,
    other_ref,
    normal_ref,
    scale_ref,
    gain_ref,
    low_ref,
    half_ref,
    stats_ref,
):
    rows = grad_ref.shape[0] // 2
    branch = mine_ref[...].astype(jnp.float32) + other_ref[...].astype(jnp.float32)
    pushed = grad_ref[...] + branch
    normal = normal_ref[...]
    grads = normalize_back(pushed, normal, scale_ref[...], gain_ref[...])
    low_ref[...] = grads.astype(low_ref.dtype)
    half_ref[0] = jnp.where(facts[1] == 0, grads[:rows], grads[rows:])
    row_kernel_stats(stats_ref, pl.program_id(0), [grads, pushed * normal, pushed])


def by_rows(kernel, name, block, operands, results, facts=None, stats=0):
    def spec(shape, dealt=False):
        if dealt:
            return pl.BlockSpec((1,) + shape[1:], lambda step, facts: (step ^ facts[2], 0, 0))
        if shape[0] == 1:
            return pl.BlockSpec(shape, lambda step, *_: (0, 0))
        return pl.BlockSpec((block, shape[1]), lambda step, *_: (step, 0))

    length = next(item.shape[0] for item in operands if item.ndim == 2 and item.shape[0] > 1)
    out_specs = [spec(item.shape, item.ndim == 3) for item in results]
    if stats:
        results = results + [jax.ShapeDtypeStruct((8, stats), jnp.float32)]
        out_specs.append(pl.BlockSpec((8, stats), lambda step, *_: (0, 0)))
    return pl.pallas_call(
        kernel,
        grid_spec=pltpu.PrefetchScalarGridSpec(
            num_scalar_prefetch=0 if facts is None else 1,
            grid=(length // block,),
            in_specs=[spec(item.shape, item.ndim == 3) for item in operands],
            out_specs=out_specs,
        ),
        out_shape=results,
        name=name,
        compiler_params=pltpu.CompilerParams(vmem_limit_bytes=20 << 20),
    )(*([] if facts is None else [facts]), *operands)


def grad_pre_kernel(low_ref, weight_ref, slope_ref, out_ref, stats_ref):
    grads = plain_dot(low_ref[...], weight_ref[...]) * slope_ref[...].astype(jnp.float32)
    grads = grads.astype(out_ref.dtype)
    out_ref[...] = grads
    row_kernel_stats(stats_ref, pl.program_id(0), [grads.astype(jnp.float32)])


def wide_layer(kernel, name, block, low, weight, operands, count, stats=0):
    length, width = low.shape[0], weight.shape[1]

    def spec(shape):
        if shape[0] == 1:
            return pl.BlockSpec(shape, lambda step: (0, 0))
        return pl.BlockSpec((block, shape[1]), lambda step: (step, 0))

    out_specs = [pl.BlockSpec((block, width), lambda step: (step, 0))] * count
    out_shape = [jax.ShapeDtypeStruct((length, width), jnp.bfloat16)] * count
    if stats:
        out_specs = out_specs + [pl.BlockSpec((8, width), lambda step: (0, 0))]
        out_shape = out_shape + [jax.ShapeDtypeStruct((8, width), jnp.float32)]
    return pl.pallas_call(
        kernel,
        grid=(length // block,),
        in_specs=[spec(low.shape), pl.BlockSpec(weight.shape, lambda step: (0, 0))]
        + [spec(item.shape) for item in operands],
        out_specs=out_specs,
        out_shape=out_shape,
        name=name,
        compiler_params=pltpu.CompilerParams(vmem_limit_bytes=20 << 20),
    )(low, weight, *operands)


def rows_kernel(left_ref, right_ref, out_ref, *, transposed):
    product = (rows_by_rows if transposed else plain_dot)(left_ref[...], right_ref[...])
    out_ref[...] = product.astype(out_ref.dtype)


def rows_times(left, right, block, transposed):
    length, depth = left.shape
    width = right.shape[0] if transposed else right.shape[1]
    return pl.pallas_call(
        lambda *refs: rows_kernel(*refs, transposed=transposed),
        grid=(length // block,),
        in_specs=[
            pl.BlockSpec((block, depth), lambda step: (step, 0)),
            pl.BlockSpec(right.shape, lambda step: (0, 0)),
        ],
        out_specs=pl.BlockSpec((block, width), lambda step: (step, 0)),
        out_shape=jax.ShapeDtypeStruct((length, width), jnp.bfloat16),
        name="rows_times",
        compiler_params=pltpu.CompilerParams(vmem_limit_bytes=14 << 20),
    )(left, right)


def pick_kernel(seat, in_ref, out_ref):
    out_ref[...] = in_ref[...]


def pick_halves(seat, blocks):
    count, rows, width = blocks.shape
    half = (1, rows // 2, width)
    return pl.pallas_call(
        pick_kernel,
        grid_spec=pltpu.PrefetchScalarGridSpec(
            num_scalar_prefetch=1,
            grid=(count,),
            in_specs=[pl.BlockSpec(half, lambda step, seat: (step ^ seat[1], seat[0], 0))],
            out_specs=pl.BlockSpec(half, lambda step, seat: (step, 0, 0)),
        ),
        out_shape=jax.ShapeDtypeStruct((count,) + half[1:], blocks.dtype),
        name="pick_halves",
        compiler_params=pltpu.CompilerParams(vmem_limit_bytes=4 << 20),
    )(seat, blocks)


def input_back_kernel(facts, grad_ref, weight_ref, mine_ref, other_ref):
    total = rows_by_rows(grad_ref[...], weight_ref[...]).astype(mine_ref.dtype)
    rows = mine_ref.shape[1]
    first = facts[1] == 0
    mine_ref[0] = jnp.where(first, total[:rows], total[rows:])
    other_ref[0] = jnp.where(first, total[rows:], total[:rows])


def input_back(facts, grads, weight, block):
    length, width = grads.shape
    half = (1, block // 2, weight.shape[0])
    return pl.pallas_call(
        input_back_kernel,
        grid_spec=pltpu.PrefetchScalarGridSpec(
            num_scalar_prefetch=1,
            grid=(length // block,),
            in_specs=[
                pl.BlockSpec((block, width), lambda step, facts: (step, 0)),
                pl.BlockSpec((weight.shape[0], width), lambda step, facts: (0, 0)),
            ],
            out_specs=[pl.BlockSpec(half, lambda step, facts: (step ^ facts[2], 0, 0))] * 2,
        ),
        out_shape=[jax.ShapeDtypeStruct((length // block,) + half[1:], jnp.bfloat16)] * 2,
        name="input_back",
        compiler_params=pltpu.CompilerParams(vmem_limit_bytes=10 << 20),
    )(facts, grads, weight)


def pack_kernel(second_ref, first_ref, up_ref, qkv_ref, count_ref, out_ref):
    width = out_ref.shape[1]
    out_ref[...] = jnp.zeros_like(out_ref)
    out_ref[0:4, :] = second_ref[0:4, :]
    out_ref[4:7, :] = first_ref[0:3, :]
    row = 7
    for ref in (up_ref, qkv_ref, count_ref):
        for start in range(0, ref.shape[1], width):
            span = min(width, ref.shape[1] - start)
            out_ref[row : row + 1, :span] = ref[0:1, start : start + span]
            row += 1


def pack(second, first, up, qkv, count):
    width = second.shape[1]
    rows = 7 + sum(-(-item.shape[1] // width) for item in (up, qkv, count))
    return pl.pallas_call(
        pack_kernel,
        out_shape=jax.ShapeDtypeStruct((-(-rows // 8) * 8, width), jnp.float32),
        name="pack",
        compiler_params=pltpu.CompilerParams(vmem_limit_bytes=2 << 20),
    )(second, first, up, qkv, count)


def join_kernel(facts, ratio_ref, own_ref, other_ref, out_ref):
    rows = own_ref.shape[1]
    for ref, half in ((own_ref, facts[0]), (other_ref, 1 - facts[0])):
        values = ref[0].astype(jnp.float32) * ratio_ref[0]
        out_ref[0, pl.ds(pl.multiple_of(half * rows, rows), rows), :] = values.astype(out_ref.dtype)


def join_halves(seat, half, ratio=None, dtype=jnp.bfloat16):
    count, rows, width = half.shape
    ratio = jnp.ones((1,), jnp.float32) if ratio is None else ratio.reshape(1)
    return pl.pallas_call(
        join_kernel,
        grid_spec=pltpu.PrefetchScalarGridSpec(
            num_scalar_prefetch=1,
            grid=(count,),
            in_specs=[pl.BlockSpec(memory_space=pltpu.SMEM)]
            + [pl.BlockSpec((1, rows, width), lambda step, facts: (step, 0, 0))] * 2,
            out_specs=pl.BlockSpec(
                (1, 2 * rows, width), lambda step, facts: (step ^ facts[1], 0, 0)
            ),
        ),
        out_shape=jax.ShapeDtypeStruct((count, 2 * rows, width), dtype),
        name="join_halves",
        compiler_params=pltpu.CompilerParams(vmem_limit_bytes=4 << 20),
    )(seat, ratio, half, swap(half, "tp", 1))


def weight_grad_kernel(places, *refs, chunks, fsdp, count, order):
    kinds = len(chunks)
    left_refs, right_refs = refs[:kinds], refs[kinds : 2 * kinds]
    out_refs, held = refs[2 * kinds : -1], refs[-1]
    step = pl.program_id(0)
    first = 0
    for left_ref, right_ref, chunk in zip(left_refs, right_refs, chunks):

        @pl.when(jnp.logical_and(step >= first, step < first + chunk))
        def _():
            total = lax.dot_general(
                left_ref[...],
                right_ref[...],
                (((0,), (0,)), ((), ())),
                preferred_element_type=jnp.float32,
            )
            held[...] = total.astype(held.dtype)

        first += chunk
    rows = held.shape[0] // (fsdp * count)
    if order == "fsdp":
        own = rows * count
        for half in range(2):
            for index in range(fsdp // 2):
                start = lax.bitwise_xor(places[1], jnp.int32(half + 2 * index)) * own
                out_refs[half][index * own : (index + 1) * own, :] = held[
                    pl.ds(pl.multiple_of(start, own), own), :
                ]
    else:
        steps = list(range(0, fsdp, 2)) + list(range(1, fsdp, 2))
        for s in range(count):
            for index, d in enumerate(steps):
                start = lax.bitwise_xor(places[1], jnp.int32(d)) * (rows * count)
                start = start + lax.bitwise_xor(places[0], jnp.int32(s)) * rows
                out_refs[s][index * rows : (index + 1) * rows, :] = held[
                    pl.ds(pl.multiple_of(start, rows), rows), :
                ]


def weight_grad(places, pairs, order="ctx"):
    fsdp, count = lax.axis_size("fsdp"), lax.axis_size("ctx")
    tokens, rows = pairs[0][0].shape
    columns = [right.shape[1] for _, right in pairs]
    width = max(
        item for item in range(LANES, 6 * LANES + 1, LANES) if not any(c % item for c in columns)
    )
    chunks = [item // width for item in columns]
    firsts = [sum(chunks[:index]) for index in range(len(chunks))]
    pieces = count if order == "ctx" else 2
    right_spec = lambda first, chunk: pl.BlockSpec(
        (tokens, width), lambda step, places: (0, jnp.clip(step - first, 0, chunk - 1))
    )
    return pl.pallas_call(
        lambda *refs: weight_grad_kernel(
            *refs, chunks=chunks, fsdp=fsdp, count=count, order=order
        ),
        grid_spec=pltpu.PrefetchScalarGridSpec(
            num_scalar_prefetch=1,
            grid=(sum(chunks),),
            in_specs=[pl.BlockSpec((tokens, rows), lambda step, places: (0, 0))] * len(pairs)
            + [right_spec(first, chunk) for first, chunk in zip(firsts, chunks)],
            out_specs=[pl.BlockSpec((rows // pieces, width), lambda step, places: (0, step))]
            * pieces,
            scratch_shapes=[pltpu.VMEM((rows, width), jnp.bfloat16)],
        ),
        out_shape=[jax.ShapeDtypeStruct((rows // pieces, sum(columns)), jnp.bfloat16)] * pieces,
        name="weight_grad",
        compiler_params=pltpu.CompilerParams(vmem_limit_bytes=14 << 20),
    )(places, *[left for left, _ in pairs], *[right for _, right in pairs])


def halve(kept, brought):
    rows = kept.shape[0] // 2
    return [
        low(wide(kept[cut]) + wide(brought[cut]))
        for cut in (slice(0, rows), slice(rows, 2 * rows))
    ]


def sum_kernel(*refs):
    part_refs, (kept_ref, sent_ref) = refs[:-2], refs[-2:]
    total = part_refs[0][...].astype(jnp.float32) + part_refs[1][...].astype(jnp.float32)
    for first, second in zip(part_refs[2::2], part_refs[3::2]):
        total = total + (first[...].astype(jnp.float32) + second[...].astype(jnp.float32))
    rows = kept_ref.shape[0]
    kept_ref[...] = total[:rows].astype(kept_ref.dtype)
    sent_ref[...] = total[rows:].astype(sent_ref.dtype)


def sum_and_cut(parts):
    rows, columns = parts[0].shape
    return pl.pallas_call(
        sum_kernel,
        out_shape=[jax.ShapeDtypeStruct((rows // 2, columns), jnp.bfloat16)] * 2,
        name="sum_and_cut",
        compiler_params=pltpu.CompilerParams(vmem_limit_bytes=8 << 20),
    )(*parts)


def join_rows_kernel(ratio_ref, *refs):
    out_ref, start = refs[-1], 0
    for first, second in zip(refs[0:-1:2], refs[1:-1:2]):
        total = first[...].astype(jnp.float32) + second[...].astype(jnp.float32)
        out_ref[start : start + first.shape[0], :] = total * ratio_ref[0]
        start += first.shape[0]


def join_rows(pairs, ratio):
    rows = sum(first.shape[0] for first, _ in pairs)
    operands = [item for pair in pairs for item in pair]
    vmem = pl.BlockSpec(memory_space=pltpu.VMEM)
    return pl.pallas_call(
        join_rows_kernel,
        in_specs=[pl.BlockSpec(memory_space=pltpu.SMEM)] + [vmem] * len(operands),
        out_specs=vmem,
        out_shape=jax.ShapeDtypeStruct((rows, operands[0].shape[1]), jnp.float32),
        name="join_rows",
        compiler_params=pltpu.CompilerParams(vmem_limit_bytes=8 << 20),
    )(ratio.reshape(1), *operands)


def place_kernel(places, ratio_ref, *refs, kinds):
    part_refs, out_ref = refs[:-1], refs[-1]
    rows, columns = part_refs[0].shape
    pairs = columns // (kinds * LANES)
    ratio = ratio_ref[0]
    for s in range(len(part_refs)):
        start = lax.bitwise_xor(places[0], jnp.int32(s)) * rows
        start = pl.multiple_of(start, rows)
        for kind in range(kinds):
            for pair in range(pairs):
                source = (pair * kinds + kind) * LANES
                target = (kind * pairs + pair) * LANES
                out_ref[pl.ds(start, rows), target : target + LANES] = (
                    part_refs[s][:, source : source + LANES].astype(jnp.float32) * ratio
                )


def place_rows(places, parts, ratio, kinds=1):
    rows, columns = parts[0].shape
    block = pl.BlockSpec((rows, columns), lambda step, places: (0, 0))
    return pl.pallas_call(
        lambda *refs: place_kernel(*refs, kinds=kinds),
        grid_spec=pltpu.PrefetchScalarGridSpec(
            num_scalar_prefetch=1,
            grid=(1,),
            in_specs=[pl.BlockSpec(memory_space=pltpu.SMEM)] + [block] * len(parts),
            out_specs=pl.BlockSpec((rows * len(parts), columns), lambda step, places: (0, 0)),
        ),
        out_shape=jax.ShapeDtypeStruct((rows * len(parts), columns), jnp.float32),
        name="place_rows",
        compiler_params=pltpu.CompilerParams(vmem_limit_bytes=6 << 20),
    )(places, ratio.reshape(1), *parts)


def whole_local(
    hidden_in,
    valid_mask,
    teacher,
    qkv_weight,
    qv_bias,
    out_weight,
    out_bias,
    norm1_gain,
    norm1_shift,
    up_weight,
    up_bias,
    down_weight,
    down_bias,
    norm2_gain,
    norm2_shift,
):
    seq_count, block_len, model_width = hidden_in.shape
    ctx_count = lax.axis_size("ctx")
    place, depth, core = lax.axis_index("ctx"), lax.axis_index("fsdp"), lax.axis_index("tp")
    inner_width = qkv_weight.shape[2]
    hidden_width = up_weight.shape[1]
    row_count = seq_count * block_len
    shape = hidden_in.shape
    places = jnp.stack([place, depth])
    seat = jnp.stack([core, place])
    lane = jnp.arange(LANES, dtype=jnp.int32)
    chosen = wide(lane == place)
    seat_rows = wide(jnp.where(lane == 0, seat[:, None], 0))
    fsdp_count = lax.axis_size("fsdp")
    row = lambda values: values.reshape(1, -1)
    struct = jax.ShapeDtypeStruct
    part_rows = qkv_weight.shape[0] // ctx_count
    own_part = lambda weight: lax.dynamic_slice_in_dim(weight, place * part_rows, part_rows, 0)
    qkv_out = jnp.concatenate([by_pairs(qkv_weight), out_weight], axis=1)
    local_counts = jnp.sum(wide(valid_mask), axis=1)
    hidden_own, weight_own = together(own_half(hidden_in), own_part(qkv_out))
    weight_rows = swap_all(weight_own, "fsdp")
    hidden_half = deal(hidden_own, "ctx")
    count_rows = jnp.broadcast_to(
        jnp.pad(low(local_counts), (0, qkv_out.shape[1] - seq_count)), (16, qkv_out.shape[1])
    )
    full_bias = row(by_pairs(jnp.stack([qv_bias[0], jnp.zeros_like(qv_bias[0]), qv_bias[1]])))
    teacher_own = pick_halves(seat, teacher)
    (
        places,
        seat,
        chosen,
        seat_rows,
        weight_rows,
        hidden_half,
        count_rows,
        up_own,
        down_own,
        teacher_own,
        full_bias,
    ) = together(
        places,
        seat,
        chosen,
        seat_rows,
        weight_rows,
        hidden_half,
        count_rows,
        own_part(up_weight),
        own_part(down_weight),
        teacher_own,
        full_bias,
    )
    weight_part = stack_rows(weight_rows + [count_rows])
    weight_parts = [weight_part] + swap_all(weight_part, "ctx")
    up_rows = relay_all(up_own, "fsdp")
    flat_in = join_halves(seat * jnp.array([1, 0], jnp.int32), hidden_half).reshape(row_count, model_width)
    weight_parts, flat_in, up_rows, down_own = together(
        weight_parts, flat_in, up_rows, down_own
    )
    up_part = stack_rows(up_rows)
    up_parts = [up_part] + swap_all(up_part, "ctx")
    down_rows = [swap(down_own, "fsdp", 1), swap(down_own, "fsdp", 2)]
    counts = sum(wide(item[-16, :LANES]) for item in weight_parts)
    facts = jnp.sum(jnp.concatenate([(counts * chosen)[None], seat_rows]), axis=1)
    facts = facts.astype(jnp.int32)
    projected, full_qkv_out = gathered_layer(
        project_kernel,
        "project",
        block_len,
        places,
        flat_in,
        [full_bias],
        qkv_out,
        weight_parts,
        [3 * inner_width],
        fsdp_count,
    )
    projected, down_first = together(projected, down_rows[0])
    down_rows = [down_first, down_rows[1], swap(down_first, "fsdp", 2)]
    full_out = full_qkv_out[:, 3 * inner_width :]
    attended, log_total = attend(facts, projected, block_len)
    attended, up_parts, down_rows = together(attended, up_parts, down_rows)
    down_part = stack_rows(down_rows)
    down_parts = [down_part] + swap_all(down_part, "ctx")
    branch = rows_times(attended, full_out, block_len, True)
    normal1, scale1, normed1_low = by_rows(
        first_norm_kernel,
        "first_norm",
        block_len,
        [flat_in, branch, swap(branch, "tp", 1), row(out_bias), row(norm1_gain), row(norm1_shift)],
        [
            struct((row_count, model_width), jnp.float32),
            struct((row_count, 1), jnp.float32),
            struct((row_count, model_width), jnp.bfloat16),
        ],
    )
    active, slope, full_up = gathered_layer(
        up_kernel,
        "up",
        block_len,
        places,
        normed1_low,
        [row(up_bias)],
        up_weight,
        up_parts,
        [hidden_width, hidden_width],
        fsdp_count,
    )
    active, down_parts = together(active, down_parts)
    teacher_pieces = [teacher_own[s] for s in range(ctx_count)]
    teacher_pieces = teacher_pieces[:1] + swap_each(teacher_pieces, "ctx")
    branch, full_down = gathered_layer(
        down_kernel,
        "down",
        block_len,
        places,
        active,
        [],
        down_weight,
        down_parts,
        [model_width],
        fsdp_count,
    )
    branch, teacher_pieces = together(branch, teacher_pieces)
    teacher_half = stack_rows(teacher_pieces).reshape(ctx_count, block_len // 2, model_width)
    layer_half, grad_resid2, grad_resid2_low, stats2 = by_rows(
        second_norm_kernel,
        "second_norm",
        block_len,
        [
            normal1,
            row(norm1_gain),
            row(norm1_shift),
            branch,
            swap(branch, "tp", 1),
            row(down_bias),
            row(norm2_gain),
            row(norm2_shift),
            teacher_half,
            swap(teacher_half, "tp", 1),
        ],
        [
            struct(teacher_half.shape, jnp.bfloat16),
            struct((row_count, model_width), jnp.float32),
            struct((row_count, model_width), jnp.bfloat16),
        ],
        facts=facts,
        stats=model_width,
    )
    down_kept, down_sent = weight_grad(places, [(grad_resid2_low, active)], "fsdp")
    down_kept, down_sent, grad_resid2_low = together(down_kept, down_sent, grad_resid2_low)
    down_brought = swap(down_sent, "fsdp", 1)
    layer_pieces = [layer_half[s] for s in range(ctx_count)]
    layer_pieces = layer_pieces[:1] + swap_each(layer_pieces, "ctx")
    grad_pre, stats_up = wide_layer(
        grad_pre_kernel, "grad_pre", block_len, grad_resid2_low, full_down, [slope], 1, hidden_width
    )
    branch = rows_times(grad_pre, full_up, block_len, True)
    branch, grad_pre, layer_pieces = together(branch, grad_pre, layer_pieces)
    layer_out = join_halves(seat, stack_rows(layer_pieces).reshape(layer_half.shape))
    up_pieces = weight_grad(places, [(normed1_low, grad_pre)])
    up_brought = swap_each(up_pieces, "ctx")
    grad_resid1_low, grad_half, stats1 = by_rows(
        first_norm_back_kernel,
        "first_norm_back",
        block_len,
        [grad_resid2, branch, swap(branch, "tp", 1), normal1, scale1, row(norm1_gain)],
        [
            struct((row_count, model_width), jnp.bfloat16),
            struct(layer_half.shape, jnp.float32),
        ],
        facts=facts,
        stats=model_width,
    )
    out_kept, out_sent = weight_grad(places, [(grad_resid1_low, attended)], "fsdp")
    grad_attended = rows_times(grad_resid1_low, full_out, block_len, False)
    out_kept, out_sent, grad_attended, layer_out = together(
        out_kept, out_sent, grad_attended, layer_out
    )
    out_brought = swap(out_sent, "fsdp", 1)
    grad_qkv, stats_qkv = attend_back(facts, projected, grad_attended, log_total, block_len)
    grad_qkv, down_brought, out_brought = together(grad_qkv, down_brought, out_brought)
    local_count = jnp.broadcast_to(jnp.sum(local_counts), (1, LANES))
    small = pack(stats2, stats1, stats_up, stats_qkv, local_count)
    small_other = swap(small, "ctx", 1)
    last_pieces = weight_grad(places, [(flat_in, grad_qkv)])
    down_kept, down_sent = sum_and_cut([down_kept, down_brought])
    out_kept, out_sent = sum_and_cut([out_kept, out_brought])
    last_pieces, grad_qkv, down_sent, out_sent, small_other = together(
        last_pieces, grad_qkv, down_sent, out_sent, small_other
    )
    last_brought = swap_each(last_pieces, "ctx")
    down_brought = swap(down_sent, "fsdp", 2)
    mine, other = input_back(facts, grad_qkv, full_qkv_out, block_len)
    up_kept, up_sent = sum_and_cut([up_pieces[0]] + up_brought)
    small = small + small_other
    small_other = swap(small, "ctx", 2)
    last_brought, mine, other, up_sent, out_sent, small, small_other = together(
        last_brought, mine, other, up_sent, out_sent, small, small_other
    )
    last_kept, last_sent = sum_and_cut([last_pieces[0]] + last_brought)
    last_sent, other, down_brought, up_sent, out_sent, small, small_other = together(
        last_sent, other, down_brought, up_sent, out_sent, small, small_other
    )
    last_brought = swap(last_sent, "fsdp", 1)
    other = swap(other, "tp", 1)
    cut = down_kept.shape[0] // 2
    owned_down = [
        low(wide(down_kept[span]) + wide(down_brought[span]))
        for span in (slice(0, cut), slice(cut, 2 * cut))
    ]
    down_other = [swap(owned_down[0], "ctx", 1), swap(owned_down[1], "ctx", 2)]
    small = small + small_other
    small_other = swap(small, "fsdp", 1)
    last_brought, other, up_sent, out_sent, small, small_other = together(
        last_brought, other, up_sent, out_sent, small, small_other
    )
    last_kept, last_sent = sum_and_cut([last_kept, last_brought])
    half = low(grad_half + (wide(mine) + wide(other)))
    small = small + small_other
    last_sent, half, up_sent, out_sent, small = together(
        last_sent, half, up_sent, out_sent, small
    )
    last_brought = swap(last_sent, "fsdp", 2)
    up_brought = swap(up_sent, "fsdp", 1)
    half_pieces = [half[s] for s in range(ctx_count)]
    half_brought = [half_pieces[0], swap(half_pieces[1], "ctx", 1)]
    small_other = swap(small, "fsdp", 2)
    last_brought, up_brought, down_other, out_sent, small_other, half_pieces = together(
        last_brought, up_brought, down_other, out_sent, small_other, half_pieces
    )
    part = low(wide(last_kept) + wide(last_brought))
    up_kept, up_sent = sum_and_cut([up_kept, up_brought])
    owned_down = [low(wide(mine) + wide(other)) for mine, other in zip(owned_down, down_other)]
    small = small + small_other
    part, up_sent, owned_down, out_sent, small, half_pieces = together(
        part, up_sent, owned_down, out_sent, small, half_pieces
    )
    out_brought = swap(out_sent, "fsdp", 2)
    shared = [part, swap(part, "ctx", 1), swap(part, "ctx", 2)]
    up_brought = swap(up_sent, "fsdp", 2)
    down_other = [swap(owned_down[0], "ctx", 2), swap(owned_down[1], "ctx", 1)]
    shared, up_brought, out_brought, half_pieces, down_other = together(
        shared, up_brought, out_brought, half_pieces, down_other
    )
    up_part = low(wide(up_kept) + wide(up_brought))
    owned_out = low(wide(out_kept) + wide(out_brought))
    up_part, owned_out, shared, half_pieces = together(up_part, owned_out, shared, half_pieces)
    shared = shared + [swap(shared[1], "ctx", 2)]
    up_shared = [up_part, swap(up_part, "ctx", 1), swap(up_part, "ctx", 2)]
    half_brought = half_brought + [swap(half_pieces[s], "ctx", s) for s in range(2, ctx_count)]
    up_shared, shared, half_brought, owned_out = together(
        up_shared, shared, half_brought, owned_out
    )
    up_shared = up_shared + [swap(up_shared[1], "ctx", 2)]
    input_half = stack_rows(half_brought).reshape(half.shape)
    out_other = swap(owned_out, "ctx", 1)
    owned_out, out_other, input_half, up_shared = together(
        owned_out, out_other, input_half, up_shared
    )
    owned_out = low(wide(owned_out) + wide(out_other))
    out_other = swap(owned_out, "ctx", 2)
    at = 7 + -(-hidden_width // model_width)
    last_row = at + -(-3 * inner_width // model_width)
    counted = small[last_row : last_row + 1, :1]
    ratio = float(row_count * ctx_count * fsdp_count) / counted
    loss = jnp.sum(small[3:4], axis=1, keepdims=True) / (counted * model_width)
    scaled = small * ratio
    input_grad = join_halves(seat, input_half, ratio, jnp.float32)
    owned_qkv = place_rows(places, shared, ratio, 3)
    owned_down = join_rows(list(zip(owned_down, down_other)), ratio)
    owned_up = place_rows(places, up_shared, ratio)
    owned_qkv, owned_up, owned_down, out_other, input_grad, scaled = together(
        owned_qkv, owned_up, owned_down, out_other, input_grad, scaled
    )
    owned_qkv = owned_qkv.reshape(qkv_weight.shape)
    owned_out = (wide(owned_out) + wide(out_other)) * ratio
    grad_up_bias = scaled[7:at].reshape(-1)[:hidden_width]
    grad_qv_bias = by_kinds(
        scaled[at : at + -(-3 * inner_width // model_width)].reshape(-1)[: 3 * inner_width]
    )[0::2]
    return (
        layer_out,
        input_grad,
        loss.reshape(()),
        owned_qkv,
        grad_qv_bias,
        owned_out,
        scaled[4],
        scaled[5],
        scaled[6],
        owned_up,
        grad_up_bias,
        owned_down,
        scaled[0],
        scaled[1],
        scaled[2],
    )


def spread_local(
    hidden_in,
    valid_mask,
    teacher,
    qkv_weight,
    qv_bias,
    out_weight,
    out_bias,
    norm1_gain,
    norm1_shift,
    up_weight,
    up_bias,
    down_weight,
    down_bias,
    norm2_gain,
    norm2_shift,
):
    seq_count, block_len, model_width = hidden_in.shape
    ctx_count = lax.axis_size("ctx")
    ctx_place = lax.axis_index("ctx")
    key_span = 2 * block_len
    seq_length = block_len * ctx_count
    row_count = seq_count * block_len
    scaling = HEAD_DIM ** (-0.5)
    full_qkv, full_out, full_up, full_down = (
        lax.all_gather(qkv_weight, "fsdp", axis=0, tiled=True),
        lax.all_gather(out_weight, "fsdp", axis=0, tiled=True),
        lax.all_gather(up_weight, "fsdp", axis=0, tiled=True),
        lax.all_gather(down_weight, "fsdp", axis=0, tiled=True),
    )
    inner_width = full_qkv.shape[2]
    head_count = inner_width // HEAD_DIM
    flat_in = hidden_in.reshape(row_count, model_width)
    full_bias = jnp.stack([qv_bias[0], jnp.zeros_like(qv_bias[0]), qv_bias[1]])
    projected = (
        jnp.einsum("td,dje->tje", flat_in, full_qkv, preferred_element_type=jnp.float32) + full_bias
    ).astype(jnp.bfloat16)
    queries = projected[:, 0].reshape(seq_count, block_len, inner_width)
    key_own = projected[:, 1].reshape(seq_count, block_len, inner_width)
    value_own = projected[:, 2].reshape(seq_count, block_len, inner_width)
    keep_own = valid_mask.astype(jnp.bfloat16)
    keys_all, values_all, keep_all = (
        lax.all_gather(key_own, "ctx", axis=1, tiled=True),
        lax.all_gather(value_own, "ctx", axis=1, tiled=True),
        lax.all_gather(keep_own, "ctx", axis=1, tiled=True),
    )
    query_heads = split_heads(queries)
    seen_limit = (ctx_place + 1) * block_len
    trip_count = ctx_place // 2 + 1
    offsets = jnp.arange(key_span, dtype=jnp.int32)

    def key_block(block_index):
        key_start = block_index * key_span
        key_heads = split_heads(lax.dynamic_slice_in_dim(keys_all, key_start, key_span, 1))
        value_heads = split_heads(lax.dynamic_slice_in_dim(values_all, key_start, key_span, 1))
        live_keys = lax.dynamic_slice_in_dim(keep_all, key_start, key_span, 1) > 0.5
        allowed = jnp.logical_and(live_keys, (key_start + offsets)[None, :] < seen_limit)
        return (key_heads, value_heads, allowed[:, None, None, :])

    def attend_step(block_index, carried):
        run_top, run_total, gathered = carried
        key_heads, value_heads, allowed = key_block(block_index)
        raw_scores = scores_of(query_heads, key_heads, allowed, scaling)
        new_top = jnp.maximum(run_top, jnp.max(raw_scores, axis=-1))
        shrink = jnp.exp(run_top - new_top)
        weights_now = jnp.exp(raw_scores - new_top[..., None])
        run_total = run_total * shrink + jnp.sum(weights_now, axis=-1)
        gathered = gathered * jnp.swapaxes(shrink, 1, 2)[..., None] + jnp.einsum(
            "shqk,skhd->sqhd",
            weights_now.astype(jnp.bfloat16),
            value_heads,
            preferred_element_type=jnp.float32,
        )
        return (new_top, run_total, gathered)

    start_top = jnp.full((seq_count, head_count, block_len), MASKED, jnp.float32)
    empty_heads = jnp.zeros((seq_count, block_len, head_count, HEAD_DIM), jnp.float32)
    run_top, run_total, gathered = lax.fori_loop(
        0, trip_count, attend_step, (start_top, jnp.zeros_like(start_top), empty_heads)
    )
    log_total = run_top + jnp.log(run_total)
    attended_exact = gathered / jnp.swapaxes(run_total, 1, 2)[..., None]
    attended = attended_exact.astype(jnp.bfloat16).reshape(row_count, inner_width)
    attn_branch = lax.psum(
        jnp.einsum("te,de->td", attended, full_out, preferred_element_type=jnp.float32).astype(
            jnp.bfloat16
        ),
        "tp",
    ).astype(jnp.float32)
    resid1 = flat_in.astype(jnp.float32) + attn_branch + out_bias
    normed1, norm1_back = jax.vjp(layer_norm, resid1, norm1_gain, norm1_shift)
    normed1_low = normed1.astype(jnp.bfloat16)
    pre_act = jnp.dot(normed1_low, full_up, preferred_element_type=jnp.float32) + up_bias
    active, gelu_back = jax.vjp(gelu_exact, pre_act)
    active = active.astype(jnp.bfloat16)
    ffn_branch = lax.psum(
        jnp.einsum("tf,df->td", active, full_down, preferred_element_type=jnp.float32).astype(
            jnp.bfloat16
        ),
        "tp",
    ).astype(jnp.float32)
    resid2 = normed1 + ffn_branch + down_bias
    output, norm2_back = jax.vjp(layer_norm, resid2, norm2_gain, norm2_shift)
    layer_out = output.astype(jnp.bfloat16).reshape(seq_count, block_len, model_width)
    keep_rows = valid_mask.reshape(row_count, 1).astype(jnp.float32)
    residue = (output - teacher.reshape(row_count, model_width).astype(jnp.float32)) * keep_rows
    squared = jnp.sum(residue * residue)
    counted = jnp.sum(keep_rows)
    grad_resid2, grad_gain2, grad_shift2 = norm2_back(residue)
    grad_down_bias = jnp.sum(grad_resid2, axis=0)
    grad_resid2_low = grad_resid2.astype(jnp.bfloat16)
    grad_active = jnp.dot(grad_resid2_low, full_down, preferred_element_type=jnp.float32)
    grad_down_weight = jnp.einsum(
        "td,tf->df", grad_resid2_low, active, preferred_element_type=jnp.float32
    )
    grad_pre = gelu_back(grad_active)[0].astype(jnp.bfloat16)
    grad_up_bias = jnp.sum(grad_pre.astype(jnp.float32), axis=0)
    grad_up_weight = jnp.einsum(
        "td,tf->df", normed1_low, grad_pre, preferred_element_type=jnp.float32
    )
    ffn_input_grad = lax.psum(
        jnp.einsum("tf,df->td", grad_pre, full_up, preferred_element_type=jnp.float32).astype(
            jnp.bfloat16
        ),
        "tp",
    ).astype(jnp.float32)
    grad_normed1 = grad_resid2 + ffn_input_grad
    grad_resid1, grad_gain1, grad_shift1 = norm1_back(grad_normed1)
    grad_out_bias = jnp.sum(grad_resid1, axis=0)
    grad_resid1_low = grad_resid1.astype(jnp.bfloat16)
    grad_mixed = jnp.dot(grad_resid1_low, full_out, preferred_element_type=jnp.float32)
    grad_out_weight = jnp.einsum(
        "td,te->de", grad_resid1_low, attended, preferred_element_type=jnp.float32
    )
    grad_attended = grad_mixed.astype(jnp.bfloat16).reshape(
        seq_count, block_len, head_count, HEAD_DIM
    )
    delta = jnp.swapaxes(jnp.sum(grad_attended.astype(jnp.float32) * attended_exact, axis=-1), 1, 2)

    def query_grads(block_index):
        key_heads, value_heads, allowed = key_block(block_index)
        prob_rows = jnp.exp(
            scores_of(query_heads, key_heads, allowed, scaling) - log_total[..., None]
        )
        push = jnp.einsum(
            "sqhd,skhd->shqk", grad_attended, value_heads, preferred_element_type=jnp.float32
        )
        slope = (prob_rows * (push - delta[..., None])).astype(jnp.bfloat16)
        grad_part = (
            jnp.einsum("shqk,skhd->sqhd", slope, key_heads, preferred_element_type=jnp.float32)
            * scaling
        )
        return (prob_rows, slope, grad_part)

    def back_step(block_index, carried):
        grad_query, spread = carried
        prob_rows, slope, grad_part = query_grads(block_index)
        grad_key = (
            jnp.einsum("shqk,sqhd->skhd", slope, query_heads, preferred_element_type=jnp.float32)
            * scaling
        )
        grad_value = jnp.einsum(
            "shqk,sqhd->skhd",
            prob_rows.astype(jnp.bfloat16),
            grad_attended,
            preferred_element_type=jnp.float32,
        )
        piece = jnp.stack(
            [
                grad_key.reshape(seq_count, key_span, inner_width),
                grad_value.reshape(seq_count, key_span, inner_width),
            ],
            axis=2,
        )
        spread = lax.dynamic_update_slice_in_dim(spread, piece, block_index * key_span, 1)
        return (grad_query + grad_part, spread)

    spread_start = jnp.zeros((seq_count, seq_length, 2, inner_width), jnp.float32)
    grad_query, spread = lax.fori_loop(0, trip_count, back_step, (empty_heads, spread_start))
    own_grads = lax.psum_scatter(
        spread.astype(jnp.bfloat16), "ctx", scatter_dimension=1, tiled=True
    ).astype(jnp.float32)
    grad_key_own = own_grads[:, :, 0]
    grad_value_own = own_grads[:, :, 1]
    grad_qkv = jnp.stack(
        [
            grad_query.reshape(row_count, inner_width),
            grad_key_own.reshape(row_count, inner_width),
            grad_value_own.reshape(row_count, inner_width),
        ],
        axis=1,
    ).astype(jnp.bfloat16)
    grad_qv_bias = jnp.sum(grad_qkv[:, 0::2].astype(jnp.float32), axis=0)
    grad_qkv_weight = jnp.einsum(
        "td,tje->dje", flat_in, grad_qkv, preferred_element_type=jnp.float32
    )
    input_part = lax.psum(
        jnp.einsum("tje,dje->td", grad_qkv, full_qkv, preferred_element_type=jnp.float32).astype(
            jnp.bfloat16
        ),
        "tp",
    ).astype(jnp.float32)
    grad_input = grad_resid1 + input_part
    vectors = jnp.stack(
        [grad_out_bias, grad_gain1, grad_shift1, grad_down_bias, grad_gain2, grad_shift2]
    )
    squared, counted, vectors, grad_qv_bias, grad_up_bias = lax.psum(
        (squared, counted, vectors, grad_qv_bias, grad_up_bias), ("fsdp", "ctx")
    )
    local_grads = (grad_qkv_weight, grad_out_weight, grad_up_weight, grad_down_weight)
    owned = (
        lax.psum_scatter(
            local_grads[0].astype(jnp.bfloat16), "fsdp", scatter_dimension=0, tiled=True
        ).astype(jnp.float32),
        lax.psum_scatter(
            local_grads[1].astype(jnp.bfloat16), "fsdp", scatter_dimension=0, tiled=True
        ).astype(jnp.float32),
        lax.psum_scatter(
            local_grads[2].astype(jnp.bfloat16), "fsdp", scatter_dimension=0, tiled=True
        ).astype(jnp.float32),
        lax.psum_scatter(
            local_grads[3].astype(jnp.bfloat16), "fsdp", scatter_dimension=0, tiled=True
        ).astype(jnp.float32),
    )
    owned = (
        lax.psum(owned[0].astype(jnp.bfloat16), "ctx").astype(jnp.float32),
        lax.psum(owned[1].astype(jnp.bfloat16), "ctx").astype(jnp.float32),
        lax.psum(owned[2].astype(jnp.bfloat16), "ctx").astype(jnp.float32),
        lax.psum(owned[3].astype(jnp.bfloat16), "ctx").astype(jnp.float32),
    )
    token_total = float(seq_count * seq_length * lax.axis_size("fsdp"))
    ratio = token_total / counted
    loss = squared / (counted * model_width)
    input_grad = (grad_input * ratio).reshape(seq_count, block_len, model_width)
    return (
        layer_out,
        input_grad,
        loss,
        owned[0] * ratio,
        grad_qv_bias * ratio,
        owned[1] * ratio,
        vectors[0] * ratio,
        vectors[1] * ratio,
        vectors[2] * ratio,
        owned[2] * ratio,
        grad_up_bias * ratio,
        owned[3] * ratio,
        vectors[3] * ratio,
        vectors[4] * ratio,
        vectors[5] * ratio,
    )


def local(hidden_in, *others):
    seq_count, block_len, model_width = hidden_in.shape
    ctx_count, fsdp_count = lax.axis_size("ctx"), lax.axis_size("fsdp")
    rows, inner_width = others[2].shape[0], others[2].shape[2]
    whole = (
        seq_count == ctx_count
        and ctx_count & (ctx_count - 1) == 0
        and fsdp_count == 4
        and lax.axis_size("tp") == 2
        and block_len % LANES == 0
        and others[5].shape[0] >= inner_width
        and inner_width % LANES == 0
        and rows % (16 * ctx_count) == 0
    )
    return (whole_local if whole else spread_local)(hidden_in, *others)


def solution(mesh):
    in_specs = (
        P("fsdp", "ctx", None),
        P("fsdp", "ctx"),
        P("fsdp", "ctx", None),
        P("fsdp", None, "tp"),
        P(None, "tp"),
        P("fsdp", "tp"),
        P(),
        P(),
        P(),
        P("fsdp", "tp"),
        P("tp"),
        P("fsdp", "tp"),
        P(),
        P(),
        P(),
    )
    out_specs = (
        P("fsdp", "ctx", None),
        P("fsdp", "ctx", None),
        P(),
        P("fsdp", None, "tp"),
        P(None, "tp"),
        P("fsdp", "tp"),
        P(),
        P(),
        P(),
        P("fsdp", "tp"),
        P("tp"),
        P("fsdp", "tp"),
        P(),
        P(),
        P(),
    )
    return jax.shard_map(local, mesh=mesh, in_specs=in_specs, out_specs=out_specs, check_vma=False)
```
